32 devices in a mesh: dp: 8 (over z, y), row: 2 (over x), col: 2 (over core).
Axes of the slice: x: 2, y: 2, z: 4, core: 2. Of those that a mesh axis runs over, the one named last changes fastest.
Arguments:
- tokens: bfloat16 [12288, 1024], P('dp', 'row'), may hold values from -6 to 6
- gain_attn: float32 [1024], replicated, may hold values from 0.5 to 1.5
- w_qkv: float32 [1024, 16, 192], P('row', 'col'), may hold values from -0.1875 to 0.1875
- w_out: float32 [1024, 1024], P('col', 'row'), may hold values from -3 to 3
- gain_mlp: float32 [1024], replicated, may hold values from 0.5 to 1.5
- w_in: float32 [1024, 2, 2624], P('row', None, 'col'), may hold values from -0.1875 to 0.1875
- w_down: float32 [2624, 1024], P('col', 'row'), may hold values from -0.125 to 0.125
- cotangent: bfloat16 [12288, 1024], P('dp', 'row'), may hold values from -6 to 6
- seq_lengths: int32 [16], replicated, may hold values from 256 to 1024, as said below
- seq_offsets: int32 [16], replicated, may hold values from 0 to 11264, as said below
- deal: int32 [16], replicated, may hold values from 0 to 15, as said below
Outputs:
- layer_out: bfloat16 [12288, 1024], P('dp', 'row')
- tokens_grad: bfloat16 [12288, 1024], P('dp', 'row')
- gain_attn_grad: float32 [1024], P(('dp', 'row'))
- w_qkv_grad: float32 [1024, 16, 192], P(('dp', 'row'), 'col')
- w_out_grad: float32 [1024, 1024], P('col', ('dp', 'row'))
- gain_mlp_grad: float32 [1024], P(('dp', 'row'))
- w_in_grad: float32 [1024, 2, 2624], P(('dp', 'row'), None, 'col')
- w_down_grad: float32 [2624, 1024], P('col', ('dp', 'row'))
The draws below stay inside these ranges and needn't reach their ends.
Inputs may be any that keep to these rules, and one draw needn't show every extreme that they name: `seq_lengths`: each group holds one sequence of 1024 tokens, its others have at most half of 1024, and some group fills all 1536 slots. Sequence 16 - 1 has 1024 tokens. Sequences 0 to 14 lie end to end in index order from place 0: seq_offsets[s] is the sum of the lengths of sequences 0 to s - 1. Sequence 16 - 1 ends at the last token place; places between belong to no sequence. `deal`: A permutation of the 16 sequences.
All inputs are finite; a program needn't handle non-finite values.
Results may differ from the reference program's by a relative error of at most 0.017.
Values may be sent and summed in bfloat16 or wider, within the bound.
No kernel may reach another device: no remote copies, remote signals or barrier semaphores. Data moves between devices by JAX's collectives and lax.ppermute only.
A program may use at most 192 MiB of HBM per device.

```python
import math
import jax
import jax.numpy as jnp
from jax import lax

D = 1024
HEADS = 16
HEAD_DIM = 64
FF = 2624
SEQ_MAX = 1024
SEQ_MIN = 256
SEQ_GRP = 2
CAP = 1536
NSEQ = 16
TOKENS = 12288


def packing(key):
    every_count = NSEQ
    group_count = every_count // SEQ_GRP
    dealing = jax.random.permutation(jax.random.fold_in(key, 7), every_count).astype(jnp.int32)
    shorter = jax.random.randint(jax.random.fold_in(key, 11), (group_count, SEQ_GRP), SEQ_MIN, SEQ_MAX // 2 + 1, dtype=jnp.int32)
    longest = jax.random.randint(jax.random.fold_in(key, 13), (group_count, 1), 0, SEQ_GRP, dtype=jnp.int32)
    fullest = jax.random.randint(jax.random.fold_in(key, 17), (), 0, group_count, dtype=jnp.int32)
    members = jnp.arange(SEQ_GRP, dtype=jnp.int32)[None, :]
    owners = jnp.arange(group_count, dtype=jnp.int32)[:, None]
    shorter = jnp.where(owners == fullest, SEQ_MAX // 2, shorter)
    dealt = jnp.where(members == longest, SEQ_MAX, shorter).reshape(every_count)
    spots = jnp.arange(every_count, dtype=jnp.int32)
    long_spot = longest[0, 0]
    last_spot = jnp.sum(jnp.where(dealing == every_count - 1, spots, 0))
    moved = jnp.sum(jnp.where(spots == long_spot, dealing, 0))
    dealing = jnp.where(spots == long_spot, every_count - 1, jnp.where(spots == last_spot, moved, dealing)).astype(jnp.int32)
    lengths = jnp.zeros((every_count,), jnp.int32).at[dealing].set(dealt)
    offsets = jnp.cumsum(lengths) - lengths
    offsets = jnp.where(spots == every_count - 1, TOKENS - SEQ_MAX, offsets)
    return (lengths.astype(jnp.int32), offsets.astype(jnp.int32), dealing)


def draw_seq_lengths(key, part):
    return packing(key)[0]


def draw_seq_offsets(key, part):
    return packing(key)[1]


def draw_deal(key, part):
    return packing(key)[2]


def steps_of(key, shape, shards, smallest, high):
    def one(dim, blocks):
        steps = jax.random.uniform(jax.random.fold_in(jax.random.fold_in(key, 6), dim), (blocks,), jnp.float32, smallest / len(shards), high / len(shards))
        return jnp.repeat(jnp.exp(steps), shape[dim] // blocks).reshape((-1,) + (1,) * (len(shape) - dim - 1))

    loudness = one(*shards[0])
    for cut in shards[1:]:
        loudness = loudness * one(*cut)
    return loudness


def gaussian(stream_key, extent, scale, limit, split=(), kind=jnp.bfloat16):
    values = scale * jax.random.normal(stream_key, extent, jnp.float32)
    if split:
        values = values * steps_of(stream_key, extent, split, -0.22, 0.18)
    return jnp.clip(values, -limit, limit).astype(kind)


def setup_inputs(seed: int = 0) -> dict:
    key_of = jax.random.split(jax.random.key(seed), 12)
    tokens = gaussian(key_of[0], (TOKENS, D), 1.0, 6.0, ((0, 8), (1, 2)))
    gain_attn = jnp.clip(1.0 + 0.1 * jax.random.normal(key_of[1], (D,), jnp.float32), 0.5, 1.5)
    w_qkv = gaussian(key_of[2], (D, HEADS, 3 * HEAD_DIM), D ** -0.5, 0.1875, ((0, 2), (1, 2)), jnp.float32)
    w_out = gaussian(key_of[3], (D, D), (max(D * 4 // SEQ_MAX, 1)) ** -0.5, 3.0, ((0, 2), (1, 2)), jnp.float32)
    gain_mlp = jnp.clip(1.0 + 0.1 * jax.random.normal(key_of[4], (D,), jnp.float32), 0.5, 1.5)
    w_in = gaussian(key_of[5], (D, 2, FF), D ** -0.5, 0.1875, ((0, 2), (2, 2)), jnp.float32)
    w_down = gaussian(key_of[6], (FF, D), FF ** -0.5, 0.125, ((0, 2), (1, 2)), jnp.float32)
    cotangent = gaussian(key_of[7], (TOKENS, D), 1.0, 6.0, ((0, 8), (1, 2)))
    seq_lengths = draw_seq_lengths(jax.random.fold_in(key_of[11], 71), 0)
    seq_offsets = draw_seq_offsets(jax.random.fold_in(key_of[11], 71), 0)
    deal = draw_deal(jax.random.fold_in(key_of[11], 71), 0)
    return {"tokens": tokens, "gain_attn": gain_attn, "w_qkv": w_qkv, "w_out": w_out, "gain_mlp": gain_mlp, "w_in": w_in, "w_down": w_down, "cotangent": cotangent, "seq_lengths": seq_lengths, "seq_offsets": seq_offsets, "deal": deal}


epsilon = 1e-05
rope_base = 160000.0
highest = lax.Precision.HIGHEST

@jax.custom_vjp
def low(v):
    return lax.optimization_barrier(v.astype(jnp.bfloat16)).astype(jnp.float32)

@jax.custom_vjp
def low_back(v):
    return v

def low_keep(v):
    return (low(v), None)

def low_pass(kept, grad):
    return (grad,)

def back_keep(v):
    return (v, None)

def back_low(kept, grad):
    return (low(grad),)
low.defvjp(low_keep, low_pass)
low_back.defvjp(back_keep, back_low)

def slot_table(seq_lengths, seq_offsets, deal, group_index):
    members = lax.dynamic_slice_in_dim(deal, (group_index * SEQ_GRP).astype(jnp.int32), SEQ_GRP)
    every = jnp.arange(deal.shape[0], dtype=jnp.int32)
    matches = every[None, :] == members[:, None]
    member_lengths = lax.optimization_barrier(jnp.sum(jnp.where(matches, seq_lengths[None, :], 0), axis=1))
    member_offsets = lax.optimization_barrier(jnp.sum(jnp.where(matches, seq_offsets[None, :], 0), axis=1))
    member_starts = jnp.cumsum(member_lengths) - member_lengths
    slots = jnp.arange(CAP, dtype=jnp.int32)
    inside = (slots[:, None] >= member_starts[None, :]) & (slots[:, None] < (member_starts + member_lengths)[None, :])
    live = jnp.any(inside, axis=1)
    places = slots - lax.optimization_barrier(jnp.sum(jnp.where(inside, member_starts[None, :], 0), axis=1))
    segment = lax.optimization_barrier(jnp.sum(jnp.where(inside, jnp.arange(SEQ_GRP, dtype=jnp.int32)[None, :], 0), axis=1)) + jnp.where(live, 0, SEQ_GRP)
    source = jnp.where(live, lax.optimization_barrier(jnp.sum(jnp.where(inside, member_offsets[None, :], 0), axis=1)) + places, -1)
    return (source.astype(jnp.int32), places.astype(jnp.int32), segment.astype(jnp.int32))

def rope_tables(places, head_width):
    freq = rope_base ** (-(jnp.arange(0, head_width, 2, dtype=jnp.float32) / head_width))
    angle = places.astype(jnp.float32)[:, None, None] * freq[None, None, :]
    return (jnp.cos(angle), jnp.sin(angle))

def turn(part, cosine, sine):
    half = part.shape[-1] // 2
    first_half = part[..., :half]
    second_half = part[..., half:]
    return jnp.concatenate([first_half * cosine - second_half * sine, second_half * cosine + first_half * sine], axis=-1)

def layer_norm(value):
    center = value - lax.optimization_barrier(jnp.mean(value, axis=-1, keepdims=True))
    return center * lax.rsqrt(lax.optimization_barrier(jnp.mean(center * center, axis=-1, keepdims=True)) + epsilon)

def attend_head(triple, segment):
    head_width = triple.shape[-1] // 3
    query = triple[:, :head_width]
    keys = triple[:, head_width:2 * head_width]
    values = triple[:, 2 * head_width:]
    scores = low_back(jnp.dot(query, keys.T, precision=highest) * (1.0 / math.sqrt(head_width)))
    same_seq = segment[:, None] == segment[None, :]
    scores = jnp.where(same_seq, scores, -1e+30)
    top_score = lax.optimization_barrier(jnp.max(scores, axis=-1, keepdims=True))
    raised = jnp.exp(scores - top_score)
    probs = low(raised / lax.optimization_barrier(jnp.sum(raised, axis=-1, keepdims=True)))
    return jnp.dot(probs, values, precision=highest)

def group_forward(block, gain_attn, w_qkv, w_out, gain_mlp, w_in, w_down, places, segment):
    head_width = w_qkv.shape[2] // 3
    normed = low(layer_norm(block) * gain_attn)
    triples = low_back(jnp.einsum('td,dhe->the', normed, low(w_qkv), precision=highest))
    cosine, sine = rope_tables(places, head_width)
    turned = low(jnp.concatenate([turn(triples[..., :head_width], cosine, sine), turn(triples[..., head_width:2 * head_width], cosine, sine), triples[..., 2 * head_width:]], axis=-1))
    attend = jax.checkpoint(lambda triple: attend_head(triple, segment))
    attended = lax.map(attend, jnp.swapaxes(turned, 0, 1))
    attended = low_back(low(jnp.swapaxes(attended, 0, 1).reshape(block.shape[0], -1)))
    mixed = block + low_back(jnp.dot(attended, low(w_out), precision=highest))
    normed_mlp = low(layer_norm(mixed) * gain_mlp)
    both = low_back(jnp.einsum('td,dgf->tgf', normed_mlp, low(w_in), precision=highest))
    hidden = low(jax.nn.gelu(both[:, 0], approximate=False) * both[:, 1])
    return mixed + low_back(jnp.dot(hidden, low(w_down), precision=highest))

def reference(tokens, gain_attn, w_qkv, w_out, gain_mlp, w_in, w_down, cotangent, seq_lengths, seq_offsets, deal):
    params = tuple((weight.astype(jnp.float32) for weight in (gain_attn, w_qkv, w_out, gain_mlp, w_in, w_down)))
    group_count = deal.shape[0] // SEQ_GRP

    def one_group(totals, group_index):
        source, places, segment = slot_table(seq_lengths, seq_offsets, deal, group_index)
        live = (source >= 0)[:, None]
        picked = jnp.clip(source, 0, tokens.shape[0] - 1).astype(jnp.int32)
        block = jnp.where(live, tokens[picked].astype(jnp.float32), 0.0)
        grad_block = jnp.where(live, cotangent[picked].astype(jnp.float32), 0.0)

        def forward(value, *weights):
            return group_forward(value, *weights, places, segment)
        result, pullback = jax.vjp(forward, block, *params)
        grads = pullback(grad_block)
        totals = tuple((total + grad for total, grad in zip(totals, grads[1:])))
        return (totals, (result, grads[0], source))
    zeros = tuple((jnp.zeros_like(weight) for weight in params))
    totals, (results, input_grads, sources) = lax.scan(one_group, zeros, jnp.arange(group_count, dtype=jnp.int32))
    flat = sources.reshape(-1)
    target = jnp.where(flat >= 0, flat, tokens.shape[0]).astype(jnp.int32)
    layer_out = jnp.zeros(tokens.shape, jnp.float32).at[target].set(results.reshape(-1, tokens.shape[1]), mode='drop')
    tokens_grad = jnp.zeros(tokens.shape, jnp.float32).at[target].set(input_grads.reshape(-1, tokens.shape[1]), mode='drop')
    return (layer_out.astype(jnp.bfloat16), tokens_grad.astype(jnp.bfloat16), totals[0], totals[1], totals[2], totals[3], totals[4], totals[5])
```

```python
import functools
import math

import jax
import jax.numpy as jnp
from jax import lax
from jax.experimental import pallas as pl
from jax.experimental.pallas import tpu as pltpu
from jax.sharding import PartitionSpec as P

LONGEST = 1024
BQ = 256
BK = 256
NEG = -1e30
FAR = 1e30
epsilon = 1e-05
rope_base = 160000.0
bf16 = jnp.bfloat16
f32 = jnp.float32
SWAP = [(0, 1), (1, 0)]


def nt(a, b):
    return lax.dot_general(a, b, (((1,), (1,)), ((), ())), preferred_element_type=f32)


def tn(a, b):
    return lax.dot_general(a, b, (((0,), (0,)), ((), ())), preferred_element_type=f32)


def nn(a, b):
    return jnp.dot(a, b, preferred_element_type=f32)


def half_mask(width, heads, head):
    lane = lax.broadcasted_iota(jnp.int32, (1, width), 1)
    half = width // 2
    lane = jnp.where(lane >= half, lane - half, lane)
    step = half // heads
    return (lane >= head * step) & (lane < (head + 1) * step)


def whole_mask(width, heads, head):
    lane = lax.broadcasted_iota(jnp.int32, (1, width), 1)
    step = width // heads
    return (lane >= head * step) & (lane < (head + 1) * step)


def stack_heads(block, heads, mask_of):
    zero = jnp.zeros_like(block)
    width = block.shape[1]
    return jnp.concatenate(
        [jnp.where(mask_of(width, heads, h), block, zero) for h in range(heads)], axis=0
    )


def same_segment(key_seg, query_seg, heads):
    tile = key_seg
    lanes = query_seg.shape[1]
    if lanes > tile.shape[1]:
        tile = jnp.concatenate([tile] * (lanes // tile.shape[1]), axis=1)
    same = tile == query_seg
    return jnp.concatenate([same] * heads, axis=1) if heads > 1 else same


def forward_kernel(heads, sets, final, bounds, *refs):
    refs = list(refs)
    q_ref, sq_ref = refs[:2]
    kv_refs = refs[2 : 2 + sets]
    sk_refs = refs[2 + sets : 2 + 2 * sets]
    rest = refs[2 + 2 * sets :]
    if final:
        acc_in, ml_in, o_ref, lse_ref = rest[:4]
        acc, m_ref, l_ref = rest[4:7]
        vt_refs = rest[7:]
    else:
        acc, ml_ref = rest[:2]
        m_ref, l_ref = rest[2:4]
        vt_refs = rest[4:]
    step = pl.program_id(0)
    rows, width = q_ref.shape
    each = width // heads

    @pl.when(step == 0)
    def _():
        for kv, vt in zip(kv_refs, vt_refs):
            for j in range(kv.shape[0] // BK):
                vt[:, j * BK : (j + 1) * BK] = kv[j * BK : (j + 1) * BK, width:].T

    if final:
        acc[...] = acc_in[0]
        m_ref[...] = ml_in[0, 0:1]
        l_ref[...] = ml_in[0, 1:2]
    else:
        acc[...] = jnp.zeros_like(acc)
        m_ref[...] = jnp.full_like(m_ref, NEG)
        l_ref[...] = jnp.zeros_like(l_ref)
    queries = stack_heads(q_ref[...], heads, half_mask)
    query_seg = sq_ref[0]
    target = acc if final else acc.at[0]

    for s in range(sets):
        kv, sk, vt = kv_refs[s], sk_refs[s], vt_refs[s]

        def body(j, carry):
            first = pl.multiple_of(j * BK, BK)
            keys = kv[pl.ds(first, BK), 0:width]
            scores = nt(keys, queries)
            same = same_segment(sk[pl.ds(first, BK), :], query_seg, heads)
            scores = jnp.where(same, scores, NEG)
            before = m_ref[...]
            top = jnp.maximum(before, jnp.max(scores, axis=0, keepdims=True))
            raised = jnp.exp(scores - top)
            shrink = jnp.exp(before - top)
            m_ref[...] = top
            l_ref[...] = l_ref[...] * shrink + jnp.sum(raised, axis=0, keepdims=True)
            low = raised.astype(bf16)
            for h in range(heads):
                part = nn(
                    vt[h * each : (h + 1) * each, pl.ds(first, BK)],
                    low[:, h * rows : (h + 1) * rows],
                )
                hold = target[h * each : (h + 1) * each, :]
                target[h * each : (h + 1) * each, :] = (
                    hold * shrink[:, h * rows : (h + 1) * rows] + part
                )
            return carry

        lax.fori_loop(
            bounds[(step * sets + s) * 2], bounds[(step * sets + s) * 2 + 1], body, 0
        )

    if final:
        live = query_seg >= 0
        total = l_ref[...]
        live_all = jnp.concatenate([live] * heads, axis=1) if heads > 1 else live
        total = jnp.where(live_all, total, 1.0)
        inverse = jnp.where(live_all, 1.0 / total, 0.0)
        for h in range(heads):
            acc[h * each : (h + 1) * each, :] = (
                acc[h * each : (h + 1) * each, :] * inverse[:, h * rows : (h + 1) * rows]
            )
        o_ref[...] = acc[...].T.astype(bf16)
        lse_ref[0] = jnp.where(live_all, m_ref[...] + jnp.log(total), FAR)
    else:
        ml_ref[0, 0:1] = m_ref[...]
        ml_ref[0, 1:2] = l_ref[...]


def whole(shape):
    zeros = (0,) * len(shape)
    return pl.BlockSpec(shape, lambda i, *_: zeros)


def attend_call(bounds, q, sq, kvs, sks, heads, state=None):
    count = q.shape[0] // BQ
    width = q.shape[1]
    sets = len(kvs)
    final = state is not None
    row_spec = pl.BlockSpec((BQ, width), lambda i, *_: (i, 0))
    acc_spec = pl.BlockSpec((1, width, BQ), lambda i, *_: (i, 0, 0))
    ml_spec = pl.BlockSpec((1, 2, heads * BQ), lambda i, *_: (i, 0, 0))
    in_specs = [row_spec, pl.BlockSpec((1, 1, BQ), lambda i, *_: (i, 0, 0))]
    in_specs += [whole(a.shape) for a in kvs] + [whole(a.shape) for a in sks]
    scratch = [pltpu.VMEM((1, heads * BQ), f32)] * 2
    scratch += [pltpu.VMEM((width, a.shape[0]), bf16) for a in kvs]
    if final:
        in_specs += [acc_spec, ml_spec]
        out_specs = [row_spec, pl.BlockSpec((1, 1, heads * BQ), lambda i, *_: (i, 0, 0))]
        out_shape = [
            jax.ShapeDtypeStruct(q.shape, bf16),
            jax.ShapeDtypeStruct((count, 1, heads * BQ), f32),
        ]
        scratch = [pltpu.VMEM((width, BQ), f32)] + scratch
    else:
        out_specs = [acc_spec, ml_spec]
        out_shape = [
            jax.ShapeDtypeStruct((count, width, BQ), f32),
            jax.ShapeDtypeStruct((count, 2, heads * BQ), f32),
        ]
    return pl.pallas_call(
        functools.partial(forward_kernel, heads, sets, final),
        grid_spec=pltpu.PrefetchScalarGridSpec(
            num_scalar_prefetch=1,
            grid=(count,),
            in_specs=in_specs,
            out_specs=out_specs,
            scratch_shapes=scratch,
        ),
        out_shape=out_shape,
        name="attend_final" if final else "attend_own",
    )(bounds, q, sq, *kvs, *sks, *(state or ()))


def backward_kernel(heads, sets, final, bounds, *refs):
    refs = list(refs)
    q_ref, do_ref, o_ref, lse_ref, sq_ref = refs[:5]
    kv_refs = refs[5 : 5 + sets]
    sk_refs = refs[5 + sets : 5 + 2 * sets]
    rest = refs[5 + 2 * sets :]
    if final:
        dq_in, dq_ref = rest[0], rest[1]
        dkv_refs = rest[2 : 2 + sets]
        dq_acc = rest[2 + sets]
        kt_refs = rest[3 + sets : 3 + 2 * sets]
        sums = dkv_refs
    else:
        dq_ref = rest[0]
        dkv_refs = rest[1 : 1 + sets]
        dq_acc = rest[1 + sets]
        kt_refs = rest[2 + sets : 2 + 2 * sets]
        sums = rest[2 + 2 * sets :]
    step = pl.program_id(0)
    rows, width = q_ref.shape
    each = width // heads
    half = width // 2
    piece = half // heads

    @pl.when(step == 0)
    def _():
        for kv, kt, total in zip(kv_refs, kt_refs, sums):
            total[...] = jnp.zeros_like(total)
            for j in range(kv.shape[0] // BK):
                kt[:, j * BK : (j + 1) * BK] = kv[j * BK : (j + 1) * BK, :width].T

    if final:
        dq_acc[...] = dq_in[0]
    else:
        dq_acc[...] = jnp.zeros_like(dq_acc)
    grads = do_ref[...]
    queries = stack_heads(q_ref[...], heads, half_mask)
    outs = stack_heads(grads, heads, whole_mask)
    query_seg = sq_ref[0]
    lse = lse_ref[0]
    product = (grads.astype(f32) * o_ref[...].astype(f32)).T
    delta = jnp.concatenate(
        [
            jnp.sum(product[h * each : (h + 1) * each], axis=0, keepdims=True)
            for h in range(heads)
        ],
        axis=1,
    )

    for s in range(sets):
        kv, sk, kt, total = kv_refs[s], sk_refs[s], kt_refs[s], sums[s]

        def body(j, carry):
            first = pl.multiple_of(j * BK, BK)
            keys = kv[pl.ds(first, BK), 0:width]
            values = kv[pl.ds(first, BK), width : 2 * width]
            scores = nt(keys, queries)
            same = same_segment(sk[pl.ds(first, BK), :], query_seg, heads)
            probs = jnp.where(same, jnp.exp(scores - lse), 0.0)
            grad_probs = nt(values, outs)
            grad_scores = (probs * (grad_probs - delta)).astype(bf16)
            low = probs.astype(bf16)
            total[pl.ds(first, BK), width : 2 * width] += nn(low, outs)
            total[pl.ds(first, BK), 0:width] += nn(grad_scores, queries)
            for h in range(heads):
                column = grad_scores[:, h * rows : (h + 1) * rows]
                for lead in (h * piece, half + h * piece):
                    dq_acc[lead : lead + piece, :] += nn(
                        kt[lead : lead + piece, pl.ds(first, BK)], column
                    )
            return carry

        lax.fori_loop(
            bounds[(step * sets + s) * 2], bounds[(step * sets + s) * 2 + 1], body, 0
        )

    if final:
        dq_ref[...] = dq_acc[...].T
    else:
        dq_ref[0] = dq_acc[...]

        @pl.when(step == pl.num_programs(0) - 1)
        def _():
            for total, out in zip(sums, dkv_refs):
                out[...] = total[...].astype(bf16)


def attend_back_call(bounds, q, do, o, lse, sq, kvs, sks, heads, state=None):
    count = q.shape[0] // BQ
    width = q.shape[1]
    sets = len(kvs)
    final = state is not None
    row_spec = pl.BlockSpec((BQ, width), lambda i, *_: (i, 0))
    acc_spec = pl.BlockSpec((1, width, BQ), lambda i, *_: (i, 0, 0))
    in_specs = [row_spec] * 3 + [
        pl.BlockSpec((1, 1, heads * BQ), lambda i, *_: (i, 0, 0)),
        pl.BlockSpec((1, 1, BQ), lambda i, *_: (i, 0, 0)),
    ]
    in_specs += [whole(a.shape) for a in kvs] + [whole(a.shape) for a in sks]
    scratch = [pltpu.VMEM((width, BQ), f32)]
    scratch += [pltpu.VMEM((width, a.shape[0]), bf16) for a in kvs]
    if final:
        in_specs += [acc_spec]
        out_specs = [row_spec]
        out_shape = [jax.ShapeDtypeStruct(q.shape, f32)]
    else:
        out_specs = [acc_spec]
        out_shape = [jax.ShapeDtypeStruct((count, width, BQ), f32)]
        scratch += [pltpu.VMEM(a.shape, f32) for a in kvs]
    out_specs += [whole(a.shape) for a in kvs]
    out_shape += [jax.ShapeDtypeStruct(a.shape, f32 if final else bf16) for a in kvs]
    return pl.pallas_call(
        functools.partial(backward_kernel, heads, sets, final),
        grid_spec=pltpu.PrefetchScalarGridSpec(
            num_scalar_prefetch=1,
            grid=(count,),
            in_specs=in_specs,
            out_specs=out_specs,
            scratch_shapes=scratch,
        ),
        out_shape=out_shape,
        name="back_own" if final else "back_halo",
    )(bounds, q, do, o, lse, sq, *kvs, *sks, *(state or ()))


def place_tables(seq_lengths, seq_offsets, first, count):
    place = first + jnp.arange(count, dtype=jnp.int32)
    ends = seq_offsets + seq_lengths
    inside = (place[:, None] >= seq_offsets[None, :]) & (place[:, None] < ends[None, :])
    live = jnp.any(inside, axis=1)
    index = jnp.arange(seq_offsets.shape[0], dtype=jnp.int32)
    segment = jnp.sum(jnp.where(inside, index[None, :], 0), axis=1)
    start = jnp.sum(jnp.where(inside, seq_offsets[None, :], 0), axis=1)
    end = jnp.sum(jnp.where(inside, ends[None, :], 0), axis=1)
    return live, segment, start, end, place


def qkv_order(heads, head_width):
    width = heads * head_width
    half = head_width // 2
    new = jnp.arange(3 * width, dtype=jnp.int32)
    kind = new // width
    inner = new % width
    side = inner // (width // 2)
    pair_head = (inner % (width // 2)) // half
    pair_old = pair_head * 3 * head_width + kind * head_width + side * half + inner % half
    value_old = (inner // head_width) * 3 * head_width + 2 * head_width + inner % head_width
    old = jnp.where(kind == 2, value_old, pair_old)
    return (old[None, :] == new[:, None]).astype(bf16)


def local(
    tokens,
    gain_attn,
    w_qkv,
    w_out,
    gain_mlp,
    w_in,
    w_down,
    cotangent,
    seq_lengths,
    seq_offsets,
    deal,
):
    R, C, B = lax.axis_size("row"), lax.axis_size("col"), lax.axis_size("dp")
    r, c, b = lax.axis_index("row"), lax.axis_index("col"), lax.axis_index("dp")
    S, Dl = tokens.shape
    D = Dl * R
    two = R == 2 and C == 2 and B == 8
    heads = w_qkv.shape[1] // R
    head_width = w_qkv.shape[2] // 3
    W = heads * head_width
    F = w_down.shape[0]
    H = LONGEST
    Sr = S // R
    zrow, zcol = (r == 0), (c == 0)

    def to_row(a):
        return lax.ppermute(a, "row", SWAP)

    def to_col(a):
        return lax.ppermute(a, "col", SWAP)

    def ordered(flag, mine, theirs, axis):
        return jnp.where(
            flag,
            jnp.concatenate([mine, theirs], axis=axis),
            jnp.concatenate([theirs, mine], axis=axis),
        )

    def own_first(a, axis):
        if not two:
            return a
        n = a.shape[axis] // 2
        return jnp.where(zrow, a, jnp.roll(a, n, axis=axis))

    def take(a, index, size, axis=0):
        return lax.dynamic_slice_in_dim(a, index * size, size, axis)

    def partner(a):
        n = a.shape[0] // 2
        got = to_row(take(a, c, n))
        return ordered(zcol, got, to_col(got), 0)

    def gather(a, axis):
        if two:
            return jnp.concatenate([a, to_row(a)], axis=axis)
        return lax.all_gather(a, "row", axis=axis, tiled=True)

    def col_sum(a):
        return a + to_col(a.astype(bf16)).astype(f32) if C == 2 else lax.psum(a, "col")

    live_x, seg_x, start_x, end_x, place_x = place_tables(seq_lengths, seq_offsets, b * S - H, S + 2 * H)
    key_seg = jnp.broadcast_to(jnp.where(live_x, seg_x, -2)[:, None], (S + 2 * H, 128))
    sk_left, sk_own, sk_right = key_seg[:H], key_seg[H : H + S], key_seg[H + S :]
    live = live_x[H : H + S]
    nq = S // BQ
    sq = jnp.where(live, seg_x[H : H + S], -1).reshape(nq, 1, BQ)
    first = jnp.min(jnp.where(live, start_x[H : H + S] - b * S, 4 * S).reshape(nq, BQ), axis=1)
    last = jnp.max(jnp.where(live, end_x[H : H + S] - b * S, -4 * S).reshape(nq, BQ), axis=1)
    own_low = jnp.clip(first, 0, S) // BK
    own_high = (jnp.clip(last, 0, S) + BK - 1) // BK
    left_low = jnp.clip(first + H, 0, H) // BK
    right_high = (jnp.clip(last - S, 0, H) + BK - 1) // BK
    own_bounds = jnp.stack([own_low, own_high], axis=1).reshape(-1).astype(jnp.int32)
    zero = jnp.zeros_like(left_low)
    halo_bounds = (
        jnp.stack([left_low, zero + H // BK, zero, right_high], axis=1).reshape(-1).astype(jnp.int32)
    )
    position = jnp.where(live, place_x[H : H + S] - start_x[H : H + S], 0)
    freq = rope_base ** (-(jnp.arange(0, head_width, 2, dtype=f32) / head_width))
    angle = position.astype(f32)[:, None] * jnp.tile(freq, heads)[None, :]
    cosine, sine = jnp.cos(angle), jnp.sin(angle)

    own_x = jnp.where(live[:, None], tokens, 0)
    own_g = jnp.where(live[:, None], cotangent, 0)
    if two:
        x_low = jnp.concatenate([own_x, partner(own_x)], axis=1)
    else:
        x_low = lax.all_gather(own_x, "row", axis=1, tiled=True)

    wq_low = w_qkv.reshape(Dl, R * 3 * W).astype(bf16)
    if two:
        wq = jnp.concatenate(
            [take(wq_low, r, 3 * W, 1), to_row(take(wq_low, 1 - r, 3 * W, 1))], axis=0
        )
    else:
        wq = lax.all_to_all(wq_low, "row", split_axis=1, concat_axis=0, tiled=True)
    order = qkv_order(heads, head_width)
    wq = nn(wq, order).astype(bf16)

    gain_one = own_first(gain_attn, 0)
    gain_two = own_first(gain_mlp, 0)

    x = x_low.astype(f32)
    center = x - jnp.mean(x, axis=-1, keepdims=True)
    inverse_one = lax.rsqrt(jnp.mean(center * center, axis=-1, keepdims=True) + epsilon)
    mean_one = jnp.mean(x, axis=-1, keepdims=True)
    h1 = (center * inverse_one * gain_one).astype(bf16)

    half = W // 2

    def turn(t, sign):
        first_half, second_half = t[:, :half], t[:, half:]
        s = sine * sign
        return jnp.concatenate(
            [first_half * cosine - second_half * s, second_half * cosine + first_half * s], axis=1
        )

    kv_raw = nn(h1, wq[:, W:])
    kv = jnp.concatenate([turn(kv_raw[:, :W], 1.0), kv_raw[:, W:]], axis=1).astype(bf16)
    up = [(i, i + 1) for i in range(B - 1)]
    down = [(i + 1, i) for i in range(B - 1)]
    kv_left = lax.ppermute(kv[S - H :], "dp", up)
    kv_right = lax.ppermute(kv[:H], "dp", down)
    q = (turn(nn(h1, wq[:, :W]), 1.0) * (1.0 / math.sqrt(head_width))).astype(bf16)
    state = attend_call(own_bounds, q, sq, [kv], [sk_own], heads)
    o, lse = attend_call(
        halo_bounds, q, sq, [kv_left, kv_right], [sk_left, sk_right], heads, state
    )

    wo = own_first(gather(w_out.astype(bf16), 1), 0)
    wi = gather(jnp.swapaxes(w_in, 0, 1).astype(bf16), 1)
    wd = gather(w_down.astype(bf16), 1)
    if two:
        g_low = jnp.concatenate([take(own_g, r, Sr), partner(take(own_g, 1 - r, Sr))], axis=1)
    else:
        g_low = lax.all_to_all(own_g, "row", split_axis=0, concat_axis=1, tiled=True)

    if two:
        o_rows = jnp.concatenate([take(o, r, Sr), to_row(take(o, 1 - r, Sr))], axis=1)
    else:
        o_rows = lax.all_to_all(o, "row", split_axis=0, concat_axis=1, tiled=True)
    x_rows = take(x_low, r, Sr).astype(f32)
    if C == 2:
        o_all = jnp.concatenate([o_rows, to_col(o_rows)], axis=1)
        wo_all = jnp.concatenate([wo, to_col(wo)], axis=0)
        x1 = x_rows + nn(o_all, wo_all)
    else:
        x1 = x_rows + lax.psum(nn(o_rows, wo), "col")

    center = x1 - jnp.mean(x1, axis=-1, keepdims=True)
    inverse_two = lax.rsqrt(jnp.mean(center * center, axis=-1, keepdims=True) + epsilon)
    n2 = center * inverse_two
    h2 = (n2 * gain_two).astype(bf16)
    a = nn(h2, wi[0])
    u = nn(h2, wi[1])
    phi = 0.5 + 0.5 * lax.erf(a * math.sqrt(0.5))
    gelu = a * phi
    slope = phi + a * jnp.exp(-0.5 * a * a) * (1.0 / math.sqrt(2.0 * math.pi))
    m = (gelu * u).astype(bf16)
    y_part = nn(m, wd)
    if two:
        n = Sr // 2
        y_half = (
            take(x1, c, n) + take(y_part, c, n) + to_col(take(y_part, 1 - c, n).astype(bf16)).astype(f32)
        ).astype(bf16)
        mine, theirs = y_half[:, :Dl], to_row(y_half[:, Dl:])
        pair = ordered(zrow, mine[None], theirs[None], 0)
        layer_out = ordered(zcol, pair[:, None], to_col(pair)[:, None], 1).reshape(S, Dl)
    else:
        y = (x1 + col_sum(y_part)).astype(bf16)
        layer_out = lax.all_to_all(y, "row", split_axis=1, concat_axis=0, tiled=True)

    dm = nt(g_low, wd)
    da = (dm * u * slope).astype(bf16)
    du = (dm * gelu).astype(bf16)
    dh2 = col_sum(nt(da, wi[0]) + nt(du, wi[1]))
    e2 = dh2 * gain_two
    dx1 = g_low.astype(f32) + inverse_two * (
        e2
        - jnp.mean(e2, axis=-1, keepdims=True)
        - n2 * jnp.mean(e2 * n2, axis=-1, keepdims=True)
    )
    dx_low = dx1.astype(bf16)
    do_rows = nt(dx_low, wo).astype(bf16)
    if two:
        do = ordered(zrow, do_rows[:, :W], to_row(do_rows[:, W:]), 0)
    else:
        do = lax.all_to_all(do_rows, "row", split_axis=1, concat_axis=0, tiled=True)
    lower_grad = tn(g_low, m).astype(bf16)
    gate_grad = jnp.stack([tn(h2, da), tn(h2, du)]).astype(bf16)
    proj_grad = tn(dx_low, own_first(o_rows, 1)).astype(bf16)

    dq_part, dkv_left, dkv_right = attend_back_call(
        halo_bounds, q, do, o, lse, sq, [kv_left, kv_right], [sk_left, sk_right], heads
    )
    from_right = lax.ppermute(dkv_left, "dp", down)
    from_left = lax.ppermute(dkv_right, "dp", up)
    dq, dkv = attend_back_call(own_bounds, q, do, o, lse, sq, [kv], [sk_own], heads, [dq_part])
    pad = jnp.zeros((S - H, 2 * W), bf16)
    dkv = (
        dkv
        + jnp.concatenate([pad, from_right], axis=0).astype(f32)
        + jnp.concatenate([from_left, pad], axis=0).astype(f32)
    )
    dq = turn(dq * (1.0 / math.sqrt(head_width)), -1.0)
    dt = jnp.concatenate([dq, turn(dkv[:, :W], -1.0), dkv[:, W:]], axis=1).astype(bf16)
    query_grad = tn(h1, dt)
    dh1_part = nt(dt, wq)

    if two:
        n = S // 2
        kept = take(dh1_part, c, n) + to_col(take(dh1_part, 1 - c, n).astype(bf16)).astype(f32)
        xs = take(x_low, c, n).astype(f32)
        inv, mean = take(inverse_one, c, n), take(mean_one, c, n)
        n1 = (xs - mean) * inv
        e1 = kept * gain_one
        sums = jnp.stack([jnp.sum(e1, axis=-1), jnp.sum(e1 * n1, axis=-1)])
        sums = (sums + to_row(sums)) * (1.0 / D)
        mine = (kept[:, :Dl] + to_row(kept[:, Dl:].astype(bf16)).astype(f32)) * gain_one[:Dl]
        moved = lax.ppermute(dx_low[:, Dl:], ("row", "col"), [(0, 2), (3, 1)])
        base = jnp.where(r == c, dx1[:, :Dl], moved.astype(f32))
        dx = base + inv * (mine - sums[0][:, None] - n1[:, :Dl] * sums[1][:, None])
        dx = dx.astype(bf16)
        tokens_grad = ordered(zcol, dx, to_col(dx), 0)
    else:
        dh1 = lax.psum_scatter(col_sum(dh1_part), "row", scatter_dimension=1, tiled=True)
        xs = own_x.astype(f32)
        n1 = (xs - mean_one) * inverse_one
        e1 = dh1 * take(gain_attn, r, Dl)
        sums = lax.psum(jnp.stack([jnp.sum(e1, axis=-1), jnp.sum(e1 * n1, axis=-1)]), "row") / D
        base = lax.all_to_all(dx_low, "row", split_axis=1, concat_axis=0, tiled=True).astype(f32)
        tokens_grad = (
            base + inverse_one * (e1 - sums[0][:, None] - n1 * sums[1][:, None])
        ).astype(bf16)

    Db = D // B
    Dd = D // (B * R)
    if two:
        y_bit, z_bits = b % 2, b // 2

        def over_y(blocks):
            send = lax.dynamic_index_in_dim(blocks, 1 - y_bit, 2, keepdims=False)
            keep = lax.dynamic_index_in_dim(blocks, y_bit, 2, keepdims=False)
            got = lax.ppermute(send.astype(bf16), "dp", [(i, i ^ 1) for i in range(B)])
            return (keep.astype(f32) + got.astype(f32)).astype(bf16)

        def over_z(blocks):
            total = lax.dynamic_index_in_dim(blocks, z_bits ^ (2 * r), 1, keepdims=False).astype(f32)
            for j in (1, 2, 3):
                send = lax.dynamic_index_in_dim(blocks, z_bits ^ (2 * r) ^ j, 1, keepdims=False)
                got = lax.ppermute(send, "dp", [(i, i ^ (2 * j)) for i in range(B)])
                total = total + got.astype(f32)
            return total

        def x_last(grad):
            lead, _, n = grad.shape
            part = over_z(over_y(grad.reshape(lead, 4, 2, Db, n))).reshape(lead, 2, Dd, n)
            send = lax.dynamic_index_in_dim(part, 1 - r, 1, keepdims=False).astype(bf16)
            return lax.dynamic_index_in_dim(part, r, 1, keepdims=False) + to_row(send).astype(f32)

        def x_first(grad):
            lead, _, n = grad.shape
            part = grad.reshape(lead, 8, 2, Dd, n)
            send = lax.dynamic_index_in_dim(part, 1 - r, 2, keepdims=False)
            keep = lax.dynamic_index_in_dim(part, r, 2, keepdims=False)
            got = jnp.roll(to_row(send), 4, axis=1)
            part = (keep.astype(f32) + got.astype(f32)).astype(bf16)
            return over_z(over_y(part.reshape(lead, 4, 2, Dd, n)))

        gate = x_first(gate_grad)
        merged = x_last(jnp.concatenate([proj_grad, lower_grad], axis=1)[None])[0]
        proj, lower = merged[:, : proj_grad.shape[1]], merged[:, proj_grad.shape[1] :]
        query = over_z(over_y(query_grad.reshape(1, 4, 2, Db, 3 * W).astype(bf16)))[0]
        wq_rows = take(wq, b ^ (4 * r), Db)
        wi_rows = take(wi, (2 * b + r) ^ (8 * r), Dd, 1)
    else:

        def scatter(grad, axis):
            return lax.psum_scatter(grad, ("dp", "row"), scatter_dimension=axis, tiled=True).astype(f32)

        gate = scatter(gate_grad, 1)
        proj = scatter(proj_grad, 0)
        lower = scatter(lower_grad, 0)
        query = lax.psum_scatter(query_grad.astype(bf16), "dp", scatter_dimension=0, tiled=True).astype(f32)
        wq_rows = take(wq, b, Db)
        wi_rows = take(wi, b * R + r, Dd, 1)

    one_part = jnp.sum(query * wq_rows.astype(f32), axis=1)
    two_part = jnp.sum(jnp.sum(gate * wi_rows.astype(f32), axis=2), axis=0)
    natural = lax.dot_general(
        query, order.astype(f32), (((1,), (1,)), ((), ())),
        precision=lax.Precision.HIGHEST, preferred_element_type=f32,
    )
    if two:
        one_part = one_part + to_row(one_part)
        one_part = take(one_part, r, Dd)
        pair = natural.reshape(2, Dd, 3 * W)
        mine = lax.dynamic_index_in_dim(pair, r, 0, keepdims=False)
        theirs = to_row(lax.dynamic_index_in_dim(pair, 1 - r, 0, keepdims=False))
        query_out = ordered(zrow, mine, theirs, 1)
    else:
        one_part = take(lax.psum(one_part, "row"), r, Dd)
        query_out = lax.all_to_all(natural, "row", split_axis=0, concat_axis=1, tiled=True)
    gains = jnp.stack([one_part, two_part])
    gains = gains + to_col(gains) if C == 2 else lax.psum(gains, "col")
    gain_attn_grad = gains[0] / take(gain_attn, b * R + r, Dd)
    gain_mlp_grad = gains[1] / take(gain_mlp, b * R + r, Dd)
    return (
        layer_out,
        tokens_grad,
        gain_attn_grad,
        query_out.reshape(Dd, R * heads, 3 * head_width),
        proj.T,
        gain_mlp_grad,
        jnp.swapaxes(gate, 0, 1),
        lower.T,
    )


def solution(mesh):
    return jax.shard_map(
        local,
        mesh=mesh,
        in_specs=(
            P("dp", "row"),
            P(),
            P("row", "col", None),
            P("col", "row"),
            P(),
            P("row", None, "col"),
            P("col", "row"),
            P("dp", "row"),
            P(),
            P(),
            P(),
        ),
        out_specs=(
            P("dp", "row"),
            P("dp", "row"),
            P(("dp", "row")),
            P(("dp", "row"), "col", None),
            P("col", ("dp", "row")),
            P(("dp", "row")),
            P(("dp", "row"), None, "col"),
            P("col", ("dp", "row")),
        ),
        check_vma=False,
    )
```

```python
import functools
import math

import jax
import jax.numpy as jnp
from jax import lax
from jax.experimental import pallas as pl
from jax.experimental.pallas import tpu as pltpu
from jax.sharding import PartitionSpec as P

LONGEST = 1024
BQ = 256
BK = 256
NEG = -1e30
FAR = 1e30
epsilon = 1e-05
rope_base = 160000.0
bf16 = jnp.bfloat16
f32 = jnp.float32
SWAP = [(0, 1), (1, 0)]


def nt(a, b):
    return lax.dot_general(a, b, (((1,), (1,)), ((), ())), preferred_element_type=f32)


def tn(a, b):
    return lax.dot_general(a, b, (((0,), (0,)), ((), ())), preferred_element_type=f32)


def nn(a, b):
    return jnp.dot(a, b, preferred_element_type=f32)


def after(a, *others):
    return lax.optimization_barrier((a, *others))[0]


def half_mask(width, heads, head):
    lane = lax.broadcasted_iota(jnp.int32, (1, width), 1)
    half = width // 2
    lane = jnp.where(lane >= half, lane - half, lane)
    step = half // heads
    return (lane >= head * step) & (lane < (head + 1) * step)


def whole_mask(width, heads, head):
    lane = lax.broadcasted_iota(jnp.int32, (1, width), 1)
    step = width // heads
    return (lane >= head * step) & (lane < (head + 1) * step)


def stack_heads(block, heads, mask_of):
    zero = jnp.zeros_like(block)
    width = block.shape[1]
    return jnp.concatenate(
        [jnp.where(mask_of(width, heads, h), block, zero) for h in range(heads)], axis=0
    )


def same_segment(key_seg, query_seg, heads):
    tile = key_seg
    lanes = query_seg.shape[1]
    if lanes > tile.shape[1]:
        tile = jnp.concatenate([tile] * (lanes // tile.shape[1]), axis=1)
    same = tile == query_seg
    return jnp.concatenate([same] * heads, axis=1) if heads > 1 else same


def forward_kernel(heads, sets, final, bounds, *refs):
    refs = list(refs)
    q_ref, sq_ref = refs[:2]
    kv_refs = refs[2 : 2 + sets]
    sk_refs = refs[2 + sets : 2 + 2 * sets]
    rest = refs[2 + 2 * sets :]
    if final:
        acc_in, ml_in, o_ref, lse_ref = rest[:4]
        acc, m_ref, l_ref = rest[4:7]
        vt_refs = rest[7:]
    else:
        acc, ml_ref = rest[:2]
        m_ref, l_ref = rest[2:4]
        vt_refs = rest[4:]
    step = pl.program_id(0)
    rows, width = q_ref.shape
    each = width // heads

    @pl.when(step == 0)
    def _():
        for kv, vt in zip(kv_refs, vt_refs):
            for j in range(kv.shape[0] // BK):
                vt[:, j * BK : (j + 1) * BK] = kv[j * BK : (j + 1) * BK, width:].T

    if final:
        acc[...] = acc_in[0]
        m_ref[...] = ml_in[0, 0:1]
        l_ref[...] = ml_in[0, 1:2]
    else:
        acc[...] = jnp.zeros_like(acc)
        m_ref[...] = jnp.full_like(m_ref, NEG)
        l_ref[...] = jnp.zeros_like(l_ref)
    queries = stack_heads(q_ref[...], heads, half_mask)
    query_seg = sq_ref[0]
    target = acc if final else acc.at[0]

    for s in range(sets):
        kv, sk, vt = kv_refs[s], sk_refs[s], vt_refs[s]

        def body(j, carry):
            first = pl.multiple_of(j * BK, BK)
            keys = kv[pl.ds(first, BK), 0:width]
            scores = nt(keys, queries)
            same = same_segment(sk[pl.ds(first, BK), :], query_seg, heads)
            scores = jnp.where(same, scores, NEG)
            before = m_ref[...]
            top = jnp.maximum(before, jnp.max(scores, axis=0, keepdims=True))
            raised = jnp.exp(scores - top)
            shrink = jnp.exp(before - top)
            m_ref[...] = top
            l_ref[...] = l_ref[...] * shrink + jnp.sum(raised, axis=0, keepdims=True)
            low = raised.astype(bf16)
            for h in range(heads):
                part = nn(
                    vt[h * each : (h + 1) * each, pl.ds(first, BK)],
                    low[:, h * rows : (h + 1) * rows],
                )
                hold = target[h * each : (h + 1) * each, :]
                target[h * each : (h + 1) * each, :] = (
                    hold * shrink[:, h * rows : (h + 1) * rows] + part
                )
            return carry

        lax.fori_loop(
            bounds[(step * sets + s) * 2], bounds[(step * sets + s) * 2 + 1], body, 0
        )

    if final:
        live = query_seg >= 0
        total = l_ref[...]
        live_all = jnp.concatenate([live] * heads, axis=1) if heads > 1 else live
        total = jnp.where(live_all, total, 1.0)
        inverse = jnp.where(live_all, 1.0 / total, 0.0)
        for h in range(heads):
            acc[h * each : (h + 1) * each, :] = (
                acc[h * each : (h + 1) * each, :] * inverse[:, h * rows : (h + 1) * rows]
            )
        o_ref[...] = acc[...].T.astype(bf16)
        lse_ref[0] = jnp.where(live_all, m_ref[...] + jnp.log(total), FAR)
    else:
        ml_ref[0, 0:1] = m_ref[...]
        ml_ref[0, 1:2] = l_ref[...]


def cost(products, q, kvs):
    pairs = q.shape[0] * 1024
    return pl.CostEstimate(
        flops=4 * products * pairs * q.shape[1],
        bytes_accessed=2 * sum(a.size for a in kvs) + 4 * q.size,
        transcendentals=4 * pairs,
    )


def whole(shape):
    zeros = (0,) * len(shape)
    return pl.BlockSpec(shape, lambda i, *_: zeros)


def attend_call(bounds, q, sq, kvs, sks, heads, state=None):
    count = q.shape[0] // BQ
    width = q.shape[1]
    sets = len(kvs)
    final = state is not None
    row_spec = pl.BlockSpec((BQ, width), lambda i, *_: (i, 0))
    acc_spec = pl.BlockSpec((1, width, BQ), lambda i, *_: (i, 0, 0))
    ml_spec = pl.BlockSpec((1, 2, heads * BQ), lambda i, *_: (i, 0, 0))
    in_specs = [row_spec, pl.BlockSpec((1, 1, BQ), lambda i, *_: (i, 0, 0))]
    in_specs += [whole(a.shape) for a in kvs] + [whole(a.shape) for a in sks]
    scratch = [pltpu.VMEM((1, heads * BQ), f32)] * 2
    scratch += [pltpu.VMEM((width, a.shape[0]), bf16) for a in kvs]
    if final:
        in_specs += [acc_spec, ml_spec]
        out_specs = [row_spec, pl.BlockSpec((1, 1, heads * BQ), lambda i, *_: (i, 0, 0))]
        out_shape = [
            jax.ShapeDtypeStruct(q.shape, bf16),
            jax.ShapeDtypeStruct((count, 1, heads * BQ), f32),
        ]
        scratch = [pltpu.VMEM((width, BQ), f32)] + scratch
    else:
        out_specs = [acc_spec, ml_spec]
        out_shape = [
            jax.ShapeDtypeStruct((count, width, BQ), f32),
            jax.ShapeDtypeStruct((count, 2, heads * BQ), f32),
        ]
    return pl.pallas_call(
        functools.partial(forward_kernel, heads, sets, final),
        grid_spec=pltpu.PrefetchScalarGridSpec(
            num_scalar_prefetch=1,
            grid=(count,),
            in_specs=in_specs,
            out_specs=out_specs,
            scratch_shapes=scratch,
        ),
        out_shape=out_shape,
        cost_estimate=cost(4, q, kvs),
        name="attend_final" if final else "attend_own",
    )(bounds, q, sq, *kvs, *sks, *(state or ()))


def backward_kernel(heads, sets, final, bounds, *refs):
    refs = list(refs)
    q_ref, do_ref, o_ref, lse_ref, sq_ref = refs[:5]
    kv_refs = refs[5 : 5 + sets]
    sk_refs = refs[5 + sets : 5 + 2 * sets]
    rest = refs[5 + 2 * sets :]
    if final:
        dq_in, dq_ref = rest[0], rest[1]
        dkv_refs = rest[2 : 2 + sets]
        dq_acc = rest[2 + sets]
        kt_refs = rest[3 + sets : 3 + 2 * sets]
        sums = dkv_refs
    else:
        dq_ref = rest[0]
        dkv_refs = rest[1 : 1 + sets]
        dq_acc = rest[1 + sets]
        kt_refs = rest[2 + sets : 2 + 2 * sets]
        sums = rest[2 + 2 * sets :]
    step = pl.program_id(0)
    rows, width = q_ref.shape
    each = width // heads
    half = width // 2
    piece = half // heads

    @pl.when(step == 0)
    def _():
        for kv, kt, total in zip(kv_refs, kt_refs, sums):
            total[...] = jnp.zeros_like(total)
            for j in range(kv.shape[0] // BK):
                kt[:, j * BK : (j + 1) * BK] = kv[j * BK : (j + 1) * BK, :width].T

    if final:
        dq_acc[...] = dq_in[0]
    else:
        dq_acc[...] = jnp.zeros_like(dq_acc)
    grads = do_ref[...]
    queries = stack_heads(q_ref[...], heads, half_mask)
    outs = stack_heads(grads, heads, whole_mask)
    query_seg = sq_ref[0]
    lse = lse_ref[0]
    product = (grads.astype(f32) * o_ref[...].astype(f32)).T
    delta = jnp.concatenate(
        [
            jnp.sum(product[h * each : (h + 1) * each], axis=0, keepdims=True)
            for h in range(heads)
        ],
        axis=1,
    )

    for s in range(sets):
        kv, sk, kt, total = kv_refs[s], sk_refs[s], kt_refs[s], sums[s]

        def body(j, carry):
            first = pl.multiple_of(j * BK, BK)
            keys = kv[pl.ds(first, BK), 0:width]
            values = kv[pl.ds(first, BK), width : 2 * width]
            scores = nt(keys, queries)
            same = same_segment(sk[pl.ds(first, BK), :], query_seg, heads)
            probs = jnp.where(same, jnp.exp(scores - lse), 0.0)
            grad_probs = nt(values, outs)
            grad_scores = (probs * (grad_probs - delta)).astype(bf16)
            low = probs.astype(bf16)
            total[pl.ds(first, BK), width : 2 * width] += nn(low, outs)
            total[pl.ds(first, BK), 0:width] += nn(grad_scores, queries)
            for h in range(heads):
                column = grad_scores[:, h * rows : (h + 1) * rows]
                for lead in (h * piece, half + h * piece):
                    dq_acc[lead : lead + piece, :] += nn(
                        kt[lead : lead + piece, pl.ds(first, BK)], column
                    )
            return carry

        lax.fori_loop(
            bounds[(step * sets + s) * 2], bounds[(step * sets + s) * 2 + 1], body, 0
        )

    if final:
        dq_ref[...] = dq_acc[...].T
    else:
        dq_ref[0] = dq_acc[...]

        @pl.when(step == pl.num_programs(0) - 1)
        def _():
            for total, out in zip(sums, dkv_refs):
                out[...] = total[...].astype(bf16)


def attend_back_call(bounds, q, do, o, lse, sq, kvs, sks, heads, state=None):
    count = q.shape[0] // BQ
    width = q.shape[1]
    sets = len(kvs)
    final = state is not None
    row_spec = pl.BlockSpec((BQ, width), lambda i, *_: (i, 0))
    acc_spec = pl.BlockSpec((1, width, BQ), lambda i, *_: (i, 0, 0))
    in_specs = [row_spec] * 3 + [
        pl.BlockSpec((1, 1, heads * BQ), lambda i, *_: (i, 0, 0)),
        pl.BlockSpec((1, 1, BQ), lambda i, *_: (i, 0, 0)),
    ]
    in_specs += [whole(a.shape) for a in kvs] + [whole(a.shape) for a in sks]
    scratch = [pltpu.VMEM((width, BQ), f32)]
    scratch += [pltpu.VMEM((width, a.shape[0]), bf16) for a in kvs]
    if final:
        in_specs += [acc_spec]
        out_specs = [row_spec]
        out_shape = [jax.ShapeDtypeStruct(q.shape, f32)]
    else:
        out_specs = [acc_spec]
        out_shape = [jax.ShapeDtypeStruct((count, width, BQ), f32)]
        scratch += [pltpu.VMEM(a.shape, f32) for a in kvs]
    out_specs += [whole(a.shape) for a in kvs]
    out_shape += [jax.ShapeDtypeStruct(a.shape, f32 if final else bf16) for a in kvs]
    return pl.pallas_call(
        functools.partial(backward_kernel, heads, sets, final),
        grid_spec=pltpu.PrefetchScalarGridSpec(
            num_scalar_prefetch=1,
            grid=(count,),
            in_specs=in_specs,
            out_specs=out_specs,
            scratch_shapes=scratch,
        ),
        out_shape=out_shape,
        cost_estimate=cost(10, q, kvs),
        name="back_own" if final else "back_halo",
    )(bounds, q, do, o, lse, sq, *kvs, *sks, *(state or ()))


def place_tables(seq_lengths, seq_offsets, first, count):
    place = first + jnp.arange(count, dtype=jnp.int32)
    ends = seq_offsets + seq_lengths
    inside = (place[:, None] >= seq_offsets[None, :]) & (place[:, None] < ends[None, :])
    live = jnp.any(inside, axis=1)
    index = jnp.arange(seq_offsets.shape[0], dtype=jnp.int32)
    segment = jnp.sum(jnp.where(inside, index[None, :], 0), axis=1)
    start = jnp.sum(jnp.where(inside, seq_offsets[None, :], 0), axis=1)
    end = jnp.sum(jnp.where(inside, ends[None, :], 0), axis=1)
    return live, segment, start, end, place


def qkv_order(heads, head_width):
    width = heads * head_width
    half = head_width // 2
    new = jnp.arange(3 * width, dtype=jnp.int32)
    kind = new // width
    inner = new % width
    side = inner // (width // 2)
    pair_head = (inner % (width // 2)) // half
    pair_old = pair_head * 3 * head_width + kind * head_width + side * half + inner % half
    value_old = (inner // head_width) * 3 * head_width + 2 * head_width + inner % head_width
    old = jnp.where(kind == 2, value_old, pair_old)
    return (old[None, :] == new[:, None]).astype(bf16)


def local(
    tokens,
    gain_attn,
    w_qkv,
    w_out,
    gain_mlp,
    w_in,
    w_down,
    cotangent,
    seq_lengths,
    seq_offsets,
    deal,
):
    R, C, B = lax.axis_size("row"), lax.axis_size("col"), lax.axis_size("dp")
    r, c, b = lax.axis_index("row"), lax.axis_index("col"), lax.axis_index("dp")
    S, Dl = tokens.shape
    D = Dl * R
    two = R == 2 and C == 2 and B == 8
    heads = w_qkv.shape[1] // R
    head_width = w_qkv.shape[2] // 3
    W = heads * head_width
    F = w_down.shape[0]
    H = LONGEST
    Sr = S // R
    zrow, zcol = (r == 0), (c == 0)

    def to_row(a):
        return lax.ppermute(a, "row", SWAP)

    def to_col(a):
        return lax.ppermute(a, "col", SWAP)

    def ordered(flag, mine, theirs, axis):
        return jnp.where(
            flag,
            jnp.concatenate([mine, theirs], axis=axis),
            jnp.concatenate([theirs, mine], axis=axis),
        )

    def own_first(a, axis):
        if not two:
            return a
        n = a.shape[axis] // 2
        return jnp.where(zrow, a, jnp.roll(a, n, axis=axis))

    def take(a, index, size, axis=0):
        return lax.dynamic_slice_in_dim(a, index * size, size, axis)

    def partner(a):
        n = a.shape[0] // 2
        got = to_row(take(a, c, n))
        return ordered(zcol, got, to_col(got), 0)

    def gather(a, axis):
        if two:
            return jnp.concatenate([a, to_row(a)], axis=axis)
        return lax.all_gather(a, "row", axis=axis, tiled=True)

    def col_sum(a):
        return a + to_col(a.astype(bf16)).astype(f32) if C == 2 else lax.psum(a, "col")

    live_x, seg_x, start_x, end_x, place_x = place_tables(seq_lengths, seq_offsets, b * S - H, S + 2 * H)
    key_seg = jnp.broadcast_to(jnp.where(live_x, seg_x, -2)[:, None], (S + 2 * H, 128))
    sk_left, sk_own, sk_right = key_seg[:H], key_seg[H : H + S], key_seg[H + S :]
    live = live_x[H : H + S]
    nq = S // BQ
    sq = jnp.where(live, seg_x[H : H + S], -1).reshape(nq, 1, BQ)
    first = jnp.min(jnp.where(live, start_x[H : H + S] - b * S, 4 * S).reshape(nq, BQ), axis=1)
    last = jnp.max(jnp.where(live, end_x[H : H + S] - b * S, -4 * S).reshape(nq, BQ), axis=1)
    own_low = jnp.clip(first, 0, S) // BK
    own_high = (jnp.clip(last, 0, S) + BK - 1) // BK
    left_low = jnp.clip(first + H, 0, H) // BK
    right_high = (jnp.clip(last - S, 0, H) + BK - 1) // BK
    own_bounds = jnp.stack([own_low, own_high], axis=1).reshape(-1).astype(jnp.int32)
    zero = jnp.zeros_like(left_low)
    halo_bounds = (
        jnp.stack([left_low, zero + H // BK, zero, right_high], axis=1).reshape(-1).astype(jnp.int32)
    )
    position = jnp.where(live, place_x[H : H + S] - start_x[H : H + S], 0)
    freq = rope_base ** (-(jnp.arange(0, head_width, 2, dtype=f32) / head_width))
    angle = position.astype(f32)[:, None] * jnp.tile(freq, heads)[None, :]
    cosine, sine = lax.optimization_barrier((jnp.cos(angle), jnp.sin(angle)))

    own_x = jnp.where(live[:, None], tokens, 0)
    own_g = jnp.where(live[:, None], cotangent, 0)
    if two:
        x_got = partner(own_x)
        x_low = jnp.concatenate([own_x, x_got], axis=1)
    else:
        x_low = lax.all_gather(own_x, "row", axis=1, tiled=True)

    wq_low = w_qkv.reshape(Dl, R * 3 * W).astype(bf16)
    if two:
        wq_mine, wq_send = after((take(wq_low, r, 3 * W, 1), take(wq_low, 1 - r, 3 * W, 1)), own_x)
        wq_got = to_row(wq_send)
        wq = jnp.concatenate([wq_mine, wq_got], axis=0)
    else:
        wq = lax.all_to_all(wq_low, "row", split_axis=1, concat_axis=0, tiled=True)
    order = qkv_order(heads, head_width)
    wq = nn(wq, order).astype(bf16)

    gain_one = own_first(gain_attn, 0)
    gain_two = own_first(gain_mlp, 0)

    x = x_low.astype(f32)
    center = x - jnp.mean(x, axis=-1, keepdims=True)
    inverse_one = lax.rsqrt(jnp.mean(center * center, axis=-1, keepdims=True) + epsilon)
    mean_one = jnp.mean(x, axis=-1, keepdims=True)
    h1 = (center * inverse_one * gain_one).astype(bf16)

    half = W // 2

    def turn(t, sign):
        first_half, second_half = t[:, :half], t[:, half:]
        s = sine * sign
        return jnp.concatenate(
            [first_half * cosine - second_half * s, second_half * cosine + first_half * s], axis=1
        )

    kv_raw = nn(h1, wq[:, W:])
    kv = jnp.concatenate([turn(kv_raw[:, :W], 1.0), kv_raw[:, W:]], axis=1).astype(bf16)
    up = [(i, i + 1) for i in range(B - 1)]
    down = [(i + 1, i) for i in range(B - 1)]
    kv_left = lax.ppermute(kv[S - H :], "dp", up)
    kv_right = lax.ppermute(kv[:H], "dp", down)
    q = (turn(nn(h1, wq[:, :W]), 1.0) * (1.0 / math.sqrt(head_width))).astype(bf16)
    state = attend_call(own_bounds, q, sq, [kv], [sk_own], heads)
    o, lse = attend_call(
        halo_bounds, q, sq, [kv_left, kv_right], [sk_left, sk_right], heads, state
    )

    wo_low, wi_low = w_out.astype(bf16), jnp.swapaxes(w_in, 0, 1).astype(bf16)
    wd_low = w_down.astype(bf16)
    if two:
        wo_low = after(wo_low, x_got)
        wi_low = after(wi_low, wq_got)
    wo = own_first(gather(wo_low, 1), 0)
    wi = gather(wi_low, 1)

    if two:
        o_got = to_row(take(o, 1 - r, Sr))
        o_rows = jnp.concatenate([take(o, r, Sr), o_got], axis=1)
        own_g, wd_low = after((own_g, wd_low), o_got)
        g_low = jnp.concatenate([take(own_g, r, Sr), partner(take(own_g, 1 - r, Sr))], axis=1)
    else:
        o_rows = lax.all_to_all(o, "row", split_axis=0, concat_axis=1, tiled=True)
        g_low = lax.all_to_all(own_g, "row", split_axis=0, concat_axis=1, tiled=True)
    wd = gather(wd_low, 1)
    x_rows = take(x_low, r, Sr).astype(f32)
    if C == 2:
        o_all = jnp.concatenate([o_rows, to_col(o_rows)], axis=1)
        wo_all = jnp.concatenate([wo, to_col(wo)], axis=0)
        x1 = x_rows + nn(o_all, wo_all)
    else:
        x1 = x_rows + lax.psum(nn(o_rows, wo), "col")

    center = x1 - jnp.mean(x1, axis=-1, keepdims=True)
    inverse_two = lax.rsqrt(jnp.mean(center * center, axis=-1, keepdims=True) + epsilon)
    n2 = center * inverse_two
    h2 = (n2 * gain_two).astype(bf16)
    a = nn(h2, wi[0])
    u = nn(h2, wi[1])
    phi = 0.5 + 0.5 * lax.erf(a * math.sqrt(0.5))
    gelu = a * phi
    slope = phi + a * jnp.exp(-0.5 * a * a) * (1.0 / math.sqrt(2.0 * math.pi))
    m = (gelu * u).astype(bf16)
    y_part = nn(m, wd)
    if two:
        n = Sr // 2
        y_half = (
            take(x1, c, n) + take(y_part, c, n) + to_col(take(y_part, 1 - c, n).astype(bf16)).astype(f32)
        ).astype(bf16)
        mine, theirs = y_half[:, :Dl], to_row(y_half[:, Dl:])
        pair = ordered(zrow, mine[None], theirs[None], 0)
        layer_out = ordered(zcol, pair[:, None], to_col(pair)[:, None], 1).reshape(S, Dl)
    else:
        y = (x1 + col_sum(y_part)).astype(bf16)
        layer_out = lax.all_to_all(y, "row", split_axis=1, concat_axis=0, tiled=True)

    dm = nt(g_low, wd)
    da = (dm * u * slope).astype(bf16)
    du = (dm * gelu).astype(bf16)
    dh2 = col_sum(nt(da, wi[0]) + nt(du, wi[1]))
    e2 = dh2 * gain_two
    dx1 = g_low.astype(f32) + inverse_two * (
        e2
        - jnp.mean(e2, axis=-1, keepdims=True)
        - n2 * jnp.mean(e2 * n2, axis=-1, keepdims=True)
    )
    dx_low = dx1.astype(bf16)
    do_rows = nt(dx_low, wo).astype(bf16)
    if two:
        do_got = to_row(do_rows[:, W:])
        do = ordered(zrow, do_rows[:, :W], do_got, 0)
    else:
        do = lax.all_to_all(do_rows, "row", split_axis=1, concat_axis=0, tiled=True)
    lower_grad = tn(g_low, m).astype(bf16)
    act_grad = tn(h2, da).astype(bf16)
    lin_grad = tn(h2, du).astype(bf16)
    proj_grad = tn(dx_low, own_first(o_rows, 1)).astype(bf16)

    dq_part, dkv_left, dkv_right = attend_back_call(
        halo_bounds, q, do, o, lse, sq, [kv_left, kv_right], [sk_left, sk_right], heads
    )
    from_right = lax.ppermute(dkv_left, "dp", down)
    from_left = lax.ppermute(dkv_right, "dp", up)
    dq, dkv = attend_back_call(own_bounds, q, do, o, lse, sq, [kv], [sk_own], heads, [dq_part])
    pad = jnp.zeros((S - H, 2 * W), bf16)
    dkv = (
        dkv
        + jnp.concatenate([pad, from_right], axis=0).astype(f32)
        + jnp.concatenate([from_left, pad], axis=0).astype(f32)
    )
    dq = turn(dq * (1.0 / math.sqrt(head_width)), -1.0)
    dt = jnp.concatenate([dq, turn(dkv[:, :W], -1.0), dkv[:, W:]], axis=1).astype(bf16)
    query_grad = tn(h1, dt)
    dh1_part = nt(dt, wq)

    if two:
        n = S // 2
        kept = take(dh1_part, c, n) + to_col(take(dh1_part, 1 - c, n).astype(bf16)).astype(f32)
        xs = take(x_low, c, n).astype(f32)
        inv, mean = take(inverse_one, c, n), take(mean_one, c, n)
        n1 = (xs - mean) * inv
        e1 = kept * gain_one
        sums = jnp.stack([jnp.sum(e1, axis=-1), jnp.sum(e1 * n1, axis=-1)])
        sums = (sums + to_row(sums)) * (1.0 / D)
        mine = (kept[:, :Dl] + to_row(kept[:, Dl:].astype(bf16)).astype(f32)) * gain_one[:Dl]
        moved = lax.ppermute(after(dx_low[:, Dl:], do_got), ("row", "col"), [(0, 2), (3, 1)])
        base = jnp.where(r == c, dx1[:, :Dl], moved.astype(f32))
        dx = base + inv * (mine - sums[0][:, None] - n1[:, :Dl] * sums[1][:, None])
        dx = dx.astype(bf16)
        tokens_grad = ordered(zcol, dx, to_col(dx), 0)
    else:
        dh1 = lax.psum_scatter(col_sum(dh1_part), "row", scatter_dimension=1, tiled=True)
        xs = own_x.astype(f32)
        n1 = (xs - mean_one) * inverse_one
        e1 = dh1 * take(gain_attn, r, Dl)
        sums = lax.psum(jnp.stack([jnp.sum(e1, axis=-1), jnp.sum(e1 * n1, axis=-1)]), "row") / D
        base = lax.all_to_all(dx_low, "row", split_axis=1, concat_axis=0, tiled=True).astype(f32)
        tokens_grad = (
            base + inverse_one * (e1 - sums[0][:, None] - n1 * sums[1][:, None])
        ).astype(bf16)

    Db = D // B
    Dd = D // (B * R)
    if two:
        y_bit, z_bits = b % 2, b // 2

        def over_y(blocks):
            axis = blocks.ndim - 3
            send = lax.dynamic_index_in_dim(blocks, 1 - y_bit, axis, keepdims=False)
            keep = lax.dynamic_index_in_dim(blocks, y_bit, axis, keepdims=False)
            got = lax.ppermute(send.astype(bf16), "dp", [(i, i ^ 1) for i in range(B)])
            return keep.astype(f32) + got.astype(f32)

        def over_z(blocks):
            total = lax.dynamic_index_in_dim(blocks, z_bits ^ (2 * r), 0, keepdims=False).astype(f32)
            for j in (3, 2, 1):
                send = lax.dynamic_index_in_dim(blocks, z_bits ^ (2 * r) ^ j, 0, keepdims=False)
                got = lax.ppermute(send, "dp", [(i, i ^ (2 * j)) for i in range(B)])
                total = total + got.astype(f32)
            return total

        def x_last(grad):
            n = grad.shape[1]
            part = over_z(over_y(grad.reshape(4, 2, Db, n)).astype(bf16)).reshape(2, Dd, n)
            send = lax.dynamic_index_in_dim(part, 1 - r, 0, keepdims=False).astype(bf16)
            return lax.dynamic_index_in_dim(part, r, 0, keepdims=False) + to_row(send).astype(f32)

        def x_first(grad):
            n = grad.shape[1]
            part = grad.reshape(8, 2, Dd, n)
            send = lax.dynamic_index_in_dim(part, 1 - r, 1, keepdims=False)
            keep = lax.dynamic_index_in_dim(part, r, 1, keepdims=False)
            got = jnp.roll(to_row(send), 4, axis=0)
            part = (keep.astype(f32) + got.astype(f32)).astype(bf16)
            return over_y(over_z(part.reshape(4, 2, Dd, n)).astype(bf16))

        lower = x_last(lower_grad)
        gate = jnp.stack([x_first(after(act_grad, do_got)), x_last(lin_grad)])
        proj = x_last(proj_grad)
        query = over_z(over_y(query_grad.reshape(4, 2, Db, 3 * W)).astype(bf16))
        wq_rows = take(wq, b ^ (4 * r), Db)
        wi_rows = take(wi, (2 * b + r) ^ (8 * r), Dd, 1)
    else:

        def scatter(grad, axis):
            return lax.psum_scatter(grad, ("dp", "row"), scatter_dimension=axis, tiled=True).astype(f32)

        gate = jnp.stack([scatter(act_grad, 0), scatter(lin_grad, 0)])
        proj = scatter(proj_grad, 0)
        lower = scatter(lower_grad, 0)
        query = lax.psum_scatter(query_grad.astype(bf16), "dp", scatter_dimension=0, tiled=True).astype(f32)
        wq_rows = take(wq, b, Db)
        wi_rows = take(wi, b * R + r, Dd, 1)

    one_part = jnp.sum(query * wq_rows.astype(f32), axis=1)
    two_part = jnp.sum(jnp.sum(gate * wi_rows.astype(f32), axis=2), axis=0)
    natural = lax.dot_general(
        query, order.astype(f32), (((1,), (1,)), ((), ())),
        precision=lax.Precision.HIGHEST, preferred_element_type=f32,
    )
    if two:
        one_part = one_part + to_row(one_part)
        one_part = take(one_part, r, Dd)
        pair = natural.reshape(2, Dd, 3 * W)
        mine = lax.dynamic_index_in_dim(pair, r, 0, keepdims=False)
        theirs = to_row(lax.dynamic_index_in_dim(pair, 1 - r, 0, keepdims=False))
        query_out = ordered(zrow, mine, theirs, 1)
    else:
        one_part = take(lax.psum(one_part, "row"), r, Dd)
        query_out = lax.all_to_all(natural, "row", split_axis=0, concat_axis=1, tiled=True)
    gains = jnp.stack([one_part, two_part])
    gains = gains + to_col(gains) if C == 2 else lax.psum(gains, "col")
    gain_attn_grad = gains[0] / take(gain_attn, b * R + r, Dd)
    gain_mlp_grad = gains[1] / take(gain_mlp, b * R + r, Dd)
    return (
        layer_out,
        tokens_grad,
        gain_attn_grad,
        query_out.reshape(Dd, R * heads, 3 * head_width),
        proj.T,
        gain_mlp_grad,
        jnp.swapaxes(gate, 0, 1),
        lower.T,
    )


def solution(mesh):
    return jax.shard_map(
        local,
        mesh=mesh,
        in_specs=(
            P("dp", "row"),
            P(),
            P("row", "col", None),
            P("col", "row"),
            P(),
            P("row", None, "col"),
            P("col", "row"),
            P("dp", "row"),
            P(),
            P(),
            P(),
        ),
        out_specs=(
            P("dp", "row"),
            P("dp", "row"),
            P(("dp", "row")),
            P(("dp", "row"), "col", None),
            P("col", ("dp", "row")),
            P(("dp", "row")),
            P(("dp", "row"), None, "col"),
            P("col", ("dp", "row")),
        ),
        check_vma=False,
    )
```

```python
import functools
import math

import jax
import jax.numpy as jnp
from jax import lax
from jax.experimental import pallas as pl
from jax.experimental.pallas import tpu as pltpu
from jax.sharding import PartitionSpec as P

LONGEST = 1024
BQ = 256
BK = 256
NEG = -1e30
FAR = 1e30
epsilon = 1e-05
rope_base = 160000.0
bf16 = jnp.bfloat16
f32 = jnp.float32
SWAP = [(0, 1), (1, 0)]


def nt(a, b):
    return lax.dot_general(a, b, (((1,), (1,)), ((), ())), preferred_element_type=f32)


def tn(a, b):
    return lax.dot_general(a, b, (((0,), (0,)), ((), ())), preferred_element_type=f32)


def nn(a, b):
    return jnp.dot(a, b, preferred_element_type=f32)


def after(a, *others):
    return lax.optimization_barrier((a, *others))[0]


def half_mask(width, heads, head):
    lane = lax.broadcasted_iota(jnp.int32, (1, width), 1)
    half = width // 2
    lane = jnp.where(lane >= half, lane - half, lane)
    step = half // heads
    return (lane >= head * step) & (lane < (head + 1) * step)


def whole_mask(width, heads, head):
    lane = lax.broadcasted_iota(jnp.int32, (1, width), 1)
    step = width // heads
    return (lane >= head * step) & (lane < (head + 1) * step)


def stack_heads(block, heads, mask_of):
    zero = jnp.zeros_like(block)
    width = block.shape[1]
    return jnp.concatenate(
        [jnp.where(mask_of(width, heads, h), block, zero) for h in range(heads)], axis=0
    )


def same_segment(key_seg, query_seg, heads):
    tile = key_seg
    lanes = query_seg.shape[1]
    if lanes > tile.shape[1]:
        tile = jnp.concatenate([tile] * (lanes // tile.shape[1]), axis=1)
    same = tile == query_seg
    return jnp.concatenate([same] * heads, axis=1) if heads > 1 else same


def forward_kernel(heads, sets, final, bounds, *refs):
    refs = list(refs)
    q_ref, sq_ref = refs[:2]
    kv_refs = refs[2 : 2 + sets]
    sk_refs = refs[2 + sets : 2 + 2 * sets]
    rest = refs[2 + 2 * sets :]
    if final:
        acc_in, ml_in, o_ref, lse_ref = rest[:4]
        acc, m_ref, l_ref = rest[4:7]
        vt_refs = rest[7:]
    else:
        acc, ml_ref = rest[:2]
        m_ref, l_ref = rest[2:4]
        vt_refs = rest[4:]
    step = pl.program_id(0)
    rows, width = q_ref.shape
    each = width // heads

    @pl.when(step == 0)
    def _():
        for kv, vt in zip(kv_refs, vt_refs):
            for j in range(kv.shape[0] // BK):
                vt[:, j * BK : (j + 1) * BK] = kv[j * BK : (j + 1) * BK, width:].T

    if final:
        acc[...] = acc_in[0]
        m_ref[...] = ml_in[0, 0:1]
        l_ref[...] = ml_in[0, 1:2]
    else:
        acc[...] = jnp.zeros_like(acc)
        m_ref[...] = jnp.full_like(m_ref, NEG)
        l_ref[...] = jnp.zeros_like(l_ref)
    queries = stack_heads(q_ref[...], heads, half_mask)
    query_seg = sq_ref[0]
    target = acc if final else acc.at[0]

    for s in range(sets):
        kv, sk, vt = kv_refs[s], sk_refs[s], vt_refs[s]

        def body(j, carry):
            first = pl.multiple_of(j * BK, BK)
            keys = kv[pl.ds(first, BK), 0:width]
            scores = nt(keys, queries)
            same = same_segment(sk[pl.ds(first, BK), :], query_seg, heads)
            scores = jnp.where(same, scores, NEG)
            before = m_ref[...]
            top = jnp.maximum(before, jnp.max(scores, axis=0, keepdims=True))
            raised = jnp.exp(scores - top)
            shrink = jnp.exp(before - top)
            m_ref[...] = top
            l_ref[...] = l_ref[...] * shrink + jnp.sum(raised, axis=0, keepdims=True)
            low = raised.astype(bf16)
            for h in range(heads):
                part = nn(
                    vt[h * each : (h + 1) * each, pl.ds(first, BK)],
                    low[:, h * rows : (h + 1) * rows],
                )
                hold = target[h * each : (h + 1) * each, :]
                target[h * each : (h + 1) * each, :] = (
                    hold * shrink[:, h * rows : (h + 1) * rows] + part
                )
            return carry

        lax.fori_loop(
            bounds[(step * sets + s) * 2], bounds[(step * sets + s) * 2 + 1], body, 0
        )

    if final:
        live = query_seg >= 0
        total = l_ref[...]
        live_all = jnp.concatenate([live] * heads, axis=1) if heads > 1 else live
        total = jnp.where(live_all, total, 1.0)
        inverse = jnp.where(live_all, 1.0 / total, 0.0)
        for h in range(heads):
            acc[h * each : (h + 1) * each, :] = (
                acc[h * each : (h + 1) * each, :] * inverse[:, h * rows : (h + 1) * rows]
            )
        o_ref[...] = acc[...].T.astype(bf16)
        lse_ref[0] = jnp.where(live_all, m_ref[...] + jnp.log(total), FAR)
    else:
        ml_ref[0, 0:1] = m_ref[...]
        ml_ref[0, 1:2] = l_ref[...]


def cost(products, q, kvs):
    pairs = q.shape[0] * 1024
    return pl.CostEstimate(
        flops=4 * products * pairs * q.shape[1],
        bytes_accessed=2 * sum(a.size for a in kvs) + 4 * q.size,
        transcendentals=4 * pairs,
    )


def whole(shape):
    zeros = (0,) * len(shape)
    return pl.BlockSpec(shape, lambda i, *_: zeros)


def attend_call(bounds, q, sq, kvs, sks, heads, state=None):
    count = q.shape[0] // BQ
    width = q.shape[1]
    sets = len(kvs)
    final = state is not None
    row_spec = pl.BlockSpec((BQ, width), lambda i, *_: (i, 0))
    acc_spec = pl.BlockSpec((1, width, BQ), lambda i, *_: (i, 0, 0))
    ml_spec = pl.BlockSpec((1, 2, heads * BQ), lambda i, *_: (i, 0, 0))
    in_specs = [row_spec, pl.BlockSpec((1, 1, BQ), lambda i, *_: (i, 0, 0))]
    in_specs += [whole(a.shape) for a in kvs] + [whole(a.shape) for a in sks]
    scratch = [pltpu.VMEM((1, heads * BQ), f32)] * 2
    scratch += [pltpu.VMEM((width, a.shape[0]), bf16) for a in kvs]
    if final:
        in_specs += [acc_spec, ml_spec]
        out_specs = [row_spec, pl.BlockSpec((1, 1, heads * BQ), lambda i, *_: (i, 0, 0))]
        out_shape = [
            jax.ShapeDtypeStruct(q.shape, bf16),
            jax.ShapeDtypeStruct((count, 1, heads * BQ), f32),
        ]
        scratch = [pltpu.VMEM((width, BQ), f32)] + scratch
    else:
        out_specs = [acc_spec, ml_spec]
        out_shape = [
            jax.ShapeDtypeStruct((count, width, BQ), f32),
            jax.ShapeDtypeStruct((count, 2, heads * BQ), f32),
        ]
    return pl.pallas_call(
        functools.partial(forward_kernel, heads, sets, final),
        grid_spec=pltpu.PrefetchScalarGridSpec(
            num_scalar_prefetch=1,
            grid=(count,),
            in_specs=in_specs,
            out_specs=out_specs,
            scratch_shapes=scratch,
        ),
        out_shape=out_shape,
        cost_estimate=cost(4, q, kvs),
        name="attend_final" if final else "attend_own",
    )(bounds, q, sq, *kvs, *sks, *(state or ()))


def backward_kernel(heads, sets, final, bounds, *refs):
    refs = list(refs)
    q_ref, do_ref, o_ref, lse_ref, sq_ref = refs[:5]
    kv_refs = refs[5 : 5 + sets]
    sk_refs = refs[5 + sets : 5 + 2 * sets]
    rest = refs[5 + 2 * sets :]
    if final:
        dq_in, dq_ref = rest[0], rest[1]
        dkv_refs = rest[2 : 2 + sets]
        dq_acc = rest[2 + sets]
        kt_refs = rest[3 + sets : 3 + 2 * sets]
        sums = dkv_refs
    else:
        dq_ref = rest[0]
        dkv_refs = rest[1 : 1 + sets]
        dq_acc = rest[1 + sets]
        kt_refs = rest[2 + sets : 2 + 2 * sets]
        sums = rest[2 + 2 * sets :]
    step = pl.program_id(0)
    rows, width = q_ref.shape
    each = width // heads
    half = width // 2
    piece = half // heads

    @pl.when(step == 0)
    def _():
        for kv, kt, total in zip(kv_refs, kt_refs, sums):
            total[...] = jnp.zeros_like(total)
            for j in range(kv.shape[0] // BK):
                kt[:, j * BK : (j + 1) * BK] = kv[j * BK : (j + 1) * BK, :width].T

    if final:
        dq_acc[...] = dq_in[0]
    else:
        dq_acc[...] = jnp.zeros_like(dq_acc)
    grads = do_ref[...]
    queries = stack_heads(q_ref[...], heads, half_mask)
    outs = stack_heads(grads, heads, whole_mask)
    query_seg = sq_ref[0]
    lse = lse_ref[0]
    product = (grads.astype(f32) * o_ref[...].astype(f32)).T
    delta = jnp.concatenate(
        [
            jnp.sum(product[h * each : (h + 1) * each], axis=0, keepdims=True)
            for h in range(heads)
        ],
        axis=1,
    )

    for s in range(sets):
        kv, sk, kt, total = kv_refs[s], sk_refs[s], kt_refs[s], sums[s]

        def body(j, carry):
            first = pl.multiple_of(j * BK, BK)
            keys = kv[pl.ds(first, BK), 0:width]
            values = kv[pl.ds(first, BK), width : 2 * width]
            scores = nt(keys, queries)
            same = same_segment(sk[pl.ds(first, BK), :], query_seg, heads)
            probs = jnp.where(same, jnp.exp(scores - lse), 0.0)
            grad_probs = nt(values, outs)
            grad_scores = (probs * (grad_probs - delta)).astype(bf16)
            low = probs.astype(bf16)
            total[pl.ds(first, BK), width : 2 * width] += nn(low, outs)
            total[pl.ds(first, BK), 0:width] += nn(grad_scores, queries)
            for h in range(heads):
                column = grad_scores[:, h * rows : (h + 1) * rows]
                for lead in (h * piece, half + h * piece):
                    dq_acc[lead : lead + piece, :] += nn(
                        kt[lead : lead + piece, pl.ds(first, BK)], column
                    )
            return carry

        lax.fori_loop(
            bounds[(step * sets + s) * 2], bounds[(step * sets + s) * 2 + 1], body, 0
        )

    if final:
        dq_ref[...] = dq_acc[...].T
    else:
        dq_ref[0] = dq_acc[...]

        @pl.when(step == pl.num_programs(0) - 1)
        def _():
            for total, out in zip(sums, dkv_refs):
                out[...] = total[...].astype(bf16)


def attend_back_call(bounds, q, do, o, lse, sq, kvs, sks, heads, state=None):
    count = q.shape[0] // BQ
    width = q.shape[1]
    sets = len(kvs)
    final = state is not None
    row_spec = pl.BlockSpec((BQ, width), lambda i, *_: (i, 0))
    acc_spec = pl.BlockSpec((1, width, BQ), lambda i, *_: (i, 0, 0))
    in_specs = [row_spec] * 3 + [
        pl.BlockSpec((1, 1, heads * BQ), lambda i, *_: (i, 0, 0)),
        pl.BlockSpec((1, 1, BQ), lambda i, *_: (i, 0, 0)),
    ]
    in_specs += [whole(a.shape) for a in kvs] + [whole(a.shape) for a in sks]
    scratch = [pltpu.VMEM((width, BQ), f32)]
    scratch += [pltpu.VMEM((width, a.shape[0]), bf16) for a in kvs]
    if final:
        in_specs += [acc_spec]
        out_specs = [row_spec]
        out_shape = [jax.ShapeDtypeStruct(q.shape, f32)]
    else:
        out_specs = [acc_spec]
        out_shape = [jax.ShapeDtypeStruct((count, width, BQ), f32)]
        scratch += [pltpu.VMEM(a.shape, f32) for a in kvs]
    out_specs += [whole(a.shape) for a in kvs]
    out_shape += [jax.ShapeDtypeStruct(a.shape, f32 if final else bf16) for a in kvs]
    return pl.pallas_call(
        functools.partial(backward_kernel, heads, sets, final),
        grid_spec=pltpu.PrefetchScalarGridSpec(
            num_scalar_prefetch=1,
            grid=(count,),
            in_specs=in_specs,
            out_specs=out_specs,
            scratch_shapes=scratch,
        ),
        out_shape=out_shape,
        cost_estimate=cost(10, q, kvs),
        name="back_own" if final else "back_halo",
    )(bounds, q, do, o, lse, sq, *kvs, *sks, *(state or ()))


def place_tables(seq_lengths, seq_offsets, first, count):
    place = first + jnp.arange(count, dtype=jnp.int32)
    ends = seq_offsets + seq_lengths
    inside = (place[:, None] >= seq_offsets[None, :]) & (place[:, None] < ends[None, :])
    live = jnp.any(inside, axis=1)
    index = jnp.arange(seq_offsets.shape[0], dtype=jnp.int32)
    segment = jnp.sum(jnp.where(inside, index[None, :], 0), axis=1)
    start = jnp.sum(jnp.where(inside, seq_offsets[None, :], 0), axis=1)
    end = jnp.sum(jnp.where(inside, ends[None, :], 0), axis=1)
    return live, segment, start, end, place


def qkv_order(heads, head_width):
    width = heads * head_width
    half = head_width // 2
    new = jnp.arange(3 * width, dtype=jnp.int32)
    kind = new // width
    inner = new % width
    side = inner // (width // 2)
    pair_head = (inner % (width // 2)) // half
    pair_old = pair_head * 3 * head_width + kind * head_width + side * half + inner % half
    value_old = (inner // head_width) * 3 * head_width + 2 * head_width + inner % head_width
    old = jnp.where(kind == 2, value_old, pair_old)
    return (old[None, :] == new[:, None]).astype(bf16)


def local(
    tokens,
    gain_attn,
    w_qkv,
    w_out,
    gain_mlp,
    w_in,
    w_down,
    cotangent,
    seq_lengths,
    seq_offsets,
    deal,
):
    R, C, B = lax.axis_size("row"), lax.axis_size("col"), lax.axis_size("dp")
    r, c, b = lax.axis_index("row"), lax.axis_index("col"), lax.axis_index("dp")
    S, Dl = tokens.shape
    D = Dl * R
    two = R == 2 and C == 2 and B == 8
    heads = w_qkv.shape[1] // R
    head_width = w_qkv.shape[2] // 3
    W = heads * head_width
    F = w_down.shape[0]
    H = LONGEST
    Sr = S // R
    zrow, zcol = (r == 0), (c == 0)

    def to_row(a):
        return lax.ppermute(a, "row", SWAP)

    def to_col(a):
        return lax.ppermute(a, "col", SWAP)

    def ordered(flag, mine, theirs, axis):
        return jnp.where(
            flag,
            jnp.concatenate([mine, theirs], axis=axis),
            jnp.concatenate([theirs, mine], axis=axis),
        )

    def own_first(a, axis):
        if not two:
            return a
        n = a.shape[axis] // 2
        return jnp.where(zrow, a, jnp.roll(a, n, axis=axis))

    def take(a, index, size, axis=0):
        return lax.dynamic_slice_in_dim(a, index * size, size, axis)

    def partner(a):
        n = a.shape[0] // 2
        got = to_row(take(a, c, n))
        return ordered(zcol, got, to_col(got), 0)

    def gather(a, axis):
        if two:
            return jnp.concatenate([a, to_row(a)], axis=axis)
        return lax.all_gather(a, "row", axis=axis, tiled=True)

    def col_sum(a):
        return a + to_col(a.astype(bf16)).astype(f32) if C == 2 else lax.psum(a, "col")

    live_x, seg_x, start_x, end_x, place_x = place_tables(seq_lengths, seq_offsets, b * S - H, S + 2 * H)
    key_seg = jnp.broadcast_to(jnp.where(live_x, seg_x, -2)[:, None], (S + 2 * H, 128))
    sk_left, sk_own, sk_right = key_seg[:H], key_seg[H : H + S], key_seg[H + S :]
    live = live_x[H : H + S]
    nq = S // BQ
    sq = jnp.where(live, seg_x[H : H + S], -1).reshape(nq, 1, BQ)
    first = jnp.min(jnp.where(live, start_x[H : H + S] - b * S, 4 * S).reshape(nq, BQ), axis=1)
    last = jnp.max(jnp.where(live, end_x[H : H + S] - b * S, -4 * S).reshape(nq, BQ), axis=1)
    own_low = jnp.clip(first, 0, S) // BK
    own_high = (jnp.clip(last, 0, S) + BK - 1) // BK
    left_low = jnp.clip(first + H, 0, H) // BK
    right_high = (jnp.clip(last - S, 0, H) + BK - 1) // BK
    own_bounds = jnp.stack([own_low, own_high], axis=1).reshape(-1).astype(jnp.int32)
    zero = jnp.zeros_like(left_low)
    halo_bounds = (
        jnp.stack([left_low, zero + H // BK, zero, right_high], axis=1).reshape(-1).astype(jnp.int32)
    )
    position = jnp.where(live, place_x[H : H + S] - start_x[H : H + S], 0)
    freq = rope_base ** (-(jnp.arange(0, head_width, 2, dtype=f32) / head_width))
    angle = position.astype(f32)[:, None] * jnp.tile(freq, heads)[None, :]
    cosine, sine = lax.optimization_barrier((jnp.cos(angle), jnp.sin(angle)))

    live_column = live[:, None]
    if two:
        x_got = partner(tokens)
        x_low = jnp.where(live_column, jnp.concatenate([tokens, x_got], axis=1), 0)
    else:
        own_x = jnp.where(live_column, tokens, 0)
        x_low = lax.all_gather(own_x, "row", axis=1, tiled=True)

    wq_low = w_qkv.reshape(Dl, R * 3 * W).astype(bf16)
    if two:
        wq_mine = take(wq_low, r, 3 * W, 1)
        wq_got = to_row(take(wq_low, 1 - r, 3 * W, 1))
    else:
        wq = lax.all_to_all(wq_low, "row", split_axis=1, concat_axis=0, tiled=True)
    order = qkv_order(heads, head_width)

    gain_one = own_first(gain_attn, 0)
    gain_two = own_first(gain_mlp, 0)

    x = x_low.astype(f32)
    center = x - jnp.mean(x, axis=-1, keepdims=True)
    inverse_one = lax.rsqrt(jnp.mean(center * center, axis=-1, keepdims=True) + epsilon)
    mean_one = jnp.mean(x, axis=-1, keepdims=True)
    h1 = (center * inverse_one * gain_one).astype(bf16)
    if two:
        h1, wq_mine, wq_got = lax.optimization_barrier((h1, wq_mine, wq_got))
        wq = jnp.concatenate([wq_mine, wq_got], axis=0)
    wq = nn(wq, order).astype(bf16)

    half = W // 2

    def turn(t, sign):
        first_half, second_half = t[:, :half], t[:, half:]
        s = sine * sign
        return jnp.concatenate(
            [first_half * cosine - second_half * s, second_half * cosine + first_half * s], axis=1
        )

    kv_raw = nn(h1, wq[:, W:])
    kv = jnp.concatenate([turn(kv_raw[:, :W], 1.0), kv_raw[:, W:]], axis=1).astype(bf16)
    up = [(i, i + 1) for i in range(B - 1)]
    down = [(i + 1, i) for i in range(B - 1)]
    kv_left = lax.ppermute(kv[S - H :], "dp", up)
    kv_right = lax.ppermute(kv[:H], "dp", down)
    q = (turn(nn(h1, wq[:, :W]), 1.0) * (1.0 / math.sqrt(head_width))).astype(bf16)
    state = attend_call(own_bounds, q, sq, [kv], [sk_own], heads)
    o, lse = attend_call(
        halo_bounds, q, sq, [kv_left, kv_right], [sk_left, sk_right], heads, state
    )

    wo_low, wd_low = w_out.astype(bf16), w_down.astype(bf16)
    act_low, lin_low = w_in[:, 0].astype(bf16), w_in[:, 1].astype(bf16)
    if two:
        wo_low = after(wo_low, x_got)
        act_low, lin_low = after((act_low, lin_low), wq_got)
        wo_got, act_got, lin_got = to_row(wo_low), to_row(act_low), to_row(lin_low)
        o, wo_got = lax.optimization_barrier((o, wo_got))
        wo = own_first(jnp.concatenate([wo_low, wo_got], axis=1), 0)
    else:
        wo = gather(wo_low, 1)

    if two:
        o_got = to_row(take(o, 1 - r, Sr))
        o_rows = jnp.concatenate([take(o, r, Sr), o_got], axis=1)
        g_send, wd_send = after((take(cotangent, 1 - r, Sr), wd_low), o_got)
        wd_got = to_row(wd_send)
        g_low = jnp.concatenate([take(cotangent, r, Sr), partner(g_send)], axis=1)
        g_low = jnp.where(take(live, r, Sr)[:, None], g_low, 0)
        wds = [wd_low, wd_got]
        acts, lins = [act_low, act_got], [lin_low, lin_got]
    else:
        o_rows = lax.all_to_all(o, "row", split_axis=0, concat_axis=1, tiled=True)
        own_g = jnp.where(live_column, cotangent, 0)
        g_low = lax.all_to_all(own_g, "row", split_axis=0, concat_axis=1, tiled=True)
        wds, acts, lins = [gather(wd_low, 1)], [gather(act_low, 0)], [gather(lin_low, 0)]

    def split_nn(a, parts):
        n = a.shape[1] // len(parts)
        return sum(nn(a[:, i * n : (i + 1) * n], w) for i, w in enumerate(parts))

    def split_nt(a, parts):
        n = a.shape[1] // len(parts)
        return sum(nt(a[:, i * n : (i + 1) * n], w) for i, w in enumerate(parts))

    def wide(parts):
        return parts[0] if len(parts) == 1 else jnp.concatenate(parts, axis=1)

    x_rows = take(x_low, r, Sr).astype(f32)
    if C == 2:
        o_all = jnp.concatenate([o_rows, to_col(o_rows)], axis=1)
        wo_all = jnp.concatenate([wo, to_col(wo)], axis=0)
        x1 = x_rows + nn(o_all, wo_all)
    else:
        x1 = x_rows + lax.psum(nn(o_rows, wo), "col")

    center = x1 - jnp.mean(x1, axis=-1, keepdims=True)
    inverse_two = lax.rsqrt(jnp.mean(center * center, axis=-1, keepdims=True) + epsilon)
    n2 = center * inverse_two
    h2 = (n2 * gain_two).astype(bf16)
    a = split_nn(h2, acts)
    u = split_nn(h2, lins)
    phi = 0.5 + 0.5 * lax.erf(a * math.sqrt(0.5))
    gelu = a * phi
    slope = phi + a * jnp.exp(-0.5 * a * a) * (1.0 / math.sqrt(2.0 * math.pi))
    m = (gelu * u).astype(bf16)
    y_part = wide([nn(m, w) for w in wds])
    if two:
        n = Sr // 2
        y_half = (
            take(x1, c, n) + take(y_part, c, n) + to_col(take(y_part, 1 - c, n).astype(bf16)).astype(f32)
        ).astype(bf16)
        mine, theirs = y_half[:, :Dl], to_row(y_half[:, Dl:])
        pair = ordered(zrow, mine[None], theirs[None], 0)
        layer_out = ordered(zcol, pair[:, None], to_col(pair)[:, None], 1).reshape(S, Dl)
    else:
        y = (x1 + col_sum(y_part)).astype(bf16)
        layer_out = lax.all_to_all(y, "row", split_axis=1, concat_axis=0, tiled=True)

    dm = split_nt(g_low, wds)
    da = (dm * u * slope).astype(bf16)
    du = (dm * gelu).astype(bf16)
    dh2 = col_sum(wide([nt(da, v) + nt(du, w) for v, w in zip(acts, lins)]))
    e2 = dh2 * gain_two
    dx1 = g_low.astype(f32) + inverse_two * (
        e2
        - jnp.mean(e2, axis=-1, keepdims=True)
        - n2 * jnp.mean(e2 * n2, axis=-1, keepdims=True)
    )
    dx_low = dx1.astype(bf16)
    do_rows = nt(dx_low, wo).astype(bf16)
    if two:
        do_got = to_row(do_rows[:, W:])
        do = ordered(zrow, do_rows[:, :W], do_got, 0)
    else:
        do = lax.all_to_all(do_rows, "row", split_axis=1, concat_axis=0, tiled=True)

    dq_part, dkv_left, dkv_right = attend_back_call(
        halo_bounds, q, do, o, lse, sq, [kv_left, kv_right], [sk_left, sk_right], heads
    )
    from_right = lax.ppermute(dkv_left, "dp", down)
    from_left = lax.ppermute(dkv_right, "dp", up)
    dq, dkv = attend_back_call(own_bounds, q, do, o, lse, sq, [kv], [sk_own], heads, [dq_part])
    pad = jnp.zeros((S - H, 2 * W), bf16)
    dkv = (
        dkv
        + jnp.concatenate([pad, from_right], axis=0).astype(f32)
        + jnp.concatenate([from_left, pad], axis=0).astype(f32)
    )
    dq = turn(dq * (1.0 / math.sqrt(head_width)), -1.0)
    dt = jnp.concatenate([dq, turn(dkv[:, :W], -1.0), dkv[:, W:]], axis=1).astype(bf16)
    dh1_part = nt(dt, wq)

    if two:
        n = S // 2
        kept = take(dh1_part, c, n) + to_col(take(dh1_part, 1 - c, n).astype(bf16)).astype(f32)
        xs = take(x_low, c, n).astype(f32)
        inv, mean = take(inverse_one, c, n), take(mean_one, c, n)
        n1 = (xs - mean) * inv
        e1 = kept * gain_one
        sums = jnp.stack([jnp.sum(e1, axis=-1), jnp.sum(e1 * n1, axis=-1)])
        sums = (sums + to_row(sums)) * (1.0 / D)
        mine = (kept[:, :Dl] + to_row(kept[:, Dl:].astype(bf16)).astype(f32)) * gain_one[:Dl]
        moved = lax.ppermute(after(dx_low[:, Dl:], do_got), ("row", "col"), [(0, 2), (3, 1)])
        base = jnp.where(r == c, dx1[:, :Dl], moved.astype(f32))
        dx = base + inv * (mine - sums[0][:, None] - n1[:, :Dl] * sums[1][:, None])
        dx = dx.astype(bf16)
        tokens_grad = ordered(zcol, dx, to_col(dx), 0)
    else:
        dh1 = lax.psum_scatter(col_sum(dh1_part), "row", scatter_dimension=1, tiled=True)
        xs = own_x.astype(f32)
        n1 = (xs - mean_one) * inverse_one
        e1 = dh1 * take(gain_attn, r, Dl)
        sums = lax.psum(jnp.stack([jnp.sum(e1, axis=-1), jnp.sum(e1 * n1, axis=-1)]), "row") / D
        base = lax.all_to_all(dx_low, "row", split_axis=1, concat_axis=0, tiled=True).astype(f32)
        tokens_grad = (
            base + inverse_one * (e1 - sums[0][:, None] - n1 * sums[1][:, None])
        ).astype(bf16)

    Db = D // B
    Dd = D // (B * R)
    if two:
        y_bit, z_bits = b % 2, b // 2

        def relative(a, outer):
            n = jnp.arange(D, dtype=jnp.int32)
            high, middle, low = n // (D // 2), n // Db % 4, n // Dd % 2
            y_rel, x_rel = (high, low) if outer == "y" else (low, high)
            column = ((z_bits ^ middle) * 2 + (y_bit ^ y_rel)) * Db + n % Dd
            column = column + (low if outer == "y" and a.shape[0] == S else r ^ x_rel) * Dd
            column = column ^ (r * (D // 2))
            return nn(a, (n[:, None] == column[None, :]).astype(bf16)).astype(bf16)

        def to_y(a):
            return lax.ppermute(a.astype(bf16), "dp", [(i, i ^ 1) for i in range(B)])

        def over_z(a):
            n = a.shape[1] // 4
            total = a[:, :n].astype(f32)
            for j in (3, 2, 1):
                got = lax.ppermute(a[:, j * n : (j + 1) * n], "dp", [(i, i ^ (2 * j)) for i in range(B)])
                total = total + got.astype(f32)
            return total

        def halve(left, right, move):
            got = move(tn(left, right[:, D // 2 :]).astype(bf16))
            return (tn(left, right[:, : D // 2]) + got.astype(f32)).astype(bf16)

        def x_last(left, right):
            part = over_z(halve(left, right, to_y))
            return part[:, :Dd] + to_row(part[:, Dd:].astype(bf16)).astype(f32)

        def x_first(left, right):
            part = over_z(halve(left, right, to_row))
            return part[:, :Dd] + to_y(part[:, Dd:]).astype(f32)

        lower = x_last(m, relative(g_low, "y"))
        act = x_first(da, after(relative(h2, "x"), do_got))
        lin = x_last(du, relative(h2, "y"))
        gate = jnp.stack([act.T, lin.T])
        proj = x_last(own_first(o_rows, 1), relative(dx_low, "y"))
        query = over_z(halve(dt, relative(h1, "y"), to_y)).T
        wq_rows = take(wq, b ^ (4 * r), Db)
        place = (2 * b + r) ^ (8 * r)
        side, inner = place // 8, place % 8
        wi_rows = jnp.stack(
            [take(jnp.where(side == 0, w[0], w[1]), inner, Dd) for w in (acts, lins)]
        )
    else:

        def scatter(grad):
            return lax.psum_scatter(grad, ("dp", "row"), scatter_dimension=1, tiled=True).astype(f32)

        gate = jnp.stack([scatter(tn(da, h2).astype(bf16)).T, scatter(tn(du, h2).astype(bf16)).T])
        proj = scatter(tn(o_rows, dx_low).astype(bf16))
        lower = scatter(tn(m, g_low).astype(bf16))
        query = lax.psum_scatter(
            tn(h1, dt).astype(bf16), "dp", scatter_dimension=0, tiled=True
        ).astype(f32)
        wq_rows = take(wq, b, Db)
        wi_rows = jnp.stack([take(acts[0], b * R + r, Dd), take(lins[0], b * R + r, Dd)])

    one_part = jnp.sum(query * wq_rows.astype(f32), axis=1)
    two_part = jnp.sum(jnp.sum(gate * wi_rows.astype(f32), axis=2), axis=0)
    natural = lax.dot_general(
        query, order.astype(f32), (((1,), (1,)), ((), ())),
        precision=lax.Precision.HIGHEST, preferred_element_type=f32,
    )
    if two:
        one_part = one_part + to_row(one_part)
        one_part = take(one_part, r, Dd)
        pair = natural.reshape(2, Dd, 3 * W)
        mine = lax.dynamic_index_in_dim(pair, r, 0, keepdims=False)
        theirs = to_row(lax.dynamic_index_in_dim(pair, 1 - r, 0, keepdims=False))
        query_out = ordered(zrow, mine, theirs, 1)
    else:
        one_part = take(lax.psum(one_part, "row"), r, Dd)
        query_out = lax.all_to_all(natural, "row", split_axis=0, concat_axis=1, tiled=True)
    gains = jnp.stack([one_part, two_part])
    gains = gains + to_col(gains) if C == 2 else lax.psum(gains, "col")
    gain_attn_grad = gains[0] / take(gain_attn, b * R + r, Dd)
    gain_mlp_grad = gains[1] / take(gain_mlp, b * R + r, Dd)
    return (
        layer_out,
        tokens_grad,
        gain_attn_grad,
        query_out.reshape(Dd, R * heads, 3 * head_width),
        proj,
        gain_mlp_grad,
        jnp.swapaxes(gate, 0, 1),
        lower,
    )


def solution(mesh):
    return jax.shard_map(
        local,
        mesh=mesh,
        in_specs=(
            P("dp", "row"),
            P(),
            P("row", "col", None),
            P("col", "row"),
            P(),
            P("row", None, "col"),
            P("col", "row"),
            P("dp", "row"),
            P(),
            P(),
            P(),
        ),
        out_specs=(
            P("dp", "row"),
            P("dp", "row"),
            P(("dp", "row")),
            P(("dp", "row"), "col", None),
            P("col", ("dp", "row")),
            P(("dp", "row")),
            P(("dp", "row"), None, "col"),
            P("col", ("dp", "row")),
        ),
        check_vma=False,
    )
```

```python
import functools
import math

import jax
import jax.numpy as jnp
from jax import lax
from jax.experimental import pallas as pl
from jax.experimental.pallas import tpu as pltpu
from jax.sharding import PartitionSpec as P

LONGEST = 1024
BQ = 256
BK = 256
NEG = -1e30
FAR = 1e30
epsilon = 1e-05
rope_base = 160000.0
bf16 = jnp.bfloat16
f32 = jnp.float32
SWAP = [(0, 1), (1, 0)]


def nt(a, b):
    return lax.dot_general(a, b, (((1,), (1,)), ((), ())), preferred_element_type=f32)


def tn(a, b):
    return lax.dot_general(a, b, (((0,), (0,)), ((), ())), preferred_element_type=f32)


def nn(a, b):
    return jnp.dot(a, b, preferred_element_type=f32)


def after(a, *others):
    return lax.optimization_barrier((a, *others))[0]


def half_mask(width, heads, head):
    lane = lax.broadcasted_iota(jnp.int32, (1, width), 1)
    half = width // 2
    lane = jnp.where(lane >= half, lane - half, lane)
    step = half // heads
    return (lane >= head * step) & (lane < (head + 1) * step)


def whole_mask(width, heads, head):
    lane = lax.broadcasted_iota(jnp.int32, (1, width), 1)
    step = width // heads
    return (lane >= head * step) & (lane < (head + 1) * step)


def stack_heads(block, heads, mask_of):
    zero = jnp.zeros_like(block)
    width = block.shape[1]
    return jnp.concatenate(
        [jnp.where(mask_of(width, heads, h), block, zero) for h in range(heads)], axis=0
    )


def same_segment(key_seg, query_seg, heads):
    tile = key_seg
    lanes = query_seg.shape[1]
    if lanes > tile.shape[1]:
        tile = jnp.concatenate([tile] * (lanes // tile.shape[1]), axis=1)
    same = tile == query_seg
    return jnp.concatenate([same] * heads, axis=1) if heads > 1 else same


def forward_kernel(heads, sets, final, bounds, *refs):
    refs = list(refs)
    q_ref, sq_ref = refs[:2]
    kv_refs = refs[2 : 2 + sets]
    sk_refs = refs[2 + sets : 2 + 2 * sets]
    rest = refs[2 + 2 * sets :]
    if final:
        acc_in, ml_in, o_ref, lse_ref = rest[:4]
        acc, m_ref, l_ref = rest[4:7]
        vt_refs = rest[7:]
    else:
        acc, ml_ref = rest[:2]
        m_ref, l_ref = rest[2:4]
        vt_refs = rest[4:]
    step = pl.program_id(0)
    rows, width = q_ref.shape
    each = width // heads

    @pl.when(step == 0)
    def _():
        for kv, vt in zip(kv_refs, vt_refs):
            for j in range(kv.shape[0] // BK):
                vt[:, j * BK : (j + 1) * BK] = kv[j * BK : (j + 1) * BK, width:].T

    if final:
        acc[...] = acc_in[0]
        m_ref[...] = ml_in[0, 0:1]
        l_ref[...] = ml_in[0, 1:2]
    else:
        acc[...] = jnp.zeros_like(acc)
        m_ref[...] = jnp.full_like(m_ref, NEG)
        l_ref[...] = jnp.zeros_like(l_ref)
    queries = stack_heads(q_ref[...], heads, half_mask)
    query_seg = sq_ref[0]
    target = acc if final else acc.at[0]

    for s in range(sets):
        kv, sk, vt = kv_refs[s], sk_refs[s], vt_refs[s]

        def body(j, carry):
            first = pl.multiple_of(j * BK, BK)
            keys = kv[pl.ds(first, BK), 0:width]
            scores = nt(keys, queries)
            same = same_segment(sk[pl.ds(first, BK), :], query_seg, heads)
            scores = jnp.where(same, scores, NEG)
            before = m_ref[...]
            top = jnp.maximum(before, jnp.max(scores, axis=0, keepdims=True))
            raised = jnp.exp(scores - top)
            shrink = jnp.exp(before - top)
            m_ref[...] = top
            l_ref[...] = l_ref[...] * shrink + jnp.sum(raised, axis=0, keepdims=True)
            low = raised.astype(bf16)
            for h in range(heads):
                part = nn(
                    vt[h * each : (h + 1) * each, pl.ds(first, BK)],
                    low[:, h * rows : (h + 1) * rows],
                )
                hold = target[h * each : (h + 1) * each, :]
                target[h * each : (h + 1) * each, :] = (
                    hold * shrink[:, h * rows : (h + 1) * rows] + part
                )
            return carry

        lax.fori_loop(
            bounds[(step * sets + s) * 2], bounds[(step * sets + s) * 2 + 1], body, 0
        )

    if final:
        live = query_seg >= 0
        total = l_ref[...]
        live_all = jnp.concatenate([live] * heads, axis=1) if heads > 1 else live
        total = jnp.where(live_all, total, 1.0)
        inverse = jnp.where(live_all, 1.0 / total, 0.0)
        for h in range(heads):
            acc[h * each : (h + 1) * each, :] = (
                acc[h * each : (h + 1) * each, :] * inverse[:, h * rows : (h + 1) * rows]
            )
        o_ref[...] = acc[...].T.astype(bf16)
        lse_ref[0] = jnp.where(live_all, m_ref[...] + jnp.log(total), FAR)
    else:
        ml_ref[0, 0:1] = m_ref[...]
        ml_ref[0, 1:2] = l_ref[...]


def cost(products, q, kvs):
    pairs = q.shape[0]
    return pl.CostEstimate(
        flops=4 * products * pairs * q.shape[1],
        bytes_accessed=2 * sum(a.size for a in kvs) + 4 * q.size,
        transcendentals=4 * pairs,
    )


def whole(shape):
    zeros = (0,) * len(shape)
    return pl.BlockSpec(shape, lambda i, *_: zeros)


def attend_call(bounds, q, sq, kvs, sks, heads, state=None):
    count = q.shape[0] // BQ
    width = q.shape[1]
    sets = len(kvs)
    final = state is not None
    row_spec = pl.BlockSpec((BQ, width), lambda i, *_: (i, 0))
    acc_spec = pl.BlockSpec((1, width, BQ), lambda i, *_: (i, 0, 0))
    ml_spec = pl.BlockSpec((1, 2, heads * BQ), lambda i, *_: (i, 0, 0))
    in_specs = [row_spec, pl.BlockSpec((1, 1, BQ), lambda i, *_: (i, 0, 0))]
    in_specs += [whole(a.shape) for a in kvs] + [whole(a.shape) for a in sks]
    scratch = [pltpu.VMEM((1, heads * BQ), f32)] * 2
    scratch += [pltpu.VMEM((width, a.shape[0]), bf16) for a in kvs]
    if final:
        in_specs += [acc_spec, ml_spec]
        out_specs = [row_spec, pl.BlockSpec((1, 1, heads * BQ), lambda i, *_: (i, 0, 0))]
        out_shape = [
            jax.ShapeDtypeStruct(q.shape, bf16),
            jax.ShapeDtypeStruct((count, 1, heads * BQ), f32),
        ]
        scratch = [pltpu.VMEM((width, BQ), f32)] + scratch
    else:
        out_specs = [acc_spec, ml_spec]
        out_shape = [
            jax.ShapeDtypeStruct((count, width, BQ), f32),
            jax.ShapeDtypeStruct((count, 2, heads * BQ), f32),
        ]
    return pl.pallas_call(
        functools.partial(forward_kernel, heads, sets, final),
        grid_spec=pltpu.PrefetchScalarGridSpec(
            num_scalar_prefetch=1,
            grid=(count,),
            in_specs=in_specs,
            out_specs=out_specs,
            scratch_shapes=scratch,
        ),
        out_shape=out_shape,
        cost_estimate=cost(4, q, kvs),
        name="attend_final" if final else "attend_own",
    )(bounds, q, sq, *kvs, *sks, *(state or ()))


def backward_kernel(heads, sets, final, bounds, *refs):
    refs = list(refs)
    q_ref, do_ref, o_ref, lse_ref, sq_ref = refs[:5]
    kv_refs = refs[5 : 5 + sets]
    sk_refs = refs[5 + sets : 5 + 2 * sets]
    rest = refs[5 + 2 * sets :]
    if final:
        dq_in, dq_ref = rest[0], rest[1]
        dkv_refs = rest[2 : 2 + sets]
        dq_acc = rest[2 + sets]
        kt_refs = rest[3 + sets : 3 + 2 * sets]
        sums = dkv_refs
    else:
        dq_ref = rest[0]
        dkv_refs = rest[1 : 1 + sets]
        dq_acc = rest[1 + sets]
        kt_refs = rest[2 + sets : 2 + 2 * sets]
        sums = rest[2 + 2 * sets :]
    step = pl.program_id(0)
    rows, width = q_ref.shape
    each = width // heads
    half = width // 2
    piece = half // heads

    @pl.when(step == 0)
    def _():
        for kv, kt, total in zip(kv_refs, kt_refs, sums):
            total[...] = jnp.zeros_like(total)
            for j in range(kv.shape[0] // BK):
                kt[:, j * BK : (j + 1) * BK] = kv[j * BK : (j + 1) * BK, :width].T

    if final:
        dq_acc[...] = dq_in[0]
    else:
        dq_acc[...] = jnp.zeros_like(dq_acc)
    grads = do_ref[...]
    queries = stack_heads(q_ref[...], heads, half_mask)
    outs = stack_heads(grads, heads, whole_mask)
    query_seg = sq_ref[0]
    lse = lse_ref[0]
    product = (grads.astype(f32) * o_ref[...].astype(f32)).T
    delta = jnp.concatenate(
        [
            jnp.sum(product[h * each : (h + 1) * each], axis=0, keepdims=True)
            for h in range(heads)
        ],
        axis=1,
    )

    for s in range(sets):
        kv, sk, kt, total = kv_refs[s], sk_refs[s], kt_refs[s], sums[s]

        def body(j, carry):
            first = pl.multiple_of(j * BK, BK)
            keys = kv[pl.ds(first, BK), 0:width]
            values = kv[pl.ds(first, BK), width : 2 * width]
            scores = nt(keys, queries)
            same = same_segment(sk[pl.ds(first, BK), :], query_seg, heads)
            probs = jnp.where(same, jnp.exp(scores - lse), 0.0)
            grad_probs = nt(values, outs)
            grad_scores = (probs * (grad_probs - delta)).astype(bf16)
            low = probs.astype(bf16)
            total[pl.ds(first, BK), width : 2 * width] += nn(low, outs)
            total[pl.ds(first, BK), 0:width] += nn(grad_scores, queries)
            for h in range(heads):
                column = grad_scores[:, h * rows : (h + 1) * rows]
                for lead in (h * piece, half + h * piece):
                    dq_acc[lead : lead + piece, :] += nn(
                        kt[lead : lead + piece, pl.ds(first, BK)], column
                    )
            return carry

        lax.fori_loop(
            bounds[(step * sets + s) * 2], bounds[(step * sets + s) * 2 + 1], body, 0
        )

    if final:
        dq_ref[...] = dq_acc[...].T
    else:
        dq_ref[0] = dq_acc[...]

        @pl.when(step == pl.num_programs(0) - 1)
        def _():
            for total, out in zip(sums, dkv_refs):
                out[...] = total[...].astype(bf16)


def attend_back_call(bounds, q, do, o, lse, sq, kvs, sks, heads, state=None):
    count = q.shape[0] // BQ
    width = q.shape[1]
    sets = len(kvs)
    final = state is not None
    row_spec = pl.BlockSpec((BQ, width), lambda i, *_: (i, 0))
    acc_spec = pl.BlockSpec((1, width, BQ), lambda i, *_: (i, 0, 0))
    in_specs = [row_spec] * 3 + [
        pl.BlockSpec((1, 1, heads * BQ), lambda i, *_: (i, 0, 0)),
        pl.BlockSpec((1, 1, BQ), lambda i, *_: (i, 0, 0)),
    ]
    in_specs += [whole(a.shape) for a in kvs] + [whole(a.shape) for a in sks]
    scratch = [pltpu.VMEM((width, BQ), f32)]
    scratch += [pltpu.VMEM((width, a.shape[0]), bf16) for a in kvs]
    if final:
        in_specs += [acc_spec]
        out_specs = [row_spec]
        out_shape = [jax.ShapeDtypeStruct(q.shape, f32)]
    else:
        out_specs = [acc_spec]
        out_shape = [jax.ShapeDtypeStruct((count, width, BQ), f32)]
        scratch += [pltpu.VMEM(a.shape, f32) for a in kvs]
    out_specs += [whole(a.shape) for a in kvs]
    out_shape += [jax.ShapeDtypeStruct(a.shape, f32 if final else bf16) for a in kvs]
    return pl.pallas_call(
        functools.partial(backward_kernel, heads, sets, final),
        grid_spec=pltpu.PrefetchScalarGridSpec(
            num_scalar_prefetch=1,
            grid=(count,),
            in_specs=in_specs,
            out_specs=out_specs,
            scratch_shapes=scratch,
        ),
        out_shape=out_shape,
        cost_estimate=cost(10, q, kvs),
        name="back_own" if final else "back_halo",
    )(bounds, q, do, o, lse, sq, *kvs, *sks, *(state or ()))


def place_tables(seq_lengths, seq_offsets, first, count):
    place = first + jnp.arange(count, dtype=jnp.int32)
    ends = seq_offsets + seq_lengths
    inside = (place[:, None] >= seq_offsets[None, :]) & (place[:, None] < ends[None, :])
    live = jnp.any(inside, axis=1)
    index = jnp.arange(seq_offsets.shape[0], dtype=jnp.int32)
    segment = jnp.sum(jnp.where(inside, index[None, :], 0), axis=1)
    start = jnp.sum(jnp.where(inside, seq_offsets[None, :], 0), axis=1)
    end = jnp.sum(jnp.where(inside, ends[None, :], 0), axis=1)
    return live, segment, start, end, place


def qkv_order(heads, head_width):
    width = heads * head_width
    half = head_width // 2
    new = jnp.arange(3 * width, dtype=jnp.int32)
    kind = new // width
    inner = new % width
    side = inner // (width // 2)
    pair_head = (inner % (width // 2)) // half
    pair_old = pair_head * 3 * head_width + kind * head_width + side * half + inner % half
    value_old = (inner // head_width) * 3 * head_width + 2 * head_width + inner % head_width
    old = jnp.where(kind == 2, value_old, pair_old)
    return (old[None, :] == new[:, None]).astype(bf16)


def local(
    tokens,
    gain_attn,
    w_qkv,
    w_out,
    gain_mlp,
    w_in,
    w_down,
    cotangent,
    seq_lengths,
    seq_offsets,
    deal,
):
    R, C, B = lax.axis_size("row"), lax.axis_size("col"), lax.axis_size("dp")
    r, c, b = lax.axis_index("row"), lax.axis_index("col"), lax.axis_index("dp")
    S, Dl = tokens.shape
    D = Dl * R
    two = R == 2 and C == 2 and B == 8
    heads = w_qkv.shape[1] // R
    head_width = w_qkv.shape[2] // 3
    W = heads * head_width
    F = w_down.shape[0]
    H = LONGEST
    Sr = S // R
    zrow, zcol = (r == 0), (c == 0)

    def to_row(a):
        return lax.ppermute(a, "row", SWAP)

    def to_col(a):
        return lax.ppermute(a, "col", SWAP)

    def ordered(flag, mine, theirs, axis):
        return jnp.where(
            flag,
            jnp.concatenate([mine, theirs], axis=axis),
            jnp.concatenate([theirs, mine], axis=axis),
        )

    def own_first(a, axis):
        if not two:
            return a
        n = a.shape[axis] // 2
        return jnp.where(zrow, a, jnp.roll(a, n, axis=axis))

    def take(a, index, size, axis=0):
        return lax.dynamic_slice_in_dim(a, index * size, size, axis)

    def partner(a):
        n = a.shape[0] // 2
        got = to_row(take(a, c, n))
        return ordered(zcol, got, to_col(got), 0)

    def gather(a, axis):
        if two:
            return jnp.concatenate([a, to_row(a)], axis=axis)
        return lax.all_gather(a, "row", axis=axis, tiled=True)

    def col_sum(a):
        return a + to_col(a.astype(bf16)).astype(f32) if C == 2 else lax.psum(a, "col")

    live_x, seg_x, start_x, end_x, place_x = place_tables(seq_lengths, seq_offsets, b * S - H, S + 2 * H)
    key_seg = jnp.broadcast_to(jnp.where(live_x, seg_x, -2)[:, None], (S + 2 * H, 128))
    sk_left, sk_own, sk_right = key_seg[:H], key_seg[H : H + S], key_seg[H + S :]
    live = live_x[H : H + S]
    nq = S // BQ
    sq = jnp.where(live, seg_x[H : H + S], -1).reshape(nq, 1, BQ)
    first = jnp.min(jnp.where(live, start_x[H : H + S] - b * S, 4 * S).reshape(nq, BQ), axis=1)
    last = jnp.max(jnp.where(live, end_x[H : H + S] - b * S, -4 * S).reshape(nq, BQ), axis=1)
    own_low = jnp.clip(first, 0, S) // BK
    own_high = (jnp.clip(last, 0, S) + BK - 1) // BK
    left_low = jnp.clip(first + H, 0, H) // BK
    right_high = (jnp.clip(last - S, 0, H) + BK - 1) // BK
    own_bounds = jnp.stack([own_low, own_high], axis=1).reshape(-1).astype(jnp.int32)
    zero = jnp.zeros_like(left_low)
    halo_bounds = (
        jnp.stack([left_low, zero + H // BK, zero, right_high], axis=1).reshape(-1).astype(jnp.int32)
    )
    position = jnp.where(live, place_x[H : H + S] - start_x[H : H + S], 0)
    freq = rope_base ** (-(jnp.arange(0, head_width, 2, dtype=f32) / head_width))
    angle = position.astype(f32)[:, None] * jnp.tile(freq, heads)[None, :]
    cosine, sine = lax.optimization_barrier((jnp.cos(angle), jnp.sin(angle)))

    live_column = live[:, None]
    if two:
        x_got = partner(tokens)
        x_low = jnp.where(live_column, jnp.concatenate([tokens, x_got], axis=1), 0)
    else:
        own_x = jnp.where(live_column, tokens, 0)
        x_low = lax.all_gather(own_x, "row", axis=1, tiled=True)

    wq_low = w_qkv.reshape(Dl, R * 3 * W).astype(bf16)
    if two:
        wq_mine = take(wq_low, r, 3 * W, 1)
        wq_got = to_row(take(wq_low, 1 - r, 3 * W, 1))
    else:
        wq = lax.all_to_all(wq_low, "row", split_axis=1, concat_axis=0, tiled=True)
    order = qkv_order(heads, head_width)

    gain_one = own_first(gain_attn, 0)
    gain_two = own_first(gain_mlp, 0)

    x = x_low.astype(f32)
    center = x - jnp.mean(x, axis=-1, keepdims=True)
    inverse_one = lax.rsqrt(jnp.mean(center * center, axis=-1, keepdims=True) + epsilon)
    mean_one = jnp.mean(x, axis=-1, keepdims=True)
    h1 = (center * inverse_one * gain_one).astype(bf16)
    if two:
        h1, wq_mine, wq_got = lax.optimization_barrier((h1, wq_mine, wq_got))
        wq = jnp.concatenate([wq_mine, wq_got], axis=0)
    wq = nn(wq, order).astype(bf16)

    half = W // 2

    def turn(t, sign):
        first_half, second_half = t[:, :half], t[:, half:]
        s = sine * sign
        return jnp.concatenate(
            [first_half * cosine - second_half * s, second_half * cosine + first_half * s], axis=1
        )

    kv_raw = nn(h1, wq[:, W:])
    kv = jnp.concatenate([turn(kv_raw[:, :W], 1.0), kv_raw[:, W:]], axis=1).astype(bf16)
    up = [(i, i + 1) for i in range(B - 1)]
    down = [(i + 1, i) for i in range(B - 1)]
    kv_left = lax.ppermute(kv[S - H :], "dp", up)
    kv_right = lax.ppermute(kv[:H], "dp", down)
    q = (turn(nn(h1, wq[:, :W]), 1.0) * (1.0 / math.sqrt(head_width))).astype(bf16)
    wo_low, wd_low = w_out.astype(bf16), w_down.astype(bf16)
    act_low, lin_low = w_in[:, 0].astype(bf16), w_in[:, 1].astype(bf16)
    if two:
        act_got = to_row(act_low)
        q, act_got = lax.optimization_barrier((q, act_got))
        lin_got = to_row(after(lin_low, act_got))
    state = attend_call(own_bounds, q, sq, [kv], [sk_own], heads)
    if two:
        state, lin_got = lax.optimization_barrier((state, lin_got))
        wo_got = to_row(after(wo_low, lin_got))
    o, lse = attend_call(
        halo_bounds, q, sq, [kv_left, kv_right], [sk_left, sk_right], heads, state
    )

    if two:
        o, wo_got = lax.optimization_barrier((o, wo_got))
        wo = own_first(jnp.concatenate([wo_low, wo_got], axis=1), 0)
    else:
        wo = gather(wo_low, 1)

    if two:
        o_got = to_row(take(o, 1 - r, Sr))
        o_rows = jnp.concatenate([take(o, r, Sr), o_got], axis=1)
        g_send, wd_send = after((take(cotangent, 1 - r, Sr), wd_low), o_got)
        wd_got = to_row(wd_send)
        g_low = jnp.concatenate([take(cotangent, r, Sr), partner(g_send)], axis=1)
        g_low = jnp.where(take(live, r, Sr)[:, None], g_low, 0)
        wds = [wd_low, wd_got]
        acts, lins = [act_low, act_got], [lin_low, lin_got]
    else:
        o_rows = lax.all_to_all(o, "row", split_axis=0, concat_axis=1, tiled=True)
        own_g = jnp.where(live_column, cotangent, 0)
        g_low = lax.all_to_all(own_g, "row", split_axis=0, concat_axis=1, tiled=True)
        wds, acts, lins = [gather(wd_low, 1)], [gather(act_low, 0)], [gather(lin_low, 0)]

    def split_nn(a, parts):
        n = a.shape[1] // len(parts)
        return sum(nn(a[:, i * n : (i + 1) * n], w) for i, w in enumerate(parts))

    def split_nt(a, parts):
        n = a.shape[1] // len(parts)
        return sum(nt(a[:, i * n : (i + 1) * n], w) for i, w in enumerate(parts))

    def wide(parts):
        return parts[0] if len(parts) == 1 else jnp.concatenate(parts, axis=1)

    x_rows = take(x_low, r, Sr).astype(f32)
    if C == 2:
        o_all = jnp.concatenate([o_rows, to_col(o_rows)], axis=1)
        wo_all = jnp.concatenate([wo, to_col(wo)], axis=0)
        x1 = x_rows + nn(o_all, wo_all)
    else:
        x1 = x_rows + lax.psum(nn(o_rows, wo), "col")

    center = x1 - jnp.mean(x1, axis=-1, keepdims=True)
    inverse_two = lax.rsqrt(jnp.mean(center * center, axis=-1, keepdims=True) + epsilon)
    n2 = center * inverse_two
    h2 = (n2 * gain_two).astype(bf16)
    a = split_nn(h2, acts)
    u = split_nn(h2, lins)
    phi = 0.5 + 0.5 * lax.erf(a * math.sqrt(0.5))
    gelu = a * phi
    slope = phi + a * jnp.exp(-0.5 * a * a) * (1.0 / math.sqrt(2.0 * math.pi))
    m = (gelu * u).astype(bf16)
    y_part = wide([nn(m, w) for w in wds])
    if two:
        n = Sr // 2
        y_half = (
            take(x1, c, n) + take(y_part, c, n) + to_col(take(y_part, 1 - c, n).astype(bf16)).astype(f32)
        ).astype(bf16)
        y_got = to_row(y_half[:, Dl:])
    else:
        y = (x1 + col_sum(y_part)).astype(bf16)
        layer_out = lax.all_to_all(y, "row", split_axis=1, concat_axis=0, tiled=True)

    dm = split_nt(g_low, wds)
    da = (dm * u * slope).astype(bf16)
    du = (dm * gelu).astype(bf16)
    dh2 = col_sum(wide([nt(da, v) + nt(du, w) for v, w in zip(acts, lins)]))
    e2 = dh2 * gain_two
    dx1 = g_low.astype(f32) + inverse_two * (
        e2
        - jnp.mean(e2, axis=-1, keepdims=True)
        - n2 * jnp.mean(e2 * n2, axis=-1, keepdims=True)
    )
    dx_low = dx1.astype(bf16)
    do_rows = nt(dx_low, wo).astype(bf16)
    if two:
        do_got = to_row(do_rows[:, W:])
        do = ordered(zrow, do_rows[:, :W], do_got, 0)
        pair = ordered(zrow, y_half[None, :, :Dl], y_got[None], 0)
        layer_out = ordered(zcol, pair[:, None], to_col(pair)[:, None], 1).reshape(S, Dl)
    else:
        do = lax.all_to_all(do_rows, "row", split_axis=1, concat_axis=0, tiled=True)

    Db = D // B
    Dd = D // (B * R)
    if two:
        y_bit, z_bits = b % 2, b // 2

        def relative(a, bits):
            n = jnp.arange(D, dtype=jnp.int32)
            rel = {"w": 0 * n, "x": 0 * n}
            for i, bit in enumerate(bits):
                rel[bit] = n // (D >> (i + 1)) % 2
            z_rel = 2 * rel["Z"] + rel["z"]
            column = ((z_bits ^ z_rel) * 2 + (y_bit ^ rel["y"])) * Db + n % Dd
            column = column + (rel["w"] if "w" in bits else r ^ rel["x"]) * Dd
            column = column ^ (r * (D // 2))
            return nn(a, (n[:, None] == column[None, :]).astype(bf16)).astype(bf16)

        def to_y(a):
            return lax.ppermute(a, "dp", [(i, i ^ 1) for i in range(B)])

        def to_z(a, j):
            return lax.ppermute(a, "dp", [(i, i ^ (2 * j)) for i in range(B)])

        def first(a):
            return a[:, : a.shape[1] // 2]

        def second(a):
            return a[:, a.shape[1] // 2 :].astype(bf16)

        def product(left, right):
            return tn(left, second(right)).astype(bf16)

        def halved(left, right, got):
            return tn(left, first(right)) + got.astype(f32)

        def joined(part, got):
            return first(part).astype(f32) + got.astype(f32)

        o_heads = own_first(o_rows, 1)
        g_y, dx_y = relative(g_low, "yzZx"), relative(dx_low, "yzZx")
        h_act, h_lin = relative(h2, "xzZy"), relative(h2, "xyzZ")
        lower_got = to_y(product(m, g_y))
        lower_got = after(lower_got, do_rows)
        lower = halved(m, g_y, lower_got)
        lower_got = to_z(second(lower), 1)
        proj_got = to_y(product(o_heads, dx_y))
        gate_send = jnp.concatenate([product(da, h_act), product(du, h_lin)], axis=0)
        gate_got = to_row(after(gate_send, do_got))
        do, lower, layer_out = lax.optimization_barrier((do, lower, layer_out))

    dq_part, dkv_left, dkv_right = attend_back_call(
        halo_bounds, q, do, o, lse, sq, [kv_left, kv_right], [sk_left, sk_right], heads
    )
    from_right = lax.ppermute(dkv_left, "dp", down)
    from_left = lax.ppermute(dkv_right, "dp", up)
    if two:
        dq_part, lower_got = lax.optimization_barrier((dq_part, lower_got))
    dq, dkv = attend_back_call(own_bounds, q, do, o, lse, sq, [kv], [sk_own], heads, [dq_part])
    if two:
        dkv, from_right, from_left, gate_got, proj_got = lax.optimization_barrier(
            (dkv, from_right, from_left, gate_got, proj_got)
        )
    pad = jnp.zeros((S - H, 2 * W), bf16)
    dkv = (
        dkv
        + jnp.concatenate([pad, from_right], axis=0).astype(f32)
        + jnp.concatenate([from_left, pad], axis=0).astype(f32)
    )
    dq = turn(dq * (1.0 / math.sqrt(head_width)), -1.0)
    dt = jnp.concatenate([dq, turn(dkv[:, :W], -1.0), dkv[:, W:]], axis=1).astype(bf16)
    dh1_part = nt(dt, wq)

    if two:
        n = S // 2
        kept = take(dh1_part, c, n) + to_col(take(dh1_part, 1 - c, n).astype(bf16)).astype(f32)
        xs = take(x_low, c, n).astype(f32)
        inv, mean = take(inverse_one, c, n), take(mean_one, c, n)
        n1 = (xs - mean) * inv
        e1 = kept * gain_one
        sums = jnp.stack([jnp.sum(e1, axis=-1), jnp.sum(e1 * n1, axis=-1)])
        sums = (sums + to_row(sums)) * (1.0 / D)
        mine = (kept[:, :Dl] + to_row(kept[:, Dl:].astype(bf16)).astype(f32)) * gain_one[:Dl]
        moved = lax.ppermute(after(dx_low[:, Dl:], from_left), ("row", "col"), [(0, 2), (3, 1)])
        base = jnp.where(r == c, dx1[:, :Dl], moved.astype(f32))
        dx = base + inv * (mine - sums[0][:, None] - n1[:, :Dl] * sums[1][:, None])
        dx = dx.astype(bf16)
        tokens_grad = ordered(zcol, dx, to_col(dx), 0)
    else:
        dh1 = lax.psum_scatter(col_sum(dh1_part), "row", scatter_dimension=1, tiled=True)
        xs = own_x.astype(f32)
        n1 = (xs - mean_one) * inverse_one
        e1 = dh1 * take(gain_attn, r, Dl)
        sums = lax.psum(jnp.stack([jnp.sum(e1, axis=-1), jnp.sum(e1 * n1, axis=-1)]), "row") / D
        base = lax.all_to_all(dx_low, "row", split_axis=1, concat_axis=0, tiled=True).astype(f32)
        tokens_grad = (
            base + inverse_one * (e1 - sums[0][:, None] - n1 * sums[1][:, None])
        ).astype(bf16)

    if two:
        h1_y = relative(h1, "yzZw")
        query = halved(dt, h1_y, after(to_y(product(dt, h1_y)), kept))
        lower_got = after(lower_got, from_left)
        n = F
        lower = joined(lower, lower_got)
        lower_got = after(to_z(second(lower), 2), kept)
        act = halved(da, h_act, gate_got[:n])
        lin = halved(du, h_lin, gate_got[n:])
        proj = halved(o_heads, dx_y, proj_got)
        both_got = after(to_z(jnp.concatenate([second(act), second(proj)], axis=0), 1), kept)
        lin = joined(lin, after(to_y(second(lin)), kept))
        act, proj = joined(act, both_got[:n]), joined(proj, both_got[n:])
        both_got = to_z(jnp.concatenate([second(act), second(proj)], axis=0), 2)
        lin = joined(lin, to_z(second(lin), 1))
        act, proj = joined(act, both_got[:n]), joined(proj, both_got[n:])
        lower = joined(lower, lower_got)
        last_got = to_row(jnp.concatenate([second(lower), second(proj)], axis=0))
        lower, proj = joined(lower, last_got[:n]), joined(proj, last_got[n:])
        act = joined(act, to_y(second(act)))
        lin = joined(lin, to_z(second(lin), 2))
        gate = jnp.stack([act.T, lin.T])
        query = joined(query, to_z(second(query), 1))
        query = joined(query, to_z(second(query), 2)).T
        wq_rows = take(wq, b ^ (4 * r), Db)
        place = (2 * b + r) ^ (8 * r)
        side, inner = place // 8, place % 8
        wi_rows = jnp.stack(
            [take(jnp.where(side == 0, w[0], w[1]), inner, Dd) for w in (acts, lins)]
        )
    else:

        def scatter(grad):
            return lax.psum_scatter(grad, ("dp", "row"), scatter_dimension=1, tiled=True).astype(f32)

        gate = jnp.stack([scatter(tn(da, h2).astype(bf16)).T, scatter(tn(du, h2).astype(bf16)).T])
        proj = scatter(tn(o_rows, dx_low).astype(bf16))
        lower = scatter(tn(m, g_low).astype(bf16))
        query = lax.psum_scatter(
            tn(h1, dt).astype(bf16), "dp", scatter_dimension=0, tiled=True
        ).astype(f32)
        wq_rows = take(wq, b, Db)
        wi_rows = jnp.stack([take(acts[0], b * R + r, Dd), take(lins[0], b * R + r, Dd)])

    one_part = jnp.sum(query * wq_rows.astype(f32), axis=1)
    two_part = jnp.sum(jnp.sum(gate * wi_rows.astype(f32), axis=2), axis=0)
    natural = lax.dot_general(
        query, order.astype(f32), (((1,), (1,)), ((), ())),
        precision=lax.Precision.HIGHEST, preferred_element_type=f32,
    )
    if two:
        one_part = one_part + to_row(one_part)
        one_part = take(one_part, r, Dd)
        pair = natural.reshape(2, Dd, 3 * W)
        mine = lax.dynamic_index_in_dim(pair, r, 0, keepdims=False)
        theirs = to_row(lax.dynamic_index_in_dim(pair, 1 - r, 0, keepdims=False))
        query_out = ordered(zrow, mine, theirs, 1)
    else:
        one_part = take(lax.psum(one_part, "row"), r, Dd)
        query_out = lax.all_to_all(natural, "row", split_axis=0, concat_axis=1, tiled=True)
    gains = jnp.stack([one_part, two_part])
    gains = gains + to_col(gains) if C == 2 else lax.psum(gains, "col")
    gain_attn_grad = gains[0] / take(gain_attn, b * R + r, Dd)
    gain_mlp_grad = gains[1] / take(gain_mlp, b * R + r, Dd)
    return (
        layer_out,
        tokens_grad,
        gain_attn_grad,
        query_out.reshape(Dd, R * heads, 3 * head_width),
        proj,
        gain_mlp_grad,
        jnp.swapaxes(gate, 0, 1),
        lower,
    )


def solution(mesh):
    return jax.shard_map(
        local,
        mesh=mesh,
        in_specs=(
            P("dp", "row"),
            P(),
            P("row", "col", None),
            P("col", "row"),
            P(),
            P("row", None, "col"),
            P("col", "row"),
            P("dp", "row"),
            P(),
            P(),
            P(),
        ),
        out_specs=(
            P("dp", "row"),
            P("dp", "row"),
            P(("dp", "row")),
            P(("dp", "row"), "col", None),
            P("col", ("dp", "row")),
            P(("dp", "row")),
            P(("dp", "row"), None, "col"),
            P("col", ("dp", "row")),
        ),
        check_vma=False,
    )
```

```python
import functools
import math

import jax
import jax.numpy as jnp
from jax import lax
from jax.experimental import pallas as pl
from jax.experimental.pallas import tpu as pltpu
from jax.sharding import PartitionSpec as P

LONGEST = 1024
BQ = 256
BK = 256
NEG = -1e30
FAR = 1e30
epsilon = 1e-05
rope_base = 160000.0
bf16 = jnp.bfloat16
f32 = jnp.float32
SWAP = [(0, 1), (1, 0)]


def nt(a, b):
    return lax.dot_general(a, b, (((1,), (1,)), ((), ())), preferred_element_type=f32)


def tn(a, b):
    return lax.dot_general(a, b, (((0,), (0,)), ((), ())), preferred_element_type=f32)


def nn(a, b):
    return jnp.dot(a, b, preferred_element_type=f32)


def after(a, *others):
    return lax.optimization_barrier((a, *others))[0]


def half_mask(width, heads, head):
    lane = lax.broadcasted_iota(jnp.int32, (1, width), 1)
    half = width // 2
    lane = jnp.where(lane >= half, lane - half, lane)
    step = half // heads
    return (lane >= head * step) & (lane < (head + 1) * step)


def whole_mask(width, heads, head):
    lane = lax.broadcasted_iota(jnp.int32, (1, width), 1)
    step = width // heads
    return (lane >= head * step) & (lane < (head + 1) * step)


def stack_heads(block, heads, mask_of):
    zero = jnp.zeros_like(block)
    width = block.shape[1]
    return jnp.concatenate(
        [jnp.where(mask_of(width, heads, h), block, zero) for h in range(heads)], axis=0
    )


def same_segment(key_seg, query_seg, heads):
    tile = key_seg
    lanes = query_seg.shape[1]
    if lanes > tile.shape[1]:
        tile = jnp.concatenate([tile] * (lanes // tile.shape[1]), axis=1)
    same = tile == query_seg
    return jnp.concatenate([same] * heads, axis=1) if heads > 1 else same


def forward_kernel(heads, sets, final, bounds, *refs):
    refs = list(refs)
    q_ref, sq_ref = refs[:2]
    kv_refs = refs[2 : 2 + sets]
    sk_refs = refs[2 + sets : 2 + 2 * sets]
    rest = refs[2 + 2 * sets :]
    if final:
        acc_in, ml_in, o_ref, lse_ref = rest[:4]
        acc, m_ref, l_ref = rest[4:7]
        vt_refs = rest[7:]
    else:
        acc, ml_ref = rest[:2]
        m_ref, l_ref = rest[2:4]
        vt_refs = rest[4:]
    step = pl.program_id(0)
    rows, width = q_ref.shape
    each = width // heads

    @pl.when(step == 0)
    def _():
        for kv, vt in zip(kv_refs, vt_refs):
            for j in range(kv.shape[0] // BK):
                vt[:, j * BK : (j + 1) * BK] = kv[j * BK : (j + 1) * BK, width:].T

    if final:
        acc[...] = acc_in[0]
        m_ref[...] = ml_in[0, 0:1]
        l_ref[...] = ml_in[0, 1:2]
    else:
        acc[...] = jnp.zeros_like(acc)
        m_ref[...] = jnp.full_like(m_ref, NEG)
        l_ref[...] = jnp.zeros_like(l_ref)
    queries = stack_heads(q_ref[...], heads, half_mask)
    query_seg = sq_ref[0]
    target = acc if final else acc.at[0]

    for s in range(sets):
        kv, sk, vt = kv_refs[s], sk_refs[s], vt_refs[s]

        def body(j, carry):
            first = pl.multiple_of(j * BK, BK)
            keys = kv[pl.ds(first, BK), 0:width]
            scores = nt(keys, queries)
            same = same_segment(sk[pl.ds(first, BK), :], query_seg, heads)
            scores = jnp.where(same, scores, NEG)
            before = m_ref[...]
            top = jnp.maximum(before, jnp.max(scores, axis=0, keepdims=True))
            raised = jnp.exp(scores - top)
            shrink = jnp.exp(before - top)
            m_ref[...] = top
            l_ref[...] = l_ref[...] * shrink + jnp.sum(raised, axis=0, keepdims=True)
            low = raised.astype(bf16)
            for h in range(heads):
                part = nn(
                    vt[h * each : (h + 1) * each, pl.ds(first, BK)],
                    low[:, h * rows : (h + 1) * rows],
                )
                hold = target[h * each : (h + 1) * each, :]
                target[h * each : (h + 1) * each, :] = (
                    hold * shrink[:, h * rows : (h + 1) * rows] + part
                )
            return carry

        lax.fori_loop(
            bounds[(step * sets + s) * 2], bounds[(step * sets + s) * 2 + 1], body, 0
        )

    if final:
        live = query_seg >= 0
        total = l_ref[...]
        live_all = jnp.concatenate([live] * heads, axis=1) if heads > 1 else live
        total = jnp.where(live_all, total, 1.0)
        inverse = jnp.where(live_all, 1.0 / total, 0.0)
        for h in range(heads):
            acc[h * each : (h + 1) * each, :] = (
                acc[h * each : (h + 1) * each, :] * inverse[:, h * rows : (h + 1) * rows]
            )
        o_ref[...] = acc[...].T.astype(bf16)
        lse_ref[0] = jnp.where(live_all, m_ref[...] + jnp.log(total), FAR)
    else:
        ml_ref[0, 0:1] = m_ref[...]
        ml_ref[0, 1:2] = l_ref[...]


def cost(products, q, kvs):
    pairs = q.shape[0]
    return pl.CostEstimate(
        flops=4 * products * pairs * q.shape[1],
        bytes_accessed=2 * sum(a.size for a in kvs) + 4 * q.size,
        transcendentals=4 * pairs,
    )


def whole(shape):
    zeros = (0,) * len(shape)
    return pl.BlockSpec(shape, lambda i, *_: zeros)


def attend_call(bounds, q, sq, kvs, sks, heads, state=None):
    count = q.shape[0] // BQ
    width = q.shape[1]
    sets = len(kvs)
    final = state is not None
    row_spec = pl.BlockSpec((BQ, width), lambda i, *_: (i, 0))
    acc_spec = pl.BlockSpec((1, width, BQ), lambda i, *_: (i, 0, 0))
    ml_spec = pl.BlockSpec((1, 2, heads * BQ), lambda i, *_: (i, 0, 0))
    in_specs = [row_spec, pl.BlockSpec((1, 1, BQ), lambda i, *_: (i, 0, 0))]
    in_specs += [whole(a.shape) for a in kvs] + [whole(a.shape) for a in sks]
    scratch = [pltpu.VMEM((1, heads * BQ), f32)] * 2
    scratch += [pltpu.VMEM((width, a.shape[0]), bf16) for a in kvs]
    if final:
        in_specs += [acc_spec, ml_spec]
        out_specs = [row_spec, pl.BlockSpec((1, 1, heads * BQ), lambda i, *_: (i, 0, 0))]
        out_shape = [
            jax.ShapeDtypeStruct(q.shape, bf16),
            jax.ShapeDtypeStruct((count, 1, heads * BQ), f32),
        ]
        scratch = [pltpu.VMEM((width, BQ), f32)] + scratch
    else:
        out_specs = [acc_spec, ml_spec]
        out_shape = [
            jax.ShapeDtypeStruct((count, width, BQ), f32),
            jax.ShapeDtypeStruct((count, 2, heads * BQ), f32),
        ]
    return pl.pallas_call(
        functools.partial(forward_kernel, heads, sets, final),
        grid_spec=pltpu.PrefetchScalarGridSpec(
            num_scalar_prefetch=1,
            grid=(count,),
            in_specs=in_specs,
            out_specs=out_specs,
            scratch_shapes=scratch,
        ),
        out_shape=out_shape,
        cost_estimate=cost(4, q, kvs),
        name="attend_final" if final else "attend_own",
    )(bounds, q, sq, *kvs, *sks, *(state or ()))


def backward_kernel(heads, sets, final, bounds, *refs):
    refs = list(refs)
    q_ref, do_ref, o_ref, lse_ref, sq_ref = refs[:5]
    kv_refs = refs[5 : 5 + sets]
    sk_refs = refs[5 + sets : 5 + 2 * sets]
    rest = refs[5 + 2 * sets :]
    if final:
        dq_in, dq_ref = rest[0], rest[1]
        dkv_refs = rest[2 : 2 + sets]
        dq_acc = rest[2 + sets]
        kt_refs = rest[3 + sets : 3 + 2 * sets]
        sums = dkv_refs
    else:
        dq_ref = rest[0]
        dkv_refs = rest[1 : 1 + sets]
        dq_acc = rest[1 + sets]
        kt_refs = rest[2 + sets : 2 + 2 * sets]
        sums = rest[2 + 2 * sets :]
    step = pl.program_id(0)
    rows, width = q_ref.shape
    each = width // heads
    half = width // 2
    piece = half // heads

    @pl.when(step == 0)
    def _():
        for kv, kt, total in zip(kv_refs, kt_refs, sums):
            total[...] = jnp.zeros_like(total)
            for j in range(kv.shape[0] // BK):
                kt[:, j * BK : (j + 1) * BK] = kv[j * BK : (j + 1) * BK, :width].T

    if final:
        dq_acc[...] = dq_in[0]
    else:
        dq_acc[...] = jnp.zeros_like(dq_acc)
    grads = do_ref[...]
    queries = stack_heads(q_ref[...], heads, half_mask)
    outs = stack_heads(grads, heads, whole_mask)
    query_seg = sq_ref[0]
    lse = lse_ref[0]
    product = (grads.astype(f32) * o_ref[...].astype(f32)).T
    delta = jnp.concatenate(
        [
            jnp.sum(product[h * each : (h + 1) * each], axis=0, keepdims=True)
            for h in range(heads)
        ],
        axis=1,
    )

    for s in range(sets):
        kv, sk, kt, total = kv_refs[s], sk_refs[s], kt_refs[s], sums[s]

        def body(j, carry):
            first = pl.multiple_of(j * BK, BK)
            keys = kv[pl.ds(first, BK), 0:width]
            values = kv[pl.ds(first, BK), width : 2 * width]
            scores = nt(keys, queries)
            same = same_segment(sk[pl.ds(first, BK), :], query_seg, heads)
            probs = jnp.where(same, jnp.exp(scores - lse), 0.0)
            grad_probs = nt(values, outs)
            grad_scores = (probs * (grad_probs - delta)).astype(bf16)
            low = probs.astype(bf16)
            total[pl.ds(first, BK), width : 2 * width] += nn(low, outs)
            total[pl.ds(first, BK), 0:width] += nn(grad_scores, queries)
            for h in range(heads):
                column = grad_scores[:, h * rows : (h + 1) * rows]
                for lead in (h * piece, half + h * piece):
                    dq_acc[lead : lead + piece, :] += nn(
                        kt[lead : lead + piece, pl.ds(first, BK)], column
                    )
            return carry

        lax.fori_loop(
            bounds[(step * sets + s) * 2], bounds[(step * sets + s) * 2 + 1], body, 0
        )

    if final:
        dq_ref[...] = dq_acc[...].T
    else:
        dq_ref[0] = dq_acc[...]

        @pl.when(step == pl.num_programs(0) - 1)
        def _():
            for total, out in zip(sums, dkv_refs):
                out[...] = total[...].astype(bf16)


def attend_back_call(bounds, q, do, o, lse, sq, kvs, sks, heads, state=None):
    count = q.shape[0] // BQ
    width = q.shape[1]
    sets = len(kvs)
    final = state is not None
    row_spec = pl.BlockSpec((BQ, width), lambda i, *_: (i, 0))
    acc_spec = pl.BlockSpec((1, width, BQ), lambda i, *_: (i, 0, 0))
    in_specs = [row_spec] * 3 + [
        pl.BlockSpec((1, 1, heads * BQ), lambda i, *_: (i, 0, 0)),
        pl.BlockSpec((1, 1, BQ), lambda i, *_: (i, 0, 0)),
    ]
    in_specs += [whole(a.shape) for a in kvs] + [whole(a.shape) for a in sks]
    scratch = [pltpu.VMEM((width, BQ), f32)]
    scratch += [pltpu.VMEM((width, a.shape[0]), bf16) for a in kvs]
    if final:
        in_specs += [acc_spec]
        out_specs = [row_spec]
        out_shape = [jax.ShapeDtypeStruct(q.shape, f32)]
    else:
        out_specs = [acc_spec]
        out_shape = [jax.ShapeDtypeStruct((count, width, BQ), f32)]
        scratch += [pltpu.VMEM(a.shape, f32) for a in kvs]
    out_specs += [whole(a.shape) for a in kvs]
    out_shape += [jax.ShapeDtypeStruct(a.shape, f32 if final else bf16) for a in kvs]
    return pl.pallas_call(
        functools.partial(backward_kernel, heads, sets, final),
        grid_spec=pltpu.PrefetchScalarGridSpec(
            num_scalar_prefetch=1,
            grid=(count,),
            in_specs=in_specs,
            out_specs=out_specs,
            scratch_shapes=scratch,
        ),
        out_shape=out_shape,
        cost_estimate=cost(10, q, kvs),
        name="back_own" if final else "back_halo",
    )(bounds, q, do, o, lse, sq, *kvs, *sks, *(state or ()))


def place_tables(seq_lengths, seq_offsets, first, count):
    place = first + jnp.arange(count, dtype=jnp.int32)
    ends = seq_offsets + seq_lengths
    inside = (place[:, None] >= seq_offsets[None, :]) & (place[:, None] < ends[None, :])
    live = jnp.any(inside, axis=1)
    index = jnp.arange(seq_offsets.shape[0], dtype=jnp.int32)
    segment = jnp.sum(jnp.where(inside, index[None, :], 0), axis=1)
    start = jnp.sum(jnp.where(inside, seq_offsets[None, :], 0), axis=1)
    end = jnp.sum(jnp.where(inside, ends[None, :], 0), axis=1)
    return live, segment, start, end, place


def qkv_order(heads, head_width):
    width = heads * head_width
    half = head_width // 2
    new = jnp.arange(3 * width, dtype=jnp.int32)
    kind = new // width
    inner = new % width
    side = inner // (width // 2)
    pair_head = (inner % (width // 2)) // half
    pair_old = pair_head * 3 * head_width + kind * head_width + side * half + inner % half
    value_old = (inner // head_width) * 3 * head_width + 2 * head_width + inner % head_width
    old = jnp.where(kind == 2, value_old, pair_old)
    return (old[None, :] == new[:, None]).astype(bf16)


def local(
    tokens,
    gain_attn,
    w_qkv,
    w_out,
    gain_mlp,
    w_in,
    w_down,
    cotangent,
    seq_lengths,
    seq_offsets,
    deal,
):
    R, C, B = lax.axis_size("row"), lax.axis_size("col"), lax.axis_size("dp")
    r, c, b = lax.axis_index("row"), lax.axis_index("col"), lax.axis_index("dp")
    S, Dl = tokens.shape
    D = Dl * R
    two = R == 2 and C == 2 and B == 8
    heads = w_qkv.shape[1] // R
    head_width = w_qkv.shape[2] // 3
    W = heads * head_width
    F = w_down.shape[0]
    H = LONGEST
    Sr = S // R
    zrow, zcol = (r == 0), (c == 0)

    def to_row(a):
        return lax.ppermute(a, "row", SWAP)

    def to_col(a):
        return lax.ppermute(a, "col", SWAP)

    def ordered(flag, mine, theirs, axis):
        return jnp.where(
            flag,
            jnp.concatenate([mine, theirs], axis=axis),
            jnp.concatenate([theirs, mine], axis=axis),
        )

    def own_first(a, axis):
        if not two:
            return a
        n = a.shape[axis] // 2
        return jnp.where(zrow, a, jnp.roll(a, n, axis=axis))

    def take(a, index, size, axis=0):
        return lax.dynamic_slice_in_dim(a, index * size, size, axis)

    def partner(a):
        n = a.shape[0] // 2
        got = to_row(take(a, c, n))
        return ordered(zcol, got, to_col(got), 0)

    def gather(a, axis):
        if two:
            return jnp.concatenate([a, to_row(a)], axis=axis)
        return lax.all_gather(a, "row", axis=axis, tiled=True)

    def col_sum(a):
        return a + to_col(a.astype(bf16)).astype(f32) if C == 2 else lax.psum(a, "col")

    live_x, seg_x, start_x, end_x, place_x = place_tables(seq_lengths, seq_offsets, b * S - H, S + 2 * H)
    key_seg = jnp.broadcast_to(jnp.where(live_x, seg_x, -2)[:, None], (S + 2 * H, 128))
    sk_left, sk_own, sk_right = key_seg[:H], key_seg[H : H + S], key_seg[H + S :]
    live = live_x[H : H + S]
    nq = S // BQ
    sq = jnp.where(live, seg_x[H : H + S], -1).reshape(nq, 1, BQ)
    first = jnp.min(jnp.where(live, start_x[H : H + S] - b * S, 4 * S).reshape(nq, BQ), axis=1)
    last = jnp.max(jnp.where(live, end_x[H : H + S] - b * S, -4 * S).reshape(nq, BQ), axis=1)
    own_low = jnp.clip(first, 0, S) // BK
    own_high = (jnp.clip(last, 0, S) + BK - 1) // BK
    left_low = jnp.clip(first + H, 0, H) // BK
    right_high = (jnp.clip(last - S, 0, H) + BK - 1) // BK
    own_bounds = jnp.stack([own_low, own_high], axis=1).reshape(-1).astype(jnp.int32)
    zero = jnp.zeros_like(left_low)
    halo_bounds = (
        jnp.stack([left_low, zero + H // BK, zero, right_high], axis=1).reshape(-1).astype(jnp.int32)
    )
    position = jnp.where(live, place_x[H : H + S] - start_x[H : H + S], 0)
    freq = rope_base ** (-(jnp.arange(0, head_width, 2, dtype=f32) / head_width))
    angle = position.astype(f32)[:, None] * jnp.tile(freq, heads)[None, :]
    cosine, sine = lax.optimization_barrier((jnp.cos(angle), jnp.sin(angle)))

    live_column = live[:, None]
    if two:
        x_got = partner(tokens)
        x_low = jnp.where(live_column, jnp.concatenate([tokens, x_got], axis=1), 0)
    else:
        own_x = jnp.where(live_column, tokens, 0)
        x_low = lax.all_gather(own_x, "row", axis=1, tiled=True)

    wq_low = w_qkv.reshape(Dl, R * 3 * W).astype(bf16)
    if two:
        wq_mine = take(wq_low, r, 3 * W, 1)
        wq_got = to_row(take(wq_low, 1 - r, 3 * W, 1))
    else:
        wq = lax.all_to_all(wq_low, "row", split_axis=1, concat_axis=0, tiled=True)
    order = qkv_order(heads, head_width)

    gain_one = own_first(gain_attn, 0)
    gain_two = own_first(gain_mlp, 0)

    x = x_low.astype(f32)
    center = x - jnp.mean(x, axis=-1, keepdims=True)
    inverse_one = lax.rsqrt(jnp.mean(center * center, axis=-1, keepdims=True) + epsilon)
    mean_one = jnp.mean(x, axis=-1, keepdims=True)
    h1 = (center * inverse_one * gain_one).astype(bf16)
    if two:
        h1, wq_mine, wq_got = lax.optimization_barrier((h1, wq_mine, wq_got))
        wq = jnp.concatenate([wq_mine, wq_got], axis=0)
    wq = nn(wq, order).astype(bf16)

    half = W // 2

    def turn(t, sign):
        first_half, second_half = t[:, :half], t[:, half:]
        s = sine * sign
        return jnp.concatenate(
            [first_half * cosine - second_half * s, second_half * cosine + first_half * s], axis=1
        )

    kv_raw = nn(h1, wq[:, W:])
    kv = jnp.concatenate([turn(kv_raw[:, :W], 1.0), kv_raw[:, W:]], axis=1).astype(bf16)
    up = [(i, i + 1) for i in range(B - 1)]
    down = [(i + 1, i) for i in range(B - 1)]
    kv_left = lax.ppermute(kv[S - H :], "dp", up)
    kv_right = lax.ppermute(kv[:H], "dp", down)
    q = (turn(nn(h1, wq[:, :W]), 1.0) * (1.0 / math.sqrt(head_width))).astype(bf16)
    wo_low, wd_low = w_out.astype(bf16), w_down.astype(bf16)
    act_low, lin_low = w_in[:, 0].astype(bf16), w_in[:, 1].astype(bf16)
    if two:
        even = (b // 2) % 2 == 0
        in_got, wo_got = to_row(jnp.where(even, act_low, lin_low)), to_row(wo_low)
        g_got = to_row(take(take(cotangent, 1 - r, Sr), c, Sr // 2))
        wd_half = take(wd_low, (b // 2) % 2, F // 2)

        def to_z(a, j):
            return lax.ppermute(a, "dp", [(i, i ^ (2 * j)) for i in range(B)])

    state = attend_call(own_bounds, q, sq, [kv], [sk_own], heads)
    if two:
        kv_left, kv_right, in_got, wo_got, g_got, wd_half = after(
            (kv_left, kv_right, in_got, wo_got, g_got, wd_half), state
        )
        in_other, wd_got = to_z(in_got, 1), to_row(wd_half)
    o, lse = attend_call(
        halo_bounds, q, sq, [kv_left, kv_right], [sk_left, sk_right], heads, state
    )

    if two:
        o, wd_got = lax.optimization_barrier((o, wd_got))
        wo = own_first(jnp.concatenate([wo_low, wo_got], axis=1), 0)
    else:
        wo = gather(wo_low, 1)

    if two:
        o_got = to_row(take(o, 1 - r, Sr))
        o_rows = jnp.concatenate([take(o, r, Sr), o_got], axis=1)
        wd_other, in_other = to_z(wd_got, 1), after(in_other, o_got)
        act_got, lin_got = jnp.where(even, in_got, in_other), jnp.where(even, in_other, in_got)
        wd_got = ordered(even, wd_got, wd_other, 0)
        g_got = ordered(zcol, g_got, to_col(g_got), 0)
        g_low = jnp.concatenate([take(cotangent, r, Sr), g_got], axis=1)
        g_low = jnp.where(take(live, r, Sr)[:, None], g_low, 0)
        wds = [wd_low, wd_got]
        acts, lins = [act_low, act_got], [lin_low, lin_got]
    else:
        o_rows = lax.all_to_all(o, "row", split_axis=0, concat_axis=1, tiled=True)
        own_g = jnp.where(live_column, cotangent, 0)
        g_low = lax.all_to_all(own_g, "row", split_axis=0, concat_axis=1, tiled=True)
        wds, acts, lins = [gather(wd_low, 1)], [gather(act_low, 0)], [gather(lin_low, 0)]

    def split_nn(a, parts):
        n = a.shape[1] // len(parts)
        return sum(nn(a[:, i * n : (i + 1) * n], w) for i, w in enumerate(parts))

    def split_nt(a, parts):
        n = a.shape[1] // len(parts)
        return sum(nt(a[:, i * n : (i + 1) * n], w) for i, w in enumerate(parts))

    def wide(parts):
        return parts[0] if len(parts) == 1 else jnp.concatenate(parts, axis=1)

    x_rows = take(x_low, r, Sr).astype(f32)
    if C == 2:
        o_all = jnp.concatenate([o_rows, to_col(o_rows)], axis=1)
        wo_all = jnp.concatenate([wo, to_col(wo)], axis=0)
        x1 = x_rows + nn(o_all, wo_all)
    else:
        x1 = x_rows + lax.psum(nn(o_rows, wo), "col")

    Db = D // B
    Dd = D // (B * R)
    if two:
        y_bit, z_bits = b % 2, b // 2

        def relative(a, bits):
            n = jnp.arange(D, dtype=jnp.int32)
            rel = {"w": 0 * n, "x": 0 * n}
            for i, bit in enumerate(bits):
                rel[bit] = n // (D >> (i + 1)) % 2
            z_rel = 2 * rel["Z"] + rel["z"]
            column = ((z_bits ^ z_rel) * 2 + (y_bit ^ rel["y"])) * Db + n % Dd
            column = column + (rel["w"] if "w" in bits else r ^ rel["x"]) * Dd
            column = column ^ (r * (D // 2))
            return nn(a, (n[:, None] == column[None, :]).astype(bf16)).astype(bf16)

        def to_y(a):
            return lax.ppermute(a, "dp", [(i, i ^ 1) for i in range(B)])

        def first(a):
            return a[:, : a.shape[1] // 2]

        def second(a):
            return a[:, a.shape[1] // 2 :].astype(bf16)

        def product(left, right):
            return tn(left, second(right)).astype(bf16)

        def halved(left, right, got):
            return tn(left, first(right)) + got.astype(f32)

        def joined(part, got):
            return first(part).astype(f32) + got.astype(f32)

    center = x1 - jnp.mean(x1, axis=-1, keepdims=True)
    inverse_two = lax.rsqrt(jnp.mean(center * center, axis=-1, keepdims=True) + epsilon)
    n2 = center * inverse_two
    h2 = (n2 * gain_two).astype(bf16)
    a = split_nn(h2, acts)
    u = split_nn(h2, lins)
    phi = 0.5 + 0.5 * lax.erf(a * math.sqrt(0.5))
    gelu = a * phi
    slope = phi + a * jnp.exp(-0.5 * a * a) * (1.0 / math.sqrt(2.0 * math.pi))
    m = (gelu * u).astype(bf16)
    y_part = wide([nn(m, w) for w in wds])
    if two:
        n = Sr // 2
        y_half = (
            take(x1, c, n) + take(y_part, c, n) + to_col(take(y_part, 1 - c, n).astype(bf16)).astype(f32)
        ).astype(bf16)
        y_got = to_row(y_half[:, Dl:])
    else:
        y = (x1 + col_sum(y_part)).astype(bf16)
        layer_out = lax.all_to_all(y, "row", split_axis=1, concat_axis=0, tiled=True)

    dm = split_nt(g_low, wds)
    da = (dm * u * slope).astype(bf16)
    du = (dm * gelu).astype(bf16)
    dh2 = col_sum(wide([nt(da, v) + nt(du, w) for v, w in zip(acts, lins)]))
    if two:
        g_y = relative(g_low, "yzZx")
        lower_got = to_y(product(m, g_y))
        dh2, lower_got = lax.optimization_barrier((dh2, lower_got))
    e2 = dh2 * gain_two
    dx1 = g_low.astype(f32) + inverse_two * (
        e2
        - jnp.mean(e2, axis=-1, keepdims=True)
        - n2 * jnp.mean(e2 * n2, axis=-1, keepdims=True)
    )
    dx_low = dx1.astype(bf16)
    do_rows = nt(dx_low, wo).astype(bf16)
    if two:
        do_got = to_row(do_rows[:, W:])
        do = ordered(zrow, do_rows[:, :W], do_got, 0)
        pair = ordered(zrow, y_half[None, :, :Dl], after(y_got, dx_low)[None], 0)
        layer_out = ordered(zcol, pair[:, None], to_col(pair)[:, None], 1).reshape(S, Dl)
    else:
        do = lax.all_to_all(do_rows, "row", split_axis=1, concat_axis=0, tiled=True)

    if two:
        o_heads = own_first(o_rows, 1)
        dx_y = relative(dx_low, "yzZx")
        h_act, h_lin = relative(h2, "xzZy"), relative(h2, "xyzZ")
        lower = halved(m, g_y, lower_got)
        lower_got = to_z(second(lower), 1)
        proj_got = to_y(product(o_heads, dx_y))
        gate_send = jnp.concatenate([product(da, h_act), product(du, h_lin)], axis=0)
        gate_got = to_row(after(gate_send, do_got))
        do, lower, layer_out = lax.optimization_barrier((do, lower, layer_out))

    dq_part, dkv_left, dkv_right = attend_back_call(
        halo_bounds, q, do, o, lse, sq, [kv_left, kv_right], [sk_left, sk_right], heads
    )
    from_right = lax.ppermute(dkv_left, "dp", down)
    from_left = lax.ppermute(dkv_right, "dp", up)
    if two:
        dq_part, lower_got = lax.optimization_barrier((dq_part, lower_got))
    dq, dkv = attend_back_call(own_bounds, q, do, o, lse, sq, [kv], [sk_own], heads, [dq_part])
    if two:
        dkv, from_right, from_left, gate_got, proj_got = lax.optimization_barrier(
            (dkv, from_right, from_left, gate_got, proj_got)
        )
    pad = jnp.zeros((S - H, 2 * W), bf16)
    dkv = (
        dkv
        + jnp.concatenate([pad, from_right], axis=0).astype(f32)
        + jnp.concatenate([from_left, pad], axis=0).astype(f32)
    )
    dq = turn(dq * (1.0 / math.sqrt(head_width)), -1.0)
    dt = jnp.concatenate([dq, turn(dkv[:, :W], -1.0), dkv[:, W:]], axis=1).astype(bf16)
    dh1_part = nt(dt, wq)

    if two:
        n = S // 2
        kept = take(dh1_part, c, n) + to_col(take(dh1_part, 1 - c, n).astype(bf16)).astype(f32)
        xs = take(x_low, c, n).astype(f32)
        inv, mean = take(inverse_one, c, n), take(mean_one, c, n)
        n1 = (xs - mean) * inv
        e1 = kept * gain_one
        sums = jnp.stack([jnp.sum(e1, axis=-1), jnp.sum(e1 * n1, axis=-1)])
        sums = (sums + to_row(sums)) * (1.0 / D)
        moved = lax.ppermute(after(dx_low[:, Dl:], from_left), ("row", "col"), [(0, 2), (3, 1)])
        kept_send, moved = lax.optimization_barrier((kept[:, Dl:].astype(bf16), moved))
        mine = (kept[:, :Dl] + to_row(kept_send).astype(f32)) * gain_one[:Dl]
        base = jnp.where(r == c, dx1[:, :Dl], moved.astype(f32))
        dx = base + inv * (mine - sums[0][:, None] - n1[:, :Dl] * sums[1][:, None])
        dx = dx.astype(bf16)
        tokens_grad = ordered(zcol, dx, to_col(dx), 0)
    else:
        dh1 = lax.psum_scatter(col_sum(dh1_part), "row", scatter_dimension=1, tiled=True)
        xs = own_x.astype(f32)
        n1 = (xs - mean_one) * inverse_one
        e1 = dh1 * take(gain_attn, r, Dl)
        sums = lax.psum(jnp.stack([jnp.sum(e1, axis=-1), jnp.sum(e1 * n1, axis=-1)]), "row") / D
        base = lax.all_to_all(dx_low, "row", split_axis=1, concat_axis=0, tiled=True).astype(f32)
        tokens_grad = (
            base + inverse_one * (e1 - sums[0][:, None] - n1 * sums[1][:, None])
        ).astype(bf16)

    if two:
        h1_y = relative(h1, "yzZw")
        query = halved(dt, h1_y, after(to_y(product(dt, h1_y)), kept))
        lower_got = after(lower_got, from_left)
        n = F
        lower = joined(lower, lower_got)
        lower_got = after(to_z(second(lower), 2), kept)
        act = halved(da, h_act, gate_got[:n])
        lin = halved(du, h_lin, gate_got[n:])
        proj = halved(o_heads, dx_y, proj_got)
        both_got = after(to_z(jnp.concatenate([second(act), second(proj)], axis=0), 1), kept)
        lin = joined(lin, after(to_y(second(lin)), kept))
        act, proj = joined(act, both_got[:n]), joined(proj, both_got[n:])
        both_got = to_z(jnp.concatenate([second(act), second(proj)], axis=0), 2)
        lin = joined(lin, to_z(second(lin), 1))
        act, proj = joined(act, both_got[:n]), joined(proj, both_got[n:])
        lower = joined(lower, lower_got)
        last_got = after(to_row(jnp.concatenate([second(lower), second(proj)], axis=0)), dx)
        lower, proj = joined(lower, last_got[:n]), joined(proj, last_got[n:])
        act = joined(act, to_y(second(act)))
        lin = joined(lin, after(to_z(second(lin), 2), dx))
        gate = jnp.stack([act.T, lin.T])
        query = joined(query, to_z(second(query), 1))
        query = joined(query, after(to_z(second(query), 2), dx)).T
        wq_rows = take(wq, b ^ (4 * r), Db)
        place = (2 * b + r) ^ (8 * r)
        wi_rows = jnp.stack(
            [jnp.where(place < 8, *(take(w, place % 8, Dd) for w in ws)) for ws in (acts, lins)]
        )
    else:

        def scatter(grad):
            return lax.psum_scatter(grad, ("dp", "row"), scatter_dimension=1, tiled=True).astype(f32)

        gate = jnp.stack([scatter(tn(da, h2).astype(bf16)).T, scatter(tn(du, h2).astype(bf16)).T])
        proj = scatter(tn(o_rows, dx_low).astype(bf16))
        lower = scatter(tn(m, g_low).astype(bf16))
        query = lax.psum_scatter(
            tn(h1, dt).astype(bf16), "dp", scatter_dimension=0, tiled=True
        ).astype(f32)
        wq_rows = take(wq, b, Db)
        wi_rows = jnp.stack([take(acts[0], b * R + r, Dd), take(lins[0], b * R + r, Dd)])

    one_part = jnp.sum(query * wq_rows.astype(f32), axis=1)
    two_part = jnp.sum(jnp.sum(gate * wi_rows.astype(f32), axis=2), axis=0)
    natural = lax.dot_general(
        query, order.astype(f32), (((1,), (1,)), ((), ())),
        precision=lax.Precision.HIGHEST, preferred_element_type=f32,
    )
    if two:
        one_part = one_part + to_row(one_part)
        one_part = take(one_part, r, Dd)
        pair = natural.reshape(2, Dd, 3 * W)
        mine = lax.dynamic_index_in_dim(pair, r, 0, keepdims=False)
        theirs = to_row(lax.dynamic_index_in_dim(pair, 1 - r, 0, keepdims=False))
        query_out = ordered(zrow, mine, theirs, 1)
    else:
        one_part = take(lax.psum(one_part, "row"), r, Dd)
        query_out = lax.all_to_all(natural, "row", split_axis=0, concat_axis=1, tiled=True)
    gains = jnp.stack([one_part, two_part])
    gains = gains + to_col(gains) if C == 2 else lax.psum(gains, "col")
    gain_attn_grad = gains[0] / take(gain_attn, b * R + r, Dd)
    gain_mlp_grad = gains[1] / take(gain_mlp, b * R + r, Dd)
    return (
        layer_out,
        tokens_grad,
        gain_attn_grad,
        query_out.reshape(Dd, R * heads, 3 * head_width),
        proj,
        gain_mlp_grad,
        jnp.swapaxes(gate, 0, 1),
        lower,
    )


def solution(mesh):
    return jax.shard_map(
        local,
        mesh=mesh,
        in_specs=(
            P("dp", "row"),
            P(),
            P("row", "col", None),
            P("col", "row"),
            P(),
            P("row", None, "col"),
            P("col", "row"),
            P("dp", "row"),
            P(),
            P(),
            P(),
        ),
        out_specs=(
            P("dp", "row"),
            P("dp", "row"),
            P(("dp", "row")),
            P(("dp", "row"), "col", None),
            P("col", ("dp", "row")),
            P(("dp", "row")),
            P(("dp", "row"), None, "col"),
            P("col", ("dp", "row")),
        ),
        check_vma=False,
    )
```

```python
import functools
import math

import jax
import jax.numpy as jnp
from jax import lax
from jax.experimental import pallas as pl
from jax.experimental.pallas import tpu as pltpu
from jax.sharding import PartitionSpec as P

LONGEST = 1024
BQ = 256
BK = 256
NEG = -1e30
FAR = 1e30
epsilon = 1e-05
rope_base = 160000.0
bf16 = jnp.bfloat16
f32 = jnp.float32
SWAP = [(0, 1), (1, 0)]


def nt(a, b):
    return lax.dot_general(a, b, (((1,), (1,)), ((), ())), preferred_element_type=f32)


def tn(a, b):
    return lax.dot_general(a, b, (((0,), (0,)), ((), ())), preferred_element_type=f32)


def nn(a, b):
    return jnp.dot(a, b, preferred_element_type=f32)


def after(a, *others):
    return lax.optimization_barrier((a, *others))[0]


def half_mask(width, heads, head):
    lane = lax.broadcasted_iota(jnp.int32, (1, width), 1)
    half = width // 2
    lane = jnp.where(lane >= half, lane - half, lane)
    step = half // heads
    return (lane >= head * step) & (lane < (head + 1) * step)


def whole_mask(width, heads, head):
    lane = lax.broadcasted_iota(jnp.int32, (1, width), 1)
    step = width // heads
    return (lane >= head * step) & (lane < (head + 1) * step)


def stack_heads(block, heads, mask_of):
    zero = jnp.zeros_like(block)
    width = block.shape[1]
    return jnp.concatenate(
        [jnp.where(mask_of(width, heads, h), block, zero) for h in range(heads)], axis=0
    )


def same_segment(key_seg, query_seg, heads):
    tile = key_seg
    lanes = query_seg.shape[1]
    if lanes > tile.shape[1]:
        tile = jnp.concatenate([tile] * (lanes // tile.shape[1]), axis=1)
    same = tile == query_seg
    return jnp.concatenate([same] * heads, axis=1) if heads > 1 else same


def forward_kernel(heads, sets, final, bounds, *refs):
    refs = list(refs)
    q_ref, sq_ref = refs[:2]
    kv_refs = refs[2 : 2 + sets]
    sk_refs = refs[2 + sets : 2 + 2 * sets]
    rest = refs[2 + 2 * sets :]
    if final:
        acc_in, ml_in, o_ref, lse_ref = rest[:4]
        acc, m_ref, l_ref = rest[4:7]
        vt_refs = rest[7:]
    else:
        acc, ml_ref = rest[:2]
        m_ref, l_ref = rest[2:4]
        vt_refs = rest[4:]
    step = pl.program_id(0)
    rows, width = q_ref.shape
    each = width // heads

    @pl.when(step == 0)
    def _():
        for kv, vt in zip(kv_refs, vt_refs):
            for j in range(kv.shape[0] // BK):
                vt[:, j * BK : (j + 1) * BK] = kv[j * BK : (j + 1) * BK, width:].T

    if final:
        acc[...] = acc_in[0]
        m_ref[...] = ml_in[0, 0:1]
        l_ref[...] = ml_in[0, 1:2]
    else:
        acc[...] = jnp.zeros_like(acc)
        m_ref[...] = jnp.full_like(m_ref, NEG)
        l_ref[...] = jnp.zeros_like(l_ref)
    queries = stack_heads(q_ref[...], heads, half_mask)
    query_seg = sq_ref[0]
    target = acc if final else acc.at[0]

    for s in range(sets):
        kv, sk, vt = kv_refs[s], sk_refs[s], vt_refs[s]

        def body(j, carry):
            first = pl.multiple_of(j * BK, BK)
            keys = kv[pl.ds(first, BK), 0:width]
            scores = nt(keys, queries)
            same = same_segment(sk[pl.ds(first, BK), :], query_seg, heads)
            scores = jnp.where(same, scores, NEG)
            before = m_ref[...]
            top = jnp.maximum(before, jnp.max(scores, axis=0, keepdims=True))
            raised = jnp.exp(scores - top)
            shrink = jnp.exp(before - top)
            m_ref[...] = top
            l_ref[...] = l_ref[...] * shrink + jnp.sum(raised, axis=0, keepdims=True)
            low = raised.astype(bf16)
            for h in range(heads):
                part = nn(
                    vt[h * each : (h + 1) * each, pl.ds(first, BK)],
                    low[:, h * rows : (h + 1) * rows],
                )
                hold = target[h * each : (h + 1) * each, :]
                target[h * each : (h + 1) * each, :] = (
                    hold * shrink[:, h * rows : (h + 1) * rows] + part
                )
            return carry

        lax.fori_loop(
            bounds[(step * sets + s) * 2], bounds[(step * sets + s) * 2 + 1], body, 0
        )

    if final:
        live = query_seg >= 0
        total = l_ref[...]
        live_all = jnp.concatenate([live] * heads, axis=1) if heads > 1 else live
        total = jnp.where(live_all, total, 1.0)
        inverse = jnp.where(live_all, 1.0 / total, 0.0)
        for h in range(heads):
            acc[h * each : (h + 1) * each, :] = (
                acc[h * each : (h + 1) * each, :] * inverse[:, h * rows : (h + 1) * rows]
            )
        o_ref[...] = acc[...].T.astype(bf16)
        lse_ref[0] = jnp.where(live_all, m_ref[...] + jnp.log(total), FAR)
    else:
        ml_ref[0, 0:1] = m_ref[...]
        ml_ref[0, 1:2] = l_ref[...]


def cost(products, q, kvs):
    pairs = q.shape[0]
    return pl.CostEstimate(
        flops=4 * products * pairs * q.shape[1],
        bytes_accessed=2 * sum(a.size for a in kvs) + 4 * q.size,
        transcendentals=4 * pairs,
    )


def whole(shape):
    zeros = (0,) * len(shape)
    return pl.BlockSpec(shape, lambda i, *_: zeros)


def attend_call(bounds, q, sq, kvs, sks, heads, state=None):
    count = q.shape[0] // BQ
    width = q.shape[1]
    sets = len(kvs)
    final = state is not None
    row_spec = pl.BlockSpec((BQ, width), lambda i, *_: (i, 0))
    acc_spec = pl.BlockSpec((1, width, BQ), lambda i, *_: (i, 0, 0))
    ml_spec = pl.BlockSpec((1, 2, heads * BQ), lambda i, *_: (i, 0, 0))
    in_specs = [row_spec, pl.BlockSpec((1, 1, BQ), lambda i, *_: (i, 0, 0))]
    in_specs += [whole(a.shape) for a in kvs] + [whole(a.shape) for a in sks]
    scratch = [pltpu.VMEM((1, heads * BQ), f32)] * 2
    scratch += [pltpu.VMEM((width, a.shape[0]), bf16) for a in kvs]
    if final:
        in_specs += [acc_spec, ml_spec]
        out_specs = [row_spec, pl.BlockSpec((1, 1, heads * BQ), lambda i, *_: (i, 0, 0))]
        out_shape = [
            jax.ShapeDtypeStruct(q.shape, bf16),
            jax.ShapeDtypeStruct((count, 1, heads * BQ), f32),
        ]
        scratch = [pltpu.VMEM((width, BQ), f32)] + scratch
    else:
        out_specs = [acc_spec, ml_spec]
        out_shape = [
            jax.ShapeDtypeStruct((count, width, BQ), f32),
            jax.ShapeDtypeStruct((count, 2, heads * BQ), f32),
        ]
    return pl.pallas_call(
        functools.partial(forward_kernel, heads, sets, final),
        grid_spec=pltpu.PrefetchScalarGridSpec(
            num_scalar_prefetch=1,
            grid=(count,),
            in_specs=in_specs,
            out_specs=out_specs,
            scratch_shapes=scratch,
        ),
        out_shape=out_shape,
        cost_estimate=cost(4, q, kvs),
        name="attend_final" if final else "attend_own",
    )(bounds, q, sq, *kvs, *sks, *(state or ()))


def backward_kernel(heads, sets, final, bounds, *refs):
    refs = list(refs)
    q_ref, do_ref, o_ref, lse_ref, sq_ref = refs[:5]
    kv_refs = refs[5 : 5 + sets]
    sk_refs = refs[5 + sets : 5 + 2 * sets]
    rest = refs[5 + 2 * sets :]
    if final:
        dq_in, dq_ref = rest[0], rest[1]
        dkv_refs = rest[2 : 2 + sets]
        dq_acc = rest[2 + sets]
        kt_refs = rest[3 + sets : 3 + 2 * sets]
        sums = dkv_refs
    else:
        dq_ref = rest[0]
        dkv_refs = rest[1 : 1 + sets]
        dq_acc = rest[1 + sets]
        kt_refs = rest[2 + sets : 2 + 2 * sets]
        sums = rest[2 + 2 * sets :]
    step = pl.program_id(0)
    rows, width = q_ref.shape
    each = width // heads
    half = width // 2
    piece = half // heads

    @pl.when(step == 0)
    def _():
        for kv, kt, total in zip(kv_refs, kt_refs, sums):
            total[...] = jnp.zeros_like(total)
            for j in range(kv.shape[0] // BK):
                kt[:, j * BK : (j + 1) * BK] = kv[j * BK : (j + 1) * BK, :width].T

    if final:
        dq_acc[...] = dq_in[0]
    else:
        dq_acc[...] = jnp.zeros_like(dq_acc)
    grads = do_ref[...]
    queries = stack_heads(q_ref[...], heads, half_mask)
    outs = stack_heads(grads, heads, whole_mask)
    query_seg = sq_ref[0]
    lse = lse_ref[0]
    product = (grads.astype(f32) * o_ref[...].astype(f32)).T
    delta = jnp.concatenate(
        [
            jnp.sum(product[h * each : (h + 1) * each], axis=0, keepdims=True)
            for h in range(heads)
        ],
        axis=1,
    )

    for s in range(sets):
        kv, sk, kt, total = kv_refs[s], sk_refs[s], kt_refs[s], sums[s]

        def body(j, carry):
            first = pl.multiple_of(j * BK, BK)
            keys = kv[pl.ds(first, BK), 0:width]
            values = kv[pl.ds(first, BK), width : 2 * width]
            scores = nt(keys, queries)
            same = same_segment(sk[pl.ds(first, BK), :], query_seg, heads)
            probs = jnp.where(same, jnp.exp(scores - lse), 0.0)
            grad_probs = nt(values, outs)
            grad_scores = (probs * (grad_probs - delta)).astype(bf16)
            low = probs.astype(bf16)
            total[pl.ds(first, BK), width : 2 * width] += nn(low, outs)
            total[pl.ds(first, BK), 0:width] += nn(grad_scores, queries)
            for h in range(heads):
                column = grad_scores[:, h * rows : (h + 1) * rows]
                for lead in (h * piece, half + h * piece):
                    dq_acc[lead : lead + piece, :] += nn(
                        kt[lead : lead + piece, pl.ds(first, BK)], column
                    )
            return carry

        lax.fori_loop(
            bounds[(step * sets + s) * 2], bounds[(step * sets + s) * 2 + 1], body, 0
        )

    if final:
        dq_ref[...] = dq_acc[...].T
    else:
        dq_ref[0] = dq_acc[...]

        @pl.when(step == pl.num_programs(0) - 1)
        def _():
            for total, out in zip(sums, dkv_refs):
                out[...] = total[...].astype(bf16)


def attend_back_call(bounds, q, do, o, lse, sq, kvs, sks, heads, state=None):
    count = q.shape[0] // BQ
    width = q.shape[1]
    sets = len(kvs)
    final = state is not None
    row_spec = pl.BlockSpec((BQ, width), lambda i, *_: (i, 0))
    acc_spec = pl.BlockSpec((1, width, BQ), lambda i, *_: (i, 0, 0))
    in_specs = [row_spec] * 3 + [
        pl.BlockSpec((1, 1, heads * BQ), lambda i, *_: (i, 0, 0)),
        pl.BlockSpec((1, 1, BQ), lambda i, *_: (i, 0, 0)),
    ]
    in_specs += [whole(a.shape) for a in kvs] + [whole(a.shape) for a in sks]
    scratch = [pltpu.VMEM((width, BQ), f32)]
    scratch += [pltpu.VMEM((width, a.shape[0]), bf16) for a in kvs]
    if final:
        in_specs += [acc_spec]
        out_specs = [row_spec]
        out_shape = [jax.ShapeDtypeStruct(q.shape, f32)]
    else:
        out_specs = [acc_spec]
        out_shape = [jax.ShapeDtypeStruct((count, width, BQ), f32)]
        scratch += [pltpu.VMEM(a.shape, f32) for a in kvs]
    out_specs += [whole(a.shape) for a in kvs]
    out_shape += [jax.ShapeDtypeStruct(a.shape, f32 if final else bf16) for a in kvs]
    return pl.pallas_call(
        functools.partial(backward_kernel, heads, sets, final),
        grid_spec=pltpu.PrefetchScalarGridSpec(
            num_scalar_prefetch=1,
            grid=(count,),
            in_specs=in_specs,
            out_specs=out_specs,
            scratch_shapes=scratch,
        ),
        out_shape=out_shape,
        cost_estimate=cost(10, q, kvs),
        name="back_own" if final else "back_halo",
    )(bounds, q, do, o, lse, sq, *kvs, *sks, *(state or ()))


def place_tables(seq_lengths, seq_offsets, first, count):
    place = first + jnp.arange(count, dtype=jnp.int32)
    ends = seq_offsets + seq_lengths
    inside = (place[:, None] >= seq_offsets[None, :]) & (place[:, None] < ends[None, :])
    live = jnp.any(inside, axis=1)
    index = jnp.arange(seq_offsets.shape[0], dtype=jnp.int32)
    segment = jnp.sum(jnp.where(inside, index[None, :], 0), axis=1)
    start = jnp.sum(jnp.where(inside, seq_offsets[None, :], 0), axis=1)
    end = jnp.sum(jnp.where(inside, ends[None, :], 0), axis=1)
    return live, segment, start, end, place


def qkv_order(heads, head_width):
    width = heads * head_width
    half = head_width // 2
    new = jnp.arange(3 * width, dtype=jnp.int32)
    kind = new // width
    inner = new % width
    side = inner // (width // 2)
    pair_head = (inner % (width // 2)) // half
    pair_old = pair_head * 3 * head_width + kind * head_width + side * half + inner % half
    value_old = (inner // head_width) * 3 * head_width + 2 * head_width + inner % head_width
    old = jnp.where(kind == 2, value_old, pair_old)
    return (old[None, :] == new[:, None]).astype(bf16)


def local(
    tokens,
    gain_attn,
    w_qkv,
    w_out,
    gain_mlp,
    w_in,
    w_down,
    cotangent,
    seq_lengths,
    seq_offsets,
    deal,
):
    R, C, B = lax.axis_size("row"), lax.axis_size("col"), lax.axis_size("dp")
    r, c, b = lax.axis_index("row"), lax.axis_index("col"), lax.axis_index("dp")
    S, Dl = tokens.shape
    D = Dl * R
    two = R == 2 and C == 2 and B == 8
    heads = w_qkv.shape[1] // R
    head_width = w_qkv.shape[2] // 3
    W = heads * head_width
    F = w_down.shape[0]
    H = LONGEST
    Sr = S // R
    zrow, zcol = (r == 0), (c == 0)

    def to_row(a):
        return lax.ppermute(a, "row", SWAP)

    def to_col(a):
        return lax.ppermute(a, "col", SWAP)

    def ordered(flag, mine, theirs, axis):
        return jnp.where(
            flag,
            jnp.concatenate([mine, theirs], axis=axis),
            jnp.concatenate([theirs, mine], axis=axis),
        )

    def own_first(a, axis):
        if not two:
            return a
        n = a.shape[axis] // 2
        return jnp.where(zrow, a, jnp.roll(a, n, axis=axis))

    def take(a, index, size, axis=0):
        return lax.dynamic_slice_in_dim(a, index * size, size, axis)

    def partner(a):
        n = a.shape[0] // 2
        got = to_row(take(a, c, n))
        return ordered(zcol, got, to_col(got), 0)

    def gather(a, axis):
        if two:
            return jnp.concatenate([a, to_row(a)], axis=axis)
        return lax.all_gather(a, "row", axis=axis, tiled=True)

    def col_sum(a):
        return a + to_col(a.astype(bf16)).astype(f32) if C == 2 else lax.psum(a, "col")

    live_x, seg_x, start_x, end_x, place_x = place_tables(seq_lengths, seq_offsets, b * S - H, S + 2 * H)
    key_seg = jnp.broadcast_to(jnp.where(live_x, seg_x, -2)[:, None], (S + 2 * H, 128))
    sk_left, sk_own, sk_right = key_seg[:H], key_seg[H : H + S], key_seg[H + S :]
    live = live_x[H : H + S]
    nq = S // BQ
    sq = jnp.where(live, seg_x[H : H + S], -1).reshape(nq, 1, BQ)
    first = jnp.min(jnp.where(live, start_x[H : H + S] - b * S, 4 * S).reshape(nq, BQ), axis=1)
    last = jnp.max(jnp.where(live, end_x[H : H + S] - b * S, -4 * S).reshape(nq, BQ), axis=1)
    own_low = jnp.clip(first, 0, S) // BK
    own_high = (jnp.clip(last, 0, S) + BK - 1) // BK
    left_low = jnp.clip(first + H, 0, H) // BK
    right_high = (jnp.clip(last - S, 0, H) + BK - 1) // BK
    own_bounds = jnp.stack([own_low, own_high], axis=1).reshape(-1).astype(jnp.int32)
    zero = jnp.zeros_like(left_low)
    halo_bounds = (
        jnp.stack([left_low, zero + H // BK, zero, right_high], axis=1).reshape(-1).astype(jnp.int32)
    )
    position = jnp.where(live, place_x[H : H + S] - start_x[H : H + S], 0)
    freq = rope_base ** (-(jnp.arange(0, head_width, 2, dtype=f32) / head_width))
    angle = position.astype(f32)[:, None] * jnp.tile(freq, heads)[None, :]
    cosine, sine = lax.optimization_barrier((jnp.cos(angle), jnp.sin(angle)))

    live_column = live[:, None]
    if two:
        x_got = partner(tokens)
        x_low = jnp.where(live_column, jnp.concatenate([tokens, x_got], axis=1), 0)
    else:
        own_x = jnp.where(live_column, tokens, 0)
        x_low = lax.all_gather(own_x, "row", axis=1, tiled=True)

    wq_low = w_qkv.reshape(Dl, R * 3 * W).astype(bf16)
    if two:
        wq_mine = take(wq_low, r, 3 * W, 1)
        wq_got = to_row(take(wq_low, 1 - r, 3 * W, 1))
    else:
        wq = lax.all_to_all(wq_low, "row", split_axis=1, concat_axis=0, tiled=True)
    order = qkv_order(heads, head_width)

    gain_one = own_first(gain_attn, 0)
    gain_two = own_first(gain_mlp, 0)

    Db = D // B
    Dd = D // (B * R)
    if two:
        y_bit, z_bits = b % 2, b // 2

        def relative(a, bits):
            n = jnp.arange(D, dtype=jnp.int32)
            rel = {"w": 0 * n, "x": 0 * n}
            for i, bit in enumerate(bits):
                rel[bit] = n // (D >> (i + 1)) % 2
            z_rel = 2 * rel["Z"] + rel["z"]
            column = ((z_bits ^ z_rel) * 2 + (y_bit ^ rel["y"])) * Db + n % Dd
            column = column + (rel["w"] if "w" in bits else r ^ rel["x"]) * Dd
            column = column ^ (r * (D // 2))
            return nn(a, (n[:, None] == column[None, :]).astype(bf16)).astype(bf16)

        def to_y(a):
            return lax.ppermute(a, "dp", [(i, i ^ 1) for i in range(B)])

        def to_z(a, j):
            return lax.ppermute(a, "dp", [(i, i ^ (2 * j)) for i in range(B)])

        def first(a):
            return a[:, : a.shape[1] // 2]

        def second(a):
            return a[:, a.shape[1] // 2 :].astype(bf16)

        def product(left, right):
            return tn(left, second(right)).astype(bf16)

        def halved(left, right, got):
            return tn(left, first(right)) + got.astype(f32)

        def joined(part, got):
            return first(part).astype(f32) + got.astype(f32)

    x = x_low.astype(f32)
    center = x - jnp.mean(x, axis=-1, keepdims=True)
    inverse_one = lax.rsqrt(jnp.mean(center * center, axis=-1, keepdims=True) + epsilon)
    mean_one = jnp.mean(x, axis=-1, keepdims=True)
    h1 = (center * inverse_one * gain_one).astype(bf16)
    if two:
        h1_y = relative(h1, "yzZw")
        h1, h1_y, wq_mine, wq_got = lax.optimization_barrier((h1, h1_y, wq_mine, wq_got))
        wq = jnp.concatenate([wq_mine, wq_got], axis=0)
    wq = nn(wq, order).astype(bf16)

    half = W // 2

    def turn(t, sign):
        first_half, second_half = t[:, :half], t[:, half:]
        s = sine * sign
        return jnp.concatenate(
            [first_half * cosine - second_half * s, second_half * cosine + first_half * s], axis=1
        )

    kv_raw = nn(h1, wq[:, W:])
    kv = jnp.concatenate([turn(kv_raw[:, :W], 1.0), kv_raw[:, W:]], axis=1).astype(bf16)
    up = [(i, i + 1) for i in range(B - 1)]
    down = [(i + 1, i) for i in range(B - 1)]
    kv_left = lax.ppermute(kv[S - H :], "dp", up)
    kv_right = lax.ppermute(kv[:H], "dp", down)
    q = (turn(nn(h1, wq[:, :W]), 1.0) * (1.0 / math.sqrt(head_width))).astype(bf16)
    wo_low, wd_low = w_out.astype(bf16), w_down.astype(bf16)
    act_low, lin_low = w_in[:, 0].astype(bf16), w_in[:, 1].astype(bf16)
    if two:
        even = (b // 2) % 2 == 0
        in_got, wo_got = to_row(jnp.where(even, act_low, lin_low)), to_row(wo_low)
        g_got = to_row(take(take(cotangent, 1 - r, Sr), c, Sr // 2))
        wd_half = take(wd_low, (b // 2) % 2, F // 2)

    state = attend_call(own_bounds, q, sq, [kv], [sk_own], heads)
    if two:
        kv_left, kv_right, sk_left, sk_right, in_got, wo_got, g_got, wd_half = after(
            (kv_left, kv_right, sk_left, sk_right, in_got, wo_got, g_got, wd_half), state
        )
        in_other, wd_got = to_z(in_got, 1), to_row(wd_half)
    o, lse = attend_call(
        halo_bounds, q, sq, [kv_left, kv_right], [sk_left, sk_right], heads, state
    )

    if two:
        o, wd_got, wo_got, g_got = lax.optimization_barrier((o, wd_got, wo_got, g_got))
        wo = own_first(jnp.concatenate([wo_low, wo_got], axis=1), 0)
    else:
        wo = gather(wo_low, 1)

    if two:
        o_got = to_row(take(o, 1 - r, Sr))
        o_rows = jnp.concatenate([take(o, r, Sr), o_got], axis=1)
        wd_other = to_z(wd_got, 1)
        wd_got = ordered(even, wd_got, wd_other, 0)
        g_got = ordered(zcol, g_got, to_col(g_got), 0)
        g_low = jnp.concatenate([take(cotangent, r, Sr), g_got], axis=1)
        g_low = jnp.where(take(live, r, Sr)[:, None], g_low, 0)
        wds = [wd_low, wd_got]
    else:
        o_rows = lax.all_to_all(o, "row", split_axis=0, concat_axis=1, tiled=True)
        own_g = jnp.where(live_column, cotangent, 0)
        g_low = lax.all_to_all(own_g, "row", split_axis=0, concat_axis=1, tiled=True)
        wds, acts, lins = [gather(wd_low, 1)], [gather(act_low, 0)], [gather(lin_low, 0)]

    def split_nn(a, parts):
        n = a.shape[1] // len(parts)
        return sum(nn(a[:, i * n : (i + 1) * n], w) for i, w in enumerate(parts))

    def split_nt(a, parts):
        n = a.shape[1] // len(parts)
        return sum(nt(a[:, i * n : (i + 1) * n], w) for i, w in enumerate(parts))

    def wide(parts):
        return parts[0] if len(parts) == 1 else jnp.concatenate(parts, axis=1)

    x_rows = take(x_low, r, Sr).astype(f32)
    if C == 2:
        o_all = jnp.concatenate([o_rows, to_col(o_rows)], axis=1)
        wo_all = jnp.concatenate([wo, to_col(wo)], axis=0)
        x1 = x_rows + nn(o_all, wo_all)
    else:
        x1 = x_rows + lax.psum(nn(o_rows, wo), "col")
    if two:
        in_got, in_other = after((in_got, in_other), o_got)
        act_got, lin_got = jnp.where(even, in_got, in_other), jnp.where(even, in_other, in_got)
        acts, lins = [act_low, act_got], [lin_low, lin_got]

    center = x1 - jnp.mean(x1, axis=-1, keepdims=True)
    inverse_two = lax.rsqrt(jnp.mean(center * center, axis=-1, keepdims=True) + epsilon)
    n2 = center * inverse_two
    h2 = (n2 * gain_two).astype(bf16)
    a = split_nn(h2, acts)
    u = split_nn(h2, lins)
    phi = 0.5 + 0.5 * lax.erf(a * math.sqrt(0.5))
    gelu = a * phi
    slope = phi + a * jnp.exp(-0.5 * a * a) * (1.0 / math.sqrt(2.0 * math.pi))
    m = (gelu * u).astype(bf16)
    y_part = wide([nn(m, w) for w in wds])
    if two:
        n = Sr // 2
        y_half = (
            take(x1, c, n) + take(y_part, c, n) + to_col(take(y_part, 1 - c, n).astype(bf16)).astype(f32)
        ).astype(bf16)
        y_got = to_row(y_half[:, Dl:])
    else:
        y = (x1 + col_sum(y_part)).astype(bf16)
        layer_out = lax.all_to_all(y, "row", split_axis=1, concat_axis=0, tiled=True)

    dm = split_nt(g_low, wds)
    da = (dm * u * slope).astype(bf16)
    du = (dm * gelu).astype(bf16)
    dh2 = col_sum(wide([nt(da, v) + nt(du, w) for v, w in zip(acts, lins)]))
    if two:
        g_y = relative(g_low, "yzZx")
        lower_got = to_y(product(m, g_y))
    e2 = dh2 * gain_two
    dx1 = g_low.astype(f32) + inverse_two * (
        e2
        - jnp.mean(e2, axis=-1, keepdims=True)
        - n2 * jnp.mean(e2 * n2, axis=-1, keepdims=True)
    )
    dx_low = dx1.astype(bf16)
    do_rows = nt(dx_low, wo).astype(bf16)
    if two:
        do_got = to_row(do_rows[:, W:])
        do = ordered(zrow, do_rows[:, :W], do_got, 0)
        pair = ordered(zrow, y_half[None, :, :Dl], after(y_got, dx_low)[None], 0)
        layer_out = ordered(zcol, pair[:, None], to_col(pair)[:, None], 1).reshape(S, Dl)
    else:
        do = lax.all_to_all(do_rows, "row", split_axis=1, concat_axis=0, tiled=True)

    if two:
        h2, da, du, o_heads, dx_late = after((h2, da, du, own_first(o_rows, 1), dx_low), do_rows)
        dx_y = relative(dx_late, "yzZx")
        h_act, h_lin = relative(h2, "xzZy"), relative(h2, "xyzZ")
        proj_got = to_y(product(o_heads, dx_y))
        gate_send = jnp.concatenate([product(da, h_act), product(du, h_lin)], axis=0)
        gate_got = to_row(after(gate_send, do_got))
        lower = halved(m, g_y, after(lower_got, gate_send))
        lower_got = to_z(second(lower), 1)
        do, lower, layer_out = lax.optimization_barrier((do, lower, layer_out))

    dq_part, dkv_left, dkv_right = attend_back_call(
        halo_bounds, q, do, o, lse, sq, [kv_left, kv_right], [sk_left, sk_right], heads
    )
    from_right = lax.ppermute(dkv_left, "dp", down)
    from_left = lax.ppermute(dkv_right, "dp", up)
    if two:
        lower = joined(lower, after(lower_got, dq_part))
        lower_got = to_z(second(lower), 2)
        dq_part, lower = lax.optimization_barrier((dq_part, lower))
    dq, dkv = attend_back_call(own_bounds, q, do, o, lse, sq, [kv], [sk_own], heads, [dq_part])
    if two:
        dkv, from_right, from_left, gate_got, proj_got, lower_got = lax.optimization_barrier(
            (dkv, from_right, from_left, gate_got, proj_got, lower_got)
        )
    pad = jnp.zeros((S - H, 2 * W), bf16)
    dkv = (
        dkv
        + jnp.concatenate([pad, from_right], axis=0).astype(f32)
        + jnp.concatenate([from_left, pad], axis=0).astype(f32)
    )
    dq = turn(dq * (1.0 / math.sqrt(head_width)), -1.0)
    dt = jnp.concatenate([dq, turn(dkv[:, :W], -1.0), dkv[:, W:]], axis=1).astype(bf16)
    dh1_part = nt(dt, wq)
    if two:
        query_send = product(dt, h1_y)
        gate_got, proj_got, lower_got = after((gate_got, proj_got, lower_got), query_send, dh1_part)

    if two:
        n = S // 2
        kept = take(dh1_part, c, n) + to_col(take(dh1_part, 1 - c, n).astype(bf16)).astype(f32)
        xs = take(x_low, c, n).astype(f32)
        inv, mean = take(inverse_one, c, n), take(mean_one, c, n)
        n1 = (xs - mean) * inv
        e1 = kept * gain_one
        sums = jnp.stack([jnp.sum(e1, axis=-1), jnp.sum(e1 * n1, axis=-1)])
        sums = (sums + to_row(sums)) * (1.0 / D)
        moved = lax.ppermute(after(dx_low[:, Dl:], from_left), ("row", "col"), [(0, 2), (3, 1)])
        kept_send, moved = lax.optimization_barrier((kept[:, Dl:].astype(bf16), moved))
        mine = (kept[:, :Dl] + to_row(kept_send).astype(f32)) * gain_one[:Dl]
        base = jnp.where(r == c, dx1[:, :Dl], moved.astype(f32))
        dx = base + inv * (mine - sums[0][:, None] - n1[:, :Dl] * sums[1][:, None])
        dx = dx.astype(bf16)
        tokens_grad = ordered(zcol, dx, to_col(dx), 0)
    else:
        dh1 = lax.psum_scatter(col_sum(dh1_part), "row", scatter_dimension=1, tiled=True)
        xs = own_x.astype(f32)
        n1 = (xs - mean_one) * inverse_one
        e1 = dh1 * take(gain_attn, r, Dl)
        sums = lax.psum(jnp.stack([jnp.sum(e1, axis=-1), jnp.sum(e1 * n1, axis=-1)]), "row") / D
        base = lax.all_to_all(dx_low, "row", split_axis=1, concat_axis=0, tiled=True).astype(f32)
        tokens_grad = (
            base + inverse_one * (e1 - sums[0][:, None] - n1 * sums[1][:, None])
        ).astype(bf16)

    if two:
        query = halved(dt, h1_y, after(to_y(query_send), kept))
        n = F
        act = halved(da, h_act, gate_got[:n])
        lin = halved(du, h_lin, gate_got[n:])
        proj = halved(o_heads, dx_y, proj_got)
        both_got = after(to_z(jnp.concatenate([second(act), second(proj)], axis=0), 1), kept)
        lin = joined(lin, after(to_y(second(lin)), kept))
        act, proj = joined(act, both_got[:n]), joined(proj, both_got[n:])
        both_got = to_z(jnp.concatenate([second(act), second(proj)], axis=0), 2)
        lin = joined(lin, to_z(second(lin), 1))
        act, proj = joined(act, both_got[:n]), joined(proj, both_got[n:])
        lower = joined(lower, lower_got)
        last_got = after(to_row(jnp.concatenate([second(lower), second(proj)], axis=0)), dx)
        lower, proj = joined(lower, last_got[:n]), joined(proj, last_got[n:])
        act = joined(act, to_y(second(act)))
        lin = joined(lin, after(to_z(second(lin), 2), dx))
        gate = jnp.stack([act.T, lin.T])
        query = joined(query, to_z(second(query), 1))
        query = joined(query, after(to_z(second(query), 2), dx)).T
        wq_rows = take(wq, b ^ (4 * r), Db)
        place = (2 * b + r) ^ (8 * r)
        wi_rows = jnp.stack(
            [jnp.where(place < 8, *(take(w, place % 8, Dd) for w in ws)) for ws in after((acts, lins), kept)]
        )
    else:

        def scatter(grad):
            return lax.psum_scatter(grad, ("dp", "row"), scatter_dimension=1, tiled=True).astype(f32)

        gate = jnp.stack([scatter(tn(da, h2).astype(bf16)).T, scatter(tn(du, h2).astype(bf16)).T])
        proj = scatter(tn(o_rows, dx_low).astype(bf16))
        lower = scatter(tn(m, g_low).astype(bf16))
        query = lax.psum_scatter(
            tn(h1, dt).astype(bf16), "dp", scatter_dimension=0, tiled=True
        ).astype(f32)
        wq_rows = take(wq, b, Db)
        wi_rows = jnp.stack([take(acts[0], b * R + r, Dd), take(lins[0], b * R + r, Dd)])

    one_part = jnp.sum(query * wq_rows.astype(f32), axis=1)
    two_part = jnp.sum(jnp.sum(gate * wi_rows.astype(f32), axis=2), axis=0)
    natural = lax.dot_general(
        query, order.astype(f32), (((1,), (1,)), ((), ())),
        precision=lax.Precision.HIGHEST, preferred_element_type=f32,
    )
    if two:
        pair = jnp.concatenate([natural, jnp.broadcast_to(one_part[:, None], (Db, 128))], axis=1)
        pair = pair.reshape(2, Dd, 3 * W + 128)
        mine = lax.dynamic_index_in_dim(pair, r, 0, keepdims=False)
        theirs = to_row(lax.dynamic_index_in_dim(pair, 1 - r, 0, keepdims=False))
        theirs = after(theirs, tokens_grad)
        one_part = mine[:, 3 * W] + theirs[:, 3 * W]
        query_out = ordered(zrow, mine[:, : 3 * W], theirs[:, : 3 * W], 1)
    else:
        one_part = take(lax.psum(one_part, "row"), r, Dd)
        query_out = lax.all_to_all(natural, "row", split_axis=0, concat_axis=1, tiled=True)
    gains = jnp.stack([one_part, two_part])
    gains = gains + to_col(gains) if C == 2 else lax.psum(gains, "col")
    gain_attn_grad = gains[0] / take(gain_attn, b * R + r, Dd)
    gain_mlp_grad = gains[1] / take(gain_mlp, b * R + r, Dd)
    return (
        layer_out,
        tokens_grad,
        gain_attn_grad,
        query_out.reshape(Dd, R * heads, 3 * head_width),
        proj,
        gain_mlp_grad,
        jnp.swapaxes(gate, 0, 1),
        lower,
    )


def solution(mesh):
    return jax.shard_map(
        local,
        mesh=mesh,
        in_specs=(
            P("dp", "row"),
            P(),
            P("row", "col", None),
            P("col", "row"),
            P(),
            P("row", None, "col"),
            P("col", "row"),
            P("dp", "row"),
            P(),
            P(),
            P(),
        ),
        out_specs=(
            P("dp", "row"),
            P("dp", "row"),
            P(("dp", "row")),
            P(("dp", "row"), "col", None),
            P("col", ("dp", "row")),
            P(("dp", "row")),
            P(("dp", "row"), None, "col"),
            P("col", ("dp", "row")),
        ),
        check_vma=False,
    )
```

```python
import functools
import math

import jax
import jax.numpy as jnp
from jax import lax
from jax.experimental import pallas as pl
from jax.experimental.pallas import tpu as pltpu
from jax.sharding import PartitionSpec as P

LONGEST = 1024
BQ = 256
BK = 256
NEG = -1e30
FAR = 1e30
epsilon = 1e-05
rope_base = 160000.0
bf16 = jnp.bfloat16
f32 = jnp.float32
SWAP = [(0, 1), (1, 0)]


def nt(a, b):
    return lax.dot_general(a, b, (((1,), (1,)), ((), ())), preferred_element_type=f32)


def tn(a, b):
    return lax.dot_general(a, b, (((0,), (0,)), ((), ())), preferred_element_type=f32)


def nn(a, b):
    return jnp.dot(a, b, preferred_element_type=f32)


def after(a, *others):
    return lax.optimization_barrier((a, *others))[0]


def half_mask(width, heads, head):
    lane = lax.broadcasted_iota(jnp.int32, (1, width), 1)
    half = width // 2
    lane = jnp.where(lane >= half, lane - half, lane)
    step = half // heads
    return (lane >= head * step) & (lane < (head + 1) * step)


def whole_mask(width, heads, head):
    lane = lax.broadcasted_iota(jnp.int32, (1, width), 1)
    step = width // heads
    return (lane >= head * step) & (lane < (head + 1) * step)


def stack_heads(block, heads, mask_of):
    zero = jnp.zeros_like(block)
    width = block.shape[1]
    return jnp.concatenate(
        [jnp.where(mask_of(width, heads, h), block, zero) for h in range(heads)], axis=0
    )


def same_segment(key_seg, query_seg, heads):
    tile = key_seg
    lanes = query_seg.shape[1]
    if lanes > tile.shape[1]:
        tile = jnp.concatenate([tile] * (lanes // tile.shape[1]), axis=1)
    same = tile == query_seg
    return jnp.concatenate([same] * heads, axis=1) if heads > 1 else same


def forward_kernel(heads, sets, final, bounds, *refs):
    refs = list(refs)
    q_ref, sq_ref = refs[:2]
    kv_refs = refs[2 : 2 + sets]
    sk_refs = refs[2 + sets : 2 + 2 * sets]
    rest = refs[2 + 2 * sets :]
    if final:
        acc_in, ml_in, o_ref, lse_ref = rest[:4]
        acc, m_ref, l_ref = rest[4:7]
        vt_refs = rest[7:]
    else:
        acc, ml_ref = rest[:2]
        m_ref, l_ref = rest[2:4]
        vt_refs = rest[4:]
    step = pl.program_id(0)
    rows, width = q_ref.shape
    each = width // heads

    @pl.when(step == 0)
    def _():
        for kv, vt in zip(kv_refs, vt_refs):
            for j in range(kv.shape[0] // BK):
                vt[:, j * BK : (j + 1) * BK] = kv[j * BK : (j + 1) * BK, width:].T

    if final:
        acc[...] = acc_in[0]
        m_ref[...] = ml_in[0, 0:1]
        l_ref[...] = ml_in[0, 1:2]
    else:
        acc[...] = jnp.zeros_like(acc)
        m_ref[...] = jnp.full_like(m_ref, NEG)
        l_ref[...] = jnp.zeros_like(l_ref)
    queries = stack_heads(q_ref[...], heads, half_mask)
    query_seg = sq_ref[0]
    target = acc if final else acc.at[0]

    for s in range(sets):
        kv, sk, vt = kv_refs[s], sk_refs[s], vt_refs[s]

        def body(j, carry):
            first = pl.multiple_of(j * BK, BK)
            keys = kv[pl.ds(first, BK), 0:width]
            scores = nt(keys, queries)
            same = same_segment(sk[pl.ds(first, BK), :], query_seg, heads)
            scores = jnp.where(same, scores, NEG)
            before = m_ref[...]
            top = jnp.maximum(before, jnp.max(scores, axis=0, keepdims=True))
            raised = jnp.exp(scores - top)
            shrink = jnp.exp(before - top)
            m_ref[...] = top
            l_ref[...] = l_ref[...] * shrink + jnp.sum(raised, axis=0, keepdims=True)
            low = raised.astype(bf16)
            for h in range(heads):
                part = nn(
                    vt[h * each : (h + 1) * each, pl.ds(first, BK)],
                    low[:, h * rows : (h + 1) * rows],
                )
                hold = target[h * each : (h + 1) * each, :]
                target[h * each : (h + 1) * each, :] = (
                    hold * shrink[:, h * rows : (h + 1) * rows] + part
                )
            return carry

        lax.fori_loop(
            bounds[(step * sets + s) * 2], bounds[(step * sets + s) * 2 + 1], body, 0
        )

    if final:
        live = query_seg >= 0
        total = l_ref[...]
        live_all = jnp.concatenate([live] * heads, axis=1) if heads > 1 else live
        total = jnp.where(live_all, total, 1.0)
        inverse = jnp.where(live_all, 1.0 / total, 0.0)
        for h in range(heads):
            acc[h * each : (h + 1) * each, :] = (
                acc[h * each : (h + 1) * each, :] * inverse[:, h * rows : (h + 1) * rows]
            )
        o_ref[...] = acc[...].T.astype(bf16)
        lse_ref[0] = jnp.where(live_all, m_ref[...] + jnp.log(total), FAR)
    else:
        ml_ref[0, 0:1] = m_ref[...]
        ml_ref[0, 1:2] = l_ref[...]


def cost(products, q, kvs):
    pairs = q.shape[0]
    return pl.CostEstimate(
        flops=4 * products * pairs * q.shape[1],
        bytes_accessed=2 * sum(a.size for a in kvs) + 4 * q.size,
        transcendentals=4 * pairs,
    )


def whole(shape):
    zeros = (0,) * len(shape)
    return pl.BlockSpec(shape, lambda i, *_: zeros)


def attend_call(bounds, q, sq, kvs, sks, heads, state=None):
    count = q.shape[0] // BQ
    width = q.shape[1]
    sets = len(kvs)
    final = state is not None
    row_spec = pl.BlockSpec((BQ, width), lambda i, *_: (i, 0))
    acc_spec = pl.BlockSpec((1, width, BQ), lambda i, *_: (i, 0, 0))
    ml_spec = pl.BlockSpec((1, 2, heads * BQ), lambda i, *_: (i, 0, 0))
    in_specs = [row_spec, pl.BlockSpec((1, 1, BQ), lambda i, *_: (i, 0, 0))]
    in_specs += [whole(a.shape) for a in kvs] + [whole(a.shape) for a in sks]
    scratch = [pltpu.VMEM((1, heads * BQ), f32)] * 2
    scratch += [pltpu.VMEM((width, a.shape[0]), bf16) for a in kvs]
    if final:
        in_specs += [acc_spec, ml_spec]
        out_specs = [row_spec, pl.BlockSpec((1, 1, heads * BQ), lambda i, *_: (i, 0, 0))]
        out_shape = [
            jax.ShapeDtypeStruct(q.shape, bf16),
            jax.ShapeDtypeStruct((count, 1, heads * BQ), f32),
        ]
        scratch = [pltpu.VMEM((width, BQ), f32)] + scratch
    else:
        out_specs = [acc_spec, ml_spec]
        out_shape = [
            jax.ShapeDtypeStruct((count, width, BQ), f32),
            jax.ShapeDtypeStruct((count, 2, heads * BQ), f32),
        ]
    return pl.pallas_call(
        functools.partial(forward_kernel, heads, sets, final),
        grid_spec=pltpu.PrefetchScalarGridSpec(
            num_scalar_prefetch=1,
            grid=(count,),
            in_specs=in_specs,
            out_specs=out_specs,
            scratch_shapes=scratch,
        ),
        out_shape=out_shape,
        cost_estimate=cost(4, q, kvs),
        name="attend_final" if final else "attend_own",
    )(bounds, q, sq, *kvs, *sks, *(state or ()))


def backward_kernel(heads, sets, final, bounds, *refs):
    refs = list(refs)
    q_ref, do_ref, o_ref, lse_ref, sq_ref = refs[:5]
    kv_refs = refs[5 : 5 + sets]
    sk_refs = refs[5 + sets : 5 + 2 * sets]
    rest = refs[5 + 2 * sets :]
    if final:
        dq_in, dq_ref = rest[0], rest[1]
        dkv_refs = rest[2 : 2 + sets]
        dq_acc = rest[2 + sets]
        kt_refs = rest[3 + sets : 3 + 2 * sets]
        sums = dkv_refs
    else:
        dq_ref = rest[0]
        dkv_refs = rest[1 : 1 + sets]
        dq_acc = rest[1 + sets]
        kt_refs = rest[2 + sets : 2 + 2 * sets]
        sums = rest[2 + 2 * sets :]
    step = pl.program_id(0)
    rows, width = q_ref.shape
    each = width // heads
    half = width // 2
    piece = half // heads

    @pl.when(step == 0)
    def _():
        for kv, kt, total in zip(kv_refs, kt_refs, sums):
            total[...] = jnp.zeros_like(total)
            for j in range(kv.shape[0] // BK):
                kt[:, j * BK : (j + 1) * BK] = kv[j * BK : (j + 1) * BK, :width].T

    if final:
        dq_acc[...] = dq_in[0]
    else:
        dq_acc[...] = jnp.zeros_like(dq_acc)
    grads = do_ref[...]
    queries = stack_heads(q_ref[...], heads, half_mask)
    outs = stack_heads(grads, heads, whole_mask)
    query_seg = sq_ref[0]
    lse = lse_ref[0]
    product = (grads.astype(f32) * o_ref[...].astype(f32)).T
    delta = jnp.concatenate(
        [
            jnp.sum(product[h * each : (h + 1) * each], axis=0, keepdims=True)
            for h in range(heads)
        ],
        axis=1,
    )

    for s in range(sets):
        kv, sk, kt, total = kv_refs[s], sk_refs[s], kt_refs[s], sums[s]

        def body(j, carry):
            first = pl.multiple_of(j * BK, BK)
            keys = kv[pl.ds(first, BK), 0:width]
            values = kv[pl.ds(first, BK), width : 2 * width]
            scores = nt(keys, queries)
            same = same_segment(sk[pl.ds(first, BK), :], query_seg, heads)
            probs = jnp.where(same, jnp.exp(scores - lse), 0.0)
            grad_probs = nt(values, outs)
            grad_scores = (probs * (grad_probs - delta)).astype(bf16)
            low = probs.astype(bf16)
            total[pl.ds(first, BK), width : 2 * width] += nn(low, outs)
            total[pl.ds(first, BK), 0:width] += nn(grad_scores, queries)
            for h in range(heads):
                column = grad_scores[:, h * rows : (h + 1) * rows]
                for lead in (h * piece, half + h * piece):
                    dq_acc[lead : lead + piece, :] += nn(
                        kt[lead : lead + piece, pl.ds(first, BK)], column
                    )
            return carry

        lax.fori_loop(
            bounds[(step * sets + s) * 2], bounds[(step * sets + s) * 2 + 1], body, 0
        )

    if final:
        dq_ref[...] = dq_acc[...].T
    else:
        dq_ref[0] = dq_acc[...]

        @pl.when(step == pl.num_programs(0) - 1)
        def _():
            for total, out in zip(sums, dkv_refs):
                out[...] = total[...].astype(bf16)


def attend_back_call(bounds, q, do, o, lse, sq, kvs, sks, heads, state=None):
    count = q.shape[0] // BQ
    width = q.shape[1]
    sets = len(kvs)
    final = state is not None
    row_spec = pl.BlockSpec((BQ, width), lambda i, *_: (i, 0))
    acc_spec = pl.BlockSpec((1, width, BQ), lambda i, *_: (i, 0, 0))
    in_specs = [row_spec] * 3 + [
        pl.BlockSpec((1, 1, heads * BQ), lambda i, *_: (i, 0, 0)),
        pl.BlockSpec((1, 1, BQ), lambda i, *_: (i, 0, 0)),
    ]
    in_specs += [whole(a.shape) for a in kvs] + [whole(a.shape) for a in sks]
    scratch = [pltpu.VMEM((width, BQ), f32)]
    scratch += [pltpu.VMEM((width, a.shape[0]), bf16) for a in kvs]
    if final:
        in_specs += [acc_spec]
        out_specs = [row_spec]
        out_shape = [jax.ShapeDtypeStruct(q.shape, f32)]
    else:
        out_specs = [acc_spec]
        out_shape = [jax.ShapeDtypeStruct((count, width, BQ), f32)]
        scratch += [pltpu.VMEM(a.shape, f32) for a in kvs]
    out_specs += [whole(a.shape) for a in kvs]
    out_shape += [jax.ShapeDtypeStruct(a.shape, f32 if final else bf16) for a in kvs]
    return pl.pallas_call(
        functools.partial(backward_kernel, heads, sets, final),
        grid_spec=pltpu.PrefetchScalarGridSpec(
            num_scalar_prefetch=1,
            grid=(count,),
            in_specs=in_specs,
            out_specs=out_specs,
            scratch_shapes=scratch,
        ),
        out_shape=out_shape,
        cost_estimate=cost(10, q, kvs),
        name="back_own" if final else "back_halo",
    )(bounds, q, do, o, lse, sq, *kvs, *sks, *(state or ()))


def place_tables(seq_lengths, seq_offsets, first, count):
    place = first + jnp.arange(count, dtype=jnp.int32)
    ends = seq_offsets + seq_lengths
    inside = (place[:, None] >= seq_offsets[None, :]) & (place[:, None] < ends[None, :])
    live = jnp.any(inside, axis=1)
    index = jnp.arange(seq_offsets.shape[0], dtype=jnp.int32)
    segment = jnp.sum(jnp.where(inside, index[None, :], 0), axis=1)
    start = jnp.sum(jnp.where(inside, seq_offsets[None, :], 0), axis=1)
    end = jnp.sum(jnp.where(inside, ends[None, :], 0), axis=1)
    return live, segment, start, end, place


def qkv_order(heads, head_width):
    width = heads * head_width
    half = head_width // 2
    new = jnp.arange(3 * width, dtype=jnp.int32)
    kind = new // width
    inner = new % width
    side = inner // (width // 2)
    pair_head = (inner % (width // 2)) // half
    pair_old = pair_head * 3 * head_width + kind * head_width + side * half + inner % half
    value_old = (inner // head_width) * 3 * head_width + 2 * head_width + inner % head_width
    old = jnp.where(kind == 2, value_old, pair_old)
    return (old[None, :] == new[:, None]).astype(bf16)


def local(
    tokens,
    gain_attn,
    w_qkv,
    w_out,
    gain_mlp,
    w_in,
    w_down,
    cotangent,
    seq_lengths,
    seq_offsets,
    deal,
):
    R, C, B = lax.axis_size("row"), lax.axis_size("col"), lax.axis_size("dp")
    r, c, b = lax.axis_index("row"), lax.axis_index("col"), lax.axis_index("dp")
    S, Dl = tokens.shape
    D = Dl * R
    two = R == 2 and C == 2 and B == 8
    heads = w_qkv.shape[1] // R
    head_width = w_qkv.shape[2] // 3
    W = heads * head_width
    F = w_down.shape[0]
    H = LONGEST
    Sr = S // R
    zrow, zcol = (r == 0), (c == 0)

    def to_row(a):
        return lax.ppermute(a, "row", SWAP)

    def to_col(a):
        return lax.ppermute(a, "col", SWAP)

    def ordered(flag, mine, theirs, axis):
        return jnp.where(
            flag,
            jnp.concatenate([mine, theirs], axis=axis),
            jnp.concatenate([theirs, mine], axis=axis),
        )

    def own_first(a, axis):
        if not two:
            return a
        n = a.shape[axis] // 2
        return jnp.where(zrow, a, jnp.roll(a, n, axis=axis))

    def take(a, index, size, axis=0):
        return lax.dynamic_slice_in_dim(a, index * size, size, axis)

    def partner(a):
        n = a.shape[0] // 2
        got = to_row(take(a, c, n))
        return ordered(zcol, got, to_col(got), 0)

    def gather(a, axis):
        if two:
            return jnp.concatenate([a, to_row(a)], axis=axis)
        return lax.all_gather(a, "row", axis=axis, tiled=True)

    def col_sum(a):
        return a + to_col(a.astype(bf16)).astype(f32) if C == 2 else lax.psum(a, "col")

    live_x, seg_x, start_x, end_x, place_x = place_tables(seq_lengths, seq_offsets, b * S - H, S + 2 * H)
    key_seg = jnp.broadcast_to(jnp.where(live_x, seg_x, -2)[:, None], (S + 2 * H, 128))
    sk_left, sk_own, sk_right = key_seg[:H], key_seg[H : H + S], key_seg[H + S :]
    live = live_x[H : H + S]
    nq = S // BQ
    sq = jnp.where(live, seg_x[H : H + S], -1).reshape(nq, 1, BQ)
    first = jnp.min(jnp.where(live, start_x[H : H + S] - b * S, 4 * S).reshape(nq, BQ), axis=1)
    last = jnp.max(jnp.where(live, end_x[H : H + S] - b * S, -4 * S).reshape(nq, BQ), axis=1)
    own_low = jnp.clip(first, 0, S) // BK
    own_high = (jnp.clip(last, 0, S) + BK - 1) // BK
    left_low = jnp.clip(first + H, 0, H) // BK
    right_high = (jnp.clip(last - S, 0, H) + BK - 1) // BK
    own_bounds = jnp.stack([own_low, own_high], axis=1).reshape(-1).astype(jnp.int32)
    zero = jnp.zeros_like(left_low)
    halo_bounds = (
        jnp.stack([left_low, zero + H // BK, zero, right_high], axis=1).reshape(-1).astype(jnp.int32)
    )
    position = jnp.where(live, place_x[H : H + S] - start_x[H : H + S], 0)
    freq = rope_base ** (-(jnp.arange(0, head_width, 2, dtype=f32) / head_width))
    angle = position.astype(f32)[:, None] * jnp.tile(freq, heads)[None, :]
    cosine, sine = lax.optimization_barrier((jnp.cos(angle), jnp.sin(angle)))

    live_column = live[:, None]
    if two:
        x_got = partner(tokens)
        x_low = jnp.where(live_column, jnp.concatenate([tokens, x_got], axis=1), 0)
    else:
        own_x = jnp.where(live_column, tokens, 0)
        x_low = lax.all_gather(own_x, "row", axis=1, tiled=True)

    wq_low = w_qkv.reshape(Dl, R * 3 * W).astype(bf16)
    if two:
        wq_mine = take(wq_low, r, 3 * W, 1)
        wq_got = to_row(take(wq_low, 1 - r, 3 * W, 1))
    else:
        wq = lax.all_to_all(wq_low, "row", split_axis=1, concat_axis=0, tiled=True)
    order = qkv_order(heads, head_width)

    gain_one = own_first(gain_attn, 0)
    gain_two = own_first(gain_mlp, 0)

    Db = D // B
    Dd = D // (B * R)
    if two:
        y_bit, z_bits = b % 2, b // 2

        def relative(a, bits):
            n = jnp.arange(D, dtype=jnp.int32)
            rel = {"w": 0 * n, "x": 0 * n}
            for i, bit in enumerate(bits):
                rel[bit] = n // (D >> (i + 1)) % 2
            z_rel = 2 * rel["Z"] + rel["z"]
            column = ((z_bits ^ z_rel) * 2 + (y_bit ^ rel["y"])) * Db + n % Dd
            column = column + (rel["w"] if "w" in bits else r ^ rel["x"]) * Dd
            column = column ^ (r * (D // 2))
            return nn(a, (n[:, None] == column[None, :]).astype(bf16)).astype(bf16)

        def to_y(a):
            return lax.ppermute(a, "dp", [(i, i ^ 1) for i in range(B)])

        def to_z(a, j):
            return lax.ppermute(a, "dp", [(i, i ^ (2 * j)) for i in range(B)])

        def first(a):
            return a[:, : a.shape[1] // 2]

        def second(a):
            return a[:, a.shape[1] // 2 :].astype(bf16)

        def product(left, right):
            return tn(left, second(right)).astype(bf16)

        def halved(left, right, got):
            return tn(left, first(right)) + got.astype(f32)

        def joined(part, got):
            return first(part).astype(f32) + got.astype(f32)

    x = x_low.astype(f32)
    center = x - jnp.mean(x, axis=-1, keepdims=True)
    inverse_one = lax.rsqrt(jnp.mean(center * center, axis=-1, keepdims=True) + epsilon)
    mean_one = jnp.mean(x, axis=-1, keepdims=True)
    h1 = (center * inverse_one * gain_one).astype(bf16)
    if two:
        h1, wq_mine, wq_got = lax.optimization_barrier((h1, wq_mine, wq_got))
        wq = jnp.concatenate([wq_mine, wq_got], axis=0)
    wq = nn(wq, order).astype(bf16)

    half = W // 2

    def turn(t, sign):
        first_half, second_half = t[:, :half], t[:, half:]
        s = sine * sign
        return jnp.concatenate(
            [first_half * cosine - second_half * s, second_half * cosine + first_half * s], axis=1
        )

    kv_raw = nn(h1, wq[:, W:])
    kv = jnp.concatenate([turn(kv_raw[:, :W], 1.0), kv_raw[:, W:]], axis=1).astype(bf16)
    up = [(i, i + 1) for i in range(B - 1)]
    down = [(i + 1, i) for i in range(B - 1)]
    kv_left = lax.ppermute(kv[S - H :], "dp", up)
    kv_right = lax.ppermute(kv[:H], "dp", down)
    q = (turn(nn(h1, wq[:, :W]), 1.0) * (1.0 / math.sqrt(head_width))).astype(bf16)
    wo_low, wd_low = w_out.astype(bf16), w_down.astype(bf16)
    act_low, lin_low = w_in[:, 0].astype(bf16), w_in[:, 1].astype(bf16)
    if two:
        even = (b // 2) % 2 == 0
        in_got, wo_got = to_row(jnp.where(even, act_low, lin_low)), to_row(wo_low)
        g_got = to_row(take(take(cotangent, 1 - r, Sr), c, Sr // 2))
        wd_half = take(wd_low, (b // 2) % 2, F // 2)
        h1_y = relative(after(h1, kv), "yzZw")
        q, h1_y, sk_left, sk_right, act_low, lin_low, wd_half = lax.optimization_barrier(
            (q, h1_y, sk_left, sk_right, act_low, lin_low, wd_half)
        )

    state = attend_call(own_bounds, q, sq, [kv], [sk_own], heads)
    if two:
        kv_left, kv_right, in_got, wo_got, g_got, wd_half = after(
            (kv_left, kv_right, in_got, wo_got, g_got, wd_half), state
        )
        in_other, wd_got = to_z(in_got, 1), to_row(wd_half)
    o, lse = attend_call(
        halo_bounds, q, sq, [kv_left, kv_right], [sk_left, sk_right], heads, state
    )

    if two:
        o, wd_got, wo_got, g_got = lax.optimization_barrier((o, wd_got, wo_got, g_got))
        wo = own_first(jnp.concatenate([wo_low, wo_got], axis=1), 0)
    else:
        wo = gather(wo_low, 1)

    if two:
        o_got = to_row(take(o, 1 - r, Sr))
        o_rows = jnp.concatenate([take(o, r, Sr), o_got], axis=1)
        wd_other = to_z(wd_got, 1)
        wd_got = ordered(even, wd_got, wd_other, 0)
        g_got = ordered(zcol, g_got, to_col(g_got), 0)
        g_low = jnp.concatenate([take(cotangent, r, Sr), g_got], axis=1)
        g_low = jnp.where(take(live, r, Sr)[:, None], g_low, 0)
        wds = [wd_low, wd_got]
    else:
        o_rows = lax.all_to_all(o, "row", split_axis=0, concat_axis=1, tiled=True)
        own_g = jnp.where(live_column, cotangent, 0)
        g_low = lax.all_to_all(own_g, "row", split_axis=0, concat_axis=1, tiled=True)
        wds, acts, lins = [gather(wd_low, 1)], [gather(act_low, 0)], [gather(lin_low, 0)]

    def split_nn(a, parts):
        n = a.shape[1] // len(parts)
        return sum(nn(a[:, i * n : (i + 1) * n], w) for i, w in enumerate(parts))

    def split_nt(a, parts):
        n = a.shape[1] // len(parts)
        return sum(nt(a[:, i * n : (i + 1) * n], w) for i, w in enumerate(parts))

    def wide(parts):
        return parts[0] if len(parts) == 1 else jnp.concatenate(parts, axis=1)

    x_rows = take(x_low, r, Sr).astype(f32)
    if C == 2:
        o_all = jnp.concatenate([o_rows, to_col(o_rows)], axis=1)
        wo_all = jnp.concatenate([wo, to_col(wo)], axis=0)
        x1 = x_rows + nn(o_all, wo_all)
    else:
        x1 = x_rows + lax.psum(nn(o_rows, wo), "col")
    if two:
        in_got, in_other = after((in_got, in_other), o_got)
        act_got, lin_got = jnp.where(even, in_got, in_other), jnp.where(even, in_other, in_got)
        acts, lins = [act_low, act_got], [lin_low, lin_got]

    center = x1 - jnp.mean(x1, axis=-1, keepdims=True)
    inverse_two = lax.rsqrt(jnp.mean(center * center, axis=-1, keepdims=True) + epsilon)
    n2 = center * inverse_two
    h2 = (n2 * gain_two).astype(bf16)
    a = split_nn(h2, acts)
    u = split_nn(h2, lins)
    phi = 0.5 + 0.5 * lax.erf(a * math.sqrt(0.5))
    gelu = a * phi
    slope = phi + a * jnp.exp(-0.5 * a * a) * (1.0 / math.sqrt(2.0 * math.pi))
    m = (gelu * u).astype(bf16)
    y_part = wide([nn(m, w) for w in wds])
    if two:
        n = Sr // 2
        y_half = (
            take(x1, c, n) + take(y_part, c, n) + to_col(take(y_part, 1 - c, n).astype(bf16)).astype(f32)
        ).astype(bf16)
        y_got = to_row(y_half[:, Dl:])
    else:
        y = (x1 + col_sum(y_part)).astype(bf16)
        layer_out = lax.all_to_all(y, "row", split_axis=1, concat_axis=0, tiled=True)

    dm = split_nt(g_low, wds)
    da = (dm * u * slope).astype(bf16)
    du = (dm * gelu).astype(bf16)
    dh2 = col_sum(wide([nt(da, v) + nt(du, w) for v, w in zip(acts, lins)]))
    if two:
        g_y = relative(g_low, "yzZx")
        lower_got = to_y(product(m, g_y))
    e2 = dh2 * gain_two
    dx1 = g_low.astype(f32) + inverse_two * (
        e2
        - jnp.mean(e2, axis=-1, keepdims=True)
        - n2 * jnp.mean(e2 * n2, axis=-1, keepdims=True)
    )
    dx_low = dx1.astype(bf16)
    do_rows = nt(dx_low, wo).astype(bf16)
    if two:
        do_got = to_row(do_rows[:, W:])
        do = ordered(zrow, do_rows[:, :W], do_got, 0)
        pair = ordered(zrow, y_half[None, :, :Dl], after(y_got, dx_low)[None], 0)
        layer_out = ordered(zcol, pair[:, None], to_col(pair)[:, None], 1).reshape(S, Dl)
    else:
        do = lax.all_to_all(do_rows, "row", split_axis=1, concat_axis=0, tiled=True)

    if two:
        h2, da, du, o_heads, dx_late = after((h2, da, du, own_first(o_rows, 1), dx_low), do_rows)
        dx_y = relative(dx_late, "yzZx")
        h_act, h_lin = relative(h2, "xzZy"), relative(h2, "xyzZ")
        proj_got = to_y(product(o_heads, dx_y))
        gate_send = jnp.concatenate([product(da, h_act), product(du, h_lin)], axis=0)
        gate_got = to_row(after(gate_send, do_got))
        lower = halved(m, g_y, after(lower_got, gate_send))
        lower_got = to_z(second(lower), 1)
        do, lower, layer_out = lax.optimization_barrier((do, lower, layer_out))

    dq_part, dkv_left, dkv_right = attend_back_call(
        halo_bounds, q, do, o, lse, sq, [kv_left, kv_right], [sk_left, sk_right], heads
    )
    from_right = lax.ppermute(dkv_left, "dp", down)
    from_left = lax.ppermute(dkv_right, "dp", up)
    if two:
        lower = joined(lower, after(lower_got, dq_part))
        proj = halved(o_heads, dx_y, after(proj_got, dq_part))
        lower_got, proj_got = to_z(second(lower), 2), to_z(second(proj), 1)
        dq_part, lower, proj = lax.optimization_barrier((dq_part, lower, proj))
    dq, dkv = attend_back_call(own_bounds, q, do, o, lse, sq, [kv], [sk_own], heads, [dq_part])
    if two:
        dkv, from_right, from_left, gate_got, proj_got, lower_got = lax.optimization_barrier(
            (dkv, from_right, from_left, gate_got, proj_got, lower_got)
        )
    pad = jnp.zeros((S - H, 2 * W), bf16)
    dkv = (
        dkv
        + jnp.concatenate([pad, from_right], axis=0).astype(f32)
        + jnp.concatenate([from_left, pad], axis=0).astype(f32)
    )
    dq = turn(dq * (1.0 / math.sqrt(head_width)), -1.0)
    dt = jnp.concatenate([dq, turn(dkv[:, :W], -1.0), dkv[:, W:]], axis=1).astype(bf16)
    dh1_part = nt(dt, wq)
    if two:
        query_send = product(dt, h1_y)
        gate_got, proj_got, lower_got = after((gate_got, proj_got, lower_got), query_send, dh1_part)

    if two:
        n = S // 2
        kept = take(dh1_part, c, n) + to_col(take(dh1_part, 1 - c, n).astype(bf16)).astype(f32)
        xs = take(x_low, c, n).astype(f32)
        inv, mean = take(inverse_one, c, n), take(mean_one, c, n)
        n1 = (xs - mean) * inv
        e1 = kept * gain_one
        sums = jnp.stack([jnp.sum(e1, axis=-1), jnp.sum(e1 * n1, axis=-1)])
        sums = (sums + to_row(sums)) * (1.0 / D)
        moved = lax.ppermute(after(dx_low[:, Dl:], from_left), ("row", "col"), [(0, 2), (3, 1)])
        kept_send, moved = lax.optimization_barrier((kept[:, Dl:].astype(bf16), moved))
        mine = (kept[:, :Dl] + to_row(kept_send).astype(f32)) * gain_one[:Dl]
        base = jnp.where(r == c, dx1[:, :Dl], moved.astype(f32))
        dx = base + inv * (mine - sums[0][:, None] - n1[:, :Dl] * sums[1][:, None])
        dx = dx.astype(bf16)
        tokens_grad = ordered(zcol, dx, to_col(dx), 0)
    else:
        dh1 = lax.psum_scatter(col_sum(dh1_part), "row", scatter_dimension=1, tiled=True)
        xs = own_x.astype(f32)
        n1 = (xs - mean_one) * inverse_one
        e1 = dh1 * take(gain_attn, r, Dl)
        sums = lax.psum(jnp.stack([jnp.sum(e1, axis=-1), jnp.sum(e1 * n1, axis=-1)]), "row") / D
        base = lax.all_to_all(dx_low, "row", split_axis=1, concat_axis=0, tiled=True).astype(f32)
        tokens_grad = (
            base + inverse_one * (e1 - sums[0][:, None] - n1 * sums[1][:, None])
        ).astype(bf16)

    if two:
        query = halved(dt, h1_y, after(to_y(query_send), kept))
        n = F
        act = halved(da, h_act, gate_got[:n])
        lin = halved(du, h_lin, gate_got[n:])
        act_got = after(to_z(second(act), 1), kept)
        lin = joined(lin, after(to_y(second(lin)), kept))
        act, proj = joined(act, act_got), joined(proj, proj_got)
        both_got = to_z(jnp.concatenate([second(act), second(proj)], axis=0), 2)
        lin = joined(lin, to_z(second(lin), 1))
        act, proj = joined(act, both_got[:n]), joined(proj, both_got[n:])
        lower = joined(lower, lower_got)
        query = joined(query, after(to_z(second(query), 1), dx))
        last_got = after(to_row(jnp.concatenate([second(lower), second(proj)], axis=0)), query)
        lower, proj = joined(lower, last_got[:n]), joined(proj, last_got[n:])
        act = joined(act, after(to_y(second(act)), query))
        lin = joined(lin, after(to_z(second(lin), 2), query))
        gate = jnp.stack([act.T, lin.T])
        query = joined(query, to_z(second(query), 2)).T
        wq_rows = take(wq, b ^ (4 * r), Db)
        place = (2 * b + r) ^ (8 * r)
        wi_rows = jnp.stack(
            [jnp.where(place < 8, *(take(w, place % 8, Dd) for w in ws)) for ws in after((acts, lins), kept)]
        )
    else:

        def scatter(grad):
            return lax.psum_scatter(grad, ("dp", "row"), scatter_dimension=1, tiled=True).astype(f32)

        gate = jnp.stack([scatter(tn(da, h2).astype(bf16)).T, scatter(tn(du, h2).astype(bf16)).T])
        proj = scatter(tn(o_rows, dx_low).astype(bf16))
        lower = scatter(tn(m, g_low).astype(bf16))
        query = lax.psum_scatter(
            tn(h1, dt).astype(bf16), "dp", scatter_dimension=0, tiled=True
        ).astype(f32)
        wq_rows = take(wq, b, Db)
        wi_rows = jnp.stack([take(acts[0], b * R + r, Dd), take(lins[0], b * R + r, Dd)])

    one_part = jnp.sum(query * wq_rows.astype(f32), axis=1)
    two_part = jnp.sum(jnp.sum(gate * wi_rows.astype(f32), axis=2), axis=0)
    natural = lax.dot_general(
        query, order.astype(f32), (((1,), (1,)), ((), ())),
        precision=lax.Precision.HIGHEST, preferred_element_type=f32,
    )
    if two:
        pair = jnp.concatenate([natural, jnp.broadcast_to(one_part[:, None], (Db, 128))], axis=1)
        pair = pair.reshape(2, Dd, 3 * W + 128)
        mine = lax.dynamic_index_in_dim(pair, r, 0, keepdims=False)
        theirs = to_row(lax.dynamic_index_in_dim(pair, 1 - r, 0, keepdims=False))
        theirs = after(theirs, tokens_grad)
        one_part = mine[:, 3 * W] + theirs[:, 3 * W]
        query_out = ordered(zrow, mine[:, : 3 * W], theirs[:, : 3 * W], 1)
    else:
        one_part = take(lax.psum(one_part, "row"), r, Dd)
        query_out = lax.all_to_all(natural, "row", split_axis=0, concat_axis=1, tiled=True)
    gains = jnp.stack([one_part, two_part])
    gains = gains + to_col(gains) if C == 2 else lax.psum(gains, "col")
    gain_attn_grad = gains[0] / take(gain_attn, b * R + r, Dd)
    gain_mlp_grad = gains[1] / take(gain_mlp, b * R + r, Dd)
    return (
        layer_out,
        tokens_grad,
        gain_attn_grad,
        query_out.reshape(Dd, R * heads, 3 * head_width),
        proj,
        gain_mlp_grad,
        jnp.swapaxes(gate, 0, 1),
        lower,
    )


def solution(mesh):
    return jax.shard_map(
        local,
        mesh=mesh,
        in_specs=(
            P("dp", "row"),
            P(),
            P("row", "col", None),
            P("col", "row"),
            P(),
            P("row", None, "col"),
            P("col", "row"),
            P("dp", "row"),
            P(),
            P(),
            P(),
        ),
        out_specs=(
            P("dp", "row"),
            P("dp", "row"),
            P(("dp", "row")),
            P(("dp", "row"), "col", None),
            P("col", ("dp", "row")),
            P(("dp", "row")),
            P(("dp", "row"), None, "col"),
            P("col", ("dp", "row")),
        ),
        check_vma=False,
    )
```

```python
import functools
import math

import jax
import jax.numpy as jnp
from jax import lax
from jax.experimental import pallas as pl
from jax.experimental.pallas import tpu as pltpu
from jax.sharding import PartitionSpec as P

LONGEST = 1024
BQ = 256
BK = 256
NEG = -1e30
FAR = 1e30
epsilon = 1e-05
rope_base = 160000.0
bf16 = jnp.bfloat16
f32 = jnp.float32
SWAP = [(0, 1), (1, 0)]


def nt(a, b):
    return lax.dot_general(a, b, (((1,), (1,)), ((), ())), preferred_element_type=f32)


def tn(a, b):
    return lax.dot_general(a, b, (((0,), (0,)), ((), ())), preferred_element_type=f32)


def nn(a, b):
    return jnp.dot(a, b, preferred_element_type=f32)


def after(a, *others):
    return lax.optimization_barrier((a, *others))[0]


def half_mask(width, heads, head):
    lane = lax.broadcasted_iota(jnp.int32, (1, width), 1)
    half = width // 2
    lane = jnp.where(lane >= half, lane - half, lane)
    step = half // heads
    return (lane >= head * step) & (lane < (head + 1) * step)


def whole_mask(width, heads, head):
    lane = lax.broadcasted_iota(jnp.int32, (1, width), 1)
    step = width // heads
    return (lane >= head * step) & (lane < (head + 1) * step)


def stack_heads(block, heads, mask_of):
    zero = jnp.zeros_like(block)
    width = block.shape[1]
    return jnp.concatenate(
        [jnp.where(mask_of(width, heads, h), block, zero) for h in range(heads)], axis=0
    )


def same_segment(key_seg, query_seg, heads):
    tile = key_seg
    lanes = query_seg.shape[1]
    if lanes > tile.shape[1]:
        tile = jnp.concatenate([tile] * (lanes // tile.shape[1]), axis=1)
    same = tile == query_seg
    return jnp.concatenate([same] * heads, axis=1) if heads > 1 else same


def forward_kernel(heads, sets, final, bounds, *refs):
    refs = list(refs)
    q_ref, sq_ref = refs[:2]
    kv_refs = refs[2 : 2 + sets]
    sk_refs = refs[2 + sets : 2 + 2 * sets]
    rest = refs[2 + 2 * sets :]
    if final:
        acc_in, ml_in, o_ref, lse_ref = rest[:4]
        acc, m_ref, l_ref = rest[4:7]
        vt_refs = rest[7:]
    else:
        acc, ml_ref = rest[:2]
        m_ref, l_ref = rest[2:4]
        vt_refs = rest[4:]
    step = pl.program_id(0)
    rows, width = q_ref.shape
    each = width // heads

    @pl.when(step == 0)
    def _():
        for kv, vt in zip(kv_refs, vt_refs):
            for j in range(kv.shape[0] // BK):
                vt[:, j * BK : (j + 1) * BK] = kv[j * BK : (j + 1) * BK, width:].T

    if final:
        acc[...] = acc_in[0]
        m_ref[...] = ml_in[0, 0:1]
        l_ref[...] = ml_in[0, 1:2]
    else:
        acc[...] = jnp.zeros_like(acc)
        m_ref[...] = jnp.full_like(m_ref, NEG)
        l_ref[...] = jnp.zeros_like(l_ref)
    queries = stack_heads(q_ref[...], heads, half_mask)
    query_seg = sq_ref[0]
    target = acc if final else acc.at[0]

    for s in range(sets):
        kv, sk, vt = kv_refs[s], sk_refs[s], vt_refs[s]

        def body(j, carry):
            first = pl.multiple_of(j * BK, BK)
            keys = kv[pl.ds(first, BK), 0:width]
            scores = nt(keys, queries)
            same = same_segment(sk[pl.ds(first, BK), :], query_seg, heads)
            scores = jnp.where(same, scores, NEG)
            before = m_ref[...]
            top = jnp.maximum(before, jnp.max(scores, axis=0, keepdims=True))
            raised = jnp.exp(scores - top)
            shrink = jnp.exp(before - top)
            m_ref[...] = top
            l_ref[...] = l_ref[...] * shrink + jnp.sum(raised, axis=0, keepdims=True)
            low = raised.astype(bf16)
            for h in range(heads):
                part = nn(
                    vt[h * each : (h + 1) * each, pl.ds(first, BK)],
                    low[:, h * rows : (h + 1) * rows],
                )
                hold = target[h * each : (h + 1) * each, :]
                target[h * each : (h + 1) * each, :] = (
                    hold * shrink[:, h * rows : (h + 1) * rows] + part
                )
            return carry

        lax.fori_loop(
            bounds[(step * sets + s) * 2], bounds[(step * sets + s) * 2 + 1], body, 0
        )

    if final:
        live = query_seg >= 0
        total = l_ref[...]
        live_all = jnp.concatenate([live] * heads, axis=1) if heads > 1 else live
        total = jnp.where(live_all, total, 1.0)
        inverse = jnp.where(live_all, 1.0 / total, 0.0)
        for h in range(heads):
            acc[h * each : (h + 1) * each, :] = (
                acc[h * each : (h + 1) * each, :] * inverse[:, h * rows : (h + 1) * rows]
            )
        o_ref[...] = acc[...].T.astype(bf16)
        lse_ref[0] = jnp.where(live_all, m_ref[...] + jnp.log(total), FAR)
    else:
        ml_ref[0, 0:1] = m_ref[...]
        ml_ref[0, 1:2] = l_ref[...]


def cost(products, q, kvs):
    pairs = q.shape[0]
    return pl.CostEstimate(
        flops=4 * products * pairs * q.shape[1],
        bytes_accessed=2 * sum(a.size for a in kvs) + 4 * q.size,
        transcendentals=4 * pairs,
    )


def whole(shape):
    zeros = (0,) * len(shape)
    return pl.BlockSpec(shape, lambda i, *_: zeros)


def attend_call(bounds, q, sq, kvs, sks, heads, state=None):
    count = q.shape[0] // BQ
    width = q.shape[1]
    sets = len(kvs)
    final = state is not None
    row_spec = pl.BlockSpec((BQ, width), lambda i, *_: (i, 0))
    acc_spec = pl.BlockSpec((1, width, BQ), lambda i, *_: (i, 0, 0))
    ml_spec = pl.BlockSpec((1, 2, heads * BQ), lambda i, *_: (i, 0, 0))
    in_specs = [row_spec, pl.BlockSpec((1, 1, BQ), lambda i, *_: (i, 0, 0))]
    in_specs += [whole(a.shape) for a in kvs] + [whole(a.shape) for a in sks]
    scratch = [pltpu.VMEM((1, heads * BQ), f32)] * 2
    scratch += [pltpu.VMEM((width, a.shape[0]), bf16) for a in kvs]
    if final:
        in_specs += [acc_spec, ml_spec]
        out_specs = [row_spec, pl.BlockSpec((1, 1, heads * BQ), lambda i, *_: (i, 0, 0))]
        out_shape = [
            jax.ShapeDtypeStruct(q.shape, bf16),
            jax.ShapeDtypeStruct((count, 1, heads * BQ), f32),
        ]
        scratch = [pltpu.VMEM((width, BQ), f32)] + scratch
    else:
        out_specs = [acc_spec, ml_spec]
        out_shape = [
            jax.ShapeDtypeStruct((count, width, BQ), f32),
            jax.ShapeDtypeStruct((count, 2, heads * BQ), f32),
        ]
    return pl.pallas_call(
        functools.partial(forward_kernel, heads, sets, final),
        grid_spec=pltpu.PrefetchScalarGridSpec(
            num_scalar_prefetch=1,
            grid=(count,),
            in_specs=in_specs,
            out_specs=out_specs,
            scratch_shapes=scratch,
        ),
        out_shape=out_shape,
        cost_estimate=cost(4, q, kvs),
        name="attend_final" if final else "attend_own",
    )(bounds, q, sq, *kvs, *sks, *(state or ()))


def backward_kernel(heads, sets, final, bounds, *refs):
    refs = list(refs)
    q_ref, do_ref, o_ref, lse_ref, sq_ref = refs[:5]
    kv_refs = refs[5 : 5 + sets]
    sk_refs = refs[5 + sets : 5 + 2 * sets]
    rest = refs[5 + 2 * sets :]
    if final:
        dq_in, dq_ref = rest[0], rest[1]
        dkv_refs = rest[2 : 2 + sets]
        dq_acc = rest[2 + sets]
        kt_refs = rest[3 + sets : 3 + 2 * sets]
        sums = dkv_refs
    else:
        dq_ref = rest[0]
        dkv_refs = rest[1 : 1 + sets]
        dq_acc = rest[1 + sets]
        kt_refs = rest[2 + sets : 2 + 2 * sets]
        sums = rest[2 + 2 * sets :]
    step = pl.program_id(0)
    rows, width = q_ref.shape
    each = width // heads
    half = width // 2
    piece = half // heads

    @pl.when(step == 0)
    def _():
        for kv, kt, total in zip(kv_refs, kt_refs, sums):
            total[...] = jnp.zeros_like(total)
            for j in range(kv.shape[0] // BK):
                kt[:, j * BK : (j + 1) * BK] = kv[j * BK : (j + 1) * BK, :width].T

    if final:
        dq_acc[...] = dq_in[0]
    else:
        dq_acc[...] = jnp.zeros_like(dq_acc)
    grads = do_ref[...]
    queries = stack_heads(q_ref[...], heads, half_mask)
    outs = stack_heads(grads, heads, whole_mask)
    query_seg = sq_ref[0]
    lse = lse_ref[0]
    product = (grads.astype(f32) * o_ref[...].astype(f32)).T
    delta = jnp.concatenate(
        [
            jnp.sum(product[h * each : (h + 1) * each], axis=0, keepdims=True)
            for h in range(heads)
        ],
        axis=1,
    )

    for s in range(sets):
        kv, sk, kt, total = kv_refs[s], sk_refs[s], kt_refs[s], sums[s]

        def body(j, carry):
            first = pl.multiple_of(j * BK, BK)
            keys = kv[pl.ds(first, BK), 0:width]
            values = kv[pl.ds(first, BK), width : 2 * width]
            scores = nt(keys, queries)
            same = same_segment(sk[pl.ds(first, BK), :], query_seg, heads)
            probs = jnp.where(same, jnp.exp(scores - lse), 0.0)
            grad_probs = nt(values, outs)
            grad_scores = (probs * (grad_probs - delta)).astype(bf16)
            low = probs.astype(bf16)
            total[pl.ds(first, BK), width : 2 * width] += nn(low, outs)
            total[pl.ds(first, BK), 0:width] += nn(grad_scores, queries)
            for h in range(heads):
                column = grad_scores[:, h * rows : (h + 1) * rows]
                for lead in (h * piece, half + h * piece):
                    dq_acc[lead : lead + piece, :] += nn(
                        kt[lead : lead + piece, pl.ds(first, BK)], column
                    )
            return carry

        lax.fori_loop(
            bounds[(step * sets + s) * 2], bounds[(step * sets + s) * 2 + 1], body, 0
        )

    if final:
        dq_ref[...] = dq_acc[...].T
    else:
        dq_ref[0] = dq_acc[...]

        @pl.when(step == pl.num_programs(0) - 1)
        def _():
            for total, out in zip(sums, dkv_refs):
                out[...] = total[...].astype(bf16)


def attend_back_call(bounds, q, do, o, lse, sq, kvs, sks, heads, state=None):
    count = q.shape[0] // BQ
    width = q.shape[1]
    sets = len(kvs)
    final = state is not None
    row_spec = pl.BlockSpec((BQ, width), lambda i, *_: (i, 0))
    acc_spec = pl.BlockSpec((1, width, BQ), lambda i, *_: (i, 0, 0))
    in_specs = [row_spec] * 3 + [
        pl.BlockSpec((1, 1, heads * BQ), lambda i, *_: (i, 0, 0)),
        pl.BlockSpec((1, 1, BQ), lambda i, *_: (i, 0, 0)),
    ]
    in_specs += [whole(a.shape) for a in kvs] + [whole(a.shape) for a in sks]
    scratch = [pltpu.VMEM((width, BQ), f32)]
    scratch += [pltpu.VMEM((width, a.shape[0]), bf16) for a in kvs]
    if final:
        in_specs += [acc_spec]
        out_specs = [row_spec]
        out_shape = [jax.ShapeDtypeStruct(q.shape, f32)]
    else:
        out_specs = [acc_spec]
        out_shape = [jax.ShapeDtypeStruct((count, width, BQ), f32)]
        scratch += [pltpu.VMEM(a.shape, f32) for a in kvs]
    out_specs += [whole(a.shape) for a in kvs]
    out_shape += [jax.ShapeDtypeStruct(a.shape, f32 if final else bf16) for a in kvs]
    return pl.pallas_call(
        functools.partial(backward_kernel, heads, sets, final),
        grid_spec=pltpu.PrefetchScalarGridSpec(
            num_scalar_prefetch=1,
            grid=(count,),
            in_specs=in_specs,
            out_specs=out_specs,
            scratch_shapes=scratch,
        ),
        out_shape=out_shape,
        cost_estimate=cost(10, q, kvs),
        name="back_own" if final else "back_halo",
    )(bounds, q, do, o, lse, sq, *kvs, *sks, *(state or ()))


def place_tables(seq_lengths, seq_offsets, first, count):
    place = first + jnp.arange(count, dtype=jnp.int32)
    ends = seq_offsets + seq_lengths
    inside = (place[:, None] >= seq_offsets[None, :]) & (place[:, None] < ends[None, :])
    live = jnp.any(inside, axis=1)
    index = jnp.arange(seq_offsets.shape[0], dtype=jnp.int32)
    segment = jnp.sum(jnp.where(inside, index[None, :], 0), axis=1)
    start = jnp.sum(jnp.where(inside, seq_offsets[None, :], 0), axis=1)
    end = jnp.sum(jnp.where(inside, ends[None, :], 0), axis=1)
    return live, segment, start, end, place


def qkv_order(heads, head_width):
    width = heads * head_width
    half = head_width // 2
    new = jnp.arange(3 * width, dtype=jnp.int32)
    kind = new // width
    inner = new % width
    side = inner // (width // 2)
    pair_head = (inner % (width // 2)) // half
    pair_old = pair_head * 3 * head_width + kind * head_width + side * half + inner % half
    value_old = (inner // head_width) * 3 * head_width + 2 * head_width + inner % head_width
    old = jnp.where(kind == 2, value_old, pair_old)
    return (old[None, :] == new[:, None]).astype(bf16)


def local(
    tokens,
    gain_attn,
    w_qkv,
    w_out,
    gain_mlp,
    w_in,
    w_down,
    cotangent,
    seq_lengths,
    seq_offsets,
    deal,
):
    R, C, B = lax.axis_size("row"), lax.axis_size("col"), lax.axis_size("dp")
    r, c, b = lax.axis_index("row"), lax.axis_index("col"), lax.axis_index("dp")
    S, Dl = tokens.shape
    D = Dl * R
    two = R == 2 and C == 2 and B == 8
    heads = w_qkv.shape[1] // R
    head_width = w_qkv.shape[2] // 3
    W = heads * head_width
    F = w_down.shape[0]
    H = LONGEST
    Sr = S // R
    zrow, zcol = (r == 0), (c == 0)

    def to_row(a):
        return lax.ppermute(a, "row", SWAP)

    def to_col(a):
        return lax.ppermute(a, "col", SWAP)

    def ordered(flag, mine, theirs, axis):
        return jnp.where(
            flag,
            jnp.concatenate([mine, theirs], axis=axis),
            jnp.concatenate([theirs, mine], axis=axis),
        )

    def own_first(a, axis):
        if not two:
            return a
        n = a.shape[axis] // 2
        return jnp.where(zrow, a, jnp.roll(a, n, axis=axis))

    def take(a, index, size, axis=0):
        return lax.dynamic_slice_in_dim(a, index * size, size, axis)

    def partner(a):
        n = a.shape[0] // 2
        got = to_row(take(a, c, n))
        return ordered(zcol, got, to_col(got), 0)

    def gather(a, axis):
        if two:
            return jnp.concatenate([a, to_row(a)], axis=axis)
        return lax.all_gather(a, "row", axis=axis, tiled=True)

    def col_sum(a):
        return a + to_col(a.astype(bf16)).astype(f32) if C == 2 else lax.psum(a, "col")

    live_x, seg_x, start_x, end_x, place_x = place_tables(seq_lengths, seq_offsets, b * S - H, S + 2 * H)
    key_seg = jnp.broadcast_to(jnp.where(live_x, seg_x, -2)[:, None], (S + 2 * H, 128))
    sk_left, sk_own, sk_right = key_seg[:H], key_seg[H : H + S], key_seg[H + S :]
    live = live_x[H : H + S]
    nq = S // BQ
    sq = jnp.where(live, seg_x[H : H + S], -1).reshape(nq, 1, BQ)
    first = jnp.min(jnp.where(live, start_x[H : H + S] - b * S, 4 * S).reshape(nq, BQ), axis=1)
    last = jnp.max(jnp.where(live, end_x[H : H + S] - b * S, -4 * S).reshape(nq, BQ), axis=1)
    own_low = jnp.clip(first, 0, S) // BK
    own_high = (jnp.clip(last, 0, S) + BK - 1) // BK
    left_low = jnp.clip(first + H, 0, H) // BK
    right_high = (jnp.clip(last - S, 0, H) + BK - 1) // BK
    own_bounds = jnp.stack([own_low, own_high], axis=1).reshape(-1).astype(jnp.int32)
    zero = jnp.zeros_like(left_low)
    halo_bounds = (
        jnp.stack([left_low, zero + H // BK, zero, right_high], axis=1).reshape(-1).astype(jnp.int32)
    )
    position = jnp.where(live, place_x[H : H + S] - start_x[H : H + S], 0)
    freq = rope_base ** (-(jnp.arange(0, head_width, 2, dtype=f32) / head_width))
    angle = position.astype(f32)[:, None] * jnp.tile(freq, heads)[None, :]
    cosine, sine = lax.optimization_barrier((jnp.cos(angle), jnp.sin(angle)))

    live_column = live[:, None]
    if two:
        x_got = partner(tokens)
        x_low = jnp.where(live_column, jnp.concatenate([tokens, x_got], axis=1), 0)
    else:
        own_x = jnp.where(live_column, tokens, 0)
        x_low = lax.all_gather(own_x, "row", axis=1, tiled=True)

    wq_low = w_qkv.reshape(Dl, R * 3 * W).astype(bf16)
    if two:
        wq_mine = take(wq_low, r, 3 * W, 1)
        wq_got = to_row(take(wq_low, 1 - r, 3 * W, 1))
    else:
        wq = lax.all_to_all(wq_low, "row", split_axis=1, concat_axis=0, tiled=True)
    order = qkv_order(heads, head_width)

    gain_one = own_first(gain_attn, 0)
    gain_two = own_first(gain_mlp, 0)

    Db = D // B
    Dd = D // (B * R)
    if two:
        y_bit, z_bits = b % 2, b // 2

        def relative(a, bits):
            n = jnp.arange(D, dtype=jnp.int32)
            rel = {"w": 0 * n, "x": 0 * n}
            for i, bit in enumerate(bits):
                rel[bit] = n // (D >> (i + 1)) % 2
            z_rel = 2 * rel["Z"] + rel["z"]
            column = ((z_bits ^ z_rel) * 2 + (y_bit ^ rel["y"])) * Db + n % Dd
            column = column + (rel["w"] if "w" in bits else r ^ rel["x"]) * Dd
            column = column ^ (r * (D // 2))
            return nn(a, (n[:, None] == column[None, :]).astype(bf16)).astype(bf16)

        def to_y(a):
            return lax.ppermute(a, "dp", [(i, i ^ 1) for i in range(B)])

        def to_z(a, j):
            return lax.ppermute(a, "dp", [(i, i ^ (2 * j)) for i in range(B)])

        def first(a):
            return a[:, : a.shape[1] // 2]

        def second(a):
            return a[:, a.shape[1] // 2 :].astype(bf16)

        def product(left, right):
            return tn(left, second(right)).astype(bf16)

        def halved(left, right, got):
            return tn(left, first(right)) + got.astype(f32)

        def joined(part, got):
            return first(part).astype(f32) + got.astype(f32)

    x = x_low.astype(f32)
    center = x - jnp.mean(x, axis=-1, keepdims=True)
    inverse_one = lax.rsqrt(jnp.mean(center * center, axis=-1, keepdims=True) + epsilon)
    mean_one = jnp.mean(x, axis=-1, keepdims=True)
    h1 = (center * inverse_one * gain_one).astype(bf16)
    if two:
        h1, wq_mine, wq_got = lax.optimization_barrier((h1, wq_mine, wq_got))
        wq = jnp.concatenate([wq_mine, wq_got], axis=0)
    wq = nn(wq, order).astype(bf16)

    half = W // 2

    def turn(t, sign):
        first_half, second_half = t[:, :half], t[:, half:]
        s = sine * sign
        return jnp.concatenate(
            [first_half * cosine - second_half * s, second_half * cosine + first_half * s], axis=1
        )

    kv_raw = nn(h1, wq[:, W:])
    kv = jnp.concatenate([turn(kv_raw[:, :W], 1.0), kv_raw[:, W:]], axis=1).astype(bf16)
    up = [(i, i + 1) for i in range(B - 1)]
    down = [(i + 1, i) for i in range(B - 1)]
    kv_left = lax.ppermute(kv[S - H :], "dp", up)
    kv_right = lax.ppermute(kv[:H], "dp", down)
    q = (turn(nn(h1, wq[:, :W]), 1.0) * (1.0 / math.sqrt(head_width))).astype(bf16)
    wo_low, wd_low = w_out.astype(bf16), w_down.astype(bf16)
    act_low, lin_low = w_in[:, 0].astype(bf16), w_in[:, 1].astype(bf16)
    if two:
        even = (b // 2) % 2 == 0
        in_send, wo_send, g_send = after(
            (jnp.where(even, act_low, lin_low), wo_low, take(take(cotangent, 1 - r, Sr), c, Sr // 2)),
            cosine,
        )
        in_got, wo_got, g_got = to_row(in_send), to_row(wo_send), to_row(g_send)
        wd_half = take(wd_low, (b // 2) % 2, F // 2)
        h1_y = relative(after(h1, kv), "yzZw")
        q, h1_y, sk_left, sk_right, act_low, lin_low, wd_half = lax.optimization_barrier(
            (q, h1_y, sk_left, sk_right, act_low, lin_low, wd_half)
        )

    state = attend_call(own_bounds, q, sq, [kv], [sk_own], heads)
    if two:
        kv_left, kv_right, in_got, wo_got, g_got, wd_half = after(
            (kv_left, kv_right, in_got, wo_got, g_got, wd_half), state
        )
        in_other, wd_got = to_z(in_got, 1), to_row(wd_half)
    o, lse = attend_call(
        halo_bounds, q, sq, [kv_left, kv_right], [sk_left, sk_right], heads, state
    )

    if two:
        o, wd_got, wo_got, g_got = lax.optimization_barrier((o, wd_got, wo_got, g_got))
        wo = own_first(jnp.concatenate([wo_low, wo_got], axis=1), 0)
    else:
        wo = gather(wo_low, 1)

    if two:
        o_got = to_row(take(o, 1 - r, Sr))
        o_rows = jnp.concatenate([take(o, r, Sr), o_got], axis=1)
        wd_other = to_z(wd_got, 1)
        wd_got = ordered(even, wd_got, wd_other, 0)
        g_got = ordered(zcol, g_got, to_col(g_got), 0)
        g_low = jnp.concatenate([take(cotangent, r, Sr), g_got], axis=1)
        g_low = jnp.where(take(live, r, Sr)[:, None], g_low, 0)
        wds = [wd_low, wd_got]
    else:
        o_rows = lax.all_to_all(o, "row", split_axis=0, concat_axis=1, tiled=True)
        own_g = jnp.where(live_column, cotangent, 0)
        g_low = lax.all_to_all(own_g, "row", split_axis=0, concat_axis=1, tiled=True)
        wds, acts, lins = [gather(wd_low, 1)], [gather(act_low, 0)], [gather(lin_low, 0)]

    def split_nn(a, parts):
        n = a.shape[1] // len(parts)
        return sum(nn(a[:, i * n : (i + 1) * n], w) for i, w in enumerate(parts))

    def split_nt(a, parts):
        n = a.shape[1] // len(parts)
        return sum(nt(a[:, i * n : (i + 1) * n], w) for i, w in enumerate(parts))

    def wide(parts):
        return parts[0] if len(parts) == 1 else jnp.concatenate(parts, axis=1)

    x_rows = take(x_low, r, Sr).astype(f32)
    if C == 2:
        o_all = jnp.concatenate([o_rows, to_col(o_rows)], axis=1)
        wo_all = jnp.concatenate([wo, to_col(wo)], axis=0)
        x1 = x_rows + nn(o_all, wo_all)
    else:
        x1 = x_rows + lax.psum(nn(o_rows, wo), "col")
    if two:
        in_got, in_other = after((in_got, in_other), o_got)
        act_got, lin_got = jnp.where(even, in_got, in_other), jnp.where(even, in_other, in_got)
        acts, lins = [act_low, act_got], [lin_low, lin_got]

    center = x1 - jnp.mean(x1, axis=-1, keepdims=True)
    inverse_two = lax.rsqrt(jnp.mean(center * center, axis=-1, keepdims=True) + epsilon)
    n2 = center * inverse_two
    h2 = (n2 * gain_two).astype(bf16)
    a = split_nn(h2, acts)
    u = split_nn(h2, lins)
    phi = 0.5 + 0.5 * lax.erf(a * math.sqrt(0.5))
    gelu = a * phi
    slope = phi + a * jnp.exp(-0.5 * a * a) * (1.0 / math.sqrt(2.0 * math.pi))
    m = (gelu * u).astype(bf16)
    y_part = wide([nn(m, w) for w in wds])
    if two:
        n = Sr // 2
        y_half = (
            take(x1, c, n) + take(y_part, c, n) + to_col(take(y_part, 1 - c, n).astype(bf16)).astype(f32)
        ).astype(bf16)
        y_got = to_row(y_half[:, Dl:])
    else:
        y = (x1 + col_sum(y_part)).astype(bf16)
        layer_out = lax.all_to_all(y, "row", split_axis=1, concat_axis=0, tiled=True)

    dm = split_nt(g_low, wds)
    da = (dm * u * slope).astype(bf16)
    du = (dm * gelu).astype(bf16)
    dh2 = col_sum(wide([nt(da, v) + nt(du, w) for v, w in zip(acts, lins)]))
    if two:
        g_y = relative(g_low, "yzZx")
        lower_got = to_y(product(m, g_y))
    e2 = dh2 * gain_two
    dx1 = g_low.astype(f32) + inverse_two * (
        e2
        - jnp.mean(e2, axis=-1, keepdims=True)
        - n2 * jnp.mean(e2 * n2, axis=-1, keepdims=True)
    )
    dx_low = dx1.astype(bf16)
    do_rows = nt(dx_low, wo).astype(bf16)
    if two:
        do_got = to_row(do_rows[:, W:])
        do = ordered(zrow, do_rows[:, :W], do_got, 0)
        pair = ordered(zrow, y_half[None, :, :Dl], after(y_got, dx_low)[None], 0)
        layer_out = ordered(zcol, pair[:, None], to_col(pair)[:, None], 1).reshape(S, Dl)
    else:
        do = lax.all_to_all(do_rows, "row", split_axis=1, concat_axis=0, tiled=True)

    if two:
        h2, da, du, o_heads, dx_late = after((h2, da, du, own_first(o_rows, 1), dx_low), do_rows)
        dx_y = relative(dx_late, "yzZx")
        h_act, h_lin = relative(h2, "xzZy"), relative(h2, "xyzZ")
        proj_got = to_y(product(o_heads, dx_y))
        gate_send = jnp.concatenate([product(da, h_act), product(du, h_lin)], axis=0)
        gate_got = to_row(after(gate_send, do_got))
        lower = halved(m, g_y, after(lower_got, gate_send))
        lower_got = to_z(second(lower), 1)
        do, lower, layer_out = lax.optimization_barrier((do, lower, layer_out))

    dq_part, dkv_left, dkv_right = attend_back_call(
        halo_bounds, q, do, o, lse, sq, [kv_left, kv_right], [sk_left, sk_right], heads
    )
    from_right = lax.ppermute(dkv_left, "dp", down)
    from_left = lax.ppermute(dkv_right, "dp", up)
    if two:
        lower = joined(lower, after(lower_got, dq_part))
        lower_got = to_z(second(lower), 2)
        dq_part, lower = lax.optimization_barrier((dq_part, lower))
    dq, dkv = attend_back_call(own_bounds, q, do, o, lse, sq, [kv], [sk_own], heads, [dq_part])
    if two:
        dkv, from_right, from_left, gate_got, proj_got, lower_got = lax.optimization_barrier(
            (dkv, from_right, from_left, gate_got, proj_got, lower_got)
        )
    pad = jnp.zeros((S - H, 2 * W), bf16)
    dkv = (
        dkv
        + jnp.concatenate([pad, from_right], axis=0).astype(f32)
        + jnp.concatenate([from_left, pad], axis=0).astype(f32)
    )
    dq = turn(dq * (1.0 / math.sqrt(head_width)), -1.0)
    dt = jnp.concatenate([dq, turn(dkv[:, :W], -1.0), dkv[:, W:]], axis=1).astype(bf16)
    dh1_part = nt(dt, wq)
    if two:
        query_send = product(dt, h1_y)
        gate_got, proj_got, lower_got = after((gate_got, proj_got, lower_got), query_send, dh1_part)

    if two:
        n = S // 2
        kept = take(dh1_part, c, n) + to_col(take(dh1_part, 1 - c, n).astype(bf16)).astype(f32)
        xs = take(x_low, c, n).astype(f32)
        inv, mean = take(inverse_one, c, n), take(mean_one, c, n)
        n1 = (xs - mean) * inv
        e1 = kept * gain_one
        sums = jnp.stack([jnp.sum(e1, axis=-1), jnp.sum(e1 * n1, axis=-1)])
        sums = (sums + to_row(sums)) * (1.0 / D)
        moved = lax.ppermute(after(dx_low[:, Dl:], from_left), ("row", "col"), [(0, 2), (3, 1)])
        kept_send, moved = lax.optimization_barrier((kept[:, Dl:].astype(bf16), moved))
        mine = (kept[:, :Dl] + to_row(kept_send).astype(f32)) * gain_one[:Dl]
        base = jnp.where(r == c, dx1[:, :Dl], moved.astype(f32))
        dx = base + inv * (mine - sums[0][:, None] - n1[:, :Dl] * sums[1][:, None])
        dx = dx.astype(bf16)
        tokens_grad = ordered(zcol, dx, to_col(dx), 0)
    else:
        dh1 = lax.psum_scatter(col_sum(dh1_part), "row", scatter_dimension=1, tiled=True)
        xs = own_x.astype(f32)
        n1 = (xs - mean_one) * inverse_one
        e1 = dh1 * take(gain_attn, r, Dl)
        sums = lax.psum(jnp.stack([jnp.sum(e1, axis=-1), jnp.sum(e1 * n1, axis=-1)]), "row") / D
        base = lax.all_to_all(dx_low, "row", split_axis=1, concat_axis=0, tiled=True).astype(f32)
        tokens_grad = (
            base + inverse_one * (e1 - sums[0][:, None] - n1 * sums[1][:, None])
        ).astype(bf16)

    if two:
        query = halved(dt, h1_y, after(to_y(query_send), kept))
        n = F
        act = halved(da, h_act, gate_got[:n])
        lin = halved(du, h_lin, gate_got[n:])
        proj = halved(o_heads, dx_y, proj_got)
        both_got = after(to_z(jnp.concatenate([second(act), second(proj)], axis=0), 1), kept)
        lin = joined(lin, after(to_y(second(lin)), kept))
        act, proj = joined(act, both_got[:n]), joined(proj, both_got[n:])
        both_got = to_z(jnp.concatenate([second(act), second(proj)], axis=0), 2)
        lin = joined(lin, to_z(second(lin), 1))
        act, proj = joined(act, both_got[:n]), joined(proj, both_got[n:])
        lower = joined(lower, lower_got)
        last_got = after(to_row(jnp.concatenate([second(lower), second(proj)], axis=0)), dx)
        lower, proj = joined(lower, last_got[:n]), joined(proj, last_got[n:])
        act = joined(act, to_y(second(act)))
        lin = joined(lin, after(to_z(second(lin), 2), dx))
        gate = jnp.stack([act.T, lin.T])
        query = joined(query, to_z(second(query), 1))
        query = joined(query, after(to_z(second(query), 2), dx)).T
        wq_rows = take(wq, b ^ (4 * r), Db)
        place = (2 * b + r) ^ (8 * r)
        wi_rows = jnp.stack(
            [jnp.where(place < 8, *(take(w, place % 8, Dd) for w in ws)) for ws in after((acts, lins), kept)]
        )
    else:

        def scatter(grad):
            return lax.psum_scatter(grad, ("dp", "row"), scatter_dimension=1, tiled=True).astype(f32)

        gate = jnp.stack([scatter(tn(da, h2).astype(bf16)).T, scatter(tn(du, h2).astype(bf16)).T])
        proj = scatter(tn(o_rows, dx_low).astype(bf16))
        lower = scatter(tn(m, g_low).astype(bf16))
        query = lax.psum_scatter(
            tn(h1, dt).astype(bf16), "dp", scatter_dimension=0, tiled=True
        ).astype(f32)
        wq_rows = take(wq, b, Db)
        wi_rows = jnp.stack([take(acts[0], b * R + r, Dd), take(lins[0], b * R + r, Dd)])

    one_part = jnp.sum(query * wq_rows.astype(f32), axis=1)
    two_part = jnp.sum(jnp.sum(gate * wi_rows.astype(f32), axis=2), axis=0)
    natural = lax.dot_general(
        query, order.astype(f32), (((1,), (1,)), ((), ())),
        precision=lax.Precision.HIGHEST, preferred_element_type=f32,
    )
    if two:
        pair = jnp.concatenate([natural, jnp.broadcast_to(one_part[:, None], (Db, 128))], axis=1)
        pair = pair.reshape(2, Dd, 3 * W + 128)
        mine = lax.dynamic_index_in_dim(pair, r, 0, keepdims=False)
        theirs = to_row(lax.dynamic_index_in_dim(pair, 1 - r, 0, keepdims=False))
        theirs = after(theirs, tokens_grad)
        one_part = mine[:, 3 * W] + theirs[:, 3 * W]
        query_out = ordered(zrow, mine[:, : 3 * W], theirs[:, : 3 * W], 1)
    else:
        one_part = take(lax.psum(one_part, "row"), r, Dd)
        query_out = lax.all_to_all(natural, "row", split_axis=0, concat_axis=1, tiled=True)
    gains = jnp.stack([one_part, two_part])
    gains = gains + to_col(gains) if C == 2 else lax.psum(gains, "col")
    gain_attn_grad = gains[0] / take(gain_attn, b * R + r, Dd)
    gain_mlp_grad = gains[1] / take(gain_mlp, b * R + r, Dd)
    return (
        layer_out,
        tokens_grad,
        gain_attn_grad,
        query_out.reshape(Dd, R * heads, 3 * head_width),
        proj,
        gain_mlp_grad,
        jnp.swapaxes(gate, 0, 1),
        lower,
    )


def solution(mesh):
    return jax.shard_map(
        local,
        mesh=mesh,
        in_specs=(
            P("dp", "row"),
            P(),
            P("row", "col", None),
            P("col", "row"),
            P(),
            P("row", None, "col"),
            P("col", "row"),
            P("dp", "row"),
            P(),
            P(),
            P(),
        ),
        out_specs=(
            P("dp", "row"),
            P("dp", "row"),
            P(("dp", "row")),
            P(("dp", "row"), "col", None),
            P("col", ("dp", "row")),
            P(("dp", "row")),
            P(("dp", "row"), None, "col"),
            P("col", ("dp", "row")),
        ),
        check_vma=False,
    )
```

```python
import functools
import math

import jax
import jax.numpy as jnp
from jax import lax
from jax.experimental import pallas as pl
from jax.experimental.pallas import tpu as pltpu
from jax.sharding import PartitionSpec as P

LONGEST = 1024
BQ = 256
BK = 256
NEG = -1e30
FAR = 1e30
epsilon = 1e-05
rope_base = 160000.0
bf16 = jnp.bfloat16
f32 = jnp.float32
SWAP = [(0, 1), (1, 0)]


def nt(a, b):
    return lax.dot_general(a, b, (((1,), (1,)), ((), ())), preferred_element_type=f32)


def tn(a, b):
    return lax.dot_general(a, b, (((0,), (0,)), ((), ())), preferred_element_type=f32)


def nn(a, b):
    return jnp.dot(a, b, preferred_element_type=f32)


def after(a, *others):
    return lax.optimization_barrier((a, *others))[0]


def half_mask(width, heads, head):
    lane = lax.broadcasted_iota(jnp.int32, (1, width), 1)
    half = width // 2
    lane = jnp.where(lane >= half, lane - half, lane)
    step = half // heads
    return (lane >= head * step) & (lane < (head + 1) * step)


def whole_mask(width, heads, head):
    lane = lax.broadcasted_iota(jnp.int32, (1, width), 1)
    step = width // heads
    return (lane >= head * step) & (lane < (head + 1) * step)


def stack_heads(block, heads, mask_of):
    zero = jnp.zeros_like(block)
    width = block.shape[1]
    return jnp.concatenate(
        [jnp.where(mask_of(width, heads, h), block, zero) for h in range(heads)], axis=0
    )


def same_segment(key_seg, query_seg, heads):
    tile = key_seg
    lanes = query_seg.shape[1]
    if lanes > tile.shape[1]:
        tile = jnp.concatenate([tile] * (lanes // tile.shape[1]), axis=1)
    same = tile == query_seg
    return jnp.concatenate([same] * heads, axis=1) if heads > 1 else same


def forward_kernel(heads, sets, final, bounds, *refs):
    refs = list(refs)
    q_ref, sq_ref = refs[:2]
    kv_refs = refs[2 : 2 + sets]
    sk_refs = refs[2 + sets : 2 + 2 * sets]
    rest = refs[2 + 2 * sets :]
    if final:
        acc_in, ml_in, o_ref, lse_ref = rest[:4]
        acc, m_ref, l_ref = rest[4:7]
        vt_refs = rest[7:]
    else:
        acc, ml_ref = rest[:2]
        m_ref, l_ref = rest[2:4]
        vt_refs = rest[4:]
    step = pl.program_id(0)
    rows, width = q_ref.shape
    each = width // heads

    @pl.when(step == 0)
    def _():
        for kv, vt in zip(kv_refs, vt_refs):
            for j in range(kv.shape[0] // BK):
                vt[:, j * BK : (j + 1) * BK] = kv[j * BK : (j + 1) * BK, width:].T

    if final:
        acc[...] = acc_in[0]
        m_ref[...] = ml_in[0, 0:1]
        l_ref[...] = ml_in[0, 1:2]
    else:
        acc[...] = jnp.zeros_like(acc)
        m_ref[...] = jnp.full_like(m_ref, NEG)
        l_ref[...] = jnp.zeros_like(l_ref)
    queries = stack_heads(q_ref[...], heads, half_mask)
    query_seg = sq_ref[0]
    target = acc if final else acc.at[0]

    for s in range(sets):
        kv, sk, vt = kv_refs[s], sk_refs[s], vt_refs[s]

        def body(j, carry):
            first = pl.multiple_of(j * BK, BK)
            keys = kv[pl.ds(first, BK), 0:width]
            scores = nt(keys, queries)
            same = same_segment(sk[pl.ds(first, BK), :], query_seg, heads)
            scores = jnp.where(same, scores, NEG)
            before = m_ref[...]
            top = jnp.maximum(before, jnp.max(scores, axis=0, keepdims=True))
            raised = jnp.exp(scores - top)
            shrink = jnp.exp(before - top)
            m_ref[...] = top
            l_ref[...] = l_ref[...] * shrink + jnp.sum(raised, axis=0, keepdims=True)
            low = raised.astype(bf16)
            for h in range(heads):
                part = nn(
                    vt[h * each : (h + 1) * each, pl.ds(first, BK)],
                    low[:, h * rows : (h + 1) * rows],
                )
                hold = target[h * each : (h + 1) * each, :]
                target[h * each : (h + 1) * each, :] = (
                    hold * shrink[:, h * rows : (h + 1) * rows] + part
                )
            return carry

        lax.fori_loop(
            bounds[(step * sets + s) * 2], bounds[(step * sets + s) * 2 + 1], body, 0
        )

    if final:
        live = query_seg >= 0
        total = l_ref[...]
        live_all = jnp.concatenate([live] * heads, axis=1) if heads > 1 else live
        total = jnp.where(live_all, total, 1.0)
        inverse = jnp.where(live_all, 1.0 / total, 0.0)
        for h in range(heads):
            acc[h * each : (h + 1) * each, :] = (
                acc[h * each : (h + 1) * each, :] * inverse[:, h * rows : (h + 1) * rows]
            )
        o_ref[...] = acc[...].T.astype(bf16)
        lse_ref[0] = jnp.where(live_all, m_ref[...] + jnp.log(total), FAR)
    else:
        ml_ref[0, 0:1] = m_ref[...]
        ml_ref[0, 1:2] = l_ref[...]


def cost(products, q, kvs):
    pairs = q.shape[0]
    return pl.CostEstimate(
        flops=4 * products * pairs * q.shape[1],
        bytes_accessed=2 * sum(a.size for a in kvs) + 4 * q.size,
        transcendentals=4 * pairs,
    )


def whole(shape):
    zeros = (0,) * len(shape)
    return pl.BlockSpec(shape, lambda i, *_: zeros)


def attend_call(bounds, q, sq, kvs, sks, heads, state=None):
    count = q.shape[0] // BQ
    width = q.shape[1]
    sets = len(kvs)
    final = state is not None
    row_spec = pl.BlockSpec((BQ, width), lambda i, *_: (i, 0))
    acc_spec = pl.BlockSpec((1, width, BQ), lambda i, *_: (i, 0, 0))
    ml_spec = pl.BlockSpec((1, 2, heads * BQ), lambda i, *_: (i, 0, 0))
    in_specs = [row_spec, pl.BlockSpec((1, 1, BQ), lambda i, *_: (i, 0, 0))]
    in_specs += [whole(a.shape) for a in kvs] + [whole(a.shape) for a in sks]
    scratch = [pltpu.VMEM((1, heads * BQ), f32)] * 2
    scratch += [pltpu.VMEM((width, a.shape[0]), bf16) for a in kvs]
    if final:
        in_specs += [acc_spec, ml_spec]
        out_specs = [row_spec, pl.BlockSpec((1, 1, heads * BQ), lambda i, *_: (i, 0, 0))]
        out_shape = [
            jax.ShapeDtypeStruct(q.shape, bf16),
            jax.ShapeDtypeStruct((count, 1, heads * BQ), f32),
        ]
        scratch = [pltpu.VMEM((width, BQ), f32)] + scratch
    else:
        out_specs = [acc_spec, ml_spec]
        out_shape = [
            jax.ShapeDtypeStruct((count, width, BQ), f32),
            jax.ShapeDtypeStruct((count, 2, heads * BQ), f32),
        ]
    return pl.pallas_call(
        functools.partial(forward_kernel, heads, sets, final),
        grid_spec=pltpu.PrefetchScalarGridSpec(
            num_scalar_prefetch=1,
            grid=(count,),
            in_specs=in_specs,
            out_specs=out_specs,
            scratch_shapes=scratch,
        ),
        out_shape=out_shape,
        cost_estimate=cost(4, q, kvs),
        name="attend_final" if final else "attend_own",
    )(bounds, q, sq, *kvs, *sks, *(state or ()))


def backward_kernel(heads, sets, final, bounds, *refs):
    refs = list(refs)
    q_ref, do_ref, o_ref, lse_ref, sq_ref = refs[:5]
    kv_refs = refs[5 : 5 + sets]
    sk_refs = refs[5 + sets : 5 + 2 * sets]
    rest = refs[5 + 2 * sets :]
    if final:
        dq_in, dq_ref = rest[0], rest[1]
        dkv_refs = rest[2 : 2 + sets]
        dq_acc = rest[2 + sets]
        kt_refs = rest[3 + sets : 3 + 2 * sets]
        sums = dkv_refs
    else:
        dq_ref = rest[0]
        dkv_refs = rest[1 : 1 + sets]
        dq_acc = rest[1 + sets]
        kt_refs = rest[2 + sets : 2 + 2 * sets]
        sums = rest[2 + 2 * sets :]
    step = pl.program_id(0)
    rows, width = q_ref.shape
    each = width // heads
    half = width // 2
    piece = half // heads

    @pl.when(step == 0)
    def _():
        for kv, kt, total in zip(kv_refs, kt_refs, sums):
            total[...] = jnp.zeros_like(total)
            for j in range(kv.shape[0] // BK):
                kt[:, j * BK : (j + 1) * BK] = kv[j * BK : (j + 1) * BK, :width].T

    if final:
        dq_acc[...] = dq_in[0]
    else:
        dq_acc[...] = jnp.zeros_like(dq_acc)
    grads = do_ref[...]
    queries = stack_heads(q_ref[...], heads, half_mask)
    outs = stack_heads(grads, heads, whole_mask)
    query_seg = sq_ref[0]
    lse = lse_ref[0]
    product = (grads.astype(f32) * o_ref[...].astype(f32)).T
    delta = jnp.concatenate(
        [
            jnp.sum(product[h * each : (h + 1) * each], axis=0, keepdims=True)
            for h in range(heads)
        ],
        axis=1,
    )

    for s in range(sets):
        kv, sk, kt, total = kv_refs[s], sk_refs[s], kt_refs[s], sums[s]

        def body(j, carry):
            first = pl.multiple_of(j * BK, BK)
            keys = kv[pl.ds(first, BK), 0:width]
            values = kv[pl.ds(first, BK), width : 2 * width]
            scores = nt(keys, queries)
            same = same_segment(sk[pl.ds(first, BK), :], query_seg, heads)
            probs = jnp.where(same, jnp.exp(scores - lse), 0.0)
            grad_probs = nt(values, outs)
            grad_scores = (probs * (grad_probs - delta)).astype(bf16)
            low = probs.astype(bf16)
            total[pl.ds(first, BK), width : 2 * width] += nn(low, outs)
            total[pl.ds(first, BK), 0:width] += nn(grad_scores, queries)
            for h in range(heads):
                column = grad_scores[:, h * rows : (h + 1) * rows]
                for lead in (h * piece, half + h * piece):
                    dq_acc[lead : lead + piece, :] += nn(
                        kt[lead : lead + piece, pl.ds(first, BK)], column
                    )
            return carry

        lax.fori_loop(
            bounds[(step * sets + s) * 2], bounds[(step * sets + s) * 2 + 1], body, 0
        )

    if final:
        dq_ref[...] = dq_acc[...].T
    else:
        dq_ref[0] = dq_acc[...]

        @pl.when(step == pl.num_programs(0) - 1)
        def _():
            for total, out in zip(sums, dkv_refs):
                out[...] = total[...].astype(bf16)


def attend_back_call(bounds, q, do, o, lse, sq, kvs, sks, heads, state=None):
    count = q.shape[0] // BQ
    width = q.shape[1]
    sets = len(kvs)
    final = state is not None
    row_spec = pl.BlockSpec((BQ, width), lambda i, *_: (i, 0))
    acc_spec = pl.BlockSpec((1, width, BQ), lambda i, *_: (i, 0, 0))
    in_specs = [row_spec] * 3 + [
        pl.BlockSpec((1, 1, heads * BQ), lambda i, *_: (i, 0, 0)),
        pl.BlockSpec((1, 1, BQ), lambda i, *_: (i, 0, 0)),
    ]
    in_specs += [whole(a.shape) for a in kvs] + [whole(a.shape) for a in sks]
    scratch = [pltpu.VMEM((width, BQ), f32)]
    scratch += [pltpu.VMEM((width, a.shape[0]), bf16) for a in kvs]
    if final:
        in_specs += [acc_spec]
        out_specs = [row_spec]
        out_shape = [jax.ShapeDtypeStruct(q.shape, f32)]
    else:
        out_specs = [acc_spec]
        out_shape = [jax.ShapeDtypeStruct((count, width, BQ), f32)]
        scratch += [pltpu.VMEM(a.shape, f32) for a in kvs]
    out_specs += [whole(a.shape) for a in kvs]
    out_shape += [jax.ShapeDtypeStruct(a.shape, f32 if final else bf16) for a in kvs]
    return pl.pallas_call(
        functools.partial(backward_kernel, heads, sets, final),
        grid_spec=pltpu.PrefetchScalarGridSpec(
            num_scalar_prefetch=1,
            grid=(count,),
            in_specs=in_specs,
            out_specs=out_specs,
            scratch_shapes=scratch,
        ),
        out_shape=out_shape,
        cost_estimate=cost(10, q, kvs),
        name="back_own" if final else "back_halo",
    )(bounds, q, do, o, lse, sq, *kvs, *sks, *(state or ()))


def place_tables(seq_lengths, seq_offsets, first, count):
    place = first + jnp.arange(count, dtype=jnp.int32)
    ends = seq_offsets + seq_lengths
    inside = (place[:, None] >= seq_offsets[None, :]) & (place[:, None] < ends[None, :])
    live = jnp.any(inside, axis=1)
    index = jnp.arange(seq_offsets.shape[0], dtype=jnp.int32)
    segment = jnp.sum(jnp.where(inside, index[None, :], 0), axis=1)
    start = jnp.sum(jnp.where(inside, seq_offsets[None, :], 0), axis=1)
    end = jnp.sum(jnp.where(inside, ends[None, :], 0), axis=1)
    return live, segment, start, end, place


def qkv_order(heads, head_width):
    width = heads * head_width
    half = head_width // 2
    new = jnp.arange(3 * width, dtype=jnp.int32)
    kind = new // width
    inner = new % width
    side = inner // (width // 2)
    pair_head = (inner % (width // 2)) // half
    pair_old = pair_head * 3 * head_width + kind * head_width + side * half + inner % half
    value_old = (inner // head_width) * 3 * head_width + 2 * head_width + inner % head_width
    old = jnp.where(kind == 2, value_old, pair_old)
    return (old[None, :] == new[:, None]).astype(bf16)


def local(
    tokens,
    gain_attn,
    w_qkv,
    w_out,
    gain_mlp,
    w_in,
    w_down,
    cotangent,
    seq_lengths,
    seq_offsets,
    deal,
):
    R, C, B = lax.axis_size("row"), lax.axis_size("col"), lax.axis_size("dp")
    r, c, b = lax.axis_index("row"), lax.axis_index("col"), lax.axis_index("dp")
    S, Dl = tokens.shape
    D = Dl * R
    two = R == 2 and C == 2 and B == 8
    heads = w_qkv.shape[1] // R
    head_width = w_qkv.shape[2] // 3
    W = heads * head_width
    F = w_down.shape[0]
    H = LONGEST
    Sr = S // R
    zrow, zcol = (r == 0), (c == 0)

    def to_row(a):
        return lax.ppermute(a, "row", SWAP)

    def to_col(a):
        return lax.ppermute(a, "col", SWAP)

    def ordered(flag, mine, theirs, axis):
        return jnp.where(
            flag,
            jnp.concatenate([mine, theirs], axis=axis),
            jnp.concatenate([theirs, mine], axis=axis),
        )

    def own_first(a, axis):
        if not two:
            return a
        n = a.shape[axis] // 2
        return jnp.where(zrow, a, jnp.roll(a, n, axis=axis))

    def take(a, index, size, axis=0):
        return lax.dynamic_slice_in_dim(a, index * size, size, axis)

    def partner(a):
        n = a.shape[0] // 2
        got = to_row(take(a, c, n))
        return ordered(zcol, got, to_col(got), 0)

    def gather(a, axis):
        if two:
            return jnp.concatenate([a, to_row(a)], axis=axis)
        return lax.all_gather(a, "row", axis=axis, tiled=True)

    def col_sum(a):
        return a + to_col(a.astype(bf16)).astype(f32) if C == 2 else lax.psum(a, "col")

    live_x, seg_x, start_x, end_x, place_x = place_tables(seq_lengths, seq_offsets, b * S - H, S + 2 * H)
    key_seg = jnp.broadcast_to(jnp.where(live_x, seg_x, -2)[:, None], (S + 2 * H, 128))
    sk_left, sk_own, sk_right = key_seg[:H], key_seg[H : H + S], key_seg[H + S :]
    live = live_x[H : H + S]
    nq = S // BQ
    sq = jnp.where(live, seg_x[H : H + S], -1).reshape(nq, 1, BQ)
    first = jnp.min(jnp.where(live, start_x[H : H + S] - b * S, 4 * S).reshape(nq, BQ), axis=1)
    last = jnp.max(jnp.where(live, end_x[H : H + S] - b * S, -4 * S).reshape(nq, BQ), axis=1)
    own_low = jnp.clip(first, 0, S) // BK
    own_high = (jnp.clip(last, 0, S) + BK - 1) // BK
    left_low = jnp.clip(first + H, 0, H) // BK
    right_high = (jnp.clip(last - S, 0, H) + BK - 1) // BK
    own_bounds = jnp.stack([own_low, own_high], axis=1).reshape(-1).astype(jnp.int32)
    zero = jnp.zeros_like(left_low)
    halo_bounds = (
        jnp.stack([left_low, zero + H // BK, zero, right_high], axis=1).reshape(-1).astype(jnp.int32)
    )
    position = jnp.where(live, place_x[H : H + S] - start_x[H : H + S], 0)
    freq = rope_base ** (-(jnp.arange(0, head_width, 2, dtype=f32) / head_width))
    angle = position.astype(f32)[:, None] * jnp.tile(freq, heads)[None, :]
    cosine, sine = lax.optimization_barrier((jnp.cos(angle), jnp.sin(angle)))

    live_column = live[:, None]
    if two:
        x_got = partner(tokens)
        x_low = jnp.where(live_column, jnp.concatenate([tokens, x_got], axis=1), 0)
    else:
        own_x = jnp.where(live_column, tokens, 0)
        x_low = lax.all_gather(own_x, "row", axis=1, tiled=True)

    wq_low = w_qkv.reshape(Dl, R * 3 * W).astype(bf16)
    if two:
        wq_mine, wq_send = take(wq_low, r, 3 * W, 1), take(wq_low, 1 - r, 3 * W, 1)
        wq_got = to_row(wq_send)
    else:
        wq = lax.all_to_all(wq_low, "row", split_axis=1, concat_axis=0, tiled=True)
    order = qkv_order(heads, head_width)

    gain_one = own_first(gain_attn, 0)
    gain_two = own_first(gain_mlp, 0)

    Db = D // B
    Dd = D // (B * R)
    if two:
        y_bit, z_bits = b % 2, b // 2

        def relative(a, bits):
            n = jnp.arange(D, dtype=jnp.int32)
            rel = {"w": 0 * n, "x": 0 * n}
            for i, bit in enumerate(bits):
                rel[bit] = n // (D >> (i + 1)) % 2
            z_rel = 2 * rel["Z"] + rel["z"]
            column = ((z_bits ^ z_rel) * 2 + (y_bit ^ rel["y"])) * Db + n % Dd
            column = column + (rel["w"] if "w" in bits else r ^ rel["x"]) * Dd
            column = column ^ (r * (D // 2))
            return nn(a, (n[:, None] == column[None, :]).astype(bf16)).astype(bf16)

        def to_y(a):
            return lax.ppermute(a, "dp", [(i, i ^ 1) for i in range(B)])

        def to_z(a, j):
            return lax.ppermute(a, "dp", [(i, i ^ (2 * j)) for i in range(B)])

        def first(a):
            return a[:, : a.shape[1] // 2]

        def second(a):
            return a[:, a.shape[1] // 2 :].astype(bf16)

        def product(left, right):
            return tn(left, second(right)).astype(bf16)

        def halved(left, right, got):
            return tn(left, first(right)) + got.astype(f32)

        def joined(part, got):
            return first(part).astype(f32) + got.astype(f32)

    x = x_low.astype(f32)
    center = x - jnp.mean(x, axis=-1, keepdims=True)
    inverse_one = lax.rsqrt(jnp.mean(center * center, axis=-1, keepdims=True) + epsilon)
    mean_one = jnp.mean(x, axis=-1, keepdims=True)
    h1 = (center * inverse_one * gain_one).astype(bf16)
    if two:
        h1, wq_mine, wq_got = lax.optimization_barrier((h1, wq_mine, wq_got))
        wq = jnp.concatenate([wq_mine, wq_got], axis=0)
    wq = nn(wq, order).astype(bf16)

    half = W // 2

    def turn(t, sign):
        first_half, second_half = t[:, :half], t[:, half:]
        s = sine * sign
        return jnp.concatenate(
            [first_half * cosine - second_half * s, second_half * cosine + first_half * s], axis=1
        )

    kv_raw = nn(h1, wq[:, W:])
    kv = jnp.concatenate([turn(kv_raw[:, :W], 1.0), kv_raw[:, W:]], axis=1).astype(bf16)
    up = [(i, i + 1) for i in range(B - 1)]
    down = [(i + 1, i) for i in range(B - 1)]
    kv_left = lax.ppermute(kv[S - H :], "dp", up)
    kv_right = lax.ppermute(kv[:H], "dp", down)
    q = (turn(nn(h1, wq[:, :W]), 1.0) * (1.0 / math.sqrt(head_width))).astype(bf16)
    wo_low = w_out.astype(bf16)
    w_in_late, w_down_late = after((w_in, w_down), kv)
    wd_low = w_down_late.astype(bf16)
    act_low, lin_low = w_in_late[:, 0].astype(bf16), w_in_late[:, 1].astype(bf16)
    if two:
        even = (b // 2) % 2 == 0
        in_send, wo_send, g_send = after(
            (
                lax.dynamic_index_in_dim(w_in, (b // 2) % 2, 1, keepdims=False).astype(bf16),
                wo_low,
                take(cotangent, 2 * (1 - r) + c, Sr // 2),
            ),
            cosine,
            wq_send,
        )
        in_got, wo_got, g_got = to_row(in_send), to_row(wo_send), to_row(g_send)
        wd_half = take(wd_low, (b // 2) % 2, F // 2)
        h1_y = relative(after(h1, kv), "yzZw")
        q, h1_y, sk_left, sk_right, act_low, lin_low, wd_half = lax.optimization_barrier(
            (q, h1_y, sk_left, sk_right, act_low, lin_low, wd_half)
        )

    state = attend_call(own_bounds, q, sq, [kv], [sk_own], heads)
    if two:
        kv_left, kv_right, in_got, wo_got, g_got, wd_half = after(
            (kv_left, kv_right, in_got, wo_got, g_got, wd_half), state
        )
        in_other, wd_got = to_z(in_got, 1), to_row(wd_half)
    o, lse = attend_call(
        halo_bounds, q, sq, [kv_left, kv_right], [sk_left, sk_right], heads, state
    )

    if two:
        o, wd_got, wo_got, g_got = lax.optimization_barrier((o, wd_got, wo_got, g_got))
        wo = own_first(jnp.concatenate([wo_low, wo_got], axis=1), 0)
    else:
        wo = gather(wo_low, 1)

    if two:
        o_got = to_row(take(o, 1 - r, Sr))
        o_rows = jnp.concatenate([take(o, r, Sr), o_got], axis=1)
        wd_other = to_z(wd_got, 1)
        wd_got = ordered(even, wd_got, wd_other, 0)
        g_got = ordered(zcol, g_got, to_col(g_got), 0)
        g_low = jnp.concatenate([take(cotangent, r, Sr), g_got], axis=1)
        g_low = jnp.where(take(live, r, Sr)[:, None], g_low, 0)
        wds = [wd_low, wd_got]
    else:
        o_rows = lax.all_to_all(o, "row", split_axis=0, concat_axis=1, tiled=True)
        own_g = jnp.where(live_column, cotangent, 0)
        g_low = lax.all_to_all(own_g, "row", split_axis=0, concat_axis=1, tiled=True)
        wds, acts, lins = [gather(wd_low, 1)], [gather(act_low, 0)], [gather(lin_low, 0)]

    def split_nn(a, parts):
        n = a.shape[1] // len(parts)
        return sum(nn(a[:, i * n : (i + 1) * n], w) for i, w in enumerate(parts))

    def split_nt(a, parts):
        n = a.shape[1] // len(parts)
        return sum(nt(a[:, i * n : (i + 1) * n], w) for i, w in enumerate(parts))

    def wide(parts):
        return parts[0] if len(parts) == 1 else jnp.concatenate(parts, axis=1)

    x_rows = take(x_low, r, Sr).astype(f32)
    if C == 2:
        o_all = jnp.concatenate([o_rows, to_col(o_rows)], axis=1)
        wo_all = jnp.concatenate([wo, to_col(wo)], axis=0)
        x1 = x_rows + nn(o_all, wo_all)
    else:
        x1 = x_rows + lax.psum(nn(o_rows, wo), "col")
    if two:
        in_got, in_other = after((in_got, in_other), o_got)
        act_got, lin_got = jnp.where(even, in_got, in_other), jnp.where(even, in_other, in_got)
        acts, lins = [act_low, act_got], [lin_low, lin_got]

    center = x1 - jnp.mean(x1, axis=-1, keepdims=True)
    inverse_two = lax.rsqrt(jnp.mean(center * center, axis=-1, keepdims=True) + epsilon)
    n2 = center * inverse_two
    h2 = (n2 * gain_two).astype(bf16)
    a = split_nn(h2, acts)
    u = split_nn(h2, lins)
    phi = 0.5 + 0.5 * lax.erf(a * math.sqrt(0.5))
    gelu = a * phi
    slope = phi + a * jnp.exp(-0.5 * a * a) * (1.0 / math.sqrt(2.0 * math.pi))
    m = (gelu * u).astype(bf16)
    y_part = wide([nn(m, w) for w in wds])
    if two:
        n = Sr // 2
        y_half = (
            take(x1, c, n) + take(y_part, c, n) + to_col(take(y_part, 1 - c, n).astype(bf16)).astype(f32)
        ).astype(bf16)
        y_got = to_row(y_half[:, Dl:])
    else:
        y = (x1 + col_sum(y_part)).astype(bf16)
        layer_out = lax.all_to_all(y, "row", split_axis=1, concat_axis=0, tiled=True)

    dm = split_nt(g_low, wds)
    da = (dm * u * slope).astype(bf16)
    du = (dm * gelu).astype(bf16)
    dh2_part = wide([nt(da, v) + nt(du, w) for v, w in zip(acts, lins)])
    dh2 = col_sum(dh2_part)
    if two:
        g_y = relative(after(g_low, dh2_part), "yzZx")
        lower_got = to_y(product(m, g_y))
    e2 = dh2 * gain_two
    dx1 = g_low.astype(f32) + inverse_two * (
        e2
        - jnp.mean(e2, axis=-1, keepdims=True)
        - n2 * jnp.mean(e2 * n2, axis=-1, keepdims=True)
    )
    dx_low = dx1.astype(bf16)
    do_rows = nt(dx_low, wo).astype(bf16)
    if two:
        do_got = to_row(do_rows[:, W:])
        do = ordered(zrow, do_rows[:, :W], do_got, 0)
    else:
        do = lax.all_to_all(do_rows, "row", split_axis=1, concat_axis=0, tiled=True)

    if two:
        h2, da, du, o_heads, dx_late = after((h2, da, du, own_first(o_rows, 1), dx_low), do_rows)
        dx_y = relative(dx_late, "yzZx")
        h_act, h_lin = relative(h2, "xzZy"), relative(h2, "xyzZ")
        proj_got = to_y(product(o_heads, dx_y))
        gate_send = jnp.concatenate([product(da, h_act), product(du, h_lin)], axis=0)
        gate_got = to_row(after(gate_send, do_got))
        pair = ordered(zrow, y_half[None, :, :Dl], after(y_got, gate_send)[None], 0)
        layer_out = ordered(zcol, pair[:, None], to_col(pair)[:, None], 1).reshape(S, Dl)
        lower = halved(m, g_y, after(lower_got, gate_send))
        lower_got = to_z(second(lower), 1)
        do, lower, layer_out = lax.optimization_barrier((do, lower, layer_out))

    dq_part, dkv_left, dkv_right = attend_back_call(
        halo_bounds, q, do, o, lse, sq, [kv_left, kv_right], [sk_left, sk_right], heads
    )
    from_right = lax.ppermute(dkv_left, "dp", down)
    from_left = lax.ppermute(dkv_right, "dp", up)
    if two:
        lower = joined(lower, after(lower_got, dq_part))
        lower_got = to_z(second(lower), 2)
        dq_part, lower = lax.optimization_barrier((dq_part, lower))
    dq, dkv = attend_back_call(own_bounds, q, do, o, lse, sq, [kv], [sk_own], heads, [dq_part])
    if two:
        dkv, from_right, from_left, gate_got, proj_got, lower_got = lax.optimization_barrier(
            (dkv, from_right, from_left, gate_got, proj_got, lower_got)
        )
    pad = jnp.zeros((S - H, 2 * W), bf16)
    dkv = (
        dkv
        + jnp.concatenate([pad, from_right], axis=0).astype(f32)
        + jnp.concatenate([from_left, pad], axis=0).astype(f32)
    )
    dq = turn(dq * (1.0 / math.sqrt(head_width)), -1.0)
    dt = jnp.concatenate([dq, turn(dkv[:, :W], -1.0), dkv[:, W:]], axis=1).astype(bf16)
    dh1_part = nt(dt, wq)
    if two:
        query_send = product(dt, h1_y)
        gate_got, proj_got, lower_got = after((gate_got, proj_got, lower_got), query_send, dh1_part)

    if two:
        n = S // 2
        kept = take(dh1_part, c, n) + to_col(take(dh1_part, 1 - c, n).astype(bf16)).astype(f32)
        xs = take(x_low, c, n).astype(f32)
        inv, mean = take(inverse_one, c, n), take(mean_one, c, n)
        n1 = (xs - mean) * inv
        e1 = kept * gain_one
        sums = jnp.stack([jnp.sum(e1, axis=-1), jnp.sum(e1 * n1, axis=-1)])
        sums = (sums + to_row(sums)) * (1.0 / D)
        moved = lax.ppermute(after(dx_low[:, Dl:], from_left), ("row", "col"), [(0, 2), (3, 1)])
        kept_send, moved = lax.optimization_barrier((kept[:, Dl:].astype(bf16), moved))
        mine = (kept[:, :Dl] + to_row(kept_send).astype(f32)) * gain_one[:Dl]
        base = jnp.where(r == c, dx1[:, :Dl], moved.astype(f32))
        dx = base + inv * (mine - sums[0][:, None] - n1[:, :Dl] * sums[1][:, None])
        dx = dx.astype(bf16)
        tokens_grad = ordered(zcol, dx, to_col(dx), 0)
    else:
        dh1 = lax.psum_scatter(col_sum(dh1_part), "row", scatter_dimension=1, tiled=True)
        xs = own_x.astype(f32)
        n1 = (xs - mean_one) * inverse_one
        e1 = dh1 * take(gain_attn, r, Dl)
        sums = lax.psum(jnp.stack([jnp.sum(e1, axis=-1), jnp.sum(e1 * n1, axis=-1)]), "row") / D
        base = lax.all_to_all(dx_low, "row", split_axis=1, concat_axis=0, tiled=True).astype(f32)
        tokens_grad = (
            base + inverse_one * (e1 - sums[0][:, None] - n1 * sums[1][:, None])
        ).astype(bf16)

    if two:
        query = halved(dt, h1_y, after(to_y(query_send), kept))
        n = F
        act = halved(da, h_act, gate_got[:n])
        lin = halved(du, h_lin, gate_got[n:])
        proj = halved(o_heads, dx_y, proj_got)
        both_got = after(to_z(jnp.concatenate([second(act), second(proj)], axis=0), 1), kept)
        lin = joined(lin, after(to_y(second(lin)), kept))
        act, proj = joined(act, both_got[:n]), joined(proj, both_got[n:])
        both_got = to_z(jnp.concatenate([second(act), second(proj)], axis=0), 2)
        lin = joined(lin, to_z(second(lin), 1))
        act, proj = joined(act, both_got[:n]), joined(proj, both_got[n:])
        lower = joined(lower, lower_got)
        last_got = after(to_row(jnp.concatenate([second(lower), second(proj)], axis=0)), dx)
        lower, proj = joined(lower, last_got[:n]), joined(proj, last_got[n:])
        act = joined(act, to_y(second(act)))
        lin = joined(lin, after(to_z(second(lin), 2), dx))
        gate = jnp.stack([act.T, lin.T])
        query = joined(query, to_z(second(query), 1))
        query = joined(query, after(to_z(second(query), 2), dx)).T
        wq_rows = take(wq, b ^ (4 * r), Db)
        place = (2 * b + r) ^ (8 * r)
        wi_rows = jnp.stack(
            [jnp.where(place < 8, *(take(w, place % 8, Dd) for w in ws)) for ws in after((acts, lins), kept)]
        )
    else:

        def scatter(grad):
            return lax.psum_scatter(grad, ("dp", "row"), scatter_dimension=1, tiled=True).astype(f32)

        gate = jnp.stack([scatter(tn(da, h2).astype(bf16)).T, scatter(tn(du, h2).astype(bf16)).T])
        proj = scatter(tn(o_rows, dx_low).astype(bf16))
        lower = scatter(tn(m, g_low).astype(bf16))
        query = lax.psum_scatter(
            tn(h1, dt).astype(bf16), "dp", scatter_dimension=0, tiled=True
        ).astype(f32)
        wq_rows = take(wq, b, Db)
        wi_rows = jnp.stack([take(acts[0], b * R + r, Dd), take(lins[0], b * R + r, Dd)])

    one_part = jnp.sum(query * wq_rows.astype(f32), axis=1)
    two_part = jnp.sum(jnp.sum(gate * wi_rows.astype(f32), axis=2), axis=0)
    natural = lax.dot_general(
        query, order.astype(f32), (((1,), (1,)), ((), ())),
        precision=lax.Precision.HIGHEST, preferred_element_type=f32,
    )
    if two:
        pair = jnp.concatenate([natural, jnp.broadcast_to(one_part[:, None], (Db, 128))], axis=1)
        pair = pair.reshape(2, Dd, 3 * W + 128)
        mine = lax.dynamic_index_in_dim(pair, r, 0, keepdims=False)
        theirs = to_row(lax.dynamic_index_in_dim(pair, 1 - r, 0, keepdims=False))
        theirs = after(theirs, tokens_grad)
        one_part = mine[:, 3 * W] + theirs[:, 3 * W]
        query_out = ordered(zrow, mine[:, : 3 * W], theirs[:, : 3 * W], 1)
    else:
        one_part = take(lax.psum(one_part, "row"), r, Dd)
        query_out = lax.all_to_all(natural, "row", split_axis=0, concat_axis=1, tiled=True)
    gains = jnp.stack([one_part, two_part])
    gains = gains + to_col(gains) if C == 2 else lax.psum(gains, "col")
    gain_attn_grad = gains[0] / take(gain_attn, b * R + r, Dd)
    gain_mlp_grad = gains[1] / take(gain_mlp, b * R + r, Dd)
    return (
        layer_out,
        tokens_grad,
        gain_attn_grad,
        query_out.reshape(Dd, R * heads, 3 * head_width),
        proj,
        gain_mlp_grad,
        jnp.swapaxes(gate, 0, 1),
        lower,
    )


def solution(mesh):
    return jax.shard_map(
        local,
        mesh=mesh,
        in_specs=(
            P("dp", "row"),
            P(),
            P("row", "col", None),
            P("col", "row"),
            P(),
            P("row", None, "col"),
            P("col", "row"),
            P("dp", "row"),
            P(),
            P(),
            P(),
        ),
        out_specs=(
            P("dp", "row"),
            P("dp", "row"),
            P(("dp", "row")),
            P(("dp", "row"), "col", None),
            P("col", ("dp", "row")),
            P(("dp", "row")),
            P(("dp", "row"), None, "col"),
            P("col", ("dp", "row")),
        ),
        check_vma=False,
    )
```

```python
import functools
import math

import jax
import jax.numpy as jnp
from jax import lax
from jax.experimental import pallas as pl
from jax.experimental.pallas import tpu as pltpu
from jax.sharding import PartitionSpec as P

LONGEST = 1024
BQ = 256
BK = 256
NEG = -1e30
FAR = 1e30
epsilon = 1e-05
rope_base = 160000.0
bf16 = jnp.bfloat16
f32 = jnp.float32
SWAP = [(0, 1), (1, 0)]


def nt(a, b):
    return lax.dot_general(a, b, (((1,), (1,)), ((), ())), preferred_element_type=f32)


def tn(a, b):
    return lax.dot_general(a, b, (((0,), (0,)), ((), ())), preferred_element_type=f32)


def nn(a, b):
    return jnp.dot(a, b, preferred_element_type=f32)


def after(a, *others):
    return lax.optimization_barrier((a, *others))[0]


def half_mask(width, heads, head):
    lane = lax.broadcasted_iota(jnp.int32, (1, width), 1)
    half = width // 2
    lane = jnp.where(lane >= half, lane - half, lane)
    step = half // heads
    return (lane >= head * step) & (lane < (head + 1) * step)


def whole_mask(width, heads, head):
    lane = lax.broadcasted_iota(jnp.int32, (1, width), 1)
    step = width // heads
    return (lane >= head * step) & (lane < (head + 1) * step)


def stack_heads(block, heads, mask_of):
    zero = jnp.zeros_like(block)
    width = block.shape[1]
    return jnp.concatenate(
        [jnp.where(mask_of(width, heads, h), block, zero) for h in range(heads)], axis=0
    )


def same_segment(key_seg, query_seg, heads):
    tile = key_seg
    lanes = query_seg.shape[1]
    if lanes > tile.shape[1]:
        tile = jnp.concatenate([tile] * (lanes // tile.shape[1]), axis=1)
    same = tile == query_seg
    return jnp.concatenate([same] * heads, axis=1) if heads > 1 else same


def forward_kernel(heads, sets, final, bounds, *refs):
    refs = list(refs)
    q_ref, sq_ref = refs[:2]
    kv_refs = refs[2 : 2 + sets]
    sk_refs = refs[2 + sets : 2 + 2 * sets]
    rest = refs[2 + 2 * sets :]
    if final:
        acc_in, ml_in, o_ref, lse_ref = rest[:4]
        acc, m_ref, l_ref = rest[4:7]
        vt_refs = rest[7:]
    else:
        acc, ml_ref = rest[:2]
        m_ref, l_ref = rest[2:4]
        vt_refs = rest[4:]
    step = pl.program_id(0)
    rows, width = q_ref.shape
    each = width // heads

    @pl.when(step == 0)
    def _():
        for kv, vt in zip(kv_refs, vt_refs):
            for j in range(kv.shape[0] // BK):
                vt[:, j * BK : (j + 1) * BK] = kv[j * BK : (j + 1) * BK, width:].T

    if final:
        acc[...] = acc_in[0]
        m_ref[...] = ml_in[0, 0:1]
        l_ref[...] = ml_in[0, 1:2]
    else:
        acc[...] = jnp.zeros_like(acc)
        m_ref[...] = jnp.full_like(m_ref, NEG)
        l_ref[...] = jnp.zeros_like(l_ref)
    queries = stack_heads(q_ref[...], heads, half_mask)
    query_seg = sq_ref[0]
    target = acc if final else acc.at[0]

    for s in range(sets):
        kv, sk, vt = kv_refs[s], sk_refs[s], vt_refs[s]

        def body(j, carry):
            first = pl.multiple_of(j * BK, BK)
            keys = kv[pl.ds(first, BK), 0:width]
            scores = nt(keys, queries)
            same = same_segment(sk[pl.ds(first, BK), :], query_seg, heads)
            scores = jnp.where(same, scores, NEG)
            before = m_ref[...]
            top = jnp.maximum(before, jnp.max(scores, axis=0, keepdims=True))
            raised = jnp.exp(scores - top)
            shrink = jnp.exp(before - top)
            m_ref[...] = top
            l_ref[...] = l_ref[...] * shrink + jnp.sum(raised, axis=0, keepdims=True)
            low = raised.astype(bf16)
            for h in range(heads):
                part = nn(
                    vt[h * each : (h + 1) * each, pl.ds(first, BK)],
                    low[:, h * rows : (h + 1) * rows],
                )
                hold = target[h * each : (h + 1) * each, :]
                target[h * each : (h + 1) * each, :] = (
                    hold * shrink[:, h * rows : (h + 1) * rows] + part
                )
            return carry

        lax.fori_loop(
            bounds[(step * sets + s) * 2], bounds[(step * sets + s) * 2 + 1], body, 0
        )

    if final:
        live = query_seg >= 0
        total = l_ref[...]
        live_all = jnp.concatenate([live] * heads, axis=1) if heads > 1 else live
        total = jnp.where(live_all, total, 1.0)
        inverse = jnp.where(live_all, 1.0 / total, 0.0)
        for h in range(heads):
            acc[h * each : (h + 1) * each, :] = (
                acc[h * each : (h + 1) * each, :] * inverse[:, h * rows : (h + 1) * rows]
            )
        o_ref[...] = acc[...].T.astype(bf16)
        lse_ref[0] = jnp.where(live_all, m_ref[...] + jnp.log(total), FAR)
    else:
        ml_ref[0, 0:1] = m_ref[...]
        ml_ref[0, 1:2] = l_ref[...]


def cost(products, q, kvs):
    pairs = q.shape[0]
    return pl.CostEstimate(
        flops=4 * products * pairs * q.shape[1],
        bytes_accessed=2 * sum(a.size for a in kvs) + 4 * q.size,
        transcendentals=4 * pairs,
    )


def whole(shape):
    zeros = (0,) * len(shape)
    return pl.BlockSpec(shape, lambda i, *_: zeros)


def attend_call(bounds, q, sq, kvs, sks, heads, state=None):
    count = q.shape[0] // BQ
    width = q.shape[1]
    sets = len(kvs)
    final = state is not None
    row_spec = pl.BlockSpec((BQ, width), lambda i, *_: (i, 0))
    acc_spec = pl.BlockSpec((1, width, BQ), lambda i, *_: (i, 0, 0))
    ml_spec = pl.BlockSpec((1, 2, heads * BQ), lambda i, *_: (i, 0, 0))
    in_specs = [row_spec, pl.BlockSpec((1, 1, BQ), lambda i, *_: (i, 0, 0))]
    in_specs += [whole(a.shape) for a in kvs] + [whole(a.shape) for a in sks]
    scratch = [pltpu.VMEM((1, heads * BQ), f32)] * 2
    scratch += [pltpu.VMEM((width, a.shape[0]), bf16) for a in kvs]
    if final:
        in_specs += [acc_spec, ml_spec]
        out_specs = [row_spec, pl.BlockSpec((1, 1, heads * BQ), lambda i, *_: (i, 0, 0))]
        out_shape = [
            jax.ShapeDtypeStruct(q.shape, bf16),
            jax.ShapeDtypeStruct((count, 1, heads * BQ), f32),
        ]
        scratch = [pltpu.VMEM((width, BQ), f32)] + scratch
    else:
        out_specs = [acc_spec, ml_spec]
        out_shape = [
            jax.ShapeDtypeStruct((count, width, BQ), f32),
            jax.ShapeDtypeStruct((count, 2, heads * BQ), f32),
        ]
    return pl.pallas_call(
        functools.partial(forward_kernel, heads, sets, final),
        grid_spec=pltpu.PrefetchScalarGridSpec(
            num_scalar_prefetch=1,
            grid=(count,),
            in_specs=in_specs,
            out_specs=out_specs,
            scratch_shapes=scratch,
        ),
        out_shape=out_shape,
        cost_estimate=cost(4, q, kvs),
        name="attend_final" if final else "attend_own",
    )(bounds, q, sq, *kvs, *sks, *(state or ()))


def backward_kernel(heads, sets, final, bounds, *refs):
    refs = list(refs)
    q_ref, do_ref, o_ref, lse_ref, sq_ref = refs[:5]
    kv_refs = refs[5 : 5 + sets]
    sk_refs = refs[5 + sets : 5 + 2 * sets]
    rest = refs[5 + 2 * sets :]
    if final:
        dq_in, dq_ref = rest[0], rest[1]
        dkv_refs = rest[2 : 2 + sets]
        dq_acc = rest[2 + sets]
        kt_refs = rest[3 + sets : 3 + 2 * sets]
        sums = dkv_refs
    else:
        dq_ref = rest[0]
        dkv_refs = rest[1 : 1 + sets]
        dq_acc = rest[1 + sets]
        kt_refs = rest[2 + sets : 2 + 2 * sets]
        sums = rest[2 + 2 * sets :]
    step = pl.program_id(0)
    rows, width = q_ref.shape
    each = width // heads
    half = width // 2
    piece = half // heads

    @pl.when(step == 0)
    def _():
        for kv, kt, total in zip(kv_refs, kt_refs, sums):
            total[...] = jnp.zeros_like(total)
            for j in range(kv.shape[0] // BK):
                kt[:, j * BK : (j + 1) * BK] = kv[j * BK : (j + 1) * BK, :width].T

    if final:
        dq_acc[...] = dq_in[0]
    else:
        dq_acc[...] = jnp.zeros_like(dq_acc)
    grads = do_ref[...]
    queries = stack_heads(q_ref[...], heads, half_mask)
    outs = stack_heads(grads, heads, whole_mask)
    query_seg = sq_ref[0]
    lse = lse_ref[0]
    product = (grads.astype(f32) * o_ref[...].astype(f32)).T
    delta = jnp.concatenate(
        [
            jnp.sum(product[h * each : (h + 1) * each], axis=0, keepdims=True)
            for h in range(heads)
        ],
        axis=1,
    )

    for s in range(sets):
        kv, sk, kt, total = kv_refs[s], sk_refs[s], kt_refs[s], sums[s]

        def body(j, carry):
            first = pl.multiple_of(j * BK, BK)
            keys = kv[pl.ds(first, BK), 0:width]
            values = kv[pl.ds(first, BK), width : 2 * width]
            scores = nt(keys, queries)
            same = same_segment(sk[pl.ds(first, BK), :], query_seg, heads)
            probs = jnp.where(same, jnp.exp(scores - lse), 0.0)
            grad_probs = nt(values, outs)
            grad_scores = (probs * (grad_probs - delta)).astype(bf16)
            low = probs.astype(bf16)
            total[pl.ds(first, BK), width : 2 * width] += nn(low, outs)
            total[pl.ds(first, BK), 0:width] += nn(grad_scores, queries)
            for h in range(heads):
                column = grad_scores[:, h * rows : (h + 1) * rows]
                for lead in (h * piece, half + h * piece):
                    dq_acc[lead : lead + piece, :] += nn(
                        kt[lead : lead + piece, pl.ds(first, BK)], column
                    )
            return carry

        lax.fori_loop(
            bounds[(step * sets + s) * 2], bounds[(step * sets + s) * 2 + 1], body, 0
        )

    if final:
        dq_ref[...] = dq_acc[...].T
    else:
        dq_ref[0] = dq_acc[...]

        @pl.when(step == pl.num_programs(0) - 1)
        def _():
            for total, out in zip(sums, dkv_refs):
                out[...] = total[...].astype(bf16)


def attend_back_call(bounds, q, do, o, lse, sq, kvs, sks, heads, state=None):
    count = q.shape[0] // BQ
    width = q.shape[1]
    sets = len(kvs)
    final = state is not None
    row_spec = pl.BlockSpec((BQ, width), lambda i, *_: (i, 0))
    acc_spec = pl.BlockSpec((1, width, BQ), lambda i, *_: (i, 0, 0))
    in_specs = [row_spec] * 3 + [
        pl.BlockSpec((1, 1, heads * BQ), lambda i, *_: (i, 0, 0)),
        pl.BlockSpec((1, 1, BQ), lambda i, *_: (i, 0, 0)),
    ]
    in_specs += [whole(a.shape) for a in kvs] + [whole(a.shape) for a in sks]
    scratch = [pltpu.VMEM((width, BQ), f32)]
    scratch += [pltpu.VMEM((width, a.shape[0]), bf16) for a in kvs]
    if final:
        in_specs += [acc_spec]
        out_specs = [row_spec]
        out_shape = [jax.ShapeDtypeStruct(q.shape, f32)]
    else:
        out_specs = [acc_spec]
        out_shape = [jax.ShapeDtypeStruct((count, width, BQ), f32)]
        scratch += [pltpu.VMEM(a.shape, f32) for a in kvs]
    out_specs += [whole(a.shape) for a in kvs]
    out_shape += [jax.ShapeDtypeStruct(a.shape, f32 if final else bf16) for a in kvs]
    return pl.pallas_call(
        functools.partial(backward_kernel, heads, sets, final),
        grid_spec=pltpu.PrefetchScalarGridSpec(
            num_scalar_prefetch=1,
            grid=(count,),
            in_specs=in_specs,
            out_specs=out_specs,
            scratch_shapes=scratch,
        ),
        out_shape=out_shape,
        cost_estimate=cost(10, q, kvs),
        name="back_own" if final else "back_halo",
    )(bounds, q, do, o, lse, sq, *kvs, *sks, *(state or ()))


def place_tables(seq_lengths, seq_offsets, first, count):
    place = first + jnp.arange(count, dtype=jnp.int32)
    ends = seq_offsets + seq_lengths
    inside = (place[:, None] >= seq_offsets[None, :]) & (place[:, None] < ends[None, :])
    live = jnp.any(inside, axis=1)
    index = jnp.arange(seq_offsets.shape[0], dtype=jnp.int32)
    segment = jnp.sum(jnp.where(inside, index[None, :], 0), axis=1)
    start = jnp.sum(jnp.where(inside, seq_offsets[None, :], 0), axis=1)
    end = jnp.sum(jnp.where(inside, ends[None, :], 0), axis=1)
    return live, segment, start, end, place


def qkv_order(heads, head_width):
    width = heads * head_width
    half = head_width // 2
    new = jnp.arange(3 * width, dtype=jnp.int32)
    kind = new // width
    inner = new % width
    side = inner // (width // 2)
    pair_head = (inner % (width // 2)) // half
    pair_old = pair_head * 3 * head_width + kind * head_width + side * half + inner % half
    value_old = (inner // head_width) * 3 * head_width + 2 * head_width + inner % head_width
    old = jnp.where(kind == 2, value_old, pair_old)
    return (old[None, :] == new[:, None]).astype(bf16)


def local(
    tokens,
    gain_attn,
    w_qkv,
    w_out,
    gain_mlp,
    w_in,
    w_down,
    cotangent,
    seq_lengths,
    seq_offsets,
    deal,
):
    R, C, B = lax.axis_size("row"), lax.axis_size("col"), lax.axis_size("dp")
    r, c, b = lax.axis_index("row"), lax.axis_index("col"), lax.axis_index("dp")
    S, Dl = tokens.shape
    D = Dl * R
    two = R == 2 and C == 2 and B == 8
    heads = w_qkv.shape[1] // R
    head_width = w_qkv.shape[2] // 3
    W = heads * head_width
    F = w_down.shape[0]
    H = LONGEST
    Sr = S // R
    zrow, zcol = (r == 0), (c == 0)

    def to_row(a):
        return lax.ppermute(a, "row", SWAP)

    def to_col(a):
        return lax.ppermute(a, "col", SWAP)

    def ordered(flag, mine, theirs, axis):
        return jnp.where(
            flag,
            jnp.concatenate([mine, theirs], axis=axis),
            jnp.concatenate([theirs, mine], axis=axis),
        )

    def own_first(a, axis):
        if not two:
            return a
        n = a.shape[axis] // 2
        return jnp.where(zrow, a, jnp.roll(a, n, axis=axis))

    def take(a, index, size, axis=0):
        return lax.dynamic_slice_in_dim(a, index * size, size, axis)

    def partner(a):
        n = a.shape[0] // 2
        got = to_row(take(a, c, n))
        return ordered(zcol, got, to_col(got), 0)

    def gather(a, axis):
        if two:
            return jnp.concatenate([a, to_row(a)], axis=axis)
        return lax.all_gather(a, "row", axis=axis, tiled=True)

    def col_sum(a):
        return a + to_col(a.astype(bf16)).astype(f32) if C == 2 else lax.psum(a, "col")

    live_x, seg_x, start_x, end_x, place_x = place_tables(seq_lengths, seq_offsets, b * S - H, S + 2 * H)
    key_seg = jnp.broadcast_to(jnp.where(live_x, seg_x, -2)[:, None], (S + 2 * H, 128))
    sk_left, sk_own, sk_right = key_seg[:H], key_seg[H : H + S], key_seg[H + S :]
    live = live_x[H : H + S]
    nq = S // BQ
    sq = jnp.where(live, seg_x[H : H + S], -1).reshape(nq, 1, BQ)
    first = jnp.min(jnp.where(live, start_x[H : H + S] - b * S, 4 * S).reshape(nq, BQ), axis=1)
    last = jnp.max(jnp.where(live, end_x[H : H + S] - b * S, -4 * S).reshape(nq, BQ), axis=1)
    own_low = jnp.clip(first, 0, S) // BK
    own_high = (jnp.clip(last, 0, S) + BK - 1) // BK
    left_low = jnp.clip(first + H, 0, H) // BK
    right_high = (jnp.clip(last - S, 0, H) + BK - 1) // BK
    own_bounds = jnp.stack([own_low, own_high], axis=1).reshape(-1).astype(jnp.int32)
    zero = jnp.zeros_like(left_low)
    halo_bounds = (
        jnp.stack([left_low, zero + H // BK, zero, right_high], axis=1).reshape(-1).astype(jnp.int32)
    )
    position = jnp.where(live, place_x[H : H + S] - start_x[H : H + S], 0)
    freq = rope_base ** (-(jnp.arange(0, head_width, 2, dtype=f32) / head_width))
    angle = position.astype(f32)[:, None] * jnp.tile(freq, heads)[None, :]
    cosine, sine = lax.optimization_barrier((jnp.cos(angle), jnp.sin(angle)))

    live_column = live[:, None]
    if two:
        x_got = partner(tokens)
        x_low = jnp.where(live_column, jnp.concatenate([tokens, x_got], axis=1), 0)
    else:
        own_x = jnp.where(live_column, tokens, 0)
        x_low = lax.all_gather(own_x, "row", axis=1, tiled=True)

    wq_low = w_qkv.reshape(Dl, R * 3 * W).astype(bf16)
    if two:
        wq_mine, wq_send = take(wq_low, r, 3 * W, 1), take(wq_low, 1 - r, 3 * W, 1)
        wq_got = to_row(wq_send)
    else:
        wq = lax.all_to_all(wq_low, "row", split_axis=1, concat_axis=0, tiled=True)
    order = qkv_order(heads, head_width)

    gain_one = own_first(gain_attn, 0)
    gain_two = own_first(gain_mlp, 0)

    Db = D // B
    Dd = D // (B * R)
    if two:
        y_bit, z_bits = b % 2, b // 2

        def relative(a, bits):
            n = jnp.arange(D, dtype=jnp.int32)
            rel = {"w": 0 * n, "x": 0 * n}
            for i, bit in enumerate(bits):
                rel[bit] = n // (D >> (i + 1)) % 2
            z_rel = 2 * rel["Z"] + rel["z"]
            column = ((z_bits ^ z_rel) * 2 + (y_bit ^ rel["y"])) * Db + n % Dd
            column = column + (rel["w"] if "w" in bits else r ^ rel["x"]) * Dd
            column = column ^ (r * (D // 2))
            return nn(a, (n[:, None] == column[None, :]).astype(bf16)).astype(bf16)

        def to_y(a):
            return lax.ppermute(a, "dp", [(i, i ^ 1) for i in range(B)])

        def to_z(a, j):
            return lax.ppermute(a, "dp", [(i, i ^ (2 * j)) for i in range(B)])

        def first(a):
            return a[:, : a.shape[1] // 2]

        def second(a):
            return a[:, a.shape[1] // 2 :].astype(bf16)

        def product(left, right):
            return tn(left, second(right)).astype(bf16)

        def halved(left, right, got):
            return tn(left, first(right)) + got.astype(f32)

        def joined(part, got):
            return first(part).astype(f32) + got.astype(f32)

    x = x_low.astype(f32)
    center = x - jnp.mean(x, axis=-1, keepdims=True)
    inverse_one = lax.rsqrt(jnp.mean(center * center, axis=-1, keepdims=True) + epsilon)
    mean_one = jnp.mean(x, axis=-1, keepdims=True)
    h1 = (center * inverse_one * gain_one).astype(bf16)
    if two:
        h1, wq_mine, wq_got = lax.optimization_barrier((h1, wq_mine, wq_got))
        wq = jnp.concatenate([wq_mine, wq_got], axis=0)
    wq = nn(wq, order).astype(bf16)

    half = W // 2

    def turn(t, sign):
        first_half, second_half = t[:, :half], t[:, half:]
        s = sine * sign
        return jnp.concatenate(
            [first_half * cosine - second_half * s, second_half * cosine + first_half * s], axis=1
        )

    kv_raw = nn(h1, wq[:, W:])
    kv = jnp.concatenate([turn(kv_raw[:, :W], 1.0), kv_raw[:, W:]], axis=1).astype(bf16)
    up = [(i, i + 1) for i in range(B - 1)]
    down = [(i + 1, i) for i in range(B - 1)]
    kv_left = lax.ppermute(kv[S - H :], "dp", up)
    kv_right = lax.ppermute(kv[:H], "dp", down)
    q = (turn(nn(h1, wq[:, :W]), 1.0) * (1.0 / math.sqrt(head_width))).astype(bf16)
    wo_low = w_out.astype(bf16)
    w_in_late, w_down_late = after((w_in, w_down), kv)
    wd_low = w_down_late.astype(bf16)
    act_low, lin_low = w_in_late[:, 0].astype(bf16), w_in_late[:, 1].astype(bf16)
    if two:
        even = (b // 2) % 2 == 0
        in_send, wo_send, g_send = after(
            (
                lax.dynamic_index_in_dim(w_in, (b // 2) % 2, 1, keepdims=False).astype(bf16),
                wo_low,
                take(cotangent, 2 * (1 - r) + c, Sr // 2),
            ),
            cosine,
            wq_send,
        )
        in_got, wo_got, g_got = to_row(in_send), to_row(wo_send), to_row(g_send)
        wd_half = take(wd_low, (b // 2) % 2, F // 2)
        h1_y = relative(after(h1, kv), "yzZw")
        q, h1_y, sk_left, sk_right, act_low, lin_low, wd_half = lax.optimization_barrier(
            (q, h1_y, sk_left, sk_right, act_low, lin_low, wd_half)
        )

    state = attend_call(own_bounds, q, sq, [kv], [sk_own], heads)
    if two:
        kv_left, kv_right, in_got, wo_got, g_got, wd_half = after(
            (kv_left, kv_right, in_got, wo_got, g_got, wd_half), state
        )
        in_other, wd_got = to_z(in_got, 1), to_row(wd_half)
    o, lse = attend_call(
        halo_bounds, q, sq, [kv_left, kv_right], [sk_left, sk_right], heads, state
    )

    if two:
        o, wd_got, wo_got, g_got = lax.optimization_barrier((o, wd_got, wo_got, g_got))
        wo = own_first(jnp.concatenate([wo_low, wo_got], axis=1), 0)
    else:
        wo = gather(wo_low, 1)

    if two:
        o_got = to_row(take(o, 1 - r, Sr))
        o_rows = jnp.concatenate([take(o, r, Sr), o_got], axis=1)
        wd_other = to_z(wd_got, 1)
        wd_got = ordered(even, wd_got, wd_other, 0)
        g_got = ordered(zcol, g_got, to_col(g_got), 0)
        g_low = jnp.concatenate([take(cotangent, r, Sr), g_got], axis=1)
        g_low = jnp.where(take(live, r, Sr)[:, None], g_low, 0)
        wds = [wd_low, wd_got]
    else:
        o_rows = lax.all_to_all(o, "row", split_axis=0, concat_axis=1, tiled=True)
        own_g = jnp.where(live_column, cotangent, 0)
        g_low = lax.all_to_all(own_g, "row", split_axis=0, concat_axis=1, tiled=True)
        wds, acts, lins = [gather(wd_low, 1)], [gather(act_low, 0)], [gather(lin_low, 0)]

    def split_nn(a, parts):
        n = a.shape[1] // len(parts)
        return sum(nn(a[:, i * n : (i + 1) * n], w) for i, w in enumerate(parts))

    def split_nt(a, parts):
        n = a.shape[1] // len(parts)
        return sum(nt(a[:, i * n : (i + 1) * n], w) for i, w in enumerate(parts))

    def wide(parts):
        return parts[0] if len(parts) == 1 else jnp.concatenate(parts, axis=1)

    x_rows = take(x_low, r, Sr).astype(f32)
    if C == 2:
        o_all = jnp.concatenate([o_rows, to_col(o_rows)], axis=1)
        wo_all = jnp.concatenate([wo, to_col(wo)], axis=0)
        x1 = x_rows + nn(o_all, wo_all)
    else:
        x1 = x_rows + lax.psum(nn(o_rows, wo), "col")
    if two:
        in_got, in_other = after((in_got, in_other), o_got)
        act_got, lin_got = jnp.where(even, in_got, in_other), jnp.where(even, in_other, in_got)
        acts, lins = [act_low, act_got], [lin_low, lin_got]

    center = x1 - jnp.mean(x1, axis=-1, keepdims=True)
    inverse_two = lax.rsqrt(jnp.mean(center * center, axis=-1, keepdims=True) + epsilon)
    n2 = center * inverse_two
    h2 = (n2 * gain_two).astype(bf16)
    a = split_nn(h2, acts)
    u = split_nn(h2, lins)
    phi = 0.5 + 0.5 * lax.erf(a * math.sqrt(0.5))
    gelu = a * phi
    slope = phi + a * jnp.exp(-0.5 * a * a) * (1.0 / math.sqrt(2.0 * math.pi))
    m = (gelu * u).astype(bf16)
    y_part = wide([nn(m, w) for w in wds])
    if two:
        n = Sr // 2
        y_half = (
            take(x1, c, n) + take(y_part, c, n) + to_col(take(y_part, 1 - c, n).astype(bf16)).astype(f32)
        ).astype(bf16)
        y_got = to_row(y_half[:, Dl:])
    else:
        y = (x1 + col_sum(y_part)).astype(bf16)
        layer_out = lax.all_to_all(y, "row", split_axis=1, concat_axis=0, tiled=True)

    dm = split_nt(g_low, wds)
    da = (dm * u * slope).astype(bf16)
    du = (dm * gelu).astype(bf16)
    dh2_part = wide([nt(da, v) + nt(du, w) for v, w in zip(acts, lins)])
    dh2 = col_sum(dh2_part)
    if two:
        g_y = relative(after(g_low, dh2_part), "yzZx")
        lower_got = to_y(product(m, g_y))
    e2 = dh2 * gain_two
    dx1 = g_low.astype(f32) + inverse_two * (
        e2
        - jnp.mean(e2, axis=-1, keepdims=True)
        - n2 * jnp.mean(e2 * n2, axis=-1, keepdims=True)
    )
    dx_low = dx1.astype(bf16)
    do_rows = nt(dx_low, wo).astype(bf16)
    if two:
        do_got = to_row(do_rows[:, W:])
        do = ordered(zrow, do_rows[:, :W], do_got, 0)
    else:
        do = lax.all_to_all(do_rows, "row", split_axis=1, concat_axis=0, tiled=True)

    if two:
        h2, da, du, o_heads, dx_late = after((h2, da, du, own_first(o_rows, 1), dx_low), do_rows)
        dx_y = relative(dx_late, "yzZx")
        h_x = relative(h2, "xyzZ")
        proj_got = to_y(product(o_heads, dx_y))
        gate_send = jnp.concatenate([product(da, h_x), product(du, h_x)], axis=0)
        gate_got = to_row(after(gate_send, do_got))
        pair = ordered(zrow, y_half[None, :, :Dl], after(y_got, gate_send)[None], 0)
        layer_out = ordered(zcol, pair[:, None], to_col(pair)[:, None], 1).reshape(S, Dl)
        lower = halved(m, g_y, after(lower_got, gate_send))
        lower_got = to_z(second(lower), 1)
        do, lower, layer_out = lax.optimization_barrier((do, lower, layer_out))

    dq_part, dkv_left, dkv_right = attend_back_call(
        halo_bounds, q, do, o, lse, sq, [kv_left, kv_right], [sk_left, sk_right], heads
    )
    from_right = lax.ppermute(dkv_left, "dp", down)
    from_left = lax.ppermute(dkv_right, "dp", up)
    if two:
        lower = joined(lower, after(lower_got, dq_part))
        lower_got = to_z(second(lower), 2)
        dq_part, lower = lax.optimization_barrier((dq_part, lower))
    dq, dkv = attend_back_call(own_bounds, q, do, o, lse, sq, [kv], [sk_own], heads, [dq_part])
    if two:
        dkv, from_right, from_left, gate_got, proj_got, lower_got = lax.optimization_barrier(
            (dkv, from_right, from_left, gate_got, proj_got, lower_got)
        )
    pad = jnp.zeros((S - H, 2 * W), bf16)
    dkv = (
        dkv
        + jnp.concatenate([pad, from_right], axis=0).astype(f32)
        + jnp.concatenate([from_left, pad], axis=0).astype(f32)
    )
    dq = turn(dq * (1.0 / math.sqrt(head_width)), -1.0)
    dt = jnp.concatenate([dq, turn(dkv[:, :W], -1.0), dkv[:, W:]], axis=1).astype(bf16)
    dh1_part = nt(dt, wq)
    if two:
        query_send = product(dt, h1_y)
        gate_got, proj_got, lower_got = after((gate_got, proj_got, lower_got), query_send, dh1_part)

    if two:
        n = S // 2
        kept = take(dh1_part, c, n) + to_col(take(dh1_part, 1 - c, n).astype(bf16)).astype(f32)
        xs = take(x_low, c, n).astype(f32)
        inv, mean = take(inverse_one, c, n), take(mean_one, c, n)
        n1 = (xs - mean) * inv
        e1 = kept * gain_one
        sums = jnp.stack([jnp.sum(e1, axis=-1), jnp.sum(e1 * n1, axis=-1)])
        sums = (sums + to_row(sums)) * (1.0 / D)
        moved = lax.ppermute(after(dx_low[:, Dl:], from_left), ("row", "col"), [(0, 2), (3, 1)])
        kept_send, moved = lax.optimization_barrier((kept[:, Dl:].astype(bf16), moved))
        mine = (kept[:, :Dl] + to_row(kept_send).astype(f32)) * gain_one[:Dl]
        base = jnp.where(r == c, dx1[:, :Dl], moved.astype(f32))
        dx = base + inv * (mine - sums[0][:, None] - n1[:, :Dl] * sums[1][:, None])
        dx = dx.astype(bf16)
        tokens_grad = ordered(zcol, dx, to_col(dx), 0)
    else:
        dh1 = lax.psum_scatter(col_sum(dh1_part), "row", scatter_dimension=1, tiled=True)
        xs = own_x.astype(f32)
        n1 = (xs - mean_one) * inverse_one
        e1 = dh1 * take(gain_attn, r, Dl)
        sums = lax.psum(jnp.stack([jnp.sum(e1, axis=-1), jnp.sum(e1 * n1, axis=-1)]), "row") / D
        base = lax.all_to_all(dx_low, "row", split_axis=1, concat_axis=0, tiled=True).astype(f32)
        tokens_grad = (
            base + inverse_one * (e1 - sums[0][:, None] - n1 * sums[1][:, None])
        ).astype(bf16)

    if two:
        query = halved(dt, h1_y, after(to_y(query_send), kept))

        def pair(one, other):
            return jnp.concatenate([second(one), second(other)], axis=0)

        def joined_pair(one, other, got):
            n = one.shape[0]
            return joined(one, got[:n]), joined(other, got[n:])

        gate_got = after(gate_got, kept)
        act, lin = halved(da, h_x, gate_got[:F]), halved(du, h_x, gate_got[F:])
        gate_got = to_y(pair(act, lin))
        proj = halved(o_heads, dx_y, proj_got)
        query, proj = joined_pair(query, proj, to_z(pair(query, proj), 1))
        act, lin = joined_pair(act, lin, after(gate_got, query))
        gate_got = to_z(pair(act, lin), 1)
        query, proj = joined_pair(query, proj, to_z(pair(query, proj), 2))
        act, lin = joined_pair(act, lin, after(gate_got, dx))
        lower = joined(lower, lower_got)
        last_got = after(to_row(pair(lower, proj)), dx)
        gate_got = to_z(pair(act, lin).T, 2).T
        lower, proj = joined_pair(lower, proj, last_got)
        act, lin = joined_pair(act, lin, gate_got)
        gate = jnp.stack([act.T, lin.T])
        query = query.T
        wq_rows = take(wq, b ^ (4 * r), Db)
        place = (2 * b + r) ^ (8 * r)
        wi_rows = jnp.stack(
            [jnp.where(place < 8, *(take(w, place % 8, Dd) for w in ws)) for ws in after((acts, lins), kept)]
        )
    else:

        def scatter(grad):
            return lax.psum_scatter(grad, ("dp", "row"), scatter_dimension=1, tiled=True).astype(f32)

        gate = jnp.stack([scatter(tn(da, h2).astype(bf16)).T, scatter(tn(du, h2).astype(bf16)).T])
        proj = scatter(tn(o_rows, dx_low).astype(bf16))
        lower = scatter(tn(m, g_low).astype(bf16))
        query = lax.psum_scatter(
            tn(h1, dt).astype(bf16), "dp", scatter_dimension=0, tiled=True
        ).astype(f32)
        wq_rows = take(wq, b, Db)
        wi_rows = jnp.stack([take(acts[0], b * R + r, Dd), take(lins[0], b * R + r, Dd)])

    one_part = jnp.sum(query * wq_rows.astype(f32), axis=1)
    two_part = jnp.sum(jnp.sum(gate * wi_rows.astype(f32), axis=2), axis=0)
    natural = lax.dot_general(
        query, order.astype(f32), (((1,), (1,)), ((), ())),
        precision=lax.Precision.HIGHEST, preferred_element_type=f32,
    )
    if two:
        pair = jnp.concatenate([natural, jnp.broadcast_to(one_part[:, None], (Db, 128))], axis=1)
        pair = pair.reshape(2, Dd, 3 * W + 128)
        mine = lax.dynamic_index_in_dim(pair, r, 0, keepdims=False)
        theirs = to_row(lax.dynamic_index_in_dim(pair, 1 - r, 0, keepdims=False))
        theirs = after(theirs, tokens_grad)
        one_part = mine[:, 3 * W] + theirs[:, 3 * W]
        query_out = ordered(zrow, mine[:, : 3 * W], theirs[:, : 3 * W], 1)
    else:
        one_part = take(lax.psum(one_part, "row"), r, Dd)
        query_out = lax.all_to_all(natural, "row", split_axis=0, concat_axis=1, tiled=True)
    gains = jnp.stack([one_part, two_part])
    gains = gains + to_col(gains) if C == 2 else lax.psum(gains, "col")
    gain_attn_grad = gains[0] / take(gain_attn, b * R + r, Dd)
    gain_mlp_grad = gains[1] / take(gain_mlp, b * R + r, Dd)
    return (
        layer_out,
        tokens_grad,
        gain_attn_grad,
        query_out.reshape(Dd, R * heads, 3 * head_width),
        proj,
        gain_mlp_grad,
        jnp.swapaxes(gate, 0, 1),
        lower,
    )


def solution(mesh):
    return jax.shard_map(
        local,
        mesh=mesh,
        in_specs=(
            P("dp", "row"),
            P(),
            P("row", "col", None),
            P("col", "row"),
            P(),
            P("row", None, "col"),
            P("col", "row"),
            P("dp", "row"),
            P(),
            P(),
            P(),
        ),
        out_specs=(
            P("dp", "row"),
            P("dp", "row"),
            P(("dp", "row")),
            P(("dp", "row"), "col", None),
            P("col", ("dp", "row")),
            P(("dp", "row")),
            P(("dp", "row"), None, "col"),
            P("col", ("dp", "row")),
        ),
        check_vma=False,
    )
```

```python
import functools
import math

import jax
import jax.numpy as jnp
from jax import lax
from jax.experimental import pallas as pl
from jax.experimental.pallas import tpu as pltpu
from jax.sharding import PartitionSpec as P

LONGEST = 1024
BQ = 256
BK = 256
NEG = -1e30
FAR = 1e30
epsilon = 1e-05
rope_base = 160000.0
bf16 = jnp.bfloat16
f32 = jnp.float32
SWAP = [(0, 1), (1, 0)]


def nt(a, b):
    return lax.dot_general(a, b, (((1,), (1,)), ((), ())), preferred_element_type=f32)


def tn(a, b):
    return lax.dot_general(a, b, (((0,), (0,)), ((), ())), preferred_element_type=f32)


def nn(a, b):
    return jnp.dot(a, b, preferred_element_type=f32)


def after(a, *others):
    return lax.optimization_barrier((a, *others))[0]


def half_mask(width, heads, head):
    lane = lax.broadcasted_iota(jnp.int32, (1, width), 1)
    half = width // 2
    lane = jnp.where(lane >= half, lane - half, lane)
    step = half // heads
    return (lane >= head * step) & (lane < (head + 1) * step)


def whole_mask(width, heads, head):
    lane = lax.broadcasted_iota(jnp.int32, (1, width), 1)
    step = width // heads
    return (lane >= head * step) & (lane < (head + 1) * step)


def stack_heads(block, heads, mask_of):
    zero = jnp.zeros_like(block)
    width = block.shape[1]
    return jnp.concatenate(
        [jnp.where(mask_of(width, heads, h), block, zero) for h in range(heads)], axis=0
    )


def same_segment(key_seg, query_seg, heads):
    tile = key_seg
    lanes = query_seg.shape[1]
    if lanes > tile.shape[1]:
        tile = jnp.concatenate([tile] * (lanes // tile.shape[1]), axis=1)
    same = tile == query_seg
    return jnp.concatenate([same] * heads, axis=1) if heads > 1 else same


def forward_kernel(heads, sets, final, bounds, *refs):
    refs = list(refs)
    q_ref, sq_ref = refs[:2]
    kv_refs = refs[2 : 2 + sets]
    sk_refs = refs[2 + sets : 2 + 2 * sets]
    rest = refs[2 + 2 * sets :]
    if final:
        acc_in, ml_in, o_ref, lse_ref = rest[:4]
        acc, m_ref, l_ref = rest[4:7]
        vt_refs = rest[7:]
    else:
        acc, ml_ref = rest[:2]
        m_ref, l_ref = rest[2:4]
        vt_refs = rest[4:]
    step = pl.program_id(0)
    rows, width = q_ref.shape
    each = width // heads

    @pl.when(step == 0)
    def _():
        for kv, vt in zip(kv_refs, vt_refs):
            for j in range(kv.shape[0] // BK):
                vt[:, j * BK : (j + 1) * BK] = kv[j * BK : (j + 1) * BK, width:].T

    if final:
        acc[...] = acc_in[0]
        m_ref[...] = ml_in[0, 0:1]
        l_ref[...] = ml_in[0, 1:2]
    else:
        acc[...] = jnp.zeros_like(acc)
        m_ref[...] = jnp.full_like(m_ref, NEG)
        l_ref[...] = jnp.zeros_like(l_ref)
    queries = stack_heads(q_ref[...], heads, half_mask)
    query_seg = sq_ref[0]
    target = acc if final else acc.at[0]

    for s in range(sets):
        kv, sk, vt = kv_refs[s], sk_refs[s], vt_refs[s]

        def body(j, carry):
            first = pl.multiple_of(j * BK, BK)
            keys = kv[pl.ds(first, BK), 0:width]
            scores = nt(keys, queries)
            same = same_segment(sk[pl.ds(first, BK), :], query_seg, heads)
            scores = jnp.where(same, scores, NEG)
            before = m_ref[...]
            top = jnp.maximum(before, jnp.max(scores, axis=0, keepdims=True))
            raised = jnp.exp(scores - top)
            shrink = jnp.exp(before - top)
            m_ref[...] = top
            l_ref[...] = l_ref[...] * shrink + jnp.sum(raised, axis=0, keepdims=True)
            low = raised.astype(bf16)
            for h in range(heads):
                part = nn(
                    vt[h * each : (h + 1) * each, pl.ds(first, BK)],
                    low[:, h * rows : (h + 1) * rows],
                )
                hold = target[h * each : (h + 1) * each, :]
                target[h * each : (h + 1) * each, :] = (
                    hold * shrink[:, h * rows : (h + 1) * rows] + part
                )
            return carry

        lax.fori_loop(
            bounds[(step * sets + s) * 2], bounds[(step * sets + s) * 2 + 1], body, 0
        )

    if final:
        live = query_seg >= 0
        total = l_ref[...]
        live_all = jnp.concatenate([live] * heads, axis=1) if heads > 1 else live
        total = jnp.where(live_all, total, 1.0)
        inverse = jnp.where(live_all, 1.0 / total, 0.0)
        for h in range(heads):
            acc[h * each : (h + 1) * each, :] = (
                acc[h * each : (h + 1) * each, :] * inverse[:, h * rows : (h + 1) * rows]
            )
        o_ref[...] = acc[...].T.astype(bf16)
        lse_ref[0] = jnp.where(live_all, m_ref[...] + jnp.log(total), FAR)
    else:
        ml_ref[0, 0:1] = m_ref[...]
        ml_ref[0, 1:2] = l_ref[...]


def cost(products, q, kvs):
    pairs = q.shape[0]
    return pl.CostEstimate(
        flops=4 * products * pairs * q.shape[1],
        bytes_accessed=2 * sum(a.size for a in kvs) + 4 * q.size,
        transcendentals=4 * pairs,
    )


def whole(shape):
    zeros = (0,) * len(shape)
    return pl.BlockSpec(shape, lambda i, *_: zeros)


def attend_call(bounds, q, sq, kvs, sks, heads, state=None):
    count = q.shape[0] // BQ
    width = q.shape[1]
    sets = len(kvs)
    final = state is not None
    row_spec = pl.BlockSpec((BQ, width), lambda i, *_: (i, 0))
    acc_spec = pl.BlockSpec((1, width, BQ), lambda i, *_: (i, 0, 0))
    ml_spec = pl.BlockSpec((1, 2, heads * BQ), lambda i, *_: (i, 0, 0))
    in_specs = [row_spec, pl.BlockSpec((1, 1, BQ), lambda i, *_: (i, 0, 0))]
    in_specs += [whole(a.shape) for a in kvs] + [whole(a.shape) for a in sks]
    scratch = [pltpu.VMEM((1, heads * BQ), f32)] * 2
    scratch += [pltpu.VMEM((width, a.shape[0]), bf16) for a in kvs]
    if final:
        in_specs += [acc_spec, ml_spec]
        out_specs = [row_spec, pl.BlockSpec((1, 1, heads * BQ), lambda i, *_: (i, 0, 0))]
        out_shape = [
            jax.ShapeDtypeStruct(q.shape, bf16),
            jax.ShapeDtypeStruct((count, 1, heads * BQ), f32),
        ]
        scratch = [pltpu.VMEM((width, BQ), f32)] + scratch
    else:
        out_specs = [acc_spec, ml_spec]
        out_shape = [
            jax.ShapeDtypeStruct((count, width, BQ), f32),
            jax.ShapeDtypeStruct((count, 2, heads * BQ), f32),
        ]
    return pl.pallas_call(
        functools.partial(forward_kernel, heads, sets, final),
        grid_spec=pltpu.PrefetchScalarGridSpec(
            num_scalar_prefetch=1,
            grid=(count,),
            in_specs=in_specs,
            out_specs=out_specs,
            scratch_shapes=scratch,
        ),
        out_shape=out_shape,
        cost_estimate=cost(4, q, kvs),
        name="attend_final" if final else "attend_own",
    )(bounds, q, sq, *kvs, *sks, *(state or ()))


def backward_kernel(heads, sets, final, bounds, *refs):
    refs = list(refs)
    q_ref, do_ref, o_ref, lse_ref, sq_ref = refs[:5]
    kv_refs = refs[5 : 5 + sets]
    sk_refs = refs[5 + sets : 5 + 2 * sets]
    rest = refs[5 + 2 * sets :]
    if final:
        dq_in, dq_ref = rest[0], rest[1]
        dkv_refs = rest[2 : 2 + sets]
        dq_acc = rest[2 + sets]
        kt_refs = rest[3 + sets : 3 + 2 * sets]
        sums = dkv_refs
    else:
        dq_ref = rest[0]
        dkv_refs = rest[1 : 1 + sets]
        dq_acc = rest[1 + sets]
        kt_refs = rest[2 + sets : 2 + 2 * sets]
        sums = rest[2 + 2 * sets :]
    step = pl.program_id(0)
    rows, width = q_ref.shape
    each = width // heads
    half = width // 2
    piece = half // heads

    @pl.when(step == 0)
    def _():
        for kv, kt, total in zip(kv_refs, kt_refs, sums):
            total[...] = jnp.zeros_like(total)
            for j in range(kv.shape[0] // BK):
                kt[:, j * BK : (j + 1) * BK] = kv[j * BK : (j + 1) * BK, :width].T

    if final:
        dq_acc[...] = dq_in[0]
    else:
        dq_acc[...] = jnp.zeros_like(dq_acc)
    grads = do_ref[...]
    queries = stack_heads(q_ref[...], heads, half_mask)
    outs = stack_heads(grads, heads, whole_mask)
    query_seg = sq_ref[0]
    lse = lse_ref[0]
    product = (grads.astype(f32) * o_ref[...].astype(f32)).T
    delta = jnp.concatenate(
        [
            jnp.sum(product[h * each : (h + 1) * each], axis=0, keepdims=True)
            for h in range(heads)
        ],
        axis=1,
    )

    for s in range(sets):
        kv, sk, kt, total = kv_refs[s], sk_refs[s], kt_refs[s], sums[s]

        def body(j, carry):
            first = pl.multiple_of(j * BK, BK)
            keys = kv[pl.ds(first, BK), 0:width]
            values = kv[pl.ds(first, BK), width : 2 * width]
            scores = nt(keys, queries)
            same = same_segment(sk[pl.ds(first, BK), :], query_seg, heads)
            probs = jnp.where(same, jnp.exp(scores - lse), 0.0)
            grad_probs = nt(values, outs)
            grad_scores = (probs * (grad_probs - delta)).astype(bf16)
            low = probs.astype(bf16)
            total[pl.ds(first, BK), width : 2 * width] += nn(low, outs)
            total[pl.ds(first, BK), 0:width] += nn(grad_scores, queries)
            for h in range(heads):
                column = grad_scores[:, h * rows : (h + 1) * rows]
                for lead in (h * piece, half + h * piece):
                    dq_acc[lead : lead + piece, :] += nn(
                        kt[lead : lead + piece, pl.ds(first, BK)], column
                    )
            return carry

        lax.fori_loop(
            bounds[(step * sets + s) * 2], bounds[(step * sets + s) * 2 + 1], body, 0
        )

    if final:
        dq_ref[...] = dq_acc[...].T
    else:
        dq_ref[0] = dq_acc[...]

        @pl.when(step == pl.num_programs(0) - 1)
        def _():
            for total, out in zip(sums, dkv_refs):
                out[...] = total[...].astype(bf16)


def attend_back_call(bounds, q, do, o, lse, sq, kvs, sks, heads, state=None):
    count = q.shape[0] // BQ
    width = q.shape[1]
    sets = len(kvs)
    final = state is not None
    row_spec = pl.BlockSpec((BQ, width), lambda i, *_: (i, 0))
    acc_spec = pl.BlockSpec((1, width, BQ), lambda i, *_: (i, 0, 0))
    in_specs = [row_spec] * 3 + [
        pl.BlockSpec((1, 1, heads * BQ), lambda i, *_: (i, 0, 0)),
        pl.BlockSpec((1, 1, BQ), lambda i, *_: (i, 0, 0)),
    ]
    in_specs += [whole(a.shape) for a in kvs] + [whole(a.shape) for a in sks]
    scratch = [pltpu.VMEM((width, BQ), f32)]
    scratch += [pltpu.VMEM((width, a.shape[0]), bf16) for a in kvs]
    if final:
        in_specs += [acc_spec]
        out_specs = [row_spec]
        out_shape = [jax.ShapeDtypeStruct(q.shape, f32)]
    else:
        out_specs = [acc_spec]
        out_shape = [jax.ShapeDtypeStruct((count, width, BQ), f32)]
        scratch += [pltpu.VMEM(a.shape, f32) for a in kvs]
    out_specs += [whole(a.shape) for a in kvs]
    out_shape += [jax.ShapeDtypeStruct(a.shape, f32 if final else bf16) for a in kvs]
    return pl.pallas_call(
        functools.partial(backward_kernel, heads, sets, final),
        grid_spec=pltpu.PrefetchScalarGridSpec(
            num_scalar_prefetch=1,
            grid=(count,),
            in_specs=in_specs,
            out_specs=out_specs,
            scratch_shapes=scratch,
        ),
        out_shape=out_shape,
        cost_estimate=cost(10, q, kvs),
        name="back_own" if final else "back_halo",
    )(bounds, q, do, o, lse, sq, *kvs, *sks, *(state or ()))


def place_tables(seq_lengths, seq_offsets, first, count):
    place = first + jnp.arange(count, dtype=jnp.int32)
    ends = seq_offsets + seq_lengths
    inside = (place[:, None] >= seq_offsets[None, :]) & (place[:, None] < ends[None, :])
    live = jnp.any(inside, axis=1)
    index = jnp.arange(seq_offsets.shape[0], dtype=jnp.int32)
    segment = jnp.sum(jnp.where(inside, index[None, :], 0), axis=1)
    start = jnp.sum(jnp.where(inside, seq_offsets[None, :], 0), axis=1)
    end = jnp.sum(jnp.where(inside, ends[None, :], 0), axis=1)
    return live, segment, start, end, place


def qkv_order(heads, head_width):
    width = heads * head_width
    half = head_width // 2
    new = jnp.arange(3 * width, dtype=jnp.int32)
    kind = new // width
    inner = new % width
    side = inner // (width // 2)
    pair_head = (inner % (width // 2)) // half
    pair_old = pair_head * 3 * head_width + kind * head_width + side * half + inner % half
    value_old = (inner // head_width) * 3 * head_width + 2 * head_width + inner % head_width
    old = jnp.where(kind == 2, value_old, pair_old)
    return (old[None, :] == new[:, None]).astype(bf16)


def local(
    tokens,
    gain_attn,
    w_qkv,
    w_out,
    gain_mlp,
    w_in,
    w_down,
    cotangent,
    seq_lengths,
    seq_offsets,
    deal,
):
    R, C, B = lax.axis_size("row"), lax.axis_size("col"), lax.axis_size("dp")
    r, c, b = lax.axis_index("row"), lax.axis_index("col"), lax.axis_index("dp")
    S, Dl = tokens.shape
    D = Dl * R
    two = R == 2 and C == 2 and B == 8
    heads = w_qkv.shape[1] // R
    head_width = w_qkv.shape[2] // 3
    W = heads * head_width
    F = w_down.shape[0]
    H = LONGEST
    Sr = S // R
    zrow, zcol = (r == 0), (c == 0)

    def to_row(a):
        return lax.ppermute(a, "row", SWAP)

    def to_col(a):
        return lax.ppermute(a, "col", SWAP)

    def ordered(flag, mine, theirs, axis):
        return jnp.where(
            flag,
            jnp.concatenate([mine, theirs], axis=axis),
            jnp.concatenate([theirs, mine], axis=axis),
        )

    def own_first(a, axis):
        if not two:
            return a
        n = a.shape[axis] // 2
        return jnp.where(zrow, a, jnp.roll(a, n, axis=axis))

    def take(a, index, size, axis=0):
        return lax.dynamic_slice_in_dim(a, index * size, size, axis)

    def partner(a):
        n = a.shape[0] // 2
        got = to_row(take(a, c, n))
        return ordered(zcol, got, to_col(got), 0)

    def gather(a, axis):
        if two:
            return jnp.concatenate([a, to_row(a)], axis=axis)
        return lax.all_gather(a, "row", axis=axis, tiled=True)

    def col_sum(a):
        return a + to_col(a.astype(bf16)).astype(f32) if C == 2 else lax.psum(a, "col")

    live_x, seg_x, start_x, end_x, place_x = place_tables(seq_lengths, seq_offsets, b * S - H, S + 2 * H)
    key_seg = jnp.broadcast_to(jnp.where(live_x, seg_x, -2)[:, None], (S + 2 * H, 128))
    sk_left, sk_own, sk_right = key_seg[:H], key_seg[H : H + S], key_seg[H + S :]
    live = live_x[H : H + S]
    nq = S // BQ
    sq = jnp.where(live, seg_x[H : H + S], -1).reshape(nq, 1, BQ)
    first = jnp.min(jnp.where(live, start_x[H : H + S] - b * S, 4 * S).reshape(nq, BQ), axis=1)
    last = jnp.max(jnp.where(live, end_x[H : H + S] - b * S, -4 * S).reshape(nq, BQ), axis=1)
    own_low = jnp.clip(first, 0, S) // BK
    own_high = (jnp.clip(last, 0, S) + BK - 1) // BK
    left_low = jnp.clip(first + H, 0, H) // BK
    right_high = (jnp.clip(last - S, 0, H) + BK - 1) // BK
    own_bounds = jnp.stack([own_low, own_high], axis=1).reshape(-1).astype(jnp.int32)
    zero = jnp.zeros_like(left_low)
    halo_bounds = (
        jnp.stack([left_low, zero + H // BK, zero, right_high], axis=1).reshape(-1).astype(jnp.int32)
    )
    position = jnp.where(live, place_x[H : H + S] - start_x[H : H + S], 0)
    freq = rope_base ** (-(jnp.arange(0, head_width, 2, dtype=f32) / head_width))
    angle = position.astype(f32)[:, None] * jnp.tile(freq, heads)[None, :]
    cosine, sine = lax.optimization_barrier((jnp.cos(angle), jnp.sin(angle)))

    live_column = live[:, None]
    if two:
        x_got = partner(tokens)
        x_low = jnp.where(live_column, jnp.concatenate([tokens, x_got], axis=1), 0)
    else:
        own_x = jnp.where(live_column, tokens, 0)
        x_low = lax.all_gather(own_x, "row", axis=1, tiled=True)

    wq_low = w_qkv.reshape(Dl, R * 3 * W).astype(bf16)
    if two:
        wq_mine, wq_send = take(wq_low, r, 3 * W, 1), take(wq_low, 1 - r, 3 * W, 1)
        wq_got = to_row(wq_send)
    else:
        wq = lax.all_to_all(wq_low, "row", split_axis=1, concat_axis=0, tiled=True)
    order = qkv_order(heads, head_width)

    gain_one = own_first(gain_attn, 0)
    gain_two = own_first(gain_mlp, 0)

    Db = D // B
    Dd = D // (B * R)
    if two:
        y_bit, z_bits = b % 2, b // 2

        def relative(a, bits):
            n = jnp.arange(D, dtype=jnp.int32)
            rel = {"w": 0 * n, "x": 0 * n}
            for i, bit in enumerate(bits):
                rel[bit] = n // (D >> (i + 1)) % 2
            z_rel = 2 * rel["Z"] + rel["z"]
            column = ((z_bits ^ z_rel) * 2 + (y_bit ^ rel["y"])) * Db + n % Dd
            column = column + (rel["w"] if "w" in bits else r ^ rel["x"]) * Dd
            column = column ^ (r * (D // 2))
            return nn(a, (n[:, None] == column[None, :]).astype(bf16)).astype(bf16)

        def to_y(a):
            return lax.ppermute(a, "dp", [(i, i ^ 1) for i in range(B)])

        def to_z(a, j):
            return lax.ppermute(a, "dp", [(i, i ^ (2 * j)) for i in range(B)])

        def first(a):
            return a[:, : a.shape[1] // 2]

        def second(a):
            return a[:, a.shape[1] // 2 :].astype(bf16)

        def product(left, right):
            return tn(left, second(right)).astype(bf16)

        def halved(left, right, got):
            return tn(left, first(right)) + got.astype(f32)

        def joined(part, got):
            return first(part).astype(f32) + got.astype(f32)

    x = x_low.astype(f32)
    center = x - jnp.mean(x, axis=-1, keepdims=True)
    inverse_one = lax.rsqrt(jnp.mean(center * center, axis=-1, keepdims=True) + epsilon)
    mean_one = jnp.mean(x, axis=-1, keepdims=True)
    h1 = (center * inverse_one * gain_one).astype(bf16)
    if two:
        h1, wq_mine, wq_got = lax.optimization_barrier((h1, wq_mine, wq_got))
        wq = jnp.concatenate([wq_mine, wq_got], axis=0)
    wq = nn(wq, order).astype(bf16)

    half = W // 2

    def turn(t, sign):
        first_half, second_half = t[:, :half], t[:, half:]
        s = sine * sign
        return jnp.concatenate(
            [first_half * cosine - second_half * s, second_half * cosine + first_half * s], axis=1
        )

    kv_raw = nn(h1, wq[:, W:])
    kv = jnp.concatenate([turn(kv_raw[:, :W], 1.0), kv_raw[:, W:]], axis=1).astype(bf16)
    up = [(i, i + 1) for i in range(B - 1)]
    down = [(i + 1, i) for i in range(B - 1)]
    kv_left = lax.ppermute(kv[S - H :], "dp", up)
    kv_right = lax.ppermute(kv[:H], "dp", down)
    q = (turn(nn(h1, wq[:, :W]), 1.0) * (1.0 / math.sqrt(head_width))).astype(bf16)
    wo_low = w_out.astype(bf16)
    w_in_late, w_down_late = after((w_in, w_down), kv)
    wd_low = w_down_late.astype(bf16)
    act_low, lin_low = w_in_late[:, 0].astype(bf16), w_in_late[:, 1].astype(bf16)
    if two:
        even = (b // 2) % 2 == 0
        in_send, wo_send, g_send = after(
            (
                lax.dynamic_index_in_dim(w_in, (b // 2) % 2, 1, keepdims=False).astype(bf16),
                wo_low,
                take(cotangent, 2 * (1 - r) + c, Sr // 2),
            ),
            cosine,
            wq_send,
        )
        in_got, wo_got, g_got = to_row(in_send), to_row(wo_send), to_row(g_send)
        wd_half = take(wd_low, (b // 2) % 2, F // 2)
        h1_y = relative(after(h1, kv), "zZyw")
        q, h1_y, sk_left, sk_right, act_low, lin_low, wd_half = lax.optimization_barrier(
            (q, h1_y, sk_left, sk_right, act_low, lin_low, wd_half)
        )

    state = attend_call(own_bounds, q, sq, [kv], [sk_own], heads)
    if two:
        kv_left, kv_right, in_got, wo_got, g_got, wd_half = after(
            (kv_left, kv_right, in_got, wo_got, g_got, wd_half), state
        )
        in_other, wd_got = to_z(in_got, 1), to_row(wd_half)
    o, lse = attend_call(
        halo_bounds, q, sq, [kv_left, kv_right], [sk_left, sk_right], heads, state
    )

    if two:
        o, wd_got, wo_got, g_got = lax.optimization_barrier((o, wd_got, wo_got, g_got))
        wo = own_first(jnp.concatenate([wo_low, wo_got], axis=1), 0)
    else:
        wo = gather(wo_low, 1)

    if two:
        o_got = to_row(take(o, 1 - r, Sr))
        o_rows = jnp.concatenate([take(o, r, Sr), o_got], axis=1)
        wd_other = to_z(wd_got, 1)
        wd_got = ordered(even, wd_got, wd_other, 0)
        g_got = ordered(zcol, g_got, to_col(g_got), 0)
        g_low = jnp.concatenate([take(cotangent, r, Sr), g_got], axis=1)
        g_low = jnp.where(take(live, r, Sr)[:, None], g_low, 0)
        wds = [wd_low, wd_got]
    else:
        o_rows = lax.all_to_all(o, "row", split_axis=0, concat_axis=1, tiled=True)
        own_g = jnp.where(live_column, cotangent, 0)
        g_low = lax.all_to_all(own_g, "row", split_axis=0, concat_axis=1, tiled=True)
        wds, acts, lins = [gather(wd_low, 1)], [gather(act_low, 0)], [gather(lin_low, 0)]

    def split_nn(a, parts):
        n = a.shape[1] // len(parts)
        return sum(nn(a[:, i * n : (i + 1) * n], w) for i, w in enumerate(parts))

    def split_nt(a, parts):
        n = a.shape[1] // len(parts)
        return sum(nt(a[:, i * n : (i + 1) * n], w) for i, w in enumerate(parts))

    def wide(parts):
        return parts[0] if len(parts) == 1 else jnp.concatenate(parts, axis=1)

    x_rows = take(x_low, r, Sr).astype(f32)
    if C == 2:
        o_all = jnp.concatenate([o_rows, to_col(o_rows)], axis=1)
        wo_all = jnp.concatenate([wo, to_col(wo)], axis=0)
        x1 = x_rows + nn(o_all, wo_all)
    else:
        x1 = x_rows + lax.psum(nn(o_rows, wo), "col")
    if two:
        in_got, in_other = after((in_got, in_other), o_got)
        act_got, lin_got = jnp.where(even, in_got, in_other), jnp.where(even, in_other, in_got)
        acts, lins = [act_low, act_got], [lin_low, lin_got]

    center = x1 - jnp.mean(x1, axis=-1, keepdims=True)
    inverse_two = lax.rsqrt(jnp.mean(center * center, axis=-1, keepdims=True) + epsilon)
    n2 = center * inverse_two
    h2 = (n2 * gain_two).astype(bf16)
    a = split_nn(h2, acts)
    u = split_nn(h2, lins)
    phi = 0.5 + 0.5 * lax.erf(a * math.sqrt(0.5))
    gelu = a * phi
    slope = phi + a * jnp.exp(-0.5 * a * a) * (1.0 / math.sqrt(2.0 * math.pi))
    m = (gelu * u).astype(bf16)
    y_part = wide([nn(m, w) for w in wds])
    if two:
        n = Sr // 2
        y_half = (
            take(x1, c, n) + take(y_part, c, n) + to_col(take(y_part, 1 - c, n).astype(bf16)).astype(f32)
        ).astype(bf16)
        y_got = to_row(y_half[:, Dl:])
    else:
        y = (x1 + col_sum(y_part)).astype(bf16)
        layer_out = lax.all_to_all(y, "row", split_axis=1, concat_axis=0, tiled=True)

    dm = split_nt(g_low, wds)
    da = (dm * u * slope).astype(bf16)
    du = (dm * gelu).astype(bf16)
    dh2_part = wide([nt(da, v) + nt(du, w) for v, w in zip(acts, lins)])
    dh2 = col_sum(dh2_part)
    if two:
        g_y = relative(after(g_low, dh2_part), "yzZx")
        lower_got = to_y(product(m, g_y))
    e2 = dh2 * gain_two
    dx1 = g_low.astype(f32) + inverse_two * (
        e2
        - jnp.mean(e2, axis=-1, keepdims=True)
        - n2 * jnp.mean(e2 * n2, axis=-1, keepdims=True)
    )
    dx_low = dx1.astype(bf16)
    do_rows = nt(dx_low, wo).astype(bf16)
    if two:
        do_got = to_row(do_rows[:, W:])
        do = ordered(zrow, do_rows[:, :W], do_got, 0)
    else:
        do = lax.all_to_all(do_rows, "row", split_axis=1, concat_axis=0, tiled=True)

    if two:
        h2, da, du, o_heads, dx_late = after((h2, da, du, own_first(o_rows, 1), dx_low), do_rows)
        dx_y = relative(dx_late, "yxzZ")
        h_x = relative(h2, "xyzZ")
        proj_got = to_y(product(o_heads, dx_y))
        gate_send = jnp.concatenate([product(da, h_x), product(du, h_x)], axis=0)
        gate_got = to_row(after(gate_send, do_got))
        pair = ordered(zrow, y_half[None, :, :Dl], after(y_got, gate_send)[None], 0)
        layer_out = ordered(zcol, pair[:, None], to_col(pair)[:, None], 1).reshape(S, Dl)
        lower = halved(m, g_y, after(lower_got, gate_send))
        lower_got = to_z(second(lower), 1)
        do, lower, layer_out = lax.optimization_barrier((do, lower, layer_out))

    dq_part, dkv_left, dkv_right = attend_back_call(
        halo_bounds, q, do, o, lse, sq, [kv_left, kv_right], [sk_left, sk_right], heads
    )
    from_right = lax.ppermute(dkv_left, "dp", down)
    from_left = lax.ppermute(dkv_right, "dp", up)
    if two:
        lower = joined(lower, after(lower_got, dq_part))
        lower_got = to_z(second(lower), 2)
        dq_part, lower = lax.optimization_barrier((dq_part, lower))
    dq, dkv = attend_back_call(own_bounds, q, do, o, lse, sq, [kv], [sk_own], heads, [dq_part])
    if two:
        gate_got = after(gate_got, dq)
        act, lin = halved(da, h_x, gate_got[:F]), halved(du, h_x, gate_got[F:])
        dkv, from_right, from_left, act, lin, proj_got, lower_got = lax.optimization_barrier(
            (dkv, from_right, from_left, act, lin, proj_got, lower_got)
        )
    pad = jnp.zeros((S - H, 2 * W), bf16)
    dkv = (
        dkv
        + jnp.concatenate([pad, from_right], axis=0).astype(f32)
        + jnp.concatenate([from_left, pad], axis=0).astype(f32)
    )
    dq = turn(dq * (1.0 / math.sqrt(head_width)), -1.0)
    dt = jnp.concatenate([dq, turn(dkv[:, :W], -1.0), dkv[:, W:]], axis=1).astype(bf16)
    dh1_part = nt(dt, wq)
    if two:
        query_send = product(dt, h1_y)
        query_got = to_z(query_send, 1)
        proj_got, lower_got = after((proj_got, lower_got), query_send, dh1_part)

    if two:
        n = S // 2
        kept = take(dh1_part, c, n) + to_col(take(dh1_part, 1 - c, n).astype(bf16)).astype(f32)
        xs = take(x_low, c, n).astype(f32)
        inv, mean = take(inverse_one, c, n), take(mean_one, c, n)
        n1 = (xs - mean) * inv
        e1 = kept * gain_one
        sums = jnp.stack([jnp.sum(e1, axis=-1), jnp.sum(e1 * n1, axis=-1)])
        sums = (sums + to_row(sums)) * (1.0 / D)
        moved = lax.ppermute(after(dx_low[:, Dl:], from_left), ("row", "col"), [(0, 2), (3, 1)])
        kept_send, moved = lax.optimization_barrier((kept[:, Dl:].astype(bf16), moved))
        mine = (kept[:, :Dl] + to_row(kept_send).astype(f32)) * gain_one[:Dl]
        base = jnp.where(r == c, dx1[:, :Dl], moved.astype(f32))
        dx = base + inv * (mine - sums[0][:, None] - n1[:, :Dl] * sums[1][:, None])
        dx = dx.astype(bf16)
        tokens_grad = ordered(zcol, dx, to_col(dx), 0)
    else:
        dh1 = lax.psum_scatter(col_sum(dh1_part), "row", scatter_dimension=1, tiled=True)
        xs = own_x.astype(f32)
        n1 = (xs - mean_one) * inverse_one
        e1 = dh1 * take(gain_attn, r, Dl)
        sums = lax.psum(jnp.stack([jnp.sum(e1, axis=-1), jnp.sum(e1 * n1, axis=-1)]), "row") / D
        base = lax.all_to_all(dx_low, "row", split_axis=1, concat_axis=0, tiled=True).astype(f32)
        tokens_grad = (
            base + inverse_one * (e1 - sums[0][:, None] - n1 * sums[1][:, None])
        ).astype(bf16)

    if two:
        def pair(one, other):
            return jnp.concatenate([second(one), second(other)], axis=0)

        def joined_pair(one, other, got):
            n = one.shape[0]
            return joined(one, got[:n]), joined(other, got[n:])

        gate_got = to_y(pair(act, lin))
        lower = joined(lower, lower_got)
        proj = halved(o_heads, dx_y, proj_got)
        proj = joined(proj, to_row(second(proj)))
        last_got = to_row(second(lower))
        query = halved(dt, h1_y, after(query_got, kept))
        query_got = to_z(second(query), 2)
        act, lin = joined_pair(act, lin, after(gate_got, query))
        gate_got = to_z(jnp.concatenate([second(act), second(lin), second(proj)], axis=0), 1)
        query = joined(query, after(query_got, act, lin, proj))
        query_got = to_y(second(query))
        n = 2 * F
        act, lin = joined_pair(act, lin, after(gate_got[:n], dx))
        proj = joined(proj, after(gate_got[n:], dx))
        gate_got = to_z(jnp.concatenate([second(act), second(lin), second(proj)], axis=0).T, 2).T
        query = joined(query, after(query_got, act, lin, proj))
        lower = joined(lower, after(last_got, dx))
        act, lin = joined_pair(act, lin, gate_got[:n])
        proj = joined(proj, gate_got[n:])
        gate = jnp.stack([act.T, lin.T])
        query = query.T
        wq_rows = take(wq, b ^ (4 * r), Db)
        place = (2 * b + r) ^ (8 * r)
        wi_rows = jnp.stack(
            [jnp.where(place < 8, *(take(w, place % 8, Dd) for w in ws)) for ws in after((acts, lins), kept)]
        )
    else:

        def scatter(grad):
            return lax.psum_scatter(grad, ("dp", "row"), scatter_dimension=1, tiled=True).astype(f32)

        gate = jnp.stack([scatter(tn(da, h2).astype(bf16)).T, scatter(tn(du, h2).astype(bf16)).T])
        proj = scatter(tn(o_rows, dx_low).astype(bf16))
        lower = scatter(tn(m, g_low).astype(bf16))
        query = lax.psum_scatter(
            tn(h1, dt).astype(bf16), "dp", scatter_dimension=0, tiled=True
        ).astype(f32)
        wq_rows = take(wq, b, Db)
        wi_rows = jnp.stack([take(acts[0], b * R + r, Dd), take(lins[0], b * R + r, Dd)])

    one_part = jnp.sum(query * wq_rows.astype(f32), axis=1)
    two_part = jnp.sum(jnp.sum(gate * wi_rows.astype(f32), axis=2), axis=0)
    natural = lax.dot_general(
        query, order.astype(f32), (((1,), (1,)), ((), ())),
        precision=lax.Precision.HIGHEST, preferred_element_type=f32,
    )
    if two:
        pair = jnp.concatenate([natural, jnp.broadcast_to(one_part[:, None], (Db, 128))], axis=1)
        pair = pair.reshape(2, Dd, 3 * W + 128)
        mine = lax.dynamic_index_in_dim(pair, r, 0, keepdims=False)
        theirs = to_row(lax.dynamic_index_in_dim(pair, 1 - r, 0, keepdims=False))
        theirs = after(theirs, tokens_grad)
        one_part = mine[:, 3 * W] + theirs[:, 3 * W]
        query_out = ordered(zrow, mine[:, : 3 * W], theirs[:, : 3 * W], 1)
    else:
        one_part = take(lax.psum(one_part, "row"), r, Dd)
        query_out = lax.all_to_all(natural, "row", split_axis=0, concat_axis=1, tiled=True)
    gains = jnp.stack([one_part, two_part])
    gains = gains + to_col(gains) if C == 2 else lax.psum(gains, "col")
    gain_attn_grad = gains[0] / take(gain_attn, b * R + r, Dd)
    gain_mlp_grad = gains[1] / take(gain_mlp, b * R + r, Dd)
    return (
        layer_out,
        tokens_grad,
        gain_attn_grad,
        query_out.reshape(Dd, R * heads, 3 * head_width),
        proj,
        gain_mlp_grad,
        jnp.swapaxes(gate, 0, 1),
        lower,
    )


def solution(mesh):
    return jax.shard_map(
        local,
        mesh=mesh,
        in_specs=(
            P("dp", "row"),
            P(),
            P("row", "col", None),
            P("col", "row"),
            P(),
            P("row", None, "col"),
            P("col", "row"),
            P("dp", "row"),
            P(),
            P(),
            P(),
        ),
        out_specs=(
            P("dp", "row"),
            P("dp", "row"),
            P(("dp", "row")),
            P(("dp", "row"), "col", None),
            P("col", ("dp", "row")),
            P(("dp", "row")),
            P(("dp", "row"), None, "col"),
            P("col", ("dp", "row")),
        ),
        check_vma=False,
    )
```

```python
import functools
import math

import jax
import jax.numpy as jnp
from jax import lax
from jax.experimental import pallas as pl
from jax.experimental.pallas import tpu as pltpu
from jax.sharding import PartitionSpec as P

LONGEST = 1024
BQ = 256
BK = 256
NEG = -1e30
FAR = 1e30
epsilon = 1e-05
rope_base = 160000.0
bf16 = jnp.bfloat16
f32 = jnp.float32
SWAP = [(0, 1), (1, 0)]


def nt(a, b):
    return lax.dot_general(a, b, (((1,), (1,)), ((), ())), preferred_element_type=f32)


def tn(a, b):
    return lax.dot_general(a, b, (((0,), (0,)), ((), ())), preferred_element_type=f32)


def nn(a, b):
    return jnp.dot(a, b, preferred_element_type=f32)


def after(a, *others):
    return lax.optimization_barrier((a, *others))[0]


def half_mask(width, heads, head):
    lane = lax.broadcasted_iota(jnp.int32, (1, width), 1)
    half = width // 2
    lane = jnp.where(lane >= half, lane - half, lane)
    step = half // heads
    return (lane >= head * step) & (lane < (head + 1) * step)


def whole_mask(width, heads, head):
    lane = lax.broadcasted_iota(jnp.int32, (1, width), 1)
    step = width // heads
    return (lane >= head * step) & (lane < (head + 1) * step)


def stack_heads(block, heads, mask_of):
    zero = jnp.zeros_like(block)
    width = block.shape[1]
    return jnp.concatenate(
        [jnp.where(mask_of(width, heads, h), block, zero) for h in range(heads)], axis=0
    )


def same_segment(key_seg, query_seg, heads):
    tile = key_seg
    lanes = query_seg.shape[1]
    if lanes > tile.shape[1]:
        tile = jnp.concatenate([tile] * (lanes // tile.shape[1]), axis=1)
    same = tile == query_seg
    return jnp.concatenate([same] * heads, axis=1) if heads > 1 else same


def forward_kernel(heads, sets, final, bounds, *refs):
    refs = list(refs)
    q_ref, sq_ref = refs[:2]
    kv_refs = refs[2 : 2 + sets]
    sk_refs = refs[2 + sets : 2 + 2 * sets]
    rest = refs[2 + 2 * sets :]
    if final:
        acc_in, ml_in, o_ref, lse_ref = rest[:4]
        acc, m_ref, l_ref = rest[4:7]
        vt_refs = rest[7:]
    else:
        acc, ml_ref = rest[:2]
        m_ref, l_ref = rest[2:4]
        vt_refs = rest[4:]
    step = pl.program_id(0)
    rows, width = q_ref.shape
    each = width // heads

    @pl.when(step == 0)
    def _():
        for kv, vt in zip(kv_refs, vt_refs):
            for j in range(kv.shape[0] // BK):
                vt[:, j * BK : (j + 1) * BK] = kv[j * BK : (j + 1) * BK, width:].T

    if final:
        acc[...] = acc_in[0]
        m_ref[...] = ml_in[0, 0:1]
        l_ref[...] = ml_in[0, 1:2]
    else:
        acc[...] = jnp.zeros_like(acc)
        m_ref[...] = jnp.full_like(m_ref, NEG)
        l_ref[...] = jnp.zeros_like(l_ref)
    queries = stack_heads(q_ref[...], heads, half_mask)
    query_seg = sq_ref[0]
    target = acc if final else acc.at[0]

    for s in range(sets):
        kv, sk, vt = kv_refs[s], sk_refs[s], vt_refs[s]

        def body(j, carry):
            first = pl.multiple_of(j * BK, BK)
            keys = kv[pl.ds(first, BK), 0:width]
            scores = nt(keys, queries)
            same = same_segment(sk[pl.ds(first, BK), :], query_seg, heads)
            scores = jnp.where(same, scores, NEG)
            before = m_ref[...]
            top = jnp.maximum(before, jnp.max(scores, axis=0, keepdims=True))
            raised = jnp.exp(scores - top)
            shrink = jnp.exp(before - top)
            m_ref[...] = top
            l_ref[...] = l_ref[...] * shrink + jnp.sum(raised, axis=0, keepdims=True)
            low = raised.astype(bf16)
            for h in range(heads):
                part = nn(
                    vt[h * each : (h + 1) * each, pl.ds(first, BK)],
                    low[:, h * rows : (h + 1) * rows],
                )
                hold = target[h * each : (h + 1) * each, :]
                target[h * each : (h + 1) * each, :] = (
                    hold * shrink[:, h * rows : (h + 1) * rows] + part
                )
            return carry

        lax.fori_loop(
            bounds[(step * sets + s) * 2], bounds[(step * sets + s) * 2 + 1], body, 0
        )

    if final:
        live = query_seg >= 0
        total = l_ref[...]
        live_all = jnp.concatenate([live] * heads, axis=1) if heads > 1 else live
        total = jnp.where(live_all, total, 1.0)
        inverse = jnp.where(live_all, 1.0 / total, 0.0)
        for h in range(heads):
            acc[h * each : (h + 1) * each, :] = (
                acc[h * each : (h + 1) * each, :] * inverse[:, h * rows : (h + 1) * rows]
            )
        o_ref[...] = acc[...].T.astype(bf16)
        lse_ref[0] = jnp.where(live_all, m_ref[...] + jnp.log(total), FAR)
    else:
        ml_ref[0, 0:1] = m_ref[...]
        ml_ref[0, 1:2] = l_ref[...]


def cost(products, q, kvs):
    pairs = q.shape[0]
    return pl.CostEstimate(
        flops=4 * products * pairs * q.shape[1],
        bytes_accessed=2 * sum(a.size for a in kvs) + 4 * q.size,
        transcendentals=4 * pairs,
    )


def whole(shape):
    zeros = (0,) * len(shape)
    return pl.BlockSpec(shape, lambda i, *_: zeros)


def attend_call(bounds, q, sq, kvs, sks, heads, state=None):
    count = q.shape[0] // BQ
    width = q.shape[1]
    sets = len(kvs)
    final = state is not None
    row_spec = pl.BlockSpec((BQ, width), lambda i, *_: (i, 0))
    acc_spec = pl.BlockSpec((1, width, BQ), lambda i, *_: (i, 0, 0))
    ml_spec = pl.BlockSpec((1, 2, heads * BQ), lambda i, *_: (i, 0, 0))
    in_specs = [row_spec, pl.BlockSpec((1, 1, BQ), lambda i, *_: (i, 0, 0))]
    in_specs += [whole(a.shape) for a in kvs] + [whole(a.shape) for a in sks]
    scratch = [pltpu.VMEM((1, heads * BQ), f32)] * 2
    scratch += [pltpu.VMEM((width, a.shape[0]), bf16) for a in kvs]
    if final:
        in_specs += [acc_spec, ml_spec]
        out_specs = [row_spec, pl.BlockSpec((1, 1, heads * BQ), lambda i, *_: (i, 0, 0))]
        out_shape = [
            jax.ShapeDtypeStruct(q.shape, bf16),
            jax.ShapeDtypeStruct((count, 1, heads * BQ), f32),
        ]
        scratch = [pltpu.VMEM((width, BQ), f32)] + scratch
    else:
        out_specs = [acc_spec, ml_spec]
        out_shape = [
            jax.ShapeDtypeStruct((count, width, BQ), f32),
            jax.ShapeDtypeStruct((count, 2, heads * BQ), f32),
        ]
    return pl.pallas_call(
        functools.partial(forward_kernel, heads, sets, final),
        grid_spec=pltpu.PrefetchScalarGridSpec(
            num_scalar_prefetch=1,
            grid=(count,),
            in_specs=in_specs,
            out_specs=out_specs,
            scratch_shapes=scratch,
        ),
        out_shape=out_shape,
        cost_estimate=cost(4, q, kvs),
        name="attend_final" if final else "attend_own",
    )(bounds, q, sq, *kvs, *sks, *(state or ()))


def backward_kernel(heads, sets, final, bounds, *refs):
    refs = list(refs)
    q_ref, do_ref, o_ref, lse_ref, sq_ref = refs[:5]
    kv_refs = refs[5 : 5 + sets]
    sk_refs = refs[5 + sets : 5 + 2 * sets]
    rest = refs[5 + 2 * sets :]
    if final:
        dq_in, dq_ref = rest[0], rest[1]
        dkv_refs = rest[2 : 2 + sets]
        dq_acc = rest[2 + sets]
        kt_refs = rest[3 + sets : 3 + 2 * sets]
        sums = dkv_refs
    else:
        dq_ref = rest[0]
        dkv_refs = rest[1 : 1 + sets]
        dq_acc = rest[1 + sets]
        kt_refs = rest[2 + sets : 2 + 2 * sets]
        sums = rest[2 + 2 * sets :]
    step = pl.program_id(0)
    rows, width = q_ref.shape
    each = width // heads
    half = width // 2
    piece = half // heads

    @pl.when(step == 0)
    def _():
        for kv, kt, total in zip(kv_refs, kt_refs, sums):
            total[...] = jnp.zeros_like(total)
            for j in range(kv.shape[0] // BK):
                kt[:, j * BK : (j + 1) * BK] = kv[j * BK : (j + 1) * BK, :width].T

    if final:
        dq_acc[...] = dq_in[0]
    else:
        dq_acc[...] = jnp.zeros_like(dq_acc)
    grads = do_ref[...]
    queries = stack_heads(q_ref[...], heads, half_mask)
    outs = stack_heads(grads, heads, whole_mask)
    query_seg = sq_ref[0]
    lse = lse_ref[0]
    product = (grads.astype(f32) * o_ref[...].astype(f32)).T
    delta = jnp.concatenate(
        [
            jnp.sum(product[h * each : (h + 1) * each], axis=0, keepdims=True)
            for h in range(heads)
        ],
        axis=1,
    )

    for s in range(sets):
        kv, sk, kt, total = kv_refs[s], sk_refs[s], kt_refs[s], sums[s]

        def body(j, carry):
            first = pl.multiple_of(j * BK, BK)
            keys = kv[pl.ds(first, BK), 0:width]
            values = kv[pl.ds(first, BK), width : 2 * width]
            scores = nt(keys, queries)
            same = same_segment(sk[pl.ds(first, BK), :], query_seg, heads)
            probs = jnp.where(same, jnp.exp(scores - lse), 0.0)
            grad_probs = nt(values, outs)
            grad_scores = (probs * (grad_probs - delta)).astype(bf16)
            low = probs.astype(bf16)
            total[pl.ds(first, BK), width : 2 * width] += nn(low, outs)
            total[pl.ds(first, BK), 0:width] += nn(grad_scores, queries)
            for h in range(heads):
                column = grad_scores[:, h * rows : (h + 1) * rows]
                for lead in (h * piece, half + h * piece):
                    dq_acc[lead : lead + piece, :] += nn(
                        kt[lead : lead + piece, pl.ds(first, BK)], column
                    )
            return carry

        lax.fori_loop(
            bounds[(step * sets + s) * 2], bounds[(step * sets + s) * 2 + 1], body, 0
        )

    if final:
        dq_ref[...] = dq_acc[...].T
    else:
        dq_ref[0] = dq_acc[...]

        @pl.when(step == pl.num_programs(0) - 1)
        def _():
            for total, out in zip(sums, dkv_refs):
                out[...] = total[...].astype(bf16)


def attend_back_call(bounds, q, do, o, lse, sq, kvs, sks, heads, state=None):
    count = q.shape[0] // BQ
    width = q.shape[1]
    sets = len(kvs)
    final = state is not None
    row_spec = pl.BlockSpec((BQ, width), lambda i, *_: (i, 0))
    acc_spec = pl.BlockSpec((1, width, BQ), lambda i, *_: (i, 0, 0))
    in_specs = [row_spec] * 3 + [
        pl.BlockSpec((1, 1, heads * BQ), lambda i, *_: (i, 0, 0)),
        pl.BlockSpec((1, 1, BQ), lambda i, *_: (i, 0, 0)),
    ]
    in_specs += [whole(a.shape) for a in kvs] + [whole(a.shape) for a in sks]
    scratch = [pltpu.VMEM((width, BQ), f32)]
    scratch += [pltpu.VMEM((width, a.shape[0]), bf16) for a in kvs]
    if final:
        in_specs += [acc_spec]
        out_specs = [row_spec]
        out_shape = [jax.ShapeDtypeStruct(q.shape, f32)]
    else:
        out_specs = [acc_spec]
        out_shape = [jax.ShapeDtypeStruct((count, width, BQ), f32)]
        scratch += [pltpu.VMEM(a.shape, f32) for a in kvs]
    out_specs += [whole(a.shape) for a in kvs]
    out_shape += [jax.ShapeDtypeStruct(a.shape, f32 if final else bf16) for a in kvs]
    return pl.pallas_call(
        functools.partial(backward_kernel, heads, sets, final),
        grid_spec=pltpu.PrefetchScalarGridSpec(
            num_scalar_prefetch=1,
            grid=(count,),
            in_specs=in_specs,
            out_specs=out_specs,
            scratch_shapes=scratch,
        ),
        out_shape=out_shape,
        cost_estimate=cost(10, q, kvs),
        name="back_own" if final else "back_halo",
    )(bounds, q, do, o, lse, sq, *kvs, *sks, *(state or ()))


def place_tables(seq_lengths, seq_offsets, first, count):
    place = first + jnp.arange(count, dtype=jnp.int32)
    ends = seq_offsets + seq_lengths
    inside = (place[:, None] >= seq_offsets[None, :]) & (place[:, None] < ends[None, :])
    live = jnp.any(inside, axis=1)
    index = jnp.arange(seq_offsets.shape[0], dtype=jnp.int32)
    segment = jnp.sum(jnp.where(inside, index[None, :], 0), axis=1)
    start = jnp.sum(jnp.where(inside, seq_offsets[None, :], 0), axis=1)
    end = jnp.sum(jnp.where(inside, ends[None, :], 0), axis=1)
    return live, segment, start, end, place


def qkv_order(heads, head_width):
    width = heads * head_width
    half = head_width // 2
    new = jnp.arange(3 * width, dtype=jnp.int32)
    kind = new // width
    inner = new % width
    side = inner // (width // 2)
    pair_head = (inner % (width // 2)) // half
    pair_old = pair_head * 3 * head_width + kind * head_width + side * half + inner % half
    value_old = (inner // head_width) * 3 * head_width + 2 * head_width + inner % head_width
    old = jnp.where(kind == 2, value_old, pair_old)
    return (old[None, :] == new[:, None]).astype(bf16)


def local(
    tokens,
    gain_attn,
    w_qkv,
    w_out,
    gain_mlp,
    w_in,
    w_down,
    cotangent,
    seq_lengths,
    seq_offsets,
    deal,
):
    R, C, B = lax.axis_size("row"), lax.axis_size("col"), lax.axis_size("dp")
    r, c, b = lax.axis_index("row"), lax.axis_index("col"), lax.axis_index("dp")
    S, Dl = tokens.shape
    D = Dl * R
    two = R == 2 and C == 2 and B == 8
    heads = w_qkv.shape[1] // R
    head_width = w_qkv.shape[2] // 3
    W = heads * head_width
    F = w_down.shape[0]
    H = LONGEST
    Sr = S // R
    zrow, zcol = (r == 0), (c == 0)

    def to_row(a):
        return lax.ppermute(a, "row", SWAP)

    def to_col(a):
        return lax.ppermute(a, "col", SWAP)

    def ordered(flag, mine, theirs, axis):
        return jnp.where(
            flag,
            jnp.concatenate([mine, theirs], axis=axis),
            jnp.concatenate([theirs, mine], axis=axis),
        )

    def own_first(a, axis):
        if not two:
            return a
        n = a.shape[axis] // 2
        return jnp.where(zrow, a, jnp.roll(a, n, axis=axis))

    def take(a, index, size, axis=0):
        return lax.dynamic_slice_in_dim(a, index * size, size, axis)

    def partner(a):
        n = a.shape[0] // 2
        got = to_row(take(a, c, n))
        return ordered(zcol, got, to_col(got), 0)

    def gather(a, axis):
        if two:
            return jnp.concatenate([a, to_row(a)], axis=axis)
        return lax.all_gather(a, "row", axis=axis, tiled=True)

    def col_sum(a):
        return a + to_col(a.astype(bf16)).astype(f32) if C == 2 else lax.psum(a, "col")

    live_x, seg_x, start_x, end_x, place_x = place_tables(seq_lengths, seq_offsets, b * S - H, S + 2 * H)
    key_seg = jnp.broadcast_to(jnp.where(live_x, seg_x, -2)[:, None], (S + 2 * H, 128))
    sk_left, sk_own, sk_right = key_seg[:H], key_seg[H : H + S], key_seg[H + S :]
    live = live_x[H : H + S]
    nq = S // BQ
    sq = jnp.where(live, seg_x[H : H + S], -1).reshape(nq, 1, BQ)
    first = jnp.min(jnp.where(live, start_x[H : H + S] - b * S, 4 * S).reshape(nq, BQ), axis=1)
    last = jnp.max(jnp.where(live, end_x[H : H + S] - b * S, -4 * S).reshape(nq, BQ), axis=1)
    own_low = jnp.clip(first, 0, S) // BK
    own_high = (jnp.clip(last, 0, S) + BK - 1) // BK
    left_low = jnp.clip(first + H, 0, H) // BK
    right_high = (jnp.clip(last - S, 0, H) + BK - 1) // BK
    own_bounds = jnp.stack([own_low, own_high], axis=1).reshape(-1).astype(jnp.int32)
    zero = jnp.zeros_like(left_low)
    halo_bounds = (
        jnp.stack([left_low, zero + H // BK, zero, right_high], axis=1).reshape(-1).astype(jnp.int32)
    )
    position = jnp.where(live, place_x[H : H + S] - start_x[H : H + S], 0)
    freq = rope_base ** (-(jnp.arange(0, head_width, 2, dtype=f32) / head_width))
    angle = position.astype(f32)[:, None] * jnp.tile(freq, heads)[None, :]
    cosine, sine = lax.optimization_barrier((jnp.cos(angle), jnp.sin(angle)))

    live_column = live[:, None]
    if two:
        x_got = partner(tokens)
        x_low = jnp.where(live_column, jnp.concatenate([tokens, x_got], axis=1), 0)
    else:
        own_x = jnp.where(live_column, tokens, 0)
        x_low = lax.all_gather(own_x, "row", axis=1, tiled=True)

    wq_low = w_qkv.reshape(Dl, R * 3 * W).astype(bf16)
    if two:
        wq_mine, wq_send = take(wq_low, r, 3 * W, 1), take(wq_low, 1 - r, 3 * W, 1)
        wq_got = to_row(wq_send)
    else:
        wq = lax.all_to_all(wq_low, "row", split_axis=1, concat_axis=0, tiled=True)
    order = qkv_order(heads, head_width)

    gain_one = own_first(gain_attn, 0)
    gain_two = own_first(gain_mlp, 0)

    Db = D // B
    Dd = D // (B * R)
    if two:
        y_bit, z_bits = b % 2, b // 2

        def relative(a, bits):
            n = jnp.arange(D, dtype=jnp.int32)
            rel = {"w": 0 * n, "x": 0 * n}
            for i, bit in enumerate(bits):
                rel[bit] = n // (D >> (i + 1)) % 2
            z_rel = 2 * rel["Z"] + rel["z"]
            column = ((z_bits ^ z_rel) * 2 + (y_bit ^ rel["y"])) * Db + n % Dd
            column = column + (rel["w"] if "w" in bits else r ^ rel["x"]) * Dd
            column = column ^ (r * (D // 2))
            return nn(a, (n[:, None] == column[None, :]).astype(bf16)).astype(bf16)

        def to_y(a):
            return lax.ppermute(a, "dp", [(i, i ^ 1) for i in range(B)])

        def to_z(a, j):
            return lax.ppermute(a, "dp", [(i, i ^ (2 * j)) for i in range(B)])

        def first(a):
            return a[:, : a.shape[1] // 2]

        def second(a):
            return a[:, a.shape[1] // 2 :].astype(bf16)

        def product(left, right):
            return tn(left, second(right)).astype(bf16)

        def halved(left, right, got):
            return tn(left, first(right)) + got.astype(f32)

        def joined(part, got):
            return first(part).astype(f32) + got.astype(f32)

    x = x_low.astype(f32)
    center = x - jnp.mean(x, axis=-1, keepdims=True)
    inverse_one = lax.rsqrt(jnp.mean(center * center, axis=-1, keepdims=True) + epsilon)
    mean_one = jnp.mean(x, axis=-1, keepdims=True)
    h1 = (center * inverse_one * gain_one).astype(bf16)
    if two:
        h1, wq_mine, wq_got = lax.optimization_barrier((h1, wq_mine, wq_got))
        wq = jnp.concatenate([wq_mine, wq_got], axis=0)
    wq = nn(wq, order).astype(bf16)

    half = W // 2

    def turn(t, sign):
        first_half, second_half = t[:, :half], t[:, half:]
        s = sine * sign
        return jnp.concatenate(
            [first_half * cosine - second_half * s, second_half * cosine + first_half * s], axis=1
        )

    kv_raw = nn(h1, wq[:, W:])
    kv = jnp.concatenate([turn(kv_raw[:, :W], 1.0), kv_raw[:, W:]], axis=1).astype(bf16)
    up = [(i, i + 1) for i in range(B - 1)]
    down = [(i + 1, i) for i in range(B - 1)]
    kv_left = lax.ppermute(kv[S - H :], "dp", up)
    kv_right = lax.ppermute(kv[:H], "dp", down)
    q = (turn(nn(h1, wq[:, :W]), 1.0) * (1.0 / math.sqrt(head_width))).astype(bf16)
    wo_low = w_out.astype(bf16)
    w_in_late, w_down_late = after((w_in, w_down), kv)
    wd_low = w_down_late.astype(bf16)
    act_low, lin_low = w_in_late[:, 0].astype(bf16), w_in_late[:, 1].astype(bf16)
    if two:
        even = (b // 2) % 2 == 0
        in_send, wo_send, g_send = after(
            (
                lax.dynamic_index_in_dim(w_in, (b // 2) % 2, 1, keepdims=False).astype(bf16),
                wo_low,
                take(cotangent, 2 * (1 - r) + c, Sr // 2),
            ),
            cosine,
            wq_send,
        )
        in_got, wo_got, g_got = to_row(in_send), to_row(wo_send), to_row(g_send)
        wd_half = take(wd_low, (b // 2) % 2, F // 2)
        h1_y = relative(after(h1, kv), "zyZw")
        q, h1_y, sk_left, sk_right, act_low, lin_low, wd_half = lax.optimization_barrier(
            (q, h1_y, sk_left, sk_right, act_low, lin_low, wd_half)
        )

    state = attend_call(own_bounds, q, sq, [kv], [sk_own], heads)
    if two:
        kv_left, kv_right, in_got, wo_got, g_got, wd_half = after(
            (kv_left, kv_right, in_got, wo_got, g_got, wd_half), state
        )
        in_other, wd_got = to_z(in_got, 1), to_row(wd_half)
    o, lse = attend_call(
        halo_bounds, q, sq, [kv_left, kv_right], [sk_left, sk_right], heads, state
    )

    if two:
        o, wd_got, wo_got, g_got = lax.optimization_barrier((o, wd_got, wo_got, g_got))
        wo = own_first(jnp.concatenate([wo_low, wo_got], axis=1), 0)
    else:
        wo = gather(wo_low, 1)

    if two:
        o_got = to_row(take(o, 1 - r, Sr))
        o_rows = jnp.concatenate([take(o, r, Sr), o_got], axis=1)
        wd_other = to_z(wd_got, 1)
        wd_got = ordered(even, wd_got, wd_other, 0)
        g_got = ordered(zcol, g_got, to_col(g_got), 0)
        g_low = jnp.concatenate([take(cotangent, r, Sr), g_got], axis=1)
        g_low = jnp.where(take(live, r, Sr)[:, None], g_low, 0)
        wds = [wd_low, wd_got]
    else:
        o_rows = lax.all_to_all(o, "row", split_axis=0, concat_axis=1, tiled=True)
        own_g = jnp.where(live_column, cotangent, 0)
        g_low = lax.all_to_all(own_g, "row", split_axis=0, concat_axis=1, tiled=True)
        wds, acts, lins = [gather(wd_low, 1)], [gather(act_low, 0)], [gather(lin_low, 0)]

    def split_nn(a, parts):
        n = a.shape[1] // len(parts)
        return sum(nn(a[:, i * n : (i + 1) * n], w) for i, w in enumerate(parts))

    def split_nt(a, parts):
        n = a.shape[1] // len(parts)
        return sum(nt(a[:, i * n : (i + 1) * n], w) for i, w in enumerate(parts))

    def wide(parts):
        return parts[0] if len(parts) == 1 else jnp.concatenate(parts, axis=1)

    x_rows = take(x_low, r, Sr).astype(f32)
    if C == 2:
        o_all = jnp.concatenate([o_rows, to_col(o_rows)], axis=1)
        wo_all = jnp.concatenate([wo, to_col(wo)], axis=0)
        x1 = x_rows + nn(o_all, wo_all)
    else:
        x1 = x_rows + lax.psum(nn(o_rows, wo), "col")
    if two:
        in_got, in_other = after((in_got, in_other), o_got)
        act_got, lin_got = jnp.where(even, in_got, in_other), jnp.where(even, in_other, in_got)
        acts, lins = [act_low, act_got], [lin_low, lin_got]

    center = x1 - jnp.mean(x1, axis=-1, keepdims=True)
    inverse_two = lax.rsqrt(jnp.mean(center * center, axis=-1, keepdims=True) + epsilon)
    n2 = center * inverse_two
    h2 = (n2 * gain_two).astype(bf16)
    a = split_nn(h2, acts)
    u = split_nn(h2, lins)
    phi = 0.5 + 0.5 * lax.erf(a * math.sqrt(0.5))
    gelu = a * phi
    slope = phi + a * jnp.exp(-0.5 * a * a) * (1.0 / math.sqrt(2.0 * math.pi))
    m = (gelu * u).astype(bf16)
    y_part = wide([nn(m, w) for w in wds])
    if two:
        n = Sr // 2
        y_half = (
            take(x1, c, n) + take(y_part, c, n) + to_col(take(y_part, 1 - c, n).astype(bf16)).astype(f32)
        ).astype(bf16)
        y_got = to_row(y_half[:, Dl:])
    else:
        y = (x1 + col_sum(y_part)).astype(bf16)
        layer_out = lax.all_to_all(y, "row", split_axis=1, concat_axis=0, tiled=True)

    dm = split_nt(g_low, wds)
    da = (dm * u * slope).astype(bf16)
    du = (dm * gelu).astype(bf16)
    dh2_part = wide([nt(da, v) + nt(du, w) for v, w in zip(acts, lins)])
    dh2 = col_sum(dh2_part)
    if two:
        g_y = relative(after(g_low, dh2_part), "yzZx")
        lower_got = to_y(product(m, g_y))
    e2 = dh2 * gain_two
    dx1 = g_low.astype(f32) + inverse_two * (
        e2
        - jnp.mean(e2, axis=-1, keepdims=True)
        - n2 * jnp.mean(e2 * n2, axis=-1, keepdims=True)
    )
    dx_low = dx1.astype(bf16)
    do_rows = nt(dx_low, wo).astype(bf16)
    if two:
        do_got = to_row(do_rows[:, W:])
        do = ordered(zrow, do_rows[:, :W], do_got, 0)
    else:
        do = lax.all_to_all(do_rows, "row", split_axis=1, concat_axis=0, tiled=True)

    if two:
        h2, da, du, o_heads, dx_late = after((h2, da, du, own_first(o_rows, 1), dx_low), do_rows)
        dx_y = relative(dx_late, "yxzZ")
        h_x = relative(h2, "xyzZ")
        proj_got = to_y(product(o_heads, dx_y))
        gate_send = jnp.concatenate([product(da, h_x), product(du, h_x)], axis=0)
        gate_got = to_row(after(gate_send, do_got))
        pair = ordered(zrow, y_half[None, :, :Dl], after(y_got, gate_send)[None], 0)
        layer_out = ordered(zcol, pair[:, None], to_col(pair)[:, None], 1).reshape(S, Dl)
        lower = halved(m, g_y, after(lower_got, gate_send))
        lower_got = to_z(second(lower), 1)
        do, lower, layer_out = lax.optimization_barrier((do, lower, layer_out))

    dq_part, dkv_left, dkv_right = attend_back_call(
        halo_bounds, q, do, o, lse, sq, [kv_left, kv_right], [sk_left, sk_right], heads
    )
    from_right = lax.ppermute(dkv_left, "dp", down)
    from_left = lax.ppermute(dkv_right, "dp", up)
    if two:
        lower = joined(lower, after(lower_got, dq_part))
        lower_got = to_z(second(lower), 2)
        dq_part, lower = lax.optimization_barrier((dq_part, lower))
    dq, dkv = attend_back_call(own_bounds, q, do, o, lse, sq, [kv], [sk_own], heads, [dq_part])
    if two:
        gate_got = after(gate_got, dq)
        act, lin = halved(da, h_x, gate_got[:F]), halved(du, h_x, gate_got[F:])
        dkv, from_right, from_left, act, lin, proj_got, lower_got = lax.optimization_barrier(
            (dkv, from_right, from_left, act, lin, proj_got, lower_got)
        )
    pad = jnp.zeros((S - H, 2 * W), bf16)
    dkv = (
        dkv
        + jnp.concatenate([pad, from_right], axis=0).astype(f32)
        + jnp.concatenate([from_left, pad], axis=0).astype(f32)
    )
    dq = turn(dq * (1.0 / math.sqrt(head_width)), -1.0)
    dt = jnp.concatenate([dq, turn(dkv[:, :W], -1.0), dkv[:, W:]], axis=1).astype(bf16)
    dh1_part = nt(dt, wq)
    if two:
        query_send = product(dt, h1_y)
        query_got = to_z(query_send, 1)
        proj_got, lower_got = after((proj_got, lower_got), query_send, dh1_part)

    if two:
        n = S // 2
        kept = take(dh1_part, c, n) + to_col(take(dh1_part, 1 - c, n).astype(bf16)).astype(f32)
        xs = take(x_low, c, n).astype(f32)
        inv, mean = take(inverse_one, c, n), take(mean_one, c, n)
        n1 = (xs - mean) * inv
        e1 = kept * gain_one
        sums = jnp.stack([jnp.sum(e1, axis=-1), jnp.sum(e1 * n1, axis=-1)])
        sums = (sums + to_row(sums)) * (1.0 / D)
        moved = lax.ppermute(after(dx_low[:, Dl:], from_left), ("row", "col"), [(0, 2), (3, 1)])
        kept_send, moved = lax.optimization_barrier((kept[:, Dl:].astype(bf16), moved))
        mine = (kept[:, :Dl] + to_row(kept_send).astype(f32)) * gain_one[:Dl]
        base = jnp.where(r == c, dx1[:, :Dl], moved.astype(f32))
        dx = base + inv * (mine - sums[0][:, None] - n1[:, :Dl] * sums[1][:, None])
        dx = dx.astype(bf16)
        tokens_grad = ordered(zcol, dx, to_col(dx), 0)
    else:
        dh1 = lax.psum_scatter(col_sum(dh1_part), "row", scatter_dimension=1, tiled=True)
        xs = own_x.astype(f32)
        n1 = (xs - mean_one) * inverse_one
        e1 = dh1 * take(gain_attn, r, Dl)
        sums = lax.psum(jnp.stack([jnp.sum(e1, axis=-1), jnp.sum(e1 * n1, axis=-1)]), "row") / D
        base = lax.all_to_all(dx_low, "row", split_axis=1, concat_axis=0, tiled=True).astype(f32)
        tokens_grad = (
            base + inverse_one * (e1 - sums[0][:, None] - n1 * sums[1][:, None])
        ).astype(bf16)

    if two:
        def pair(one, other):
            return jnp.concatenate([second(one), second(other)], axis=0)

        def joined_pair(one, other, got):
            n = one.shape[0]
            return joined(one, got[:n]), joined(other, got[n:])

        gate_got = to_y(pair(act, lin))
        lower = joined(lower, lower_got)
        proj = halved(o_heads, dx_y, proj_got)
        proj = joined(proj, to_row(second(proj)))
        last_got = to_row(second(lower))
        query = halved(dt, h1_y, after(query_got, kept))
        query_got = to_y(second(query))
        act, lin = joined_pair(act, lin, after(gate_got, query))
        gate_got = to_z(jnp.concatenate([second(act), second(lin), second(proj)], axis=0), 1)
        query = joined(query, after(query_got, act, lin, proj))
        query_got = to_z(second(query), 2)
        n = 2 * F
        act, lin = joined_pair(act, lin, after(gate_got[:n], dx))
        proj = joined(proj, after(gate_got[n:], dx))
        gate_got = to_z(jnp.concatenate([second(act), second(lin), second(proj)], axis=0).T, 2).T
        query = joined(query, after(query_got, act, lin, proj))
        lower = joined(lower, after(last_got, dx))
        act, lin = joined_pair(act, lin, gate_got[:n])
        proj = joined(proj, gate_got[n:])
        gate = jnp.stack([act.T, lin.T])
        query = query.T
        wq_rows = take(wq, b ^ (4 * r), Db)
        place = (2 * b + r) ^ (8 * r)
        wi_rows = jnp.stack(
            [jnp.where(place < 8, *(take(w, place % 8, Dd) for w in ws)) for ws in after((acts, lins), kept)]
        )
    else:

        def scatter(grad):
            return lax.psum_scatter(grad, ("dp", "row"), scatter_dimension=1, tiled=True).astype(f32)

        gate = jnp.stack([scatter(tn(da, h2).astype(bf16)).T, scatter(tn(du, h2).astype(bf16)).T])
        proj = scatter(tn(o_rows, dx_low).astype(bf16))
        lower = scatter(tn(m, g_low).astype(bf16))
        query = lax.psum_scatter(
            tn(h1, dt).astype(bf16), "dp", scatter_dimension=0, tiled=True
        ).astype(f32)
        wq_rows = take(wq, b, Db)
        wi_rows = jnp.stack([take(acts[0], b * R + r, Dd), take(lins[0], b * R + r, Dd)])

    one_part = jnp.sum(query * wq_rows.astype(f32), axis=1)
    two_part = jnp.sum(jnp.sum(gate * wi_rows.astype(f32), axis=2), axis=0)
    natural = lax.dot_general(
        query, order.astype(f32), (((1,), (1,)), ((), ())),
        precision=lax.Precision.HIGHEST, preferred_element_type=f32,
    )
    if two:
        pair = jnp.concatenate([natural, jnp.broadcast_to(one_part[:, None], (Db, 128))], axis=1)
        pair = pair.reshape(2, Dd, 3 * W + 128)
        mine = lax.dynamic_index_in_dim(pair, r, 0, keepdims=False)
        theirs = to_row(lax.dynamic_index_in_dim(pair, 1 - r, 0, keepdims=False))
        theirs = after(theirs, tokens_grad)
        one_part = mine[:, 3 * W] + theirs[:, 3 * W]
        query_out = ordered(zrow, mine[:, : 3 * W], theirs[:, : 3 * W], 1)
    else:
        one_part = take(lax.psum(one_part, "row"), r, Dd)
        query_out = lax.all_to_all(natural, "row", split_axis=0, concat_axis=1, tiled=True)
    gains = jnp.stack([one_part, two_part])
    gains = gains + to_col(gains) if C == 2 else lax.psum(gains, "col")
    gain_attn_grad = gains[0] / take(gain_attn, b * R + r, Dd)
    gain_mlp_grad = gains[1] / take(gain_mlp, b * R + r, Dd)
    return (
        layer_out,
        tokens_grad,
        gain_attn_grad,
        query_out.reshape(Dd, R * heads, 3 * head_width),
        proj,
        gain_mlp_grad,
        jnp.swapaxes(gate, 0, 1),
        lower,
    )


def solution(mesh):
    return jax.shard_map(
        local,
        mesh=mesh,
        in_specs=(
            P("dp", "row"),
            P(),
            P("row", "col", None),
            P("col", "row"),
            P(),
            P("row", None, "col"),
            P("col", "row"),
            P("dp", "row"),
            P(),
            P(),
            P(),
        ),
        out_specs=(
            P("dp", "row"),
            P("dp", "row"),
            P(("dp", "row")),
            P(("dp", "row"), "col", None),
            P("col", ("dp", "row")),
            P(("dp", "row")),
            P(("dp", "row"), None, "col"),
            P("col", ("dp", "row")),
        ),
        check_vma=False,
    )
```

```python
import functools
import math

import jax
import jax.numpy as jnp
from jax import lax
from jax.experimental import pallas as pl
from jax.experimental.pallas import tpu as pltpu
from jax.sharding import PartitionSpec as P

LONGEST = 1024
BQ = 256
BK = 256
NEG = -1e30
FAR = 1e30
epsilon = 1e-05
rope_base = 160000.0
bf16 = jnp.bfloat16
f32 = jnp.float32
SWAP = [(0, 1), (1, 0)]


def nt(a, b):
    return lax.dot_general(a, b, (((1,), (1,)), ((), ())), preferred_element_type=f32)


def tn(a, b):
    return lax.dot_general(a, b, (((0,), (0,)), ((), ())), preferred_element_type=f32)


def nn(a, b):
    return jnp.dot(a, b, preferred_element_type=f32)


def after(a, *others):
    return lax.optimization_barrier((a, *others))[0]


def half_mask(width, heads, head):
    lane = lax.broadcasted_iota(jnp.int32, (1, width), 1)
    half = width // 2
    lane = jnp.where(lane >= half, lane - half, lane)
    step = half // heads
    return (lane >= head * step) & (lane < (head + 1) * step)


def whole_mask(width, heads, head):
    lane = lax.broadcasted_iota(jnp.int32, (1, width), 1)
    step = width // heads
    return (lane >= head * step) & (lane < (head + 1) * step)


def stack_heads(block, heads, mask_of):
    zero = jnp.zeros_like(block)
    width = block.shape[1]
    return jnp.concatenate(
        [jnp.where(mask_of(width, heads, h), block, zero) for h in range(heads)], axis=0
    )


def same_segment(key_seg, query_seg, heads):
    tile = key_seg
    lanes = query_seg.shape[1]
    if lanes > tile.shape[1]:
        tile = jnp.concatenate([tile] * (lanes // tile.shape[1]), axis=1)
    same = tile == query_seg
    return jnp.concatenate([same] * heads, axis=1) if heads > 1 else same


def forward_kernel(heads, sets, final, bounds, *refs):
    refs = list(refs)
    q_ref, sq_ref = refs[:2]
    kv_refs = refs[2 : 2 + sets]
    sk_refs = refs[2 + sets : 2 + 2 * sets]
    rest = refs[2 + 2 * sets :]
    if final:
        acc_in, ml_in, o_ref, lse_ref = rest[:4]
        acc, m_ref, l_ref = rest[4:7]
        vt_refs = rest[7:]
    else:
        acc, ml_ref = rest[:2]
        m_ref, l_ref = rest[2:4]
        vt_refs = rest[4:]
    step = pl.program_id(0)
    rows, width = q_ref.shape
    each = width // heads

    @pl.when(step == 0)
    def _():
        for kv, vt in zip(kv_refs, vt_refs):
            for j in range(kv.shape[0] // BK):
                vt[:, j * BK : (j + 1) * BK] = kv[j * BK : (j + 1) * BK, width:].T

    if final:
        acc[...] = acc_in[0]
        m_ref[...] = ml_in[0, 0:1]
        l_ref[...] = ml_in[0, 1:2]
    else:
        acc[...] = jnp.zeros_like(acc)
        m_ref[...] = jnp.full_like(m_ref, NEG)
        l_ref[...] = jnp.zeros_like(l_ref)
    queries = stack_heads(q_ref[...], heads, half_mask)
    query_seg = sq_ref[0]
    target = acc if final else acc.at[0]

    for s in range(sets):
        kv, sk, vt = kv_refs[s], sk_refs[s], vt_refs[s]

        def body(j, carry):
            first = pl.multiple_of(j * BK, BK)
            keys = kv[pl.ds(first, BK), 0:width]
            scores = nt(keys, queries)
            same = same_segment(sk[pl.ds(first, BK), :], query_seg, heads)
            scores = jnp.where(same, scores, NEG)
            before = m_ref[...]
            top = jnp.maximum(before, jnp.max(scores, axis=0, keepdims=True))
            raised = jnp.exp(scores - top)
            shrink = jnp.exp(before - top)
            m_ref[...] = top
            l_ref[...] = l_ref[...] * shrink + jnp.sum(raised, axis=0, keepdims=True)
            low = raised.astype(bf16)
            for h in range(heads):
                part = nn(
                    vt[h * each : (h + 1) * each, pl.ds(first, BK)],
                    low[:, h * rows : (h + 1) * rows],
                )
                hold = target[h * each : (h + 1) * each, :]
                target[h * each : (h + 1) * each, :] = (
                    hold * shrink[:, h * rows : (h + 1) * rows] + part
                )
            return carry

        lax.fori_loop(
            bounds[(step * sets + s) * 2], bounds[(step * sets + s) * 2 + 1], body, 0
        )

    if final:
        live = query_seg >= 0
        total = l_ref[...]
        live_all = jnp.concatenate([live] * heads, axis=1) if heads > 1 else live
        total = jnp.where(live_all, total, 1.0)
        inverse = jnp.where(live_all, 1.0 / total, 0.0)
        for h in range(heads):
            acc[h * each : (h + 1) * each, :] = (
                acc[h * each : (h + 1) * each, :] * inverse[:, h * rows : (h + 1) * rows]
            )
        o_ref[...] = acc[...].T.astype(bf16)
        lse_ref[0] = jnp.where(live_all, m_ref[...] + jnp.log(total), FAR)
    else:
        ml_ref[0, 0:1] = m_ref[...]
        ml_ref[0, 1:2] = l_ref[...]


def cost(products, q, kvs):
    pairs = q.shape[0]
    return pl.CostEstimate(
        flops=4 * products * pairs * q.shape[1],
        bytes_accessed=2 * sum(a.size for a in kvs) + 4 * q.size,
        transcendentals=4 * pairs,
    )


def whole(shape):
    zeros = (0,) * len(shape)
    return pl.BlockSpec(shape, lambda i, *_: zeros)


def attend_call(bounds, q, sq, kvs, sks, heads, state=None):
    count = q.shape[0] // BQ
    width = q.shape[1]
    sets = len(kvs)
    final = state is not None
    row_spec = pl.BlockSpec((BQ, width), lambda i, *_: (i, 0))
    acc_spec = pl.BlockSpec((1, width, BQ), lambda i, *_: (i, 0, 0))
    ml_spec = pl.BlockSpec((1, 2, heads * BQ), lambda i, *_: (i, 0, 0))
    in_specs = [row_spec, pl.BlockSpec((1, 1, BQ), lambda i, *_: (i, 0, 0))]
    in_specs += [whole(a.shape) for a in kvs] + [whole(a.shape) for a in sks]
    scratch = [pltpu.VMEM((1, heads * BQ), f32)] * 2
    scratch += [pltpu.VMEM((width, a.shape[0]), bf16) for a in kvs]
    if final:
        in_specs += [acc_spec, ml_spec]
        out_specs = [row_spec, pl.BlockSpec((1, 1, heads * BQ), lambda i, *_: (i, 0, 0))]
        out_shape = [
            jax.ShapeDtypeStruct(q.shape, bf16),
            jax.ShapeDtypeStruct((count, 1, heads * BQ), f32),
        ]
        scratch = [pltpu.VMEM((width, BQ), f32)] + scratch
    else:
        out_specs = [acc_spec, ml_spec]
        out_shape = [
            jax.ShapeDtypeStruct((count, width, BQ), f32),
            jax.ShapeDtypeStruct((count, 2, heads * BQ), f32),
        ]
    return pl.pallas_call(
        functools.partial(forward_kernel, heads, sets, final),
        grid_spec=pltpu.PrefetchScalarGridSpec(
            num_scalar_prefetch=1,
            grid=(count,),
            in_specs=in_specs,
            out_specs=out_specs,
            scratch_shapes=scratch,
        ),
        out_shape=out_shape,
        cost_estimate=cost(4, q, kvs),
        name="attend_final" if final else "attend_own",
    )(bounds, q, sq, *kvs, *sks, *(state or ()))


def backward_kernel(heads, sets, final, bounds, *refs):
    refs = list(refs)
    q_ref, do_ref, o_ref, lse_ref, sq_ref = refs[:5]
    kv_refs = refs[5 : 5 + sets]
    sk_refs = refs[5 + sets : 5 + 2 * sets]
    rest = refs[5 + 2 * sets :]
    if final:
        dq_in, dq_ref = rest[0], rest[1]
        dkv_refs = rest[2 : 2 + sets]
        dq_acc = rest[2 + sets]
        kt_refs = rest[3 + sets : 3 + 2 * sets]
        sums = dkv_refs
    else:
        dq_ref = rest[0]
        dkv_refs = rest[1 : 1 + sets]
        dq_acc = rest[1 + sets]
        kt_refs = rest[2 + sets : 2 + 2 * sets]
        sums = rest[2 + 2 * sets :]
    step = pl.program_id(0)
    rows, width = q_ref.shape
    each = width // heads
    half = width // 2
    piece = half // heads

    @pl.when(step == 0)
    def _():
        for kv, kt, total in zip(kv_refs, kt_refs, sums):
            total[...] = jnp.zeros_like(total)
            for j in range(kv.shape[0] // BK):
                kt[:, j * BK : (j + 1) * BK] = kv[j * BK : (j + 1) * BK, :width].T

    if final:
        dq_acc[...] = dq_in[0]
    else:
        dq_acc[...] = jnp.zeros_like(dq_acc)
    grads = do_ref[...]
    queries = stack_heads(q_ref[...], heads, half_mask)
    outs = stack_heads(grads, heads, whole_mask)
    query_seg = sq_ref[0]
    lse = lse_ref[0]
    product = (grads.astype(f32) * o_ref[...].astype(f32)).T
    delta = jnp.concatenate(
        [
            jnp.sum(product[h * each : (h + 1) * each], axis=0, keepdims=True)
            for h in range(heads)
        ],
        axis=1,
    )

    for s in range(sets):
        kv, sk, kt, total = kv_refs[s], sk_refs[s], kt_refs[s], sums[s]

        def body(j, carry):
            first = pl.multiple_of(j * BK, BK)
            keys = kv[pl.ds(first, BK), 0:width]
            values = kv[pl.ds(first, BK), width : 2 * width]
            scores = nt(keys, queries)
            same = same_segment(sk[pl.ds(first, BK), :], query_seg, heads)
            probs = jnp.where(same, jnp.exp(scores - lse), 0.0)
            grad_probs = nt(values, outs)
            grad_scores = (probs * (grad_probs - delta)).astype(bf16)
            low = probs.astype(bf16)
            total[pl.ds(first, BK), width : 2 * width] += nn(low, outs)
            total[pl.ds(first, BK), 0:width] += nn(grad_scores, queries)
            for h in range(heads):
                column = grad_scores[:, h * rows : (h + 1) * rows]
                for lead in (h * piece, half + h * piece):
                    dq_acc[lead : lead + piece, :] += nn(
                        kt[lead : lead + piece, pl.ds(first, BK)], column
                    )
            return carry

        lax.fori_loop(
            bounds[(step * sets + s) * 2], bounds[(step * sets + s) * 2 + 1], body, 0
        )

    if final:
        dq_ref[...] = dq_acc[...].T
    else:
        dq_ref[0] = dq_acc[...]

        @pl.when(step == pl.num_programs(0) - 1)
        def _():
            for total, out in zip(sums, dkv_refs):
                out[...] = total[...].astype(bf16)


def attend_back_call(bounds, q, do, o, lse, sq, kvs, sks, heads, state=None):
    count = q.shape[0] // BQ
    width = q.shape[1]
    sets = len(kvs)
    final = state is not None
    row_spec = pl.BlockSpec((BQ, width), lambda i, *_: (i, 0))
    acc_spec = pl.BlockSpec((1, width, BQ), lambda i, *_: (i, 0, 0))
    in_specs = [row_spec] * 3 + [
        pl.BlockSpec((1, 1, heads * BQ), lambda i, *_: (i, 0, 0)),
        pl.BlockSpec((1, 1, BQ), lambda i, *_: (i, 0, 0)),
    ]
    in_specs += [whole(a.shape) for a in kvs] + [whole(a.shape) for a in sks]
    scratch = [pltpu.VMEM((width, BQ), f32)]
    scratch += [pltpu.VMEM((width, a.shape[0]), bf16) for a in kvs]
    if final:
        in_specs += [acc_spec]
        out_specs = [row_spec]
        out_shape = [jax.ShapeDtypeStruct(q.shape, f32)]
    else:
        out_specs = [acc_spec]
        out_shape = [jax.ShapeDtypeStruct((count, width, BQ), f32)]
        scratch += [pltpu.VMEM(a.shape, f32) for a in kvs]
    out_specs += [whole(a.shape) for a in kvs]
    out_shape += [jax.ShapeDtypeStruct(a.shape, f32 if final else bf16) for a in kvs]
    return pl.pallas_call(
        functools.partial(backward_kernel, heads, sets, final),
        grid_spec=pltpu.PrefetchScalarGridSpec(
            num_scalar_prefetch=1,
            grid=(count,),
            in_specs=in_specs,
            out_specs=out_specs,
            scratch_shapes=scratch,
        ),
        out_shape=out_shape,
        cost_estimate=cost(10, q, kvs),
        name="back_own" if final else "back_halo",
    )(bounds, q, do, o, lse, sq, *kvs, *sks, *(state or ()))


def place_tables(seq_lengths, seq_offsets, first, count):
    place = first + jnp.arange(count, dtype=jnp.int32)
    ends = seq_offsets + seq_lengths
    inside = (place[:, None] >= seq_offsets[None, :]) & (place[:, None] < ends[None, :])
    live = jnp.any(inside, axis=1)
    index = jnp.arange(seq_offsets.shape[0], dtype=jnp.int32)
    segment = jnp.sum(jnp.where(inside, index[None, :], 0), axis=1)
    start = jnp.sum(jnp.where(inside, seq_offsets[None, :], 0), axis=1)
    end = jnp.sum(jnp.where(inside, ends[None, :], 0), axis=1)
    return live, segment, start, end, place


def qkv_order(heads, head_width):
    width = heads * head_width
    half = head_width // 2
    new = jnp.arange(3 * width, dtype=jnp.int32)
    kind = new // width
    inner = new % width
    side = inner // (width // 2)
    pair_head = (inner % (width // 2)) // half
    pair_old = pair_head * 3 * head_width + kind * head_width + side * half + inner % half
    value_old = (inner // head_width) * 3 * head_width + 2 * head_width + inner % head_width
    old = jnp.where(kind == 2, value_old, pair_old)
    return (old[None, :] == new[:, None]).astype(bf16)


def local(
    tokens,
    gain_attn,
    w_qkv,
    w_out,
    gain_mlp,
    w_in,
    w_down,
    cotangent,
    seq_lengths,
    seq_offsets,
    deal,
):
    R, C, B = lax.axis_size("row"), lax.axis_size("col"), lax.axis_size("dp")
    r, c, b = lax.axis_index("row"), lax.axis_index("col"), lax.axis_index("dp")
    S, Dl = tokens.shape
    D = Dl * R
    two = R == 2 and C == 2 and B == 8
    heads = w_qkv.shape[1] // R
    head_width = w_qkv.shape[2] // 3
    W = heads * head_width
    F = w_down.shape[0]
    H = LONGEST
    Sr = S // R
    zrow, zcol = (r == 0), (c == 0)

    def to_row(a):
        return lax.ppermute(a, "row", SWAP)

    def to_col(a):
        return lax.ppermute(a, "col", SWAP)

    def ordered(flag, mine, theirs, axis):
        return jnp.where(
            flag,
            jnp.concatenate([mine, theirs], axis=axis),
            jnp.concatenate([theirs, mine], axis=axis),
        )

    def own_first(a, axis):
        if not two:
            return a
        n = a.shape[axis] // 2
        return jnp.where(zrow, a, jnp.roll(a, n, axis=axis))

    def take(a, index, size, axis=0):
        return lax.dynamic_slice_in_dim(a, index * size, size, axis)

    def partner(a):
        n = a.shape[0] // 2
        got = to_row(take(a, c, n))
        return ordered(zcol, got, to_col(got), 0)

    def gather(a, axis):
        if two:
            return jnp.concatenate([a, to_row(a)], axis=axis)
        return lax.all_gather(a, "row", axis=axis, tiled=True)

    def col_sum(a):
        return a + to_col(a.astype(bf16)).astype(f32) if C == 2 else lax.psum(a, "col")

    live_x, seg_x, start_x, end_x, place_x = place_tables(seq_lengths, seq_offsets, b * S - H, S + 2 * H)
    key_seg = jnp.broadcast_to(jnp.where(live_x, seg_x, -2)[:, None], (S + 2 * H, 128))
    sk_left, sk_own, sk_right = key_seg[:H], key_seg[H : H + S], key_seg[H + S :]
    live = live_x[H : H + S]
    nq = S // BQ
    sq = jnp.where(live, seg_x[H : H + S], -1).reshape(nq, 1, BQ)
    first = jnp.min(jnp.where(live, start_x[H : H + S] - b * S, 4 * S).reshape(nq, BQ), axis=1)
    last = jnp.max(jnp.where(live, end_x[H : H + S] - b * S, -4 * S).reshape(nq, BQ), axis=1)
    own_low = jnp.clip(first, 0, S) // BK
    own_high = (jnp.clip(last, 0, S) + BK - 1) // BK
    left_low = jnp.clip(first + H, 0, H) // BK
    right_high = (jnp.clip(last - S, 0, H) + BK - 1) // BK
    own_bounds = jnp.stack([own_low, own_high], axis=1).reshape(-1).astype(jnp.int32)
    zero = jnp.zeros_like(left_low)
    halo_bounds = (
        jnp.stack([left_low, zero + H // BK, zero, right_high], axis=1).reshape(-1).astype(jnp.int32)
    )
    position = jnp.where(live, place_x[H : H + S] - start_x[H : H + S], 0)
    freq = rope_base ** (-(jnp.arange(0, head_width, 2, dtype=f32) / head_width))
    angle = position.astype(f32)[:, None] * jnp.tile(freq, heads)[None, :]
    cosine, sine = lax.optimization_barrier((jnp.cos(angle), jnp.sin(angle)))

    live_column = live[:, None]
    if two:
        x_got = partner(tokens)
        x_low = jnp.where(live_column, jnp.concatenate([tokens, x_got], axis=1), 0)
    else:
        own_x = jnp.where(live_column, tokens, 0)
        x_low = lax.all_gather(own_x, "row", axis=1, tiled=True)

    wq_low = w_qkv.reshape(Dl, R * 3 * W).astype(bf16)
    if two:
        wq_mine, wq_send = take(wq_low, r, 3 * W, 1), take(wq_low, 1 - r, 3 * W, 1)
        wq_got = to_row(wq_send)
    else:
        wq = lax.all_to_all(wq_low, "row", split_axis=1, concat_axis=0, tiled=True)
    order = qkv_order(heads, head_width)

    gain_one = own_first(gain_attn, 0)
    gain_two = own_first(gain_mlp, 0)

    Db = D // B
    Dd = D // (B * R)
    if two:
        y_bit, z_bits = b % 2, b // 2

        def relative(a, bits):
            n = jnp.arange(D, dtype=jnp.int32)
            rel = {"w": 0 * n, "x": 0 * n}
            for i, bit in enumerate(bits):
                rel[bit] = n // (D >> (i + 1)) % 2
            z_rel = 2 * rel["Z"] + rel["z"]
            column = ((z_bits ^ z_rel) * 2 + (y_bit ^ rel["y"])) * Db + n % Dd
            column = column + (rel["w"] if "w" in bits else r ^ rel["x"]) * Dd
            column = column ^ (r * (D // 2))
            return nn(a, (n[:, None] == column[None, :]).astype(bf16)).astype(bf16)

        def to_y(a):
            return lax.ppermute(a, "dp", [(i, i ^ 1) for i in range(B)])

        def to_z(a, j):
            return lax.ppermute(a, "dp", [(i, i ^ (2 * j)) for i in range(B)])

        def first(a):
            return a[:, : a.shape[1] // 2]

        def second(a):
            return a[:, a.shape[1] // 2 :].astype(bf16)

        def product(left, right):
            return tn(left, second(right)).astype(bf16)

        def halved(left, right, got):
            return tn(left, first(right)) + got.astype(f32)

        def joined(part, got):
            return first(part).astype(f32) + got.astype(f32)

    x = x_low.astype(f32)
    center = x - jnp.mean(x, axis=-1, keepdims=True)
    inverse_one = lax.rsqrt(jnp.mean(center * center, axis=-1, keepdims=True) + epsilon)
    mean_one = jnp.mean(x, axis=-1, keepdims=True)
    h1 = (center * inverse_one * gain_one).astype(bf16)
    if two:
        h1, wq_mine, wq_got = lax.optimization_barrier((h1, wq_mine, wq_got))
        wq = jnp.concatenate([wq_mine, wq_got], axis=0)
    wq = nn(wq, order).astype(bf16)

    half = W // 2

    def turn(t, sign):
        first_half, second_half = t[:, :half], t[:, half:]
        s = sine * sign
        return jnp.concatenate(
            [first_half * cosine - second_half * s, second_half * cosine + first_half * s], axis=1
        )

    kv_raw = nn(h1, wq[:, W:])
    kv = jnp.concatenate([turn(kv_raw[:, :W], 1.0), kv_raw[:, W:]], axis=1).astype(bf16)
    up = [(i, i + 1) for i in range(B - 1)]
    down = [(i + 1, i) for i in range(B - 1)]
    kv_left = lax.ppermute(kv[S - H :], "dp", up)
    kv_right = lax.ppermute(kv[:H], "dp", down)
    q = (turn(nn(h1, wq[:, :W]), 1.0) * (1.0 / math.sqrt(head_width))).astype(bf16)
    wo_low = w_out.astype(bf16)
    w_in_late, w_down_late = after((w_in, w_down), kv)
    wd_low = w_down_late.astype(bf16)
    act_low, lin_low = w_in_late[:, 0].astype(bf16), w_in_late[:, 1].astype(bf16)
    if two:
        even = (b // 2) % 2 == 0
        in_send, wo_send, g_send = after(
            (
                lax.dynamic_index_in_dim(w_in, (b // 2) % 2, 1, keepdims=False).astype(bf16),
                wo_low,
                take(cotangent, 2 * (1 - r) + c, Sr // 2),
            ),
            cosine,
            wq_send,
        )
        in_got, wo_got, g_got = to_row(in_send), to_row(wo_send), to_row(g_send)
        wd_half = take(wd_low, (b // 2) % 2, F // 2)
        h1_y = relative(after(h1, kv), "zyZw")
        q, h1_y, sk_left, sk_right, act_low, lin_low, wd_half = lax.optimization_barrier(
            (q, h1_y, sk_left, sk_right, act_low, lin_low, wd_half)
        )

    state = attend_call(own_bounds, q, sq, [kv], [sk_own], heads)
    if two:
        kv_left, kv_right, in_got, wo_got, g_got, wd_half = after(
            (kv_left, kv_right, in_got, wo_got, g_got, wd_half), state
        )
        in_other, wd_got = to_z(in_got, 1), to_row(wd_half)
    o, lse = attend_call(
        halo_bounds, q, sq, [kv_left, kv_right], [sk_left, sk_right], heads, state
    )

    if two:
        o, wd_got, wo_got, g_got = lax.optimization_barrier((o, wd_got, wo_got, g_got))
        wo = own_first(jnp.concatenate([wo_low, wo_got], axis=1), 0)
    else:
        wo = gather(wo_low, 1)

    if two:
        o_got = to_row(take(o, 1 - r, Sr))
        o_rows = jnp.concatenate([take(o, r, Sr), o_got], axis=1)
        wd_other = to_z(wd_got, 1)
        wd_got = ordered(even, wd_got, wd_other, 0)
        g_got = ordered(zcol, g_got, to_col(g_got), 0)
        g_low = jnp.concatenate([take(cotangent, r, Sr), g_got], axis=1)
        g_low = jnp.where(take(live, r, Sr)[:, None], g_low, 0)
        wds = [wd_low, wd_got]
    else:
        o_rows = lax.all_to_all(o, "row", split_axis=0, concat_axis=1, tiled=True)
        own_g = jnp.where(live_column, cotangent, 0)
        g_low = lax.all_to_all(own_g, "row", split_axis=0, concat_axis=1, tiled=True)
        wds, acts, lins = [gather(wd_low, 1)], [gather(act_low, 0)], [gather(lin_low, 0)]

    def split_nn(a, parts):
        n = a.shape[1] // len(parts)
        return sum(nn(a[:, i * n : (i + 1) * n], w) for i, w in enumerate(parts))

    def split_nt(a, parts):
        n = a.shape[1] // len(parts)
        return sum(nt(a[:, i * n : (i + 1) * n], w) for i, w in enumerate(parts))

    def wide(parts):
        return parts[0] if len(parts) == 1 else jnp.concatenate(parts, axis=1)

    x_rows = take(x_low, r, Sr).astype(f32)
    if C == 2:
        o_all = jnp.concatenate([o_rows, to_col(o_rows)], axis=1)
        wo_all = jnp.concatenate([wo, to_col(wo)], axis=0)
        x1 = x_rows + nn(o_all, wo_all)
    else:
        x1 = x_rows + lax.psum(nn(o_rows, wo), "col")
    if two:
        in_got, in_other = after((in_got, in_other), o_got)
        act_got, lin_got = jnp.where(even, in_got, in_other), jnp.where(even, in_other, in_got)
        acts, lins = [act_low, act_got], [lin_low, lin_got]

    center = x1 - jnp.mean(x1, axis=-1, keepdims=True)
    inverse_two = lax.rsqrt(jnp.mean(center * center, axis=-1, keepdims=True) + epsilon)
    n2 = center * inverse_two
    h2 = (n2 * gain_two).astype(bf16)
    a = split_nn(h2, acts)
    u = split_nn(h2, lins)
    phi = 0.5 + 0.5 * lax.erf(a * math.sqrt(0.5))
    gelu = a * phi
    slope = phi + a * jnp.exp(-0.5 * a * a) * (1.0 / math.sqrt(2.0 * math.pi))
    m = (gelu * u).astype(bf16)
    y_part = wide([nn(m, w) for w in wds])
    if two:
        n = Sr // 2
        y_half = (
            take(x1, c, n) + take(y_part, c, n) + to_col(take(y_part, 1 - c, n).astype(bf16)).astype(f32)
        ).astype(bf16)
        y_got = to_row(y_half[:, Dl:])
    else:
        y = (x1 + col_sum(y_part)).astype(bf16)
        layer_out = lax.all_to_all(y, "row", split_axis=1, concat_axis=0, tiled=True)

    dm = split_nt(g_low, wds)
    da = (dm * u * slope).astype(bf16)
    du = (dm * gelu).astype(bf16)
    dh2_part = wide([nt(da, v) + nt(du, w) for v, w in zip(acts, lins)])
    dh2 = col_sum(dh2_part)
    if two:
        g_y = relative(after(g_low, dh2_part), "yzZx")
        lower_got = to_y(product(m, g_y))
    e2 = dh2 * gain_two
    dx1 = g_low.astype(f32) + inverse_two * (
        e2
        - jnp.mean(e2, axis=-1, keepdims=True)
        - n2 * jnp.mean(e2 * n2, axis=-1, keepdims=True)
    )
    dx_low = dx1.astype(bf16)
    do_rows = nt(dx_low, wo).astype(bf16)
    if two:
        do_got = to_row(do_rows[:, W:])
        do = ordered(zrow, do_rows[:, :W], do_got, 0)
    else:
        do = lax.all_to_all(do_rows, "row", split_axis=1, concat_axis=0, tiled=True)

    if two:
        h2, da, du, o_heads, dx_late = after((h2, da, du, own_first(o_rows, 1), dx_low), do_rows)
        dx_y = relative(dx_late, "xyzZ")
        h_x = relative(h2, "xyzZ")
        gate_send = jnp.concatenate([product(da, h_x), product(du, h_x), product(o_heads, dx_y)], axis=0)
        gate_got = to_row(after(gate_send, do_got))
        pair = ordered(zrow, y_half[None, :, :Dl], after(y_got, gate_send)[None], 0)
        layer_out = ordered(zcol, pair[:, None], to_col(pair)[:, None], 1).reshape(S, Dl)
        do, layer_out = lax.optimization_barrier((do, layer_out))

    dq_part, dkv_left, dkv_right = attend_back_call(
        halo_bounds, q, do, o, lse, sq, [kv_left, kv_right], [sk_left, sk_right], heads
    )
    from_right = lax.ppermute(dkv_left, "dp", down)
    from_left = lax.ppermute(dkv_right, "dp", up)
    if two:
        lower = halved(m, g_y, after(lower_got, dq_part))
        lower_got = to_z(second(lower), 1)
        dq_part, lower = lax.optimization_barrier((dq_part, lower))
    dq, dkv = attend_back_call(own_bounds, q, do, o, lse, sq, [kv], [sk_own], heads, [dq_part])
    if two:
        gate_got = after(gate_got, dq)
        act, lin = halved(da, h_x, gate_got[:F]), halved(du, h_x, gate_got[F : 2 * F])
        proj = halved(o_heads, dx_y, gate_got[2 * F :])
        dkv, from_right, from_left, act, lin, proj, lower_got = lax.optimization_barrier(
            (dkv, from_right, from_left, act, lin, proj, lower_got)
        )
    pad = jnp.zeros((S - H, 2 * W), bf16)
    dkv = (
        dkv
        + jnp.concatenate([pad, from_right], axis=0).astype(f32)
        + jnp.concatenate([from_left, pad], axis=0).astype(f32)
    )
    dq = turn(dq * (1.0 / math.sqrt(head_width)), -1.0)
    dt = jnp.concatenate([dq, turn(dkv[:, :W], -1.0), dkv[:, W:]], axis=1).astype(bf16)
    dh1_part = nt(dt, wq)
    if two:
        query_send = product(dt, h1_y)
        query_got = to_z(query_send, 1)
        lower_got = after(lower_got, query_send, dh1_part)

    if two:
        n = S // 2
        kept = take(dh1_part, c, n) + to_col(take(dh1_part, 1 - c, n).astype(bf16)).astype(f32)
        xs = take(x_low, c, n).astype(f32)
        inv, mean = take(inverse_one, c, n), take(mean_one, c, n)
        n1 = (xs - mean) * inv
        e1 = kept * gain_one
        sums = jnp.stack([jnp.sum(e1, axis=-1), jnp.sum(e1 * n1, axis=-1)])
        sums = (sums + to_row(sums)) * (1.0 / D)
        moved = lax.ppermute(after(dx_low[:, Dl:], from_left), ("row", "col"), [(0, 2), (3, 1)])
        kept_send, moved = lax.optimization_barrier((kept[:, Dl:].astype(bf16), moved))
        mine = (kept[:, :Dl] + to_row(kept_send).astype(f32)) * gain_one[:Dl]
        base = jnp.where(r == c, dx1[:, :Dl], moved.astype(f32))
        dx = base + inv * (mine - sums[0][:, None] - n1[:, :Dl] * sums[1][:, None])
        dx = dx.astype(bf16)
        tokens_grad = ordered(zcol, dx, to_col(dx), 0)
    else:
        dh1 = lax.psum_scatter(col_sum(dh1_part), "row", scatter_dimension=1, tiled=True)
        xs = own_x.astype(f32)
        n1 = (xs - mean_one) * inverse_one
        e1 = dh1 * take(gain_attn, r, Dl)
        sums = lax.psum(jnp.stack([jnp.sum(e1, axis=-1), jnp.sum(e1 * n1, axis=-1)]), "row") / D
        base = lax.all_to_all(dx_low, "row", split_axis=1, concat_axis=0, tiled=True).astype(f32)
        tokens_grad = (
            base + inverse_one * (e1 - sums[0][:, None] - n1 * sums[1][:, None])
        ).astype(bf16)

    if two:
        def three(*parts):
            return jnp.concatenate([second(a) for a in parts], axis=0)

        def joined_three(parts, got):
            n = F
            return [joined(a, g) for a, g in zip(parts, (got[:n], got[n : 2 * n], got[2 * n :]))]

        gate_got = to_y(three(act, lin, proj))
        lower = joined(lower, lower_got)
        lower_got = to_z(second(lower), 2)
        query = halved(dt, h1_y, after(query_got, kept))
        query_got = to_y(second(query))
        act, lin, proj = joined_three((act, lin, proj), after(gate_got, query))
        gate_got = to_z(three(act, lin, proj), 1)
        lower = joined(lower, after(lower_got, act, lin, proj))
        last_got = to_row(second(lower))
        query = joined(query, after(query_got, act, lin, proj))
        query_got = to_z(second(query), 2)
        act, lin, proj = joined_three((act, lin, proj), after(gate_got, dx))
        gate_got = to_z(three(act, lin, proj).T, 2).T
        query = joined(query, after(query_got, act, lin, proj))
        lower = joined(lower, after(last_got, dx))
        act, lin, proj = joined_three((act, lin, proj), gate_got)
        gate = jnp.stack([act.T, lin.T])
        query = query.T
        wq_rows = take(wq, b ^ (4 * r), Db)
        place = (2 * b + r) ^ (8 * r)
        wi_rows = jnp.stack(
            [jnp.where(place < 8, *(take(w, place % 8, Dd) for w in ws)) for ws in after((acts, lins), kept)]
        )
    else:

        def scatter(grad):
            return lax.psum_scatter(grad, ("dp", "row"), scatter_dimension=1, tiled=True).astype(f32)

        gate = jnp.stack([scatter(tn(da, h2).astype(bf16)).T, scatter(tn(du, h2).astype(bf16)).T])
        proj = scatter(tn(o_rows, dx_low).astype(bf16))
        lower = scatter(tn(m, g_low).astype(bf16))
        query = lax.psum_scatter(
            tn(h1, dt).astype(bf16), "dp", scatter_dimension=0, tiled=True
        ).astype(f32)
        wq_rows = take(wq, b, Db)
        wi_rows = jnp.stack([take(acts[0], b * R + r, Dd), take(lins[0], b * R + r, Dd)])

    one_part = jnp.sum(query * wq_rows.astype(f32), axis=1)
    two_part = jnp.sum(jnp.sum(gate * wi_rows.astype(f32), axis=2), axis=0)
    natural = lax.dot_general(
        query, order.astype(f32), (((1,), (1,)), ((), ())),
        precision=lax.Precision.HIGHEST, preferred_element_type=f32,
    )
    if two:
        pair = jnp.concatenate([natural, jnp.broadcast_to(one_part[:, None], (Db, 128))], axis=1)
        pair = pair.reshape(2, Dd, 3 * W + 128)
        mine = lax.dynamic_index_in_dim(pair, r, 0, keepdims=False)
        theirs = to_row(lax.dynamic_index_in_dim(pair, 1 - r, 0, keepdims=False))
        theirs = after(theirs, tokens_grad)
        one_part = mine[:, 3 * W] + theirs[:, 3 * W]
        query_out = ordered(zrow, mine[:, : 3 * W], theirs[:, : 3 * W], 1)
    else:
        one_part = take(lax.psum(one_part, "row"), r, Dd)
        query_out = lax.all_to_all(natural, "row", split_axis=0, concat_axis=1, tiled=True)
    gains = jnp.stack([one_part, two_part])
    gains = gains + to_col(gains) if C == 2 else lax.psum(gains, "col")
    gain_attn_grad = gains[0] / take(gain_attn, b * R + r, Dd)
    gain_mlp_grad = gains[1] / take(gain_mlp, b * R + r, Dd)
    return (
        layer_out,
        tokens_grad,
        gain_attn_grad,
        query_out.reshape(Dd, R * heads, 3 * head_width),
        proj,
        gain_mlp_grad,
        jnp.swapaxes(gate, 0, 1),
        lower,
    )


def solution(mesh):
    return jax.shard_map(
        local,
        mesh=mesh,
        in_specs=(
            P("dp", "row"),
            P(),
            P("row", "col", None),
            P("col", "row"),
            P(),
            P("row", None, "col"),
            P("col", "row"),
            P("dp", "row"),
            P(),
            P(),
            P(),
        ),
        out_specs=(
            P("dp", "row"),
            P("dp", "row"),
            P(("dp", "row")),
            P(("dp", "row"), "col", None),
            P("col", ("dp", "row")),
            P(("dp", "row")),
            P(("dp", "row"), None, "col"),
            P("col", ("dp", "row")),
        ),
        check_vma=False,
    )
```

```python
import functools
import math

import jax
import jax.numpy as jnp
from jax import lax
from jax.experimental import pallas as pl
from jax.experimental.pallas import tpu as pltpu
from jax.sharding import PartitionSpec as P

LONGEST = 1024
BQ = 256
BK = 256
NEG = -1e30
FAR = 1e30
epsilon = 1e-05
rope_base = 160000.0
bf16 = jnp.bfloat16
f32 = jnp.float32
SWAP = [(0, 1), (1, 0)]


def nt(a, b):
    return lax.dot_general(a, b, (((1,), (1,)), ((), ())), preferred_element_type=f32)


def tn(a, b):
    return lax.dot_general(a, b, (((0,), (0,)), ((), ())), preferred_element_type=f32)


def nn(a, b):
    return jnp.dot(a, b, preferred_element_type=f32)


def after(a, *others):
    return lax.optimization_barrier((a, *others))[0]


def half_mask(width, heads, head):
    lane = lax.broadcasted_iota(jnp.int32, (1, width), 1)
    half = width // 2
    lane = jnp.where(lane >= half, lane - half, lane)
    step = half // heads
    return (lane >= head * step) & (lane < (head + 1) * step)


def whole_mask(width, heads, head):
    lane = lax.broadcasted_iota(jnp.int32, (1, width), 1)
    step = width // heads
    return (lane >= head * step) & (lane < (head + 1) * step)


def stack_heads(block, heads, mask_of):
    zero = jnp.zeros_like(block)
    width = block.shape[1]
    return jnp.concatenate(
        [jnp.where(mask_of(width, heads, h), block, zero) for h in range(heads)], axis=0
    )


def same_segment(key_seg, query_seg, heads):
    tile = key_seg
    lanes = query_seg.shape[1]
    if lanes > tile.shape[1]:
        tile = jnp.concatenate([tile] * (lanes // tile.shape[1]), axis=1)
    same = tile == query_seg
    return jnp.concatenate([same] * heads, axis=1) if heads > 1 else same


def forward_kernel(heads, sets, final, bounds, *refs):
    refs = list(refs)
    q_ref, sq_ref = refs[:2]
    kv_refs = refs[2 : 2 + sets]
    sk_refs = refs[2 + sets : 2 + 2 * sets]
    rest = refs[2 + 2 * sets :]
    if final:
        acc_in, ml_in, o_ref, lse_ref = rest[:4]
        acc, m_ref, l_ref = rest[4:7]
        vt_refs = rest[7:]
    else:
        acc, ml_ref = rest[:2]
        m_ref, l_ref = rest[2:4]
        vt_refs = rest[4:]
    step = pl.program_id(0)
    rows, width = q_ref.shape
    each = width // heads

    @pl.when(step == 0)
    def _():
        for kv, vt in zip(kv_refs, vt_refs):
            for j in range(kv.shape[0] // BK):
                vt[:, j * BK : (j + 1) * BK] = kv[j * BK : (j + 1) * BK, width:].T

    if final:
        acc[...] = acc_in[0]
        m_ref[...] = ml_in[0, 0:1]
        l_ref[...] = ml_in[0, 1:2]
    else:
        acc[...] = jnp.zeros_like(acc)
        m_ref[...] = jnp.full_like(m_ref, NEG)
        l_ref[...] = jnp.zeros_like(l_ref)
    queries = stack_heads(q_ref[...], heads, half_mask)
    query_seg = sq_ref[0]
    target = acc if final else acc.at[0]

    for s in range(sets):
        kv, sk, vt = kv_refs[s], sk_refs[s], vt_refs[s]

        def body(j, carry):
            first = pl.multiple_of(j * BK, BK)
            keys = kv[pl.ds(first, BK), 0:width]
            scores = nt(keys, queries)
            same = same_segment(sk[pl.ds(first, BK), :], query_seg, heads)
            scores = jnp.where(same, scores, NEG)
            before = m_ref[...]
            top = jnp.maximum(before, jnp.max(scores, axis=0, keepdims=True))
            raised = jnp.exp(scores - top)
            shrink = jnp.exp(before - top)
            m_ref[...] = top
            l_ref[...] = l_ref[...] * shrink + jnp.sum(raised, axis=0, keepdims=True)
            low = raised.astype(bf16)
            for h in range(heads):
                part = nn(
                    vt[h * each : (h + 1) * each, pl.ds(first, BK)],
                    low[:, h * rows : (h + 1) * rows],
                )
                hold = target[h * each : (h + 1) * each, :]
                target[h * each : (h + 1) * each, :] = (
                    hold * shrink[:, h * rows : (h + 1) * rows] + part
                )
            return carry

        lax.fori_loop(
            bounds[(step * sets + s) * 2], bounds[(step * sets + s) * 2 + 1], body, 0
        )

    if final:
        live = query_seg >= 0
        total = l_ref[...]
        live_all = jnp.concatenate([live] * heads, axis=1) if heads > 1 else live
        total = jnp.where(live_all, total, 1.0)
        inverse = jnp.where(live_all, 1.0 / total, 0.0)
        for h in range(heads):
            acc[h * each : (h + 1) * each, :] = (
                acc[h * each : (h + 1) * each, :] * inverse[:, h * rows : (h + 1) * rows]
            )
        o_ref[...] = acc[...].T.astype(bf16)
        lse_ref[0] = jnp.where(live_all, m_ref[...] + jnp.log(total), FAR)
    else:
        ml_ref[0, 0:1] = m_ref[...]
        ml_ref[0, 1:2] = l_ref[...]


def cost(products, q, kvs):
    pairs = q.shape[0]
    return pl.CostEstimate(
        flops=4 * products * pairs * q.shape[1],
        bytes_accessed=2 * sum(a.size for a in kvs) + 4 * q.size,
        transcendentals=4 * pairs,
    )


def whole(shape):
    zeros = (0,) * len(shape)
    return pl.BlockSpec(shape, lambda i, *_: zeros)


def attend_call(bounds, q, sq, kvs, sks, heads, state=None):
    count = q.shape[0] // BQ
    width = q.shape[1]
    sets = len(kvs)
    final = state is not None
    row_spec = pl.BlockSpec((BQ, width), lambda i, *_: (i, 0))
    acc_spec = pl.BlockSpec((1, width, BQ), lambda i, *_: (i, 0, 0))
    ml_spec = pl.BlockSpec((1, 2, heads * BQ), lambda i, *_: (i, 0, 0))
    in_specs = [row_spec, pl.BlockSpec((1, 1, BQ), lambda i, *_: (i, 0, 0))]
    in_specs += [whole(a.shape) for a in kvs] + [whole(a.shape) for a in sks]
    scratch = [pltpu.VMEM((1, heads * BQ), f32)] * 2
    scratch += [pltpu.VMEM((width, a.shape[0]), bf16) for a in kvs]
    if final:
        in_specs += [acc_spec, ml_spec]
        out_specs = [row_spec, pl.BlockSpec((1, 1, heads * BQ), lambda i, *_: (i, 0, 0))]
        out_shape = [
            jax.ShapeDtypeStruct(q.shape, bf16),
            jax.ShapeDtypeStruct((count, 1, heads * BQ), f32),
        ]
        scratch = [pltpu.VMEM((width, BQ), f32)] + scratch
    else:
        out_specs = [acc_spec, ml_spec]
        out_shape = [
            jax.ShapeDtypeStruct((count, width, BQ), f32),
            jax.ShapeDtypeStruct((count, 2, heads * BQ), f32),
        ]
    return pl.pallas_call(
        functools.partial(forward_kernel, heads, sets, final),
        grid_spec=pltpu.PrefetchScalarGridSpec(
            num_scalar_prefetch=1,
            grid=(count,),
            in_specs=in_specs,
            out_specs=out_specs,
            scratch_shapes=scratch,
        ),
        out_shape=out_shape,
        cost_estimate=cost(4, q, kvs),
        name="attend_final" if final else "attend_own",
    )(bounds, q, sq, *kvs, *sks, *(state or ()))


def backward_kernel(heads, sets, final, bounds, *refs):
    refs = list(refs)
    q_ref, do_ref, o_ref, lse_ref, sq_ref = refs[:5]
    kv_refs = refs[5 : 5 + sets]
    sk_refs = refs[5 + sets : 5 + 2 * sets]
    rest = refs[5 + 2 * sets :]
    if final:
        dq_in, dq_ref = rest[0], rest[1]
        dkv_refs = rest[2 : 2 + sets]
        dq_acc = rest[2 + sets]
        kt_refs = rest[3 + sets : 3 + 2 * sets]
        sums = dkv_refs
    else:
        dq_ref = rest[0]
        dkv_refs = rest[1 : 1 + sets]
        dq_acc = rest[1 + sets]
        kt_refs = rest[2 + sets : 2 + 2 * sets]
        sums = rest[2 + 2 * sets :]
    step = pl.program_id(0)
    rows, width = q_ref.shape
    each = width // heads
    half = width // 2
    piece = half // heads

    @pl.when(step == 0)
    def _():
        for kv, kt, total in zip(kv_refs, kt_refs, sums):
            total[...] = jnp.zeros_like(total)
            for j in range(kv.shape[0] // BK):
                kt[:, j * BK : (j + 1) * BK] = kv[j * BK : (j + 1) * BK, :width].T

    if final:
        dq_acc[...] = dq_in[0]
    else:
        dq_acc[...] = jnp.zeros_like(dq_acc)
    grads = do_ref[...]
    queries = stack_heads(q_ref[...], heads, half_mask)
    outs = stack_heads(grads, heads, whole_mask)
    query_seg = sq_ref[0]
    lse = lse_ref[0]
    product = (grads.astype(f32) * o_ref[...].astype(f32)).T
    delta = jnp.concatenate(
        [
            jnp.sum(product[h * each : (h + 1) * each], axis=0, keepdims=True)
            for h in range(heads)
        ],
        axis=1,
    )

    for s in range(sets):
        kv, sk, kt, total = kv_refs[s], sk_refs[s], kt_refs[s], sums[s]

        def body(j, carry):
            first = pl.multiple_of(j * BK, BK)
            keys = kv[pl.ds(first, BK), 0:width]
            values = kv[pl.ds(first, BK), width : 2 * width]
            scores = nt(keys, queries)
            same = same_segment(sk[pl.ds(first, BK), :], query_seg, heads)
            probs = jnp.where(same, jnp.exp(scores - lse), 0.0)
            grad_probs = nt(values, outs)
            grad_scores = (probs * (grad_probs - delta)).astype(bf16)
            low = probs.astype(bf16)
            total[pl.ds(first, BK), width : 2 * width] += nn(low, outs)
            total[pl.ds(first, BK), 0:width] += nn(grad_scores, queries)
            for h in range(heads):
                column = grad_scores[:, h * rows : (h + 1) * rows]
                for lead in (h * piece, half + h * piece):
                    dq_acc[lead : lead + piece, :] += nn(
                        kt[lead : lead + piece, pl.ds(first, BK)], column
                    )
            return carry

        lax.fori_loop(
            bounds[(step * sets + s) * 2], bounds[(step * sets + s) * 2 + 1], body, 0
        )

    if final:
        dq_ref[...] = dq_acc[...].T
    else:
        dq_ref[0] = dq_acc[...]

        @pl.when(step == pl.num_programs(0) - 1)
        def _():
            for total, out in zip(sums, dkv_refs):
                out[...] = total[...].astype(bf16)


def attend_back_call(bounds, q, do, o, lse, sq, kvs, sks, heads, state=None):
    count = q.shape[0] // BQ
    width = q.shape[1]
    sets = len(kvs)
    final = state is not None
    row_spec = pl.BlockSpec((BQ, width), lambda i, *_: (i, 0))
    acc_spec = pl.BlockSpec((1, width, BQ), lambda i, *_: (i, 0, 0))
    in_specs = [row_spec] * 3 + [
        pl.BlockSpec((1, 1, heads * BQ), lambda i, *_: (i, 0, 0)),
        pl.BlockSpec((1, 1, BQ), lambda i, *_: (i, 0, 0)),
    ]
    in_specs += [whole(a.shape) for a in kvs] + [whole(a.shape) for a in sks]
    scratch = [pltpu.VMEM((width, BQ), f32)]
    scratch += [pltpu.VMEM((width, a.shape[0]), bf16) for a in kvs]
    if final:
        in_specs += [acc_spec]
        out_specs = [row_spec]
        out_shape = [jax.ShapeDtypeStruct(q.shape, f32)]
    else:
        out_specs = [acc_spec]
        out_shape = [jax.ShapeDtypeStruct((count, width, BQ), f32)]
        scratch += [pltpu.VMEM(a.shape, f32) for a in kvs]
    out_specs += [whole(a.shape) for a in kvs]
    out_shape += [jax.ShapeDtypeStruct(a.shape, f32 if final else bf16) for a in kvs]
    return pl.pallas_call(
        functools.partial(backward_kernel, heads, sets, final),
        grid_spec=pltpu.PrefetchScalarGridSpec(
            num_scalar_prefetch=1,
            grid=(count,),
            in_specs=in_specs,
            out_specs=out_specs,
            scratch_shapes=scratch,
        ),
        out_shape=out_shape,
        cost_estimate=cost(10, q, kvs),
        name="back_own" if final else "back_halo",
    )(bounds, q, do, o, lse, sq, *kvs, *sks, *(state or ()))


def place_tables(seq_lengths, seq_offsets, first, count):
    place = first + jnp.arange(count, dtype=jnp.int32)
    ends = seq_offsets + seq_lengths
    inside = (place[:, None] >= seq_offsets[None, :]) & (place[:, None] < ends[None, :])
    live = jnp.any(inside, axis=1)
    index = jnp.arange(seq_offsets.shape[0], dtype=jnp.int32)
    segment = jnp.sum(jnp.where(inside, index[None, :], 0), axis=1)
    start = jnp.sum(jnp.where(inside, seq_offsets[None, :], 0), axis=1)
    end = jnp.sum(jnp.where(inside, ends[None, :], 0), axis=1)
    return live, segment, start, end, place


def qkv_order(heads, head_width):
    width = heads * head_width
    half = head_width // 2
    new = jnp.arange(3 * width, dtype=jnp.int32)
    kind = new // width
    inner = new % width
    side = inner // (width // 2)
    pair_head = (inner % (width // 2)) // half
    pair_old = pair_head * 3 * head_width + kind * head_width + side * half + inner % half
    value_old = (inner // head_width) * 3 * head_width + 2 * head_width + inner % head_width
    old = jnp.where(kind == 2, value_old, pair_old)
    return (old[None, :] == new[:, None]).astype(bf16)


def local(
    tokens,
    gain_attn,
    w_qkv,
    w_out,
    gain_mlp,
    w_in,
    w_down,
    cotangent,
    seq_lengths,
    seq_offsets,
    deal,
):
    R, C, B = lax.axis_size("row"), lax.axis_size("col"), lax.axis_size("dp")
    r, c, b = lax.axis_index("row"), lax.axis_index("col"), lax.axis_index("dp")
    S, Dl = tokens.shape
    D = Dl * R
    two = R == 2 and C == 2 and B == 8
    heads = w_qkv.shape[1] // R
    head_width = w_qkv.shape[2] // 3
    W = heads * head_width
    F = w_down.shape[0]
    H = LONGEST
    Sr = S // R
    zrow, zcol = (r == 0), (c == 0)

    def to_row(a):
        return lax.ppermute(a, "row", SWAP)

    def to_col(a):
        return lax.ppermute(a, "col", SWAP)

    def ordered(flag, mine, theirs, axis):
        return jnp.where(
            flag,
            jnp.concatenate([mine, theirs], axis=axis),
            jnp.concatenate([theirs, mine], axis=axis),
        )

    def own_first(a, axis):
        if not two:
            return a
        n = a.shape[axis] // 2
        return jnp.where(zrow, a, jnp.roll(a, n, axis=axis))

    def take(a, index, size, axis=0):
        return lax.dynamic_slice_in_dim(a, index * size, size, axis)

    def partner(a):
        n = a.shape[0] // 2
        got = to_row(take(a, c, n))
        return ordered(zcol, got, to_col(got), 0)

    def gather(a, axis):
        if two:
            return jnp.concatenate([a, to_row(a)], axis=axis)
        return lax.all_gather(a, "row", axis=axis, tiled=True)

    def col_sum(a):
        return a + to_col(a.astype(bf16)).astype(f32) if C == 2 else lax.psum(a, "col")

    live_x, seg_x, start_x, end_x, place_x = place_tables(seq_lengths, seq_offsets, b * S - H, S + 2 * H)
    key_seg = jnp.broadcast_to(jnp.where(live_x, seg_x, -2)[:, None], (S + 2 * H, 128))
    sk_left, sk_own, sk_right = key_seg[:H], key_seg[H : H + S], key_seg[H + S :]
    live = live_x[H : H + S]
    nq = S // BQ
    sq = jnp.where(live, seg_x[H : H + S], -1).reshape(nq, 1, BQ)
    first = jnp.min(jnp.where(live, start_x[H : H + S] - b * S, 4 * S).reshape(nq, BQ), axis=1)
    last = jnp.max(jnp.where(live, end_x[H : H + S] - b * S, -4 * S).reshape(nq, BQ), axis=1)
    own_low = jnp.clip(first, 0, S) // BK
    own_high = (jnp.clip(last, 0, S) + BK - 1) // BK
    left_low = jnp.clip(first + H, 0, H) // BK
    right_high = (jnp.clip(last - S, 0, H) + BK - 1) // BK
    own_bounds = jnp.stack([own_low, own_high], axis=1).reshape(-1).astype(jnp.int32)
    zero = jnp.zeros_like(left_low)
    halo_bounds = (
        jnp.stack([left_low, zero + H // BK, zero, right_high], axis=1).reshape(-1).astype(jnp.int32)
    )
    position = jnp.where(live, place_x[H : H + S] - start_x[H : H + S], 0)
    freq = rope_base ** (-(jnp.arange(0, head_width, 2, dtype=f32) / head_width))
    angle = position.astype(f32)[:, None] * jnp.tile(freq, heads)[None, :]
    cosine, sine = lax.optimization_barrier((jnp.cos(angle), jnp.sin(angle)))

    live_column = live[:, None]
    if two:
        x_got = partner(tokens)
        x_low = jnp.where(live_column, jnp.concatenate([tokens, x_got], axis=1), 0)
    else:
        own_x = jnp.where(live_column, tokens, 0)
        x_low = lax.all_gather(own_x, "row", axis=1, tiled=True)

    wq_low = w_qkv.reshape(Dl, R * 3 * W).astype(bf16)
    if two:
        wq_mine, wq_send = take(wq_low, r, 3 * W, 1), take(wq_low, 1 - r, 3 * W, 1)
        wq_got = to_row(wq_send)
    else:
        wq = lax.all_to_all(wq_low, "row", split_axis=1, concat_axis=0, tiled=True)
    order = qkv_order(heads, head_width)

    gain_one = own_first(gain_attn, 0)
    gain_two = own_first(gain_mlp, 0)

    Db = D // B
    Dd = D // (B * R)
    if two:
        y_bit, z_bits = b % 2, b // 2

        def relative(a, bits):
            n = jnp.arange(D, dtype=jnp.int32)
            rel = {"w": 0 * n, "x": 0 * n}
            for i, bit in enumerate(bits):
                rel[bit] = n // (D >> (i + 1)) % 2
            z_rel = 2 * rel["Z"] + rel["z"]
            column = ((z_bits ^ z_rel) * 2 + (y_bit ^ rel["y"])) * Db + n % Dd
            column = column + (rel["w"] if "w" in bits else r ^ rel["x"]) * Dd
            column = column ^ (r * (D // 2))
            return nn(a, (n[:, None] == column[None, :]).astype(bf16)).astype(bf16)

        def to_y(a):
            return lax.ppermute(a, "dp", [(i, i ^ 1) for i in range(B)])

        def to_z(a, j):
            return lax.ppermute(a, "dp", [(i, i ^ (2 * j)) for i in range(B)])

        def first(a):
            return a[:, : a.shape[1] // 2]

        def second(a):
            return a[:, a.shape[1] // 2 :].astype(bf16)

        def product(left, right):
            return tn(left, second(right)).astype(bf16)

        def halved(left, right, got):
            return tn(left, first(right)) + got.astype(f32)

        def joined(part, got):
            return first(part).astype(f32) + got.astype(f32)

    x = x_low.astype(f32)
    center = x - jnp.mean(x, axis=-1, keepdims=True)
    inverse_one = lax.rsqrt(jnp.mean(center * center, axis=-1, keepdims=True) + epsilon)
    mean_one = jnp.mean(x, axis=-1, keepdims=True)
    h1 = (center * inverse_one * gain_one).astype(bf16)
    if two:
        h1, wq_mine, wq_got = lax.optimization_barrier((h1, wq_mine, wq_got))
        wq = jnp.concatenate([wq_mine, wq_got], axis=0)
    wq = nn(wq, order).astype(bf16)

    half = W // 2

    def turn(t, sign):
        first_half, second_half = t[:, :half], t[:, half:]
        s = sine * sign
        return jnp.concatenate(
            [first_half * cosine - second_half * s, second_half * cosine + first_half * s], axis=1
        )

    kv_raw = nn(h1, wq[:, W:])
    kv = jnp.concatenate([turn(kv_raw[:, :W], 1.0), kv_raw[:, W:]], axis=1).astype(bf16)
    up = [(i, i + 1) for i in range(B - 1)]
    down = [(i + 1, i) for i in range(B - 1)]
    kv_left = lax.ppermute(kv[S - H :], "dp", up)
    kv_right = lax.ppermute(kv[:H], "dp", down)
    q = (turn(nn(h1, wq[:, :W]), 1.0) * (1.0 / math.sqrt(head_width))).astype(bf16)
    wo_low = w_out.astype(bf16)
    w_in_late, w_down_late = after((w_in, w_down), kv)
    wd_low = w_down_late.astype(bf16)
    act_low, lin_low = w_in_late[:, 0].astype(bf16), w_in_late[:, 1].astype(bf16)
    if two:
        even = (b // 2) % 2 == 0
        in_send, wo_send, g_send = after(
            (
                lax.dynamic_index_in_dim(w_in, (b // 2) % 2, 1, keepdims=False).astype(bf16),
                wo_low,
                take(cotangent, 2 * (1 - r) + c, Sr // 2),
            ),
            cosine,
            wq_send,
        )
        in_got, wo_got, g_got = to_row(in_send), to_row(wo_send), to_row(g_send)
        wd_half = take(wd_low, (b // 2) % 2, F // 2)
        h1_y = relative(after(h1, kv), "zyZw")
        q, h1_y, sk_left, sk_right, act_low, lin_low, wd_half = lax.optimization_barrier(
            (q, h1_y, sk_left, sk_right, act_low, lin_low, wd_half)
        )

    state = attend_call(own_bounds, q, sq, [kv], [sk_own], heads)
    if two:
        kv_left, kv_right, in_got, wo_got, g_got, wd_half = after(
            (kv_left, kv_right, in_got, wo_got, g_got, wd_half), state
        )
        in_other, wd_got = to_z(in_got, 1), to_row(wd_half)
    o, lse = attend_call(
        halo_bounds, q, sq, [kv_left, kv_right], [sk_left, sk_right], heads, state
    )

    if two:
        o, wd_got, wo_got, g_got = lax.optimization_barrier((o, wd_got, wo_got, g_got))
        wo = own_first(jnp.concatenate([wo_low, wo_got], axis=1), 0)
    else:
        wo = gather(wo_low, 1)

    if two:
        o_got = to_row(take(o, 1 - r, Sr))
        o_rows = jnp.concatenate([take(o, r, Sr), o_got], axis=1)
        wd_other = to_z(wd_got, 1)
        wd_got = ordered(even, wd_got, wd_other, 0)
        g_got = ordered(zcol, g_got, to_col(g_got), 0)
        g_low = jnp.concatenate([take(cotangent, r, Sr), g_got], axis=1)
        g_low = jnp.where(take(live, r, Sr)[:, None], g_low, 0)
        wds = [wd_low, wd_got]
    else:
        o_rows = lax.all_to_all(o, "row", split_axis=0, concat_axis=1, tiled=True)
        own_g = jnp.where(live_column, cotangent, 0)
        g_low = lax.all_to_all(own_g, "row", split_axis=0, concat_axis=1, tiled=True)
        wds, acts, lins = [gather(wd_low, 1)], [gather(act_low, 0)], [gather(lin_low, 0)]

    def split_nn(a, parts):
        n = a.shape[1] // len(parts)
        return sum(nn(a[:, i * n : (i + 1) * n], w) for i, w in enumerate(parts))

    def split_nt(a, parts):
        n = a.shape[1] // len(parts)
        return sum(nt(a[:, i * n : (i + 1) * n], w) for i, w in enumerate(parts))

    def wide(parts):
        return parts[0] if len(parts) == 1 else jnp.concatenate(parts, axis=1)

    x_rows = take(x_low, r, Sr).astype(f32)
    if C == 2:
        o_all = jnp.concatenate([o_rows, to_col(o_rows)], axis=1)
        wo_all = jnp.concatenate([wo, to_col(wo)], axis=0)
        x1 = x_rows + nn(o_all, wo_all)
    else:
        x1 = x_rows + lax.psum(nn(o_rows, wo), "col")
    if two:
        in_got, in_other = after((in_got, in_other), o_got)
        act_got, lin_got = jnp.where(even, in_got, in_other), jnp.where(even, in_other, in_got)
        acts, lins = [act_low, act_got], [lin_low, lin_got]

    center = x1 - jnp.mean(x1, axis=-1, keepdims=True)
    inverse_two = lax.rsqrt(jnp.mean(center * center, axis=-1, keepdims=True) + epsilon)
    n2 = center * inverse_two
    h2 = (n2 * gain_two).astype(bf16)
    a = split_nn(h2, acts)
    u = split_nn(h2, lins)
    phi = 0.5 + 0.5 * lax.erf(a * math.sqrt(0.5))
    gelu = a * phi
    slope = phi + a * jnp.exp(-0.5 * a * a) * (1.0 / math.sqrt(2.0 * math.pi))
    m = (gelu * u).astype(bf16)
    y_part = wide([nn(m, w) for w in wds])
    if two:
        n = Sr // 2
        y_half = (
            take(x1, c, n) + take(y_part, c, n) + to_col(take(y_part, 1 - c, n).astype(bf16)).astype(f32)
        ).astype(bf16)
        y_got = to_row(y_half[:, Dl:])
    else:
        y = (x1 + col_sum(y_part)).astype(bf16)
        layer_out = lax.all_to_all(y, "row", split_axis=1, concat_axis=0, tiled=True)

    dm = split_nt(g_low, wds)
    da = (dm * u * slope).astype(bf16)
    du = (dm * gelu).astype(bf16)
    dh2_part = wide([nt(da, v) + nt(du, w) for v, w in zip(acts, lins)])
    dh2 = col_sum(dh2_part)
    if two:
        g_y = relative(after(g_low, dh2_part), "yzZx")
        lower_got = to_y(product(m, g_y))
    e2 = dh2 * gain_two
    dx1 = g_low.astype(f32) + inverse_two * (
        e2
        - jnp.mean(e2, axis=-1, keepdims=True)
        - n2 * jnp.mean(e2 * n2, axis=-1, keepdims=True)
    )
    dx_low = dx1.astype(bf16)
    do_rows = nt(dx_low, wo).astype(bf16)
    if two:
        do_got = to_row(do_rows[:, W:])
        do = ordered(zrow, do_rows[:, :W], do_got, 0)
    else:
        do = lax.all_to_all(do_rows, "row", split_axis=1, concat_axis=0, tiled=True)

    if two:
        h2, da, du, o_heads, dx_late = after((h2, da, du, own_first(o_rows, 1), dx_low), do_rows)
        def three(*parts):
            return jnp.concatenate([second(a) for a in parts], axis=0)

        def joined_three(parts, got):
            n = F
            return [joined(a, g) for a, g in zip(parts, (got[:n], got[n : 2 * n], got[2 * n :]))]

        dx_y = relative(dx_late, "xyzZ")
        h_x = relative(h2, "xyzZ")
        gate_send = jnp.concatenate([product(da, h_x), product(du, h_x), product(o_heads, dx_y)], axis=0)
        gate_got = to_row(after(gate_send, do_got))
        pair = ordered(zrow, y_half[None, :, :Dl], after(y_got, gate_send)[None], 0)
        layer_out = ordered(zcol, pair[:, None], to_col(pair)[:, None], 1).reshape(S, Dl)
        do, layer_out = lax.optimization_barrier((do, layer_out))

    dq_part, dkv_left, dkv_right = attend_back_call(
        halo_bounds, q, do, o, lse, sq, [kv_left, kv_right], [sk_left, sk_right], heads
    )
    from_right = lax.ppermute(dkv_left, "dp", down)
    from_left = lax.ppermute(dkv_right, "dp", up)
    if two:
        lower = halved(m, g_y, after(lower_got, dq_part))
        lower_got = to_z(second(lower), 1)
        dq_part, lower = lax.optimization_barrier((dq_part, lower))
    dq, dkv = attend_back_call(own_bounds, q, do, o, lse, sq, [kv], [sk_own], heads, [dq_part])
    if two:
        gate_got = after(gate_got, dq)
        act, lin = halved(da, h_x, gate_got[:F]), halved(du, h_x, gate_got[F : 2 * F])
        proj = halved(o_heads, dx_y, gate_got[2 * F :])
        gate_send = three(act, lin, proj)
        dkv, from_right, from_left, act, lin, proj, gate_send, lower_got = lax.optimization_barrier(
            (dkv, from_right, from_left, act, lin, proj, gate_send, lower_got)
        )
        gate_got = to_y(gate_send)
    pad = jnp.zeros((S - H, 2 * W), bf16)
    dkv = (
        dkv
        + jnp.concatenate([pad, from_right], axis=0).astype(f32)
        + jnp.concatenate([from_left, pad], axis=0).astype(f32)
    )
    dq = turn(dq * (1.0 / math.sqrt(head_width)), -1.0)
    dt = jnp.concatenate([dq, turn(dkv[:, :W], -1.0), dkv[:, W:]], axis=1).astype(bf16)
    dh1_part = nt(dt, wq)
    if two:
        query_send = product(dt, h1_y)
        query_got = to_z(query_send, 1)
        lower_got = after(lower_got, query_send, dh1_part)

    if two:
        n = S // 2
        kept = take(dh1_part, c, n) + to_col(take(dh1_part, 1 - c, n).astype(bf16)).astype(f32)
        xs = take(x_low, c, n).astype(f32)
        inv, mean = take(inverse_one, c, n), take(mean_one, c, n)
        n1 = (xs - mean) * inv
        e1 = kept * gain_one
        sums = jnp.stack([jnp.sum(e1, axis=-1), jnp.sum(e1 * n1, axis=-1)])
        sums = (sums + to_row(sums)) * (1.0 / D)
        moved = lax.ppermute(after(dx_low[:, Dl:], from_left), ("row", "col"), [(0, 2), (3, 1)])
        kept_send, moved = lax.optimization_barrier((kept[:, Dl:].astype(bf16), moved))
        mine = (kept[:, :Dl] + to_row(kept_send).astype(f32)) * gain_one[:Dl]
        base = jnp.where(r == c, dx1[:, :Dl], moved.astype(f32))
        dx = base + inv * (mine - sums[0][:, None] - n1[:, :Dl] * sums[1][:, None])
        dx = dx.astype(bf16)
        tokens_grad = ordered(zcol, dx, to_col(dx), 0)
    else:
        dh1 = lax.psum_scatter(col_sum(dh1_part), "row", scatter_dimension=1, tiled=True)
        xs = own_x.astype(f32)
        n1 = (xs - mean_one) * inverse_one
        e1 = dh1 * take(gain_attn, r, Dl)
        sums = lax.psum(jnp.stack([jnp.sum(e1, axis=-1), jnp.sum(e1 * n1, axis=-1)]), "row") / D
        base = lax.all_to_all(dx_low, "row", split_axis=1, concat_axis=0, tiled=True).astype(f32)
        tokens_grad = (
            base + inverse_one * (e1 - sums[0][:, None] - n1 * sums[1][:, None])
        ).astype(bf16)

    if two:
        lower = joined(lower, lower_got)
        lower_got = to_z(second(lower), 2)
        query = halved(dt, h1_y, after(query_got, kept))
        query_got = to_y(second(query))
        act, lin, proj = joined_three((act, lin, proj), after(gate_got, query))
        gate_got = to_z(three(act, lin, proj), 1)
        lower = joined(lower, after(lower_got, act, lin, proj))
        last_got = to_row(second(lower))
        query = joined(query, after(query_got, act, lin, proj))
        query_got = to_z(second(query), 2)
        act, lin, proj = joined_three((act, lin, proj), after(gate_got, dx))
        gate_got = after(to_z(three(act, lin, proj).T, 2), tokens_grad).T
        query = joined(query, after(query_got, act, lin, proj))
        lower = joined(lower, after(last_got, dx))
        act, lin, proj = joined_three((act, lin, proj), gate_got)
        gate = jnp.stack([act.T, lin.T])
        query = query.T
        wq_rows = take(wq, b ^ (4 * r), Db)
        place = (2 * b + r) ^ (8 * r)
        wi_rows = jnp.stack(
            [jnp.where(place < 8, *(take(w, place % 8, Dd) for w in ws)) for ws in after((acts, lins), kept)]
        )
    else:

        def scatter(grad):
            return lax.psum_scatter(grad, ("dp", "row"), scatter_dimension=1, tiled=True).astype(f32)

        gate = jnp.stack([scatter(tn(da, h2).astype(bf16)).T, scatter(tn(du, h2).astype(bf16)).T])
        proj = scatter(tn(o_rows, dx_low).astype(bf16))
        lower = scatter(tn(m, g_low).astype(bf16))
        query = lax.psum_scatter(
            tn(h1, dt).astype(bf16), "dp", scatter_dimension=0, tiled=True
        ).astype(f32)
        wq_rows = take(wq, b, Db)
        wi_rows = jnp.stack([take(acts[0], b * R + r, Dd), take(lins[0], b * R + r, Dd)])

    one_part = jnp.sum(query * wq_rows.astype(f32), axis=1)
    two_part = jnp.sum(jnp.sum(gate * wi_rows.astype(f32), axis=2), axis=0)
    natural = lax.dot_general(
        query, order.astype(f32), (((1,), (1,)), ((), ())),
        precision=lax.Precision.HIGHEST, preferred_element_type=f32,
    )
    if two:
        pair = jnp.concatenate([natural, jnp.broadcast_to(one_part[:, None], (Db, 128))], axis=1)
        pair = pair.reshape(2, Dd, 3 * W + 128)
        mine = lax.dynamic_index_in_dim(pair, r, 0, keepdims=False)
        theirs = to_row(lax.dynamic_index_in_dim(pair, 1 - r, 0, keepdims=False))
        theirs = after(theirs, tokens_grad)
        one_part = mine[:, 3 * W] + theirs[:, 3 * W]
        query_out = ordered(zrow, mine[:, : 3 * W], theirs[:, : 3 * W], 1)
    else:
        one_part = take(lax.psum(one_part, "row"), r, Dd)
        query_out = lax.all_to_all(natural, "row", split_axis=0, concat_axis=1, tiled=True)
    gains = jnp.stack([one_part, two_part])
    gains = gains + to_col(gains) if C == 2 else lax.psum(gains, "col")
    gain_attn_grad = gains[0] / take(gain_attn, b * R + r, Dd)
    gain_mlp_grad = gains[1] / take(gain_mlp, b * R + r, Dd)
    return (
        layer_out,
        tokens_grad,
        gain_attn_grad,
        query_out.reshape(Dd, R * heads, 3 * head_width),
        proj,
        gain_mlp_grad,
        jnp.swapaxes(gate, 0, 1),
        lower,
    )


def solution(mesh):
    return jax.shard_map(
        local,
        mesh=mesh,
        in_specs=(
            P("dp", "row"),
            P(),
            P("row", "col", None),
            P("col", "row"),
            P(),
            P("row", None, "col"),
            P("col", "row"),
            P("dp", "row"),
            P(),
            P(),
            P(),
        ),
        out_specs=(
            P("dp", "row"),
            P("dp", "row"),
            P(("dp", "row")),
            P(("dp", "row"), "col", None),
            P("col", ("dp", "row")),
            P(("dp", "row")),
            P(("dp", "row"), None, "col"),
            P("col", ("dp", "row")),
        ),
        check_vma=False,
    )
```

```python
import functools
import math

import jax
import jax.numpy as jnp
from jax import lax
from jax.experimental import pallas as pl
from jax.experimental.pallas import tpu as pltpu
from jax.sharding import PartitionSpec as P

LONGEST = 1024
BQ = 256
BK = 256
NEG = -1e30
FAR = 1e30
epsilon = 1e-05
rope_base = 160000.0
bf16 = jnp.bfloat16
f32 = jnp.float32
SWAP = [(0, 1), (1, 0)]


def nt(a, b):
    return lax.dot_general(a, b, (((1,), (1,)), ((), ())), preferred_element_type=f32)


def tn(a, b):
    return lax.dot_general(a, b, (((0,), (0,)), ((), ())), preferred_element_type=f32)


def nn(a, b):
    return jnp.dot(a, b, preferred_element_type=f32)


def after(a, *others):
    return lax.optimization_barrier((a, *others))[0]


def half_mask(width, heads, head):
    lane = lax.broadcasted_iota(jnp.int32, (1, width), 1)
    half = width // 2
    lane = jnp.where(lane >= half, lane - half, lane)
    step = half // heads
    return (lane >= head * step) & (lane < (head + 1) * step)


def whole_mask(width, heads, head):
    lane = lax.broadcasted_iota(jnp.int32, (1, width), 1)
    step = width // heads
    return (lane >= head * step) & (lane < (head + 1) * step)


def stack_heads(block, heads, mask_of):
    zero = jnp.zeros_like(block)
    width = block.shape[1]
    return jnp.concatenate(
        [jnp.where(mask_of(width, heads, h), block, zero) for h in range(heads)], axis=0
    )


def same_segment(key_seg, query_seg, heads):
    tile = key_seg
    lanes = query_seg.shape[1]
    if lanes > tile.shape[1]:
        tile = jnp.concatenate([tile] * (lanes // tile.shape[1]), axis=1)
    same = tile == query_seg
    return jnp.concatenate([same] * heads, axis=1) if heads > 1 else same


def forward_kernel(heads, sets, final, bounds, *refs):
    refs = list(refs)
    q_ref, sq_ref = refs[:2]
    kv_refs = refs[2 : 2 + sets]
    sk_refs = refs[2 + sets : 2 + 2 * sets]
    rest = refs[2 + 2 * sets :]
    if final:
        acc_in, ml_in, o_ref, lse_ref = rest[:4]
        acc, m_ref, l_ref = rest[4:7]
        vt_refs = rest[7:]
    else:
        acc, ml_ref = rest[:2]
        m_ref, l_ref = rest[2:4]
        vt_refs = rest[4:]
    step = pl.program_id(0)
    rows, width = q_ref.shape
    each = width // heads

    @pl.when(step == 0)
    def _():
        for kv, vt in zip(kv_refs, vt_refs):
            for j in range(kv.shape[0] // BK):
                vt[:, j * BK : (j + 1) * BK] = kv[j * BK : (j + 1) * BK, width:].T

    if final:
        acc[...] = acc_in[0]
        m_ref[...] = ml_in[0, 0:1]
        l_ref[...] = ml_in[0, 1:2]
    else:
        acc[...] = jnp.zeros_like(acc)
        m_ref[...] = jnp.full_like(m_ref, NEG)
        l_ref[...] = jnp.zeros_like(l_ref)
    queries = stack_heads(q_ref[...], heads, half_mask)
    query_seg = sq_ref[0]
    target = acc if final else acc.at[0]

    for s in range(sets):
        kv, sk, vt = kv_refs[s], sk_refs[s], vt_refs[s]

        def body(j, carry):
            first = pl.multiple_of(j * BK, BK)
            keys = kv[pl.ds(first, BK), 0:width]
            scores = nt(keys, queries)
            same = same_segment(sk[pl.ds(first, BK), :], query_seg, heads)
            scores = jnp.where(same, scores, NEG)
            before = m_ref[...]
            top = jnp.maximum(before, jnp.max(scores, axis=0, keepdims=True))
            raised = jnp.exp(scores - top)
            shrink = jnp.exp(before - top)
            m_ref[...] = top
            l_ref[...] = l_ref[...] * shrink + jnp.sum(raised, axis=0, keepdims=True)
            low = raised.astype(bf16)
            for h in range(heads):
                part = nn(
                    vt[h * each : (h + 1) * each, pl.ds(first, BK)],
                    low[:, h * rows : (h + 1) * rows],
                )
                hold = target[h * each : (h + 1) * each, :]
                target[h * each : (h + 1) * each, :] = (
                    hold * shrink[:, h * rows : (h + 1) * rows] + part
                )
            return carry

        lax.fori_loop(
            bounds[(step * sets + s) * 2], bounds[(step * sets + s) * 2 + 1], body, 0
        )

    if final:
        live = query_seg >= 0
        total = l_ref[...]
        live_all = jnp.concatenate([live] * heads, axis=1) if heads > 1 else live
        total = jnp.where(live_all, total, 1.0)
        inverse = jnp.where(live_all, 1.0 / total, 0.0)
        for h in range(heads):
            acc[h * each : (h + 1) * each, :] = (
                acc[h * each : (h + 1) * each, :] * inverse[:, h * rows : (h + 1) * rows]
            )
        o_ref[...] = acc[...].T.astype(bf16)
        lse_ref[0] = jnp.where(live_all, m_ref[...] + jnp.log(total), FAR)
    else:
        ml_ref[0, 0:1] = m_ref[...]
        ml_ref[0, 1:2] = l_ref[...]


def cost(products, q, kvs):
    pairs = q.shape[0]
    return pl.CostEstimate(
        flops=4 * products * pairs * q.shape[1],
        bytes_accessed=2 * sum(a.size for a in kvs) + 4 * q.size,
        transcendentals=4 * pairs,
    )


def whole(shape):
    zeros = (0,) * len(shape)
    return pl.BlockSpec(shape, lambda i, *_: zeros)


def attend_call(bounds, q, sq, kvs, sks, heads, state=None):
    count = q.shape[0] // BQ
    width = q.shape[1]
    sets = len(kvs)
    final = state is not None
    row_spec = pl.BlockSpec((BQ, width), lambda i, *_: (i, 0))
    acc_spec = pl.BlockSpec((1, width, BQ), lambda i, *_: (i, 0, 0))
    ml_spec = pl.BlockSpec((1, 2, heads * BQ), lambda i, *_: (i, 0, 0))
    in_specs = [row_spec, pl.BlockSpec((1, 1, BQ), lambda i, *_: (i, 0, 0))]
    in_specs += [whole(a.shape) for a in kvs] + [whole(a.shape) for a in sks]
    scratch = [pltpu.VMEM((1, heads * BQ), f32)] * 2
    scratch += [pltpu.VMEM((width, a.shape[0]), bf16) for a in kvs]
    if final:
        in_specs += [acc_spec, ml_spec]
        out_specs = [row_spec, pl.BlockSpec((1, 1, heads * BQ), lambda i, *_: (i, 0, 0))]
        out_shape = [
            jax.ShapeDtypeStruct(q.shape, bf16),
            jax.ShapeDtypeStruct((count, 1, heads * BQ), f32),
        ]
        scratch = [pltpu.VMEM((width, BQ), f32)] + scratch
    else:
        out_specs = [acc_spec, ml_spec]
        out_shape = [
            jax.ShapeDtypeStruct((count, width, BQ), f32),
            jax.ShapeDtypeStruct((count, 2, heads * BQ), f32),
        ]
    return pl.pallas_call(
        functools.partial(forward_kernel, heads, sets, final),
        grid_spec=pltpu.PrefetchScalarGridSpec(
            num_scalar_prefetch=1,
            grid=(count,),
            in_specs=in_specs,
            out_specs=out_specs,
            scratch_shapes=scratch,
        ),
        out_shape=out_shape,
        cost_estimate=cost(4, q, kvs),
        name="attend_final" if final else "attend_own",
    )(bounds, q, sq, *kvs, *sks, *(state or ()))


def backward_kernel(heads, sets, final, bounds, *refs):
    refs = list(refs)
    q_ref, do_ref, o_ref, lse_ref, sq_ref = refs[:5]
    kv_refs = refs[5 : 5 + sets]
    sk_refs = refs[5 + sets : 5 + 2 * sets]
    rest = refs[5 + 2 * sets :]
    if final:
        dq_in, dq_ref = rest[0], rest[1]
        dkv_refs = rest[2 : 2 + sets]
        dq_acc = rest[2 + sets]
        kt_refs = rest[3 + sets : 3 + 2 * sets]
        sums = dkv_refs
    else:
        dq_ref = rest[0]
        dkv_refs = rest[1 : 1 + sets]
        dq_acc = rest[1 + sets]
        kt_refs = rest[2 + sets : 2 + 2 * sets]
        sums = rest[2 + 2 * sets :]
    step = pl.program_id(0)
    rows, width = q_ref.shape
    each = width // heads
    half = width // 2
    piece = half // heads

    @pl.when(step == 0)
    def _():
        for kv, kt, total in zip(kv_refs, kt_refs, sums):
            total[...] = jnp.zeros_like(total)
            for j in range(kv.shape[0] // BK):
                kt[:, j * BK : (j + 1) * BK] = kv[j * BK : (j + 1) * BK, :width].T

    if final:
        dq_acc[...] = dq_in[0]
    else:
        dq_acc[...] = jnp.zeros_like(dq_acc)
    grads = do_ref[...]
    queries = stack_heads(q_ref[...], heads, half_mask)
    outs = stack_heads(grads, heads, whole_mask)
    query_seg = sq_ref[0]
    lse = lse_ref[0]
    product = (grads.astype(f32) * o_ref[...].astype(f32)).T
    delta = jnp.concatenate(
        [
            jnp.sum(product[h * each : (h + 1) * each], axis=0, keepdims=True)
            for h in range(heads)
        ],
        axis=1,
    )

    for s in range(sets):
        kv, sk, kt, total = kv_refs[s], sk_refs[s], kt_refs[s], sums[s]

        def body(j, carry):
            first = pl.multiple_of(j * BK, BK)
            keys = kv[pl.ds(first, BK), 0:width]
            values = kv[pl.ds(first, BK), width : 2 * width]
            scores = nt(keys, queries)
            same = same_segment(sk[pl.ds(first, BK), :], query_seg, heads)
            probs = jnp.where(same, jnp.exp(scores - lse), 0.0)
            grad_probs = nt(values, outs)
            grad_scores = (probs * (grad_probs - delta)).astype(bf16)
            low = probs.astype(bf16)
            total[pl.ds(first, BK), width : 2 * width] += nn(low, outs)
            total[pl.ds(first, BK), 0:width] += nn(grad_scores, queries)
            for h in range(heads):
                column = grad_scores[:, h * rows : (h + 1) * rows]
                for lead in (h * piece, half + h * piece):
                    dq_acc[lead : lead + piece, :] += nn(
                        kt[lead : lead + piece, pl.ds(first, BK)], column
                    )
            return carry

        lax.fori_loop(
            bounds[(step * sets + s) * 2], bounds[(step * sets + s) * 2 + 1], body, 0
        )

    if final:
        dq_ref[...] = dq_acc[...].T
    else:
        dq_ref[0] = dq_acc[...]

        @pl.when(step == pl.num_programs(0) - 1)
        def _():
            for total, out in zip(sums, dkv_refs):
                out[...] = total[...].astype(bf16)


def attend_back_call(bounds, q, do, o, lse, sq, kvs, sks, heads, state=None):
    count = q.shape[0] // BQ
    width = q.shape[1]
    sets = len(kvs)
    final = state is not None
    row_spec = pl.BlockSpec((BQ, width), lambda i, *_: (i, 0))
    acc_spec = pl.BlockSpec((1, width, BQ), lambda i, *_: (i, 0, 0))
    in_specs = [row_spec] * 3 + [
        pl.BlockSpec((1, 1, heads * BQ), lambda i, *_: (i, 0, 0)),
        pl.BlockSpec((1, 1, BQ), lambda i, *_: (i, 0, 0)),
    ]
    in_specs += [whole(a.shape) for a in kvs] + [whole(a.shape) for a in sks]
    scratch = [pltpu.VMEM((width, BQ), f32)]
    scratch += [pltpu.VMEM((width, a.shape[0]), bf16) for a in kvs]
    if final:
        in_specs += [acc_spec]
        out_specs = [row_spec]
        out_shape = [jax.ShapeDtypeStruct(q.shape, f32)]
    else:
        out_specs = [acc_spec]
        out_shape = [jax.ShapeDtypeStruct((count, width, BQ), f32)]
        scratch += [pltpu.VMEM(a.shape, f32) for a in kvs]
    out_specs += [whole(a.shape) for a in kvs]
    out_shape += [jax.ShapeDtypeStruct(a.shape, f32 if final else bf16) for a in kvs]
    return pl.pallas_call(
        functools.partial(backward_kernel, heads, sets, final),
        grid_spec=pltpu.PrefetchScalarGridSpec(
            num_scalar_prefetch=1,
            grid=(count,),
            in_specs=in_specs,
            out_specs=out_specs,
            scratch_shapes=scratch,
        ),
        out_shape=out_shape,
        cost_estimate=cost(10, q, kvs),
        name="back_own" if final else "back_halo",
    )(bounds, q, do, o, lse, sq, *kvs, *sks, *(state or ()))


def place_tables(seq_lengths, seq_offsets, first, count):
    place = first + jnp.arange(count, dtype=jnp.int32)
    ends = seq_offsets + seq_lengths
    inside = (place[:, None] >= seq_offsets[None, :]) & (place[:, None] < ends[None, :])
    live = jnp.any(inside, axis=1)
    index = jnp.arange(seq_offsets.shape[0], dtype=jnp.int32)
    segment = jnp.sum(jnp.where(inside, index[None, :], 0), axis=1)
    start = jnp.sum(jnp.where(inside, seq_offsets[None, :], 0), axis=1)
    end = jnp.sum(jnp.where(inside, ends[None, :], 0), axis=1)
    return live, segment, start, end, place


def qkv_order(heads, head_width):
    width = heads * head_width
    half = head_width // 2
    new = jnp.arange(3 * width, dtype=jnp.int32)
    kind = new // width
    inner = new % width
    side = inner // (width // 2)
    pair_head = (inner % (width // 2)) // half
    pair_old = pair_head * 3 * head_width + kind * head_width + side * half + inner % half
    value_old = (inner // head_width) * 3 * head_width + 2 * head_width + inner % head_width
    old = jnp.where(kind == 2, value_old, pair_old)
    return (old[None, :] == new[:, None]).astype(bf16)


def local(
    tokens,
    gain_attn,
    w_qkv,
    w_out,
    gain_mlp,
    w_in,
    w_down,
    cotangent,
    seq_lengths,
    seq_offsets,
    deal,
):
    R, C, B = lax.axis_size("row"), lax.axis_size("col"), lax.axis_size("dp")
    r, c, b = lax.axis_index("row"), lax.axis_index("col"), lax.axis_index("dp")
    S, Dl = tokens.shape
    D = Dl * R
    two = R == 2 and C == 2 and B == 8
    heads = w_qkv.shape[1] // R
    head_width = w_qkv.shape[2] // 3
    W = heads * head_width
    F = w_down.shape[0]
    H = LONGEST
    Sr = S // R
    zrow, zcol = (r == 0), (c == 0)

    def to_row(a):
        return lax.ppermute(a, "row", SWAP)

    def to_col(a):
        return lax.ppermute(a, "col", SWAP)

    def ordered(flag, mine, theirs, axis):
        return jnp.where(
            flag,
            jnp.concatenate([mine, theirs], axis=axis),
            jnp.concatenate([theirs, mine], axis=axis),
        )

    def own_first(a, axis):
        if not two:
            return a
        n = a.shape[axis] // 2
        return jnp.where(zrow, a, jnp.roll(a, n, axis=axis))

    def take(a, index, size, axis=0):
        return lax.dynamic_slice_in_dim(a, index * size, size, axis)

    def partner(a):
        n = a.shape[0] // 2
        got = to_row(take(a, c, n))
        return ordered(zcol, got, to_col(got), 0)

    def gather(a, axis):
        if two:
            return jnp.concatenate([a, to_row(a)], axis=axis)
        return lax.all_gather(a, "row", axis=axis, tiled=True)

    def col_sum(a):
        return a + to_col(a.astype(bf16)).astype(f32) if C == 2 else lax.psum(a, "col")

    live_x, seg_x, start_x, end_x, place_x = place_tables(seq_lengths, seq_offsets, b * S - H, S + 2 * H)
    key_seg = jnp.broadcast_to(jnp.where(live_x, seg_x, -2)[:, None], (S + 2 * H, 128))
    sk_left, sk_own, sk_right = key_seg[:H], key_seg[H : H + S], key_seg[H + S :]
    live = live_x[H : H + S]
    nq = S // BQ
    sq = jnp.where(live, seg_x[H : H + S], -1).reshape(nq, 1, BQ)
    first = jnp.min(jnp.where(live, start_x[H : H + S] - b * S, 4 * S).reshape(nq, BQ), axis=1)
    last = jnp.max(jnp.where(live, end_x[H : H + S] - b * S, -4 * S).reshape(nq, BQ), axis=1)
    own_low = jnp.clip(first, 0, S) // BK
    own_high = (jnp.clip(last, 0, S) + BK - 1) // BK
    left_low = jnp.clip(first + H, 0, H) // BK
    right_high = (jnp.clip(last - S, 0, H) + BK - 1) // BK
    own_bounds = jnp.stack([own_low, own_high], axis=1).reshape(-1).astype(jnp.int32)
    zero = jnp.zeros_like(left_low)
    halo_bounds = (
        jnp.stack([left_low, zero + H // BK, zero, right_high], axis=1).reshape(-1).astype(jnp.int32)
    )
    position = jnp.where(live, place_x[H : H + S] - start_x[H : H + S], 0)
    freq = rope_base ** (-(jnp.arange(0, head_width, 2, dtype=f32) / head_width))
    angle = position.astype(f32)[:, None] * jnp.tile(freq, heads)[None, :]
    cosine, sine = lax.optimization_barrier((jnp.cos(angle), jnp.sin(angle)))

    live_column = live[:, None]
    if two:
        x_got = partner(tokens)
        x_low = jnp.where(live_column, jnp.concatenate([tokens, x_got], axis=1), 0)
    else:
        own_x = jnp.where(live_column, tokens, 0)
        x_low = lax.all_gather(own_x, "row", axis=1, tiled=True)

    wq_low = w_qkv.reshape(Dl, R * 3 * W).astype(bf16)
    if two:
        wq_mine, wq_send = take(wq_low, r, 3 * W, 1), take(wq_low, 1 - r, 3 * W, 1)
        wq_got = to_row(wq_send)
    else:
        wq = lax.all_to_all(wq_low, "row", split_axis=1, concat_axis=0, tiled=True)
    order = qkv_order(heads, head_width)

    gain_one = own_first(gain_attn, 0)
    gain_two = own_first(gain_mlp, 0)

    Db = D // B
    Dd = D // (B * R)
    if two:
        y_bit, z_bits = b % 2, b // 2

        def relative(a, bits):
            n = jnp.arange(D, dtype=jnp.int32)
            rel = {"w": 0 * n, "x": 0 * n}
            for i, bit in enumerate(bits):
                rel[bit] = n // (D >> (i + 1)) % 2
            z_rel = 2 * rel["Z"] + rel["z"]
            column = ((z_bits ^ z_rel) * 2 + (y_bit ^ rel["y"])) * Db + n % Dd
            column = column + (rel["w"] if "w" in bits else r ^ rel["x"]) * Dd
            column = column ^ (r * (D // 2))
            return nn(a, (n[:, None] == column[None, :]).astype(bf16)).astype(bf16)

        def to_y(a):
            return lax.ppermute(a, "dp", [(i, i ^ 1) for i in range(B)])

        def to_z(a, j):
            return lax.ppermute(a, "dp", [(i, i ^ (2 * j)) for i in range(B)])

        def first(a):
            return a[:, : a.shape[1] // 2]

        def second(a):
            return a[:, a.shape[1] // 2 :].astype(bf16)

        def product(left, right):
            return tn(left, second(right)).astype(bf16)

        def halved(left, right, got):
            return tn(left, first(right)) + got.astype(f32)

        def joined(part, got):
            return first(part).astype(f32) + got.astype(f32)

    x = x_low.astype(f32)
    center = x - jnp.mean(x, axis=-1, keepdims=True)
    inverse_one = lax.rsqrt(jnp.mean(center * center, axis=-1, keepdims=True) + epsilon)
    mean_one = jnp.mean(x, axis=-1, keepdims=True)
    h1 = (center * inverse_one * gain_one).astype(bf16)
    if two:
        h1, wq_mine, wq_got = lax.optimization_barrier((h1, wq_mine, wq_got))
        wq = jnp.concatenate([wq_mine, wq_got], axis=0)
    wq = nn(wq, order).astype(bf16)

    half = W // 2

    def turn(t, sign):
        first_half, second_half = t[:, :half], t[:, half:]
        s = sine * sign
        return jnp.concatenate(
            [first_half * cosine - second_half * s, second_half * cosine + first_half * s], axis=1
        )

    kv_raw = nn(h1, wq[:, W:])
    kv = jnp.concatenate([turn(kv_raw[:, :W], 1.0), kv_raw[:, W:]], axis=1).astype(bf16)
    up = [(i, i + 1) for i in range(B - 1)]
    down = [(i + 1, i) for i in range(B - 1)]
    kv_left = lax.ppermute(kv[S - H :], "dp", up)
    kv_right = lax.ppermute(kv[:H], "dp", down)
    q = (turn(nn(h1, wq[:, :W]), 1.0) * (1.0 / math.sqrt(head_width))).astype(bf16)
    wo_low = w_out.astype(bf16)
    w_in_late, w_down_late = after((w_in, w_down), kv)
    wd_low = w_down_late.astype(bf16)
    act_low, lin_low = w_in_late[:, 0].astype(bf16), w_in_late[:, 1].astype(bf16)
    if two:
        even = (b // 2) % 2 == 0
        in_send, wo_send, g_send = after(
            (
                lax.dynamic_index_in_dim(w_in, (b // 2) % 2, 1, keepdims=False).astype(bf16),
                wo_low,
                take(cotangent, 2 * (1 - r) + c, Sr // 2),
            ),
            cosine,
            wq_send,
        )
        in_got, wo_got, g_got = to_row(in_send), to_row(wo_send), to_row(g_send)
        wd_half = take(wd_low, (b // 2) % 2, F // 2)
        h1_y = relative(after(h1, kv), "zyZw")
        q, h1_y, sk_left, sk_right, act_low, lin_low, wd_half = lax.optimization_barrier(
            (q, h1_y, sk_left, sk_right, act_low, lin_low, wd_half)
        )

    state = attend_call(own_bounds, q, sq, [kv], [sk_own], heads)
    if two:
        kv_left, kv_right, in_got, wo_got, g_got, wd_half = after(
            (kv_left, kv_right, in_got, wo_got, g_got, wd_half), state
        )
        in_other, wd_got = to_z(in_got, 1), to_row(wd_half)
    o, lse = attend_call(
        halo_bounds, q, sq, [kv_left, kv_right], [sk_left, sk_right], heads, state
    )

    if two:
        o, wd_got, wo_got, g_got = lax.optimization_barrier((o, wd_got, wo_got, g_got))
        wo = own_first(jnp.concatenate([wo_low, wo_got], axis=1), 0)
    else:
        wo = gather(wo_low, 1)

    if two:
        o_got = to_row(take(o, 1 - r, Sr))
        o_rows = jnp.concatenate([take(o, r, Sr), o_got], axis=1)
        wd_other = to_z(wd_got, 1)
        wd_got = ordered(even, wd_got, wd_other, 0)
        g_got = ordered(zcol, g_got, to_col(g_got), 0)
        g_low = jnp.concatenate([take(cotangent, r, Sr), g_got], axis=1)
        g_low = jnp.where(take(live, r, Sr)[:, None], g_low, 0)
        wds = [wd_low, wd_got]
    else:
        o_rows = lax.all_to_all(o, "row", split_axis=0, concat_axis=1, tiled=True)
        own_g = jnp.where(live_column, cotangent, 0)
        g_low = lax.all_to_all(own_g, "row", split_axis=0, concat_axis=1, tiled=True)
        wds, acts, lins = [gather(wd_low, 1)], [gather(act_low, 0)], [gather(lin_low, 0)]

    def split_nn(a, parts):
        n = a.shape[1] // len(parts)
        return sum(nn(a[:, i * n : (i + 1) * n], w) for i, w in enumerate(parts))

    def split_nt(a, parts):
        n = a.shape[1] // len(parts)
        return sum(nt(a[:, i * n : (i + 1) * n], w) for i, w in enumerate(parts))

    def wide(parts):
        return parts[0] if len(parts) == 1 else jnp.concatenate(parts, axis=1)

    x_rows = take(x_low, r, Sr).astype(f32)
    if C == 2:
        o_all = jnp.concatenate([o_rows, to_col(o_rows)], axis=1)
        wo_all = jnp.concatenate([wo, to_col(wo)], axis=0)
        x1 = x_rows + nn(o_all, wo_all)
    else:
        x1 = x_rows + lax.psum(nn(o_rows, wo), "col")
    if two:
        in_got, in_other = after((in_got, in_other), o_got)
        act_got, lin_got = jnp.where(even, in_got, in_other), jnp.where(even, in_other, in_got)
        acts, lins = [act_low, act_got], [lin_low, lin_got]

    center = x1 - jnp.mean(x1, axis=-1, keepdims=True)
    inverse_two = lax.rsqrt(jnp.mean(center * center, axis=-1, keepdims=True) + epsilon)
    n2 = center * inverse_two
    h2 = (n2 * gain_two).astype(bf16)
    a = split_nn(h2, acts)
    u = split_nn(h2, lins)
    phi = 0.5 + 0.5 * lax.erf(a * math.sqrt(0.5))
    gelu = a * phi
    slope = phi + a * jnp.exp(-0.5 * a * a) * (1.0 / math.sqrt(2.0 * math.pi))
    m = (gelu * u).astype(bf16)
    y_part = wide([nn(m, w) for w in wds])
    if two:
        n = Sr // 2
        y_half = (
            take(x1, c, n) + take(y_part, c, n) + to_col(take(y_part, 1 - c, n).astype(bf16)).astype(f32)
        ).astype(bf16)
        y_got = to_row(y_half[:, Dl:])
    else:
        y = (x1 + col_sum(y_part)).astype(bf16)
        layer_out = lax.all_to_all(y, "row", split_axis=1, concat_axis=0, tiled=True)

    dm = split_nt(g_low, wds)
    da = (dm * u * slope).astype(bf16)
    du = (dm * gelu).astype(bf16)
    dh2_part = wide([nt(da, v) + nt(du, w) for v, w in zip(acts, lins)])
    dh2 = col_sum(dh2_part)
    if two:
        g_y = relative(after(g_low, dh2_part), "yzZx")
        lower_got = to_y(product(m, g_y))
    e2 = dh2 * gain_two
    dx1 = g_low.astype(f32) + inverse_two * (
        e2
        - jnp.mean(e2, axis=-1, keepdims=True)
        - n2 * jnp.mean(e2 * n2, axis=-1, keepdims=True)
    )
    dx_low = dx1.astype(bf16)
    do_rows = nt(dx_low, wo).astype(bf16)
    if two:
        do_got = to_row(do_rows[:, W:])
        do = ordered(zrow, do_rows[:, :W], do_got, 0)
    else:
        do = lax.all_to_all(do_rows, "row", split_axis=1, concat_axis=0, tiled=True)

    if two:
        h2, da, du, o_heads, dx_late = after((h2, da, du, own_first(o_rows, 1), dx_low), do_rows)
        dx_y = relative(dx_late, "xyzZ")
        h_x = relative(h2, "xyzZ")
        gate_send = jnp.concatenate([product(da, h_x), product(du, h_x), product(o_heads, dx_y)], axis=0)
        gate_got = to_row(after(gate_send, do_got))
        pair = ordered(zrow, y_half[None, :, :Dl], after(y_got, gate_send)[None], 0)
        layer_out = ordered(zcol, pair[:, None], to_col(pair)[:, None], 1).reshape(S, Dl)
        do, layer_out = lax.optimization_barrier((do, layer_out))

    dq_part, dkv_left, dkv_right = attend_back_call(
        halo_bounds, q, do, o, lse, sq, [kv_left, kv_right], [sk_left, sk_right], heads
    )
    from_right = lax.ppermute(dkv_left, "dp", down)
    from_left = lax.ppermute(dkv_right, "dp", up)
    if two:
        lower = halved(m, g_y, after(lower_got, dq_part))
        lower_got = to_z(second(lower), 1)
        dq_part, lower = lax.optimization_barrier((dq_part, lower))
    dq, dkv = attend_back_call(own_bounds, q, do, o, lse, sq, [kv], [sk_own], heads, [dq_part])
    if two:
        gate_got = after(gate_got, dq)
        act, lin = halved(da, h_x, gate_got[:F]), halved(du, h_x, gate_got[F : 2 * F])
        proj = halved(o_heads, dx_y, gate_got[2 * F :])
        dkv, from_right, from_left, act, lin, proj, lower_got = lax.optimization_barrier(
            (dkv, from_right, from_left, act, lin, proj, lower_got)
        )
    pad = jnp.zeros((S - H, 2 * W), bf16)
    dkv = (
        dkv
        + jnp.concatenate([pad, from_right], axis=0).astype(f32)
        + jnp.concatenate([from_left, pad], axis=0).astype(f32)
    )
    dq = turn(dq * (1.0 / math.sqrt(head_width)), -1.0)
    dt = jnp.concatenate([dq, turn(dkv[:, :W], -1.0), dkv[:, W:]], axis=1).astype(bf16)
    dh1_part = nt(dt, wq)
    if two:
        query_send = product(dt, h1_y)
        query_got = to_z(query_send, 1)
        lower_got = after(lower_got, query_send, dh1_part)

    if two:
        n = S // 2
        kept = take(dh1_part, c, n) + to_col(take(dh1_part, 1 - c, n).astype(bf16)).astype(f32)
        xs = take(x_low, c, n).astype(f32)
        inv, mean = take(inverse_one, c, n), take(mean_one, c, n)
        n1 = (xs - mean) * inv
        e1 = kept * gain_one
        sums = jnp.stack([jnp.sum(e1, axis=-1), jnp.sum(e1 * n1, axis=-1)])
        sums = (sums + to_row(sums)) * (1.0 / D)
        moved = lax.ppermute(after(dx_low[:, Dl:], from_left), ("row", "col"), [(0, 2), (3, 1)])
        kept_send, moved = lax.optimization_barrier((kept[:, Dl:].astype(bf16), moved))
        mine = (kept[:, :Dl] + to_row(kept_send).astype(f32)) * gain_one[:Dl]
        base = jnp.where(r == c, dx1[:, :Dl], moved.astype(f32))
        dx = base + inv * (mine - sums[0][:, None] - n1[:, :Dl] * sums[1][:, None])
        dx = dx.astype(bf16)
        tokens_grad = ordered(zcol, dx, to_col(dx), 0)
    else:
        dh1 = lax.psum_scatter(col_sum(dh1_part), "row", scatter_dimension=1, tiled=True)
        xs = own_x.astype(f32)
        n1 = (xs - mean_one) * inverse_one
        e1 = dh1 * take(gain_attn, r, Dl)
        sums = lax.psum(jnp.stack([jnp.sum(e1, axis=-1), jnp.sum(e1 * n1, axis=-1)]), "row") / D
        base = lax.all_to_all(dx_low, "row", split_axis=1, concat_axis=0, tiled=True).astype(f32)
        tokens_grad = (
            base + inverse_one * (e1 - sums[0][:, None] - n1 * sums[1][:, None])
        ).astype(bf16)

    if two:
        def three(*parts):
            return jnp.concatenate([second(a) for a in parts], axis=0)

        def joined_three(parts, got):
            n = F
            return [joined(a, g) for a, g in zip(parts, (got[:n], got[n : 2 * n], got[2 * n :]))]

        gate_got = to_y(three(act, lin, proj))
        lower = joined(lower, lower_got)
        lower_got = to_z(second(lower), 2)
        query = halved(dt, h1_y, after(query_got, kept))
        query_got = to_y(second(query))
        act, lin, proj = joined_three((act, lin, proj), after(gate_got, query))
        gate_got = to_z(three(act, lin, proj), 1)
        lower = joined(lower, after(lower_got, act, lin, proj))
        last_got = to_row(second(lower))
        query = joined(query, after(query_got, act, lin, proj))
        query_got = to_z(second(query), 2)
        act, lin, proj = joined_three((act, lin, proj), after(gate_got, dx))
        gate_got = after(to_z(three(act, lin, proj).T, 2), tokens_grad).T
        query = joined(query, after(query_got, act, lin, proj))
        lower = joined(lower, after(last_got, dx))
        act, lin, proj = joined_three((act, lin, proj), gate_got)
        gate = jnp.stack([act.T, lin.T])
        query = query.T
        wq_rows = take(wq, b ^ (4 * r), Db)
        place = (2 * b + r) ^ (8 * r)
        wi_rows = jnp.stack(
            [jnp.where(place < 8, *(take(w, place % 8, Dd) for w in ws)) for ws in after((acts, lins), kept)]
        )
    else:

        def scatter(grad):
            return lax.psum_scatter(grad, ("dp", "row"), scatter_dimension=1, tiled=True).astype(f32)

        gate = jnp.stack([scatter(tn(da, h2).astype(bf16)).T, scatter(tn(du, h2).astype(bf16)).T])
        proj = scatter(tn(o_rows, dx_low).astype(bf16))
        lower = scatter(tn(m, g_low).astype(bf16))
        query = lax.psum_scatter(
            tn(h1, dt).astype(bf16), "dp", scatter_dimension=0, tiled=True
        ).astype(f32)
        wq_rows = take(wq, b, Db)
        wi_rows = jnp.stack([take(acts[0], b * R + r, Dd), take(lins[0], b * R + r, Dd)])

    one_part = jnp.sum(query * wq_rows.astype(f32), axis=1)
    two_part = jnp.sum(jnp.sum(gate * wi_rows.astype(f32), axis=2), axis=0)
    natural = lax.dot_general(
        query, order.astype(f32), (((1,), (1,)), ((), ())),
        precision=lax.Precision.HIGHEST, preferred_element_type=f32,
    )
    if two:
        pair = jnp.concatenate([natural, jnp.broadcast_to(one_part[:, None], (Db, 128))], axis=1)
        pair = pair.reshape(2, Dd, 3 * W + 128)
        mine = lax.dynamic_index_in_dim(pair, r, 0, keepdims=False)
        theirs = to_row(lax.dynamic_index_in_dim(pair, 1 - r, 0, keepdims=False))
        theirs = after(theirs, tokens_grad)
        one_part = mine[:, 3 * W] + theirs[:, 3 * W]
        query_out = ordered(zrow, mine[:, : 3 * W], theirs[:, : 3 * W], 1)
    else:
        one_part = take(lax.psum(one_part, "row"), r, Dd)
        query_out = lax.all_to_all(natural, "row", split_axis=0, concat_axis=1, tiled=True)
    gains = jnp.stack([one_part, two_part])
    gains = gains + to_col(gains) if C == 2 else lax.psum(gains, "col")
    gain_attn_grad = gains[0] / take(gain_attn, b * R + r, Dd)
    gain_mlp_grad = gains[1] / take(gain_mlp, b * R + r, Dd)
    return (
        layer_out,
        tokens_grad,
        gain_attn_grad,
        query_out.reshape(Dd, R * heads, 3 * head_width),
        proj,
        gain_mlp_grad,
        jnp.swapaxes(gate, 0, 1),
        lower,
    )


def solution(mesh):
    return jax.shard_map(
        local,
        mesh=mesh,
        in_specs=(
            P("dp", "row"),
            P(),
            P("row", "col", None),
            P("col", "row"),
            P(),
            P("row", None, "col"),
            P("col", "row"),
            P("dp", "row"),
            P(),
            P(),
            P(),
        ),
        out_specs=(
            P("dp", "row"),
            P("dp", "row"),
            P(("dp", "row")),
            P(("dp", "row"), "col", None),
            P("col", ("dp", "row")),
            P(("dp", "row")),
            P(("dp", "row"), None, "col"),
            P("col", ("dp", "row")),
        ),
        check_vma=False,
    )
```

```python
import functools
import math

import jax
import jax.numpy as jnp
from jax import lax
from jax.experimental import pallas as pl
from jax.experimental.pallas import tpu as pltpu
from jax.sharding import PartitionSpec as P

LONGEST = 1024
BQ = 256
BK = 256
NEG = -1e30
FAR = 1e30
epsilon = 1e-05
rope_base = 160000.0
bf16 = jnp.bfloat16
f32 = jnp.float32
SWAP = [(0, 1), (1, 0)]


def nt(a, b):
    return lax.dot_general(a, b, (((1,), (1,)), ((), ())), preferred_element_type=f32)


def tn(a, b):
    return lax.dot_general(a, b, (((0,), (0,)), ((), ())), preferred_element_type=f32)


def nn(a, b):
    return jnp.dot(a, b, preferred_element_type=f32)


def after(a, *others):
    return lax.optimization_barrier((a, *others))[0]


def half_mask(width, heads, head):
    lane = lax.broadcasted_iota(jnp.int32, (1, width), 1)
    half = width // 2
    lane = jnp.where(lane >= half, lane - half, lane)
    step = half // heads
    return (lane >= head * step) & (lane < (head + 1) * step)


def whole_mask(width, heads, head):
    lane = lax.broadcasted_iota(jnp.int32, (1, width), 1)
    step = width // heads
    return (lane >= head * step) & (lane < (head + 1) * step)


def stack_heads(block, heads, mask_of):
    zero = jnp.zeros_like(block)
    width = block.shape[1]
    return jnp.concatenate(
        [jnp.where(mask_of(width, heads, h), block, zero) for h in range(heads)], axis=0
    )


def same_segment(key_seg, query_seg, heads):
    tile = key_seg
    lanes = query_seg.shape[1]
    if lanes > tile.shape[1]:
        tile = jnp.concatenate([tile] * (lanes // tile.shape[1]), axis=1)
    same = tile == query_seg
    return jnp.concatenate([same] * heads, axis=1) if heads > 1 else same


def forward_kernel(heads, sets, final, bounds, *refs):
    refs = list(refs)
    q_ref, sq_ref = refs[:2]
    kv_refs = refs[2 : 2 + sets]
    sk_refs = refs[2 + sets : 2 + 2 * sets]
    rest = refs[2 + 2 * sets :]
    if final:
        acc_in, ml_in, o_ref, lse_ref = rest[:4]
        acc, m_ref, l_ref = rest[4:7]
        vt_refs = rest[7:]
    else:
        acc, ml_ref = rest[:2]
        m_ref, l_ref = rest[2:4]
        vt_refs = rest[4:]
    step = pl.program_id(0)
    rows, width = q_ref.shape
    each = width // heads

    @pl.when(step == 0)
    def _():
        for kv, vt in zip(kv_refs, vt_refs):
            for j in range(kv.shape[0] // BK):
                vt[:, j * BK : (j + 1) * BK] = kv[j * BK : (j + 1) * BK, width:].T

    if final:
        acc[...] = acc_in[0]
        m_ref[...] = ml_in[0, 0:1]
        l_ref[...] = ml_in[0, 1:2]
    else:
        acc[...] = jnp.zeros_like(acc)
        m_ref[...] = jnp.full_like(m_ref, NEG)
        l_ref[...] = jnp.zeros_like(l_ref)
    queries = stack_heads(q_ref[...], heads, half_mask)
    query_seg = sq_ref[0]
    target = acc if final else acc.at[0]

    for s in range(sets):
        kv, sk, vt = kv_refs[s], sk_refs[s], vt_refs[s]

        def body(j, carry):
            first = pl.multiple_of(j * BK, BK)
            keys = kv[pl.ds(first, BK), 0:width]
            scores = nt(keys, queries)
            same = same_segment(sk[pl.ds(first, BK), :], query_seg, heads)
            scores = jnp.where(same, scores, NEG)
            before = m_ref[...]
            top = jnp.maximum(before, jnp.max(scores, axis=0, keepdims=True))
            raised = jnp.exp(scores - top)
            shrink = jnp.exp(before - top)
            m_ref[...] = top
            l_ref[...] = l_ref[...] * shrink + jnp.sum(raised, axis=0, keepdims=True)
            low = raised.astype(bf16)
            for h in range(heads):
                part = nn(
                    vt[h * each : (h + 1) * each, pl.ds(first, BK)],
                    low[:, h * rows : (h + 1) * rows],
                )
                hold = target[h * each : (h + 1) * each, :]
                target[h * each : (h + 1) * each, :] = (
                    hold * shrink[:, h * rows : (h + 1) * rows] + part
                )
            return carry

        lax.fori_loop(
            bounds[(step * sets + s) * 2], bounds[(step * sets + s) * 2 + 1], body, 0
        )

    if final:
        live = query_seg >= 0
        total = l_ref[...]
        live_all = jnp.concatenate([live] * heads, axis=1) if heads > 1 else live
        total = jnp.where(live_all, total, 1.0)
        inverse = jnp.where(live_all, 1.0 / total, 0.0)
        for h in range(heads):
            acc[h * each : (h + 1) * each, :] = (
                acc[h * each : (h + 1) * each, :] * inverse[:, h * rows : (h + 1) * rows]
            )
        o_ref[...] = acc[...].T.astype(bf16)
        lse_ref[0] = jnp.where(live_all, m_ref[...] + jnp.log(total), FAR)
    else:
        ml_ref[0, 0:1] = m_ref[...]
        ml_ref[0, 1:2] = l_ref[...]


def cost(products, q, kvs):
    pairs = q.shape[0]
    return pl.CostEstimate(
        flops=4 * products * pairs * q.shape[1],
        bytes_accessed=2 * sum(a.size for a in kvs) + 4 * q.size,
        transcendentals=4 * pairs,
    )


def whole(shape):
    zeros = (0,) * len(shape)
    return pl.BlockSpec(shape, lambda i, *_: zeros)


def attend_call(bounds, q, sq, kvs, sks, heads, state=None):
    count = q.shape[0] // BQ
    width = q.shape[1]
    sets = len(kvs)
    final = state is not None
    row_spec = pl.BlockSpec((BQ, width), lambda i, *_: (i, 0))
    acc_spec = pl.BlockSpec((1, width, BQ), lambda i, *_: (i, 0, 0))
    ml_spec = pl.BlockSpec((1, 2, heads * BQ), lambda i, *_: (i, 0, 0))
    in_specs = [row_spec, pl.BlockSpec((1, 1, BQ), lambda i, *_: (i, 0, 0))]
    in_specs += [whole(a.shape) for a in kvs] + [whole(a.shape) for a in sks]
    scratch = [pltpu.VMEM((1, heads * BQ), f32)] * 2
    scratch += [pltpu.VMEM((width, a.shape[0]), bf16) for a in kvs]
    if final:
        in_specs += [acc_spec, ml_spec]
        out_specs = [row_spec, pl.BlockSpec((1, 1, heads * BQ), lambda i, *_: (i, 0, 0))]
        out_shape = [
            jax.ShapeDtypeStruct(q.shape, bf16),
            jax.ShapeDtypeStruct((count, 1, heads * BQ), f32),
        ]
        scratch = [pltpu.VMEM((width, BQ), f32)] + scratch
    else:
        out_specs = [acc_spec, ml_spec]
        out_shape = [
            jax.ShapeDtypeStruct((count, width, BQ), f32),
            jax.ShapeDtypeStruct((count, 2, heads * BQ), f32),
        ]
    return pl.pallas_call(
        functools.partial(forward_kernel, heads, sets, final),
        grid_spec=pltpu.PrefetchScalarGridSpec(
            num_scalar_prefetch=1,
            grid=(count,),
            in_specs=in_specs,
            out_specs=out_specs,
            scratch_shapes=scratch,
        ),
        out_shape=out_shape,
        cost_estimate=cost(4, q, kvs),
        name="attend_final" if final else "attend_own",
    )(bounds, q, sq, *kvs, *sks, *(state or ()))


def backward_kernel(heads, sets, final, bounds, *refs):
    refs = list(refs)
    q_ref, do_ref, o_ref, lse_ref, sq_ref = refs[:5]
    kv_refs = refs[5 : 5 + sets]
    sk_refs = refs[5 + sets : 5 + 2 * sets]
    rest = refs[5 + 2 * sets :]
    if final:
        dq_in, dq_ref = rest[0], rest[1]
        dkv_refs = rest[2 : 2 + sets]
        dq_acc = rest[2 + sets]
        kt_refs = rest[3 + sets : 3 + 2 * sets]
        sums = dkv_refs
    else:
        dq_ref = rest[0]
        dkv_refs = rest[1 : 1 + sets]
        dq_acc = rest[1 + sets]
        kt_refs = rest[2 + sets : 2 + 2 * sets]
        sums = rest[2 + 2 * sets :]
    step = pl.program_id(0)
    rows, width = q_ref.shape
    each = width // heads
    half = width // 2
    piece = half // heads

    @pl.when(step == 0)
    def _():
        for kv, kt, total in zip(kv_refs, kt_refs, sums):
            total[...] = jnp.zeros_like(total)
            for j in range(kv.shape[0] // BK):
                kt[:, j * BK : (j + 1) * BK] = kv[j * BK : (j + 1) * BK, :width].T

    if final:
        dq_acc[...] = dq_in[0]
    else:
        dq_acc[...] = jnp.zeros_like(dq_acc)
    grads = do_ref[...]
    queries = stack_heads(q_ref[...], heads, half_mask)
    outs = stack_heads(grads, heads, whole_mask)
    query_seg = sq_ref[0]
    lse = lse_ref[0]
    product = (grads.astype(f32) * o_ref[...].astype(f32)).T
    delta = jnp.concatenate(
        [
            jnp.sum(product[h * each : (h + 1) * each], axis=0, keepdims=True)
            for h in range(heads)
        ],
        axis=1,
    )

    for s in range(sets):
        kv, sk, kt, total = kv_refs[s], sk_refs[s], kt_refs[s], sums[s]

        def body(j, carry):
            first = pl.multiple_of(j * BK, BK)
            keys = kv[pl.ds(first, BK), 0:width]
            values = kv[pl.ds(first, BK), width : 2 * width]
            scores = nt(keys, queries)
            same = same_segment(sk[pl.ds(first, BK), :], query_seg, heads)
            probs = jnp.where(same, jnp.exp(scores - lse), 0.0)
            grad_probs = nt(values, outs)
            grad_scores = (probs * (grad_probs - delta)).astype(bf16)
            low = probs.astype(bf16)
            total[pl.ds(first, BK), width : 2 * width] += nn(low, outs)
            total[pl.ds(first, BK), 0:width] += nn(grad_scores, queries)
            for h in range(heads):
                column = grad_scores[:, h * rows : (h + 1) * rows]
                for lead in (h * piece, half + h * piece):
                    dq_acc[lead : lead + piece, :] += nn(
                        kt[lead : lead + piece, pl.ds(first, BK)], column
                    )
            return carry

        lax.fori_loop(
            bounds[(step * sets + s) * 2], bounds[(step * sets + s) * 2 + 1], body, 0
        )

    if final:
        dq_ref[...] = dq_acc[...].T
    else:
        dq_ref[0] = dq_acc[...]

        @pl.when(step == pl.num_programs(0) - 1)
        def _():
            for total, out in zip(sums, dkv_refs):
                out[...] = total[...].astype(bf16)


def attend_back_call(bounds, q, do, o, lse, sq, kvs, sks, heads, state=None):
    count = q.shape[0] // BQ
    width = q.shape[1]
    sets = len(kvs)
    final = state is not None
    row_spec = pl.BlockSpec((BQ, width), lambda i, *_: (i, 0))
    acc_spec = pl.BlockSpec((1, width, BQ), lambda i, *_: (i, 0, 0))
    in_specs = [row_spec] * 3 + [
        pl.BlockSpec((1, 1, heads * BQ), lambda i, *_: (i, 0, 0)),
        pl.BlockSpec((1, 1, BQ), lambda i, *_: (i, 0, 0)),
    ]
    in_specs += [whole(a.shape) for a in kvs] + [whole(a.shape) for a in sks]
    scratch = [pltpu.VMEM((width, BQ), f32)]
    scratch += [pltpu.VMEM((width, a.shape[0]), bf16) for a in kvs]
    if final:
        in_specs += [acc_spec]
        out_specs = [row_spec]
        out_shape = [jax.ShapeDtypeStruct(q.shape, f32)]
    else:
        out_specs = [acc_spec]
        out_shape = [jax.ShapeDtypeStruct((count, width, BQ), f32)]
        scratch += [pltpu.VMEM(a.shape, f32) for a in kvs]
    out_specs += [whole(a.shape) for a in kvs]
    out_shape += [jax.ShapeDtypeStruct(a.shape, f32 if final else bf16) for a in kvs]
    return pl.pallas_call(
        functools.partial(backward_kernel, heads, sets, final),
        grid_spec=pltpu.PrefetchScalarGridSpec(
            num_scalar_prefetch=1,
            grid=(count,),
            in_specs=in_specs,
            out_specs=out_specs,
            scratch_shapes=scratch,
        ),
        out_shape=out_shape,
        cost_estimate=cost(10, q, kvs),
        name="back_own" if final else "back_halo",
    )(bounds, q, do, o, lse, sq, *kvs, *sks, *(state or ()))


def place_tables(seq_lengths, seq_offsets, first, count):
    place = first + jnp.arange(count, dtype=jnp.int32)
    ends = seq_offsets + seq_lengths
    inside = (place[:, None] >= seq_offsets[None, :]) & (place[:, None] < ends[None, :])
    live = jnp.any(inside, axis=1)
    index = jnp.arange(seq_offsets.shape[0], dtype=jnp.int32)
    segment = jnp.sum(jnp.where(inside, index[None, :], 0), axis=1)
    start = jnp.sum(jnp.where(inside, seq_offsets[None, :], 0), axis=1)
    end = jnp.sum(jnp.where(inside, ends[None, :], 0), axis=1)
    return live, segment, start, end, place


def qkv_order(heads, head_width):
    width = heads * head_width
    half = head_width // 2
    new = jnp.arange(3 * width, dtype=jnp.int32)
    kind = new // width
    inner = new % width
    side = inner // (width // 2)
    pair_head = (inner % (width // 2)) // half
    pair_old = pair_head * 3 * head_width + kind * head_width + side * half + inner % half
    value_old = (inner // head_width) * 3 * head_width + 2 * head_width + inner % head_width
    old = jnp.where(kind == 2, value_old, pair_old)
    return (old[None, :] == new[:, None]).astype(bf16)


def local(
    tokens,
    gain_attn,
    w_qkv,
    w_out,
    gain_mlp,
    w_in,
    w_down,
    cotangent,
    seq_lengths,
    seq_offsets,
    deal,
):
    R, C, B = lax.axis_size("row"), lax.axis_size("col"), lax.axis_size("dp")
    r, c, b = lax.axis_index("row"), lax.axis_index("col"), lax.axis_index("dp")
    S, Dl = tokens.shape
    D = Dl * R
    two = R == 2 and C == 2 and B == 8
    heads = w_qkv.shape[1] // R
    head_width = w_qkv.shape[2] // 3
    W = heads * head_width
    F = w_down.shape[0]
    H = LONGEST
    Sr = S // R
    zrow, zcol = (r == 0), (c == 0)

    def to_row(a):
        return lax.ppermute(a, "row", SWAP)

    def to_col(a):
        return lax.ppermute(a, "col", SWAP)

    def ordered(flag, mine, theirs, axis):
        return jnp.where(
            flag,
            jnp.concatenate([mine, theirs], axis=axis),
            jnp.concatenate([theirs, mine], axis=axis),
        )

    def own_first(a, axis):
        if not two:
            return a
        n = a.shape[axis] // 2
        return jnp.where(zrow, a, jnp.roll(a, n, axis=axis))

    def take(a, index, size, axis=0):
        return lax.dynamic_slice_in_dim(a, index * size, size, axis)

    def partner(a):
        n = a.shape[0] // 2
        got = to_row(take(a, c, n))
        return ordered(zcol, got, to_col(got), 0)

    def gather(a, axis):
        if two:
            return jnp.concatenate([a, to_row(a)], axis=axis)
        return lax.all_gather(a, "row", axis=axis, tiled=True)

    def col_sum(a):
        return a + to_col(a.astype(bf16)).astype(f32) if C == 2 else lax.psum(a, "col")

    live_x, seg_x, start_x, end_x, place_x = place_tables(seq_lengths, seq_offsets, b * S - H, S + 2 * H)
    key_seg = jnp.broadcast_to(jnp.where(live_x, seg_x, -2)[:, None], (S + 2 * H, 128))
    sk_left, sk_own, sk_right = key_seg[:H], key_seg[H : H + S], key_seg[H + S :]
    live = live_x[H : H + S]
    nq = S // BQ
    sq = jnp.where(live, seg_x[H : H + S], -1).reshape(nq, 1, BQ)
    first = jnp.min(jnp.where(live, start_x[H : H + S] - b * S, 4 * S).reshape(nq, BQ), axis=1)
    last = jnp.max(jnp.where(live, end_x[H : H + S] - b * S, -4 * S).reshape(nq, BQ), axis=1)
    own_low = jnp.clip(first, 0, S) // BK
    own_high = (jnp.clip(last, 0, S) + BK - 1) // BK
    left_low = jnp.clip(first + H, 0, H) // BK
    right_high = (jnp.clip(last - S, 0, H) + BK - 1) // BK
    own_bounds = jnp.stack([own_low, own_high], axis=1).reshape(-1).astype(jnp.int32)
    zero = jnp.zeros_like(left_low)
    halo_bounds = (
        jnp.stack([left_low, zero + H // BK, zero, right_high], axis=1).reshape(-1).astype(jnp.int32)
    )
    position = jnp.where(live, place_x[H : H + S] - start_x[H : H + S], 0)
    freq = rope_base ** (-(jnp.arange(0, head_width, 2, dtype=f32) / head_width))
    angle = position.astype(f32)[:, None] * jnp.tile(freq, heads)[None, :]
    cosine, sine = lax.optimization_barrier((jnp.cos(angle), jnp.sin(angle)))

    live_column = live[:, None]
    if two:
        x_got = partner(tokens)
        x_low = jnp.where(live_column, jnp.concatenate([tokens, x_got], axis=1), 0)
    else:
        own_x = jnp.where(live_column, tokens, 0)
        x_low = lax.all_gather(own_x, "row", axis=1, tiled=True)

    wq_low = w_qkv.reshape(Dl, R * 3 * W).astype(bf16)
    if two:
        wq_mine, wq_send = take(wq_low, r, 3 * W, 1), take(wq_low, 1 - r, 3 * W, 1)
        wq_got = to_row(wq_send)
    else:
        wq = lax.all_to_all(wq_low, "row", split_axis=1, concat_axis=0, tiled=True)
    order = qkv_order(heads, head_width)

    gain_one = own_first(gain_attn, 0)
    gain_two = own_first(gain_mlp, 0)

    Db = D // B
    Dd = D // (B * R)
    if two:
        y_bit, z_bits = b % 2, b // 2

        def relative(a, bits):
            n = jnp.arange(D, dtype=jnp.int32)
            rel = {"w": 0 * n, "x": 0 * n}
            for i, bit in enumerate(bits):
                rel[bit] = n // (D >> (i + 1)) % 2
            z_rel = 2 * rel["Z"] + rel["z"]
            column = ((z_bits ^ z_rel) * 2 + (y_bit ^ rel["y"])) * Db + n % Dd
            column = column + (rel["w"] if "w" in bits else r ^ rel["x"]) * Dd
            column = column ^ (r * (D // 2))
            return nn(a, (n[:, None] == column[None, :]).astype(bf16)).astype(bf16)

        def to_y(a):
            return lax.ppermute(a, "dp", [(i, i ^ 1) for i in range(B)])

        def to_z(a, j):
            return lax.ppermute(a, "dp", [(i, i ^ (2 * j)) for i in range(B)])

        def first(a):
            return a[:, : a.shape[1] // 2]

        def second(a):
            return a[:, a.shape[1] // 2 :].astype(bf16)

        def product(left, right):
            return tn(left, second(right)).astype(bf16)

        def halved(left, right, got):
            return tn(left, first(right)) + got.astype(f32)

        def joined(part, got):
            return first(part).astype(f32) + got.astype(f32)

    x = x_low.astype(f32)
    center = x - jnp.mean(x, axis=-1, keepdims=True)
    inverse_one = lax.rsqrt(jnp.mean(center * center, axis=-1, keepdims=True) + epsilon)
    mean_one = jnp.mean(x, axis=-1, keepdims=True)
    h1 = (center * inverse_one * gain_one).astype(bf16)
    if two:
        h1, wq_mine, wq_got = lax.optimization_barrier((h1, wq_mine, wq_got))
        wq = jnp.concatenate([wq_mine, wq_got], axis=0)
    wq = nn(wq, order).astype(bf16)

    half = W // 2

    def turn(t, sign):
        first_half, second_half = t[:, :half], t[:, half:]
        s = sine * sign
        return jnp.concatenate(
            [first_half * cosine - second_half * s, second_half * cosine + first_half * s], axis=1
        )

    kv_raw = nn(h1, wq[:, W:])
    kv = jnp.concatenate([turn(kv_raw[:, :W], 1.0), kv_raw[:, W:]], axis=1).astype(bf16)
    up = [(i, i + 1) for i in range(B - 1)]
    down = [(i + 1, i) for i in range(B - 1)]
    kv_left = lax.ppermute(kv[S - H :], "dp", up)
    kv_right = lax.ppermute(kv[:H], "dp", down)
    q = (turn(nn(h1, wq[:, :W]), 1.0) * (1.0 / math.sqrt(head_width))).astype(bf16)
    wo_low = w_out.astype(bf16)
    w_in_late, w_down_late = after((w_in, w_down), kv)
    wd_low = w_down_late.astype(bf16)
    act_low, lin_low = w_in_late[:, 0].astype(bf16), w_in_late[:, 1].astype(bf16)
    if two:
        even = (b // 2) % 2 == 0
        in_send, wo_send, g_send = after(
            (
                lax.dynamic_index_in_dim(w_in, (b // 2) % 2, 1, keepdims=False).astype(bf16),
                wo_low,
                take(cotangent, 2 * (1 - r) + c, Sr // 2),
            ),
            cosine,
            wq_send,
        )
        in_got, wo_got, g_got = to_row(in_send), to_row(wo_send), to_row(g_send)
        wd_half = take(wd_low, (b // 2) % 2, F // 2)
        h1_y = relative(after(h1, kv), "zyZw")
        q, h1_y, sk_left, sk_right, act_low, lin_low, wd_half = lax.optimization_barrier(
            (q, h1_y, sk_left, sk_right, act_low, lin_low, wd_half)
        )

    state = attend_call(own_bounds, q, sq, [kv], [sk_own], heads)
    if two:
        kv_left, kv_right, in_got, wo_got, g_got, wd_half = after(
            (kv_left, kv_right, in_got, wo_got, g_got, wd_half), state
        )
        in_other, wd_got = to_z(in_got, 1), to_row(wd_half)
    o, lse = attend_call(
        halo_bounds, q, sq, [kv_left, kv_right], [sk_left, sk_right], heads, state
    )

    if two:
        o, wd_got, wo_got, g_got = lax.optimization_barrier((o, wd_got, wo_got, g_got))
        wo = own_first(jnp.concatenate([wo_low, wo_got], axis=1), 0)
    else:
        wo = gather(wo_low, 1)

    if two:
        o_got = to_row(take(o, 1 - r, Sr))
        o_rows = jnp.concatenate([take(o, r, Sr), o_got], axis=1)
        wd_other = to_z(wd_got, 1)
        wd_got = ordered(even, wd_got, wd_other, 0)
        g_got = ordered(zcol, g_got, to_col(g_got), 0)
        g_low = jnp.concatenate([take(cotangent, r, Sr), g_got], axis=1)
        g_low = jnp.where(take(live, r, Sr)[:, None], g_low, 0)
        wds = [wd_low, wd_got]
    else:
        o_rows = lax.all_to_all(o, "row", split_axis=0, concat_axis=1, tiled=True)
        own_g = jnp.where(live_column, cotangent, 0)
        g_low = lax.all_to_all(own_g, "row", split_axis=0, concat_axis=1, tiled=True)
        wds, acts, lins = [gather(wd_low, 1)], [gather(act_low, 0)], [gather(lin_low, 0)]

    def split_nn(a, parts):
        n = a.shape[1] // len(parts)
        return sum(nn(a[:, i * n : (i + 1) * n], w) for i, w in enumerate(parts))

    def split_nt(a, parts):
        n = a.shape[1] // len(parts)
        return sum(nt(a[:, i * n : (i + 1) * n], w) for i, w in enumerate(parts))

    def wide(parts):
        return parts[0] if len(parts) == 1 else jnp.concatenate(parts, axis=1)

    x_rows = take(x_low, r, Sr).astype(f32)
    if C == 2:
        o_all = jnp.concatenate([o_rows, to_col(o_rows)], axis=1)
        wo_all = jnp.concatenate([wo, to_col(wo)], axis=0)
        x1 = x_rows + nn(o_all, wo_all)
    else:
        x1 = x_rows + lax.psum(nn(o_rows, wo), "col")
    if two:
        in_got, in_other = after((in_got, in_other), o_got)
        act_got, lin_got = jnp.where(even, in_got, in_other), jnp.where(even, in_other, in_got)
        acts, lins = [act_low, act_got], [lin_low, lin_got]

    center = x1 - jnp.mean(x1, axis=-1, keepdims=True)
    inverse_two = lax.rsqrt(jnp.mean(center * center, axis=-1, keepdims=True) + epsilon)
    n2 = center * inverse_two
    h2 = (n2 * gain_two).astype(bf16)
    a = split_nn(h2, acts)
    u = split_nn(h2, lins)
    phi = 0.5 + 0.5 * lax.erf(a * math.sqrt(0.5))
    gelu = a * phi
    slope = phi + a * jnp.exp(-0.5 * a * a) * (1.0 / math.sqrt(2.0 * math.pi))
    m = (gelu * u).astype(bf16)
    y_part = wide([nn(m, w) for w in wds])
    if two:
        n = Sr // 2
        y_half = (
            take(x1, c, n) + take(y_part, c, n) + to_col(take(y_part, 1 - c, n).astype(bf16)).astype(f32)
        ).astype(bf16)
        y_got = to_row(y_half[:, Dl:])
    else:
        y = (x1 + col_sum(y_part)).astype(bf16)
        layer_out = lax.all_to_all(y, "row", split_axis=1, concat_axis=0, tiled=True)

    dm = split_nt(g_low, wds)
    da = (dm * u * slope).astype(bf16)
    du = (dm * gelu).astype(bf16)
    dh2_part = wide([nt(da, v) + nt(du, w) for v, w in zip(acts, lins)])
    dh2 = col_sum(dh2_part)
    if two:
        g_y = relative(after(g_low, dh2_part), "yzZx")
        lower_got = to_y(product(m, g_y))
    e2 = dh2 * gain_two
    dx1 = g_low.astype(f32) + inverse_two * (
        e2
        - jnp.mean(e2, axis=-1, keepdims=True)
        - n2 * jnp.mean(e2 * n2, axis=-1, keepdims=True)
    )
    dx_low = dx1.astype(bf16)
    do_rows = nt(dx_low, wo).astype(bf16)
    if two:
        do_got = to_row(do_rows[:, W:])
        do = ordered(zrow, do_rows[:, :W], do_got, 0)
    else:
        do = lax.all_to_all(do_rows, "row", split_axis=1, concat_axis=0, tiled=True)

    if two:
        h2, da, du, o_heads, dx_late = after((h2, da, du, own_first(o_rows, 1), dx_low), do_rows)
        dx_y = relative(dx_late, "xyzZ")
        h_x = relative(h2, "xyzZ")
        gate_send = jnp.concatenate([product(da, h_x), product(du, h_x), product(o_heads, dx_y)], axis=0)
        gate_got = to_row(after(gate_send, do_got))
        pair = ordered(zrow, y_half[None, :, :Dl], after(y_got, gate_send)[None], 0)
        layer_out = ordered(zcol, pair[:, None], to_col(pair)[:, None], 1).reshape(S, Dl)
        do, layer_out = lax.optimization_barrier((do, layer_out))

    dq_part, dkv_left, dkv_right = attend_back_call(
        halo_bounds, q, do, o, lse, sq, [kv_left, kv_right], [sk_left, sk_right], heads
    )
    from_right = lax.ppermute(dkv_left, "dp", down)
    from_left = lax.ppermute(dkv_right, "dp", up)
    if two:
        lower = halved(m, g_y, after(lower_got, dq_part))
        lower_got = to_z(second(lower), 1)
        dq_part, lower = lax.optimization_barrier((dq_part, lower))
    dq, dkv = attend_back_call(own_bounds, q, do, o, lse, sq, [kv], [sk_own], heads, [dq_part])
    if two:
        gate_got = after(gate_got, dq)
        act, lin = halved(da, h_x, gate_got[:F]), halved(du, h_x, gate_got[F : 2 * F])
        proj = halved(o_heads, dx_y, gate_got[2 * F :])
        dkv, from_right, from_left, act, lin, proj, lower_got = lax.optimization_barrier(
            (dkv, from_right, from_left, act, lin, proj, lower_got)
        )
    pad = jnp.zeros((S - H, 2 * W), bf16)
    dkv = (
        dkv
        + jnp.concatenate([pad, from_right], axis=0).astype(f32)
        + jnp.concatenate([from_left, pad], axis=0).astype(f32)
    )
    dq = turn(dq * (1.0 / math.sqrt(head_width)), -1.0)
    dt = jnp.concatenate([dq, turn(dkv[:, :W], -1.0), dkv[:, W:]], axis=1).astype(bf16)
    dh1_part = nt(dt, wq)
    if two:
        query_send = product(dt, h1_y)
        query_got = to_z(query_send, 1)
        lower_got = after(lower_got, query_send, dh1_part)

    if two:
        n = S // 2
        kept = take(dh1_part, c, n) + to_col(take(dh1_part, 1 - c, n).astype(bf16)).astype(f32)
        xs = take(x_low, c, n).astype(f32)
        inv, mean = take(inverse_one, c, n), take(mean_one, c, n)
        n1 = (xs - mean) * inv
        e1 = kept * gain_one
        sums = jnp.stack([jnp.sum(e1, axis=-1), jnp.sum(e1 * n1, axis=-1)])
        sums = (sums + to_row(sums)) * (1.0 / D)
        moved = lax.ppermute(after(dx_low[:, Dl:], from_left), ("row", "col"), [(0, 2), (3, 1)])
        kept_send, moved = lax.optimization_barrier((kept[:, Dl:].astype(bf16), moved))
        mine = (kept[:, :Dl] + to_row(kept_send).astype(f32)) * gain_one[:Dl]
        base = jnp.where(r == c, dx1[:, :Dl], moved.astype(f32))
        dx = base + inv * (mine - sums[0][:, None] - n1[:, :Dl] * sums[1][:, None])
        dx = dx.astype(bf16)
        tokens_grad = ordered(zcol, dx, to_col(dx), 0)
    else:
        dh1 = lax.psum_scatter(col_sum(dh1_part), "row", scatter_dimension=1, tiled=True)
        xs = own_x.astype(f32)
        n1 = (xs - mean_one) * inverse_one
        e1 = dh1 * take(gain_attn, r, Dl)
        sums = lax.psum(jnp.stack([jnp.sum(e1, axis=-1), jnp.sum(e1 * n1, axis=-1)]), "row") / D
        base = lax.all_to_all(dx_low, "row", split_axis=1, concat_axis=0, tiled=True).astype(f32)
        tokens_grad = (
            base + inverse_one * (e1 - sums[0][:, None] - n1 * sums[1][:, None])
        ).astype(bf16)

    if two:
        def three(*parts):
            return jnp.concatenate([second(a) for a in parts], axis=0)

        def joined_three(parts, got):
            n = F
            return [joined(a, g) for a, g in zip(parts, (got[:n], got[n : 2 * n], got[2 * n :]))]

        gate_got = to_y(three(act, lin, proj))
        lower = joined(lower, lower_got)
        lower_got = to_z(second(lower), 2)
        query = halved(dt, h1_y, after(query_got, kept))
        query_got = to_y(second(query))
        act, lin, proj = joined_three((act, lin, proj), after(gate_got, query))
        gate_got = to_z(three(act, lin, proj), 1)
        lower = joined(lower, after(lower_got, act, lin, proj))
        last_got = to_row(second(lower))
        query = joined(query, after(query_got, act, lin, proj))
        query_got = to_z(second(query), 2)
        act, lin, proj = joined_three((act, lin, proj), after(gate_got, dx))
        gate_got = after(to_z(three(act, lin, proj).T, 2), tokens_grad)
        query = joined(query, after(query_got, act, lin, proj))
        lower = joined(lower, after(last_got, dx))
        gate = jnp.stack(
            [
                first(w).astype(f32).T + gate_got[:, i * F : (i + 1) * F].astype(f32)
                for i, w in enumerate((act, lin))
            ]
        )
        proj = joined(proj, gate_got[:, 2 * F :].T)
        query = query.T
        wq_rows = take(wq, b ^ (4 * r), Db)
        place = (2 * b + r) ^ (8 * r)
        wi_rows = jnp.stack(
            [jnp.where(place < 8, *(take(w, place % 8, Dd) for w in ws)) for ws in after((acts, lins), kept)]
        )
    else:

        def scatter(grad):
            return lax.psum_scatter(grad, ("dp", "row"), scatter_dimension=1, tiled=True).astype(f32)

        gate = jnp.stack([scatter(tn(da, h2).astype(bf16)).T, scatter(tn(du, h2).astype(bf16)).T])
        proj = scatter(tn(o_rows, dx_low).astype(bf16))
        lower = scatter(tn(m, g_low).astype(bf16))
        query = lax.psum_scatter(
            tn(h1, dt).astype(bf16), "dp", scatter_dimension=0, tiled=True
        ).astype(f32)
        wq_rows = take(wq, b, Db)
        wi_rows = jnp.stack([take(acts[0], b * R + r, Dd), take(lins[0], b * R + r, Dd)])

    one_part = jnp.sum(query * wq_rows.astype(f32), axis=1)
    two_part = jnp.sum(jnp.sum(gate * wi_rows.astype(f32), axis=2), axis=0)
    natural = lax.dot_general(
        query, order.astype(f32), (((1,), (1,)), ((), ())),
        precision=lax.Precision.HIGHEST, preferred_element_type=f32,
    )
    if two:
        pair = jnp.concatenate([natural, jnp.broadcast_to(one_part[:, None], (Db, 128))], axis=1)
        pair = pair.reshape(2, Dd, 3 * W + 128)
        mine = lax.dynamic_index_in_dim(pair, r, 0, keepdims=False)
        theirs = to_row(lax.dynamic_index_in_dim(pair, 1 - r, 0, keepdims=False))
        theirs = after(theirs, tokens_grad)
        one_part = mine[:, 3 * W] + theirs[:, 3 * W]
        query_out = ordered(zrow, mine[:, : 3 * W], theirs[:, : 3 * W], 1)
    else:
        one_part = take(lax.psum(one_part, "row"), r, Dd)
        query_out = lax.all_to_all(natural, "row", split_axis=0, concat_axis=1, tiled=True)
    gains = jnp.stack([one_part, two_part])
    gains = gains + to_col(gains) if C == 2 else lax.psum(gains, "col")
    gain_attn_grad = gains[0] / take(gain_attn, b * R + r, Dd)
    gain_mlp_grad = gains[1] / take(gain_mlp, b * R + r, Dd)
    return (
        layer_out,
        tokens_grad,
        gain_attn_grad,
        query_out.reshape(Dd, R * heads, 3 * head_width),
        proj,
        gain_mlp_grad,
        jnp.swapaxes(gate, 0, 1),
        lower,
    )


def solution(mesh):
    return jax.shard_map(
        local,
        mesh=mesh,
        in_specs=(
            P("dp", "row"),
            P(),
            P("row", "col", None),
            P("col", "row"),
            P(),
            P("row", None, "col"),
            P("col", "row"),
            P("dp", "row"),
            P(),
            P(),
            P(),
        ),
        out_specs=(
            P("dp", "row"),
            P("dp", "row"),
            P(("dp", "row")),
            P(("dp", "row"), "col", None),
            P("col", ("dp", "row")),
            P(("dp", "row")),
            P(("dp", "row"), None, "col"),
            P("col", ("dp", "row")),
        ),
        check_vma=False,
    )
```
